32 devices in a mesh: dp: 4 (over x, core), fsdp: 8 (over z, y).
Axes of the slice: x: 2, y: 2, z: 4, core: 2. Of those that a mesh axis runs over, the one named last changes fastest.
Arguments:
- tokens: bfloat16 [32768, 768], P(('dp', 'fsdp')), may hold values from -6 to 6
- segment_ids: int32 [32, 1024], P(('dp', 'fsdp')), may hold values from 0 to 7, never falling along the last dimension, each value on 1 to 256 neighbouring positions
- w_qkv: bfloat16 [768, 2304], P('dp', 'fsdp'), may hold values from -0.21875 to 0.21875
- w_out: bfloat16 [768, 768], P('dp', 'fsdp'), may hold values from -0.875 to 0.875
- w_in: bfloat16 [768, 3072], P('dp', 'fsdp'), may hold values from -0.21875 to 0.21875
- w_back: bfloat16 [3072, 768], P('dp', 'fsdp'), may hold values from -0.109375 to 0.109375
- biases: bfloat16 [6, 768], P(None, ('dp', 'fsdp')), may hold values from -1.5 to 1.5
- in_bias: bfloat16 [3072], P(('dp', 'fsdp')), may hold values from -1.5 to 1.5
- gains: bfloat16 [2, 768], P(None, ('dp', 'fsdp')), may hold values from 0.5 to 1.5
- out_grad: bfloat16 [32768, 768], P(('dp', 'fsdp')), may hold values from -6 to 6
Outputs:
- layer_out: bfloat16 [32768, 768], P(('dp', 'fsdp'))
- tokens_grad: bfloat16 [32768, 768], P(('dp', 'fsdp'))
- grad_qkv: float32 [768, 2304], P('dp', 'fsdp')
- grad_out: float32 [768, 768], P('dp', 'fsdp')
- grad_in: float32 [768, 3072], P('dp', 'fsdp')
- grad_back: float32 [3072, 768], P('dp', 'fsdp')
- grad_biases: float32 [6, 768], P(None, ('dp', 'fsdp'))
- grad_in_bias: float32 [3072], P(('dp', 'fsdp'))
- grad_gains: float32 [2, 768], P(None, ('dp', 'fsdp'))
The draws below stay inside these ranges and needn't reach their ends.
Inputs may be any that keep to these rules, and one draw needn't show every extreme that they name: `segment_ids`: within a sequence the numbers never fall; a document holds at most 256 positions and some document of every sequence holds exactly that many.
All inputs are finite; a program needn't handle non-finite values.
Results may differ from the reference program's by a relative error of at most 0.019.
Values may be sent and summed in bfloat16 or wider, within the bound.
No kernel may reach another device: no remote copies, remote signals or barrier semaphores. Data moves between devices by JAX's collectives and lax.ppermute only.
A program may use at most 192 MiB of HBM per device.

```python
import math
import jax
import jax.numpy as jnp
import numpy as np
from jax import lax

D = 768
HEADS = 12
HD = 64
FF = 3072
LEN = 1024
BLOCK = 512
DOCS = 8
SEQS = 32
TOKENS = 32768


def raised(array, own_key, source, target, blocks, factor):
    owner, partner = [(jnp.arange(array.shape[dim]) // (array.shape[dim] // blocks)).reshape([-1 if axis == dim else 1 for axis in range(array.ndim)]) for dim in (source, target)]
    chosen = jax.random.permutation(own_key, blocks)[partner]
    strong = (owner == chosen) | (owner == (partner + blocks // 2) % blocks)
    return jnp.where(strong, factor * array, array)


def block_levels(key, extent, pieces, least, high):
    level = 1.0
    for dim, shards_of in pieces:
        steps = jax.random.uniform(jax.random.fold_in(jax.random.fold_in(key, 6), dim), (shards_of,), jnp.float32, least / len(pieces), high / len(pieces))
        level = level * jnp.repeat(jnp.exp(steps), extent[dim] // shards_of).reshape((-1,) + (1,) * (len(extent) - 1 - dim))
    return level


def split_up(number_of, total, bound, skew):
    portions = [(1 << 20) // math.isqrt(rank ** skew) + 1 for rank in range(2, number_of + 1)]
    spare, given = total - bound - (number_of - 1), [1] * (number_of - 1)
    while spare > 0:
        candidates = [i for i in range(number_of - 1) if given[i] < bound]
        whole, remaining = sum([portions[i] for i in candidates]), spare
        for i in candidates:
            more = min(bound - given[i], max(1, remaining * portions[i] // whole), spare)
            given[i] = given[i] + more
            spare = spare - more
    return np.array([bound] + given)


def uneven(key, amount, total, bound, lean):
    if amount == 2:
        one = jax.random.randint(key, (), max(1, total - bound), min(bound, total - 1) + 1)
        return jnp.stack([one, total - one])
    lengths = jnp.asarray(split_up(amount, total, bound, lean), jnp.int32)
    pairs = (amount - 1) // 2
    giver, taker = lengths[1:1 + 2 * pairs:2], lengths[2:2 + 2 * pairs:2]
    margin = jnp.minimum(giver - 1, bound - taker)
    moved = jax.random.randint(jax.random.fold_in(key, 1), (pairs,), 0, 1 << 20) % (margin + 1)
    lengths = lengths.at[1:1 + 2 * pairs:2].set(giver - moved).at[2:2 + 2 * pairs:2].set(taker + moved)
    return lengths[jax.random.permutation(jax.random.fold_in(key, 2), amount)]


def scatter_about(rng, dims, width, reach, split=(), kind=jnp.bfloat16):
    factor_of = block_levels(rng, dims, split, -0.22, 0.18) if split else 1.0
    drawn = jax.random.normal(rng, dims, jnp.float32) * width * factor_of
    return jnp.minimum(jnp.maximum(drawn, -reach), reach).astype(kind)


def gaussian_with(own_key, dims, deviation, bound, cuts, heavy, kind=jnp.bfloat16):
    entries = deviation * jax.random.normal(own_key, dims, jnp.float32)
    if cuts:
        entries = entries * block_levels(own_key, dims, cuts, -0.22, 0.18)
    return jnp.clip(raised(entries, jax.random.fold_in(own_key, 3), *heavy), -bound, bound).astype(kind)


def setup_inputs(seed: int = 0) -> dict:
    keys = jax.random.split(jax.random.key(seed), 11)
    return {
        "tokens": gaussian_with(keys[0], (TOKENS, D), 1.0, 6.0, ((0, 32),), (0, 1, 32, 2.75)),
        "segment_ids": jax.vmap(lambda own: jnp.searchsorted(jnp.cumsum(uneven(own, DOCS, LEN, LEN // 4, 1)), jnp.arange(LEN), side="right"))(jax.random.split(keys[1], SEQS)).reshape((SEQS, LEN)).astype(jnp.int32),
        "w_qkv": scatter_about(keys[2], (D, 3 * D), D ** -0.5, 0.21875, ((0, 4), (1, 8))),
        "w_out": scatter_about(keys[3], (D, D), (D // 16) ** -0.5, 0.875, ((0, 4), (1, 8))),
        "w_in": scatter_about(keys[4], (D, FF), D ** -0.5, 0.21875, ((0, 4), (1, 8))),
        "w_back": scatter_about(keys[5], (FF, D), FF ** -0.5, 0.109375, ((0, 4), (1, 8))),
        "biases": scatter_about(keys[6], (6, D), 0.3, 1.5, ((1, 32),)),
        "in_bias": scatter_about(keys[7], (FF,), 0.3, 1.5, ((0, 32),)),
        "gains": jnp.clip(1.0 + 0.1 * jax.random.normal(keys[8], (2, D), jnp.float32), 0.5, 1.5).astype(jnp.bfloat16),
        "out_grad": gaussian_with(keys[9], (TOKENS, D), 1.0, 6.0, ((0, 32),), (0, 1, 32, 2.75)),
    }


@jax.custom_vjp
def low(v):
    return lax.optimization_barrier(v.astype(jnp.bfloat16)).astype(jnp.float32)

@jax.custom_vjp
def low_back(v):
    return v

def low_keep(v):
    return (low(v), None)

def low_pass(kept, grad):
    return (grad,)

def back_keep(v):
    return (v, None)

def back_low(kept, grad):
    return (low(grad),)
low.defvjp(low_keep, low_pass)
low_back.defvjp(back_keep, back_low)

def matmul(left, right):
    return jnp.dot(left, right, precision=lax.Precision.HIGHEST, preferred_element_type=jnp.float32)

def layer_norm(rows, gain, shift):
    center = lax.optimization_barrier(jnp.mean(rows, axis=-1, keepdims=True))
    centered = rows - center
    spread = lax.optimization_barrier(jnp.mean(centered * centered, axis=-1, keepdims=True))
    return centered * lax.rsqrt(spread + 1e-05) * gain + shift

def gelu_exact(values):
    return jax.nn.gelu(values, approximate=False)

def attention(qkv, segment_row):
    block_count = LEN // BLOCK
    blocks = qkv.reshape(block_count, BLOCK, 3, HEADS, HD)
    query_rows = blocks[:, :, 0]
    key_rows = blocks[:, :, 1]
    value_rows = blocks[:, :, 2]
    raw = jnp.einsum('bqhd,bkhd->bhqk', query_rows, key_rows, precision=lax.Precision.HIGHEST)
    scores = low_back(raw * (1.0 / math.sqrt(HD)))
    segments = segment_row.reshape(block_count, BLOCK)
    visible = segments[:, :, None] == segments[:, None, :]
    scores = jnp.where(visible[:, None], scores, -1e+30)
    highest = lax.optimization_barrier(jnp.max(scores, axis=-1, keepdims=True))
    exponent = jnp.exp(scores - highest)
    attention_weights = low(exponent / lax.optimization_barrier(jnp.sum(exponent, axis=-1, keepdims=True)))
    context = jnp.einsum('bhqk,bkhd->bqhd', attention_weights, value_rows, precision=lax.Precision.HIGHEST)
    return context.reshape(LEN, D)

def layer(params, rows, segment_row):
    w_qkv, w_out, w_in, w_back, biases, in_bias, gains = params
    qkv_bias = jnp.concatenate([biases[0], jnp.zeros((D,), biases.dtype), biases[1]])
    qkv = low_back(low(matmul(rows, w_qkv) + qkv_bias))
    context = low_back(low(attention(qkv, segment_row)))
    attn_out = low_back(matmul(context, w_out) + biases[2])
    resid_one = rows + attn_out
    normed_one = layer_norm(resid_one, gains[0], biases[3])
    pre_act = low_back(matmul(low(normed_one), w_in) + in_bias)
    hidden = low(gelu_exact(pre_act))
    ffn_out = low_back(matmul(hidden, w_back) + biases[4])
    resid_two = normed_one + ffn_out
    return layer_norm(resid_two, gains[1], biases[5])

def reference(tokens, segment_ids, w_qkv, w_out, w_in, w_back, biases, in_bias, gains, out_grad):
    params = tuple((item.astype(jnp.float32) for item in (w_qkv, w_out, w_in, w_back, biases, in_bias, gains)))
    rows_all = tokens.astype(jnp.float32).reshape(SEQS, LEN, D)
    grads_all = out_grad.astype(jnp.float32).reshape(SEQS, LEN, D)

    def step(total, item):
        rows, segment_row, cotangent = item
        result, pull = jax.vjp(lambda p, v: layer(p, v, segment_row), params, rows)
        param_grads, rows_grad = pull(cotangent)
        total = jax.tree.map(jnp.add, total, param_grads)
        return (total, (result.astype(jnp.bfloat16), rows_grad.astype(jnp.bfloat16)))
    start = jax.tree.map(jnp.zeros_like, params)
    total, (results, row_grads) = lax.scan(step, start, (rows_all, segment_ids, grads_all))
    return (results.reshape(TOKENS, D), row_grads.reshape(TOKENS, D), total[0], total[1], total[2], total[3], total[4], total[5], total[6])
```

```python
import math

import jax
import jax.numpy as jnp
from jax import lax
from jax.experimental import pallas as pl
from jax.experimental.pallas import tpu as pltpu
from jax.sharding import Mesh, PartitionSpec as P

HEADS = 12
HD = 64
BLOCK = 512
PAIR = 2 * HD
TILE = 256
VMEM = 58 * 1024 * 1024
BF = jnp.bfloat16
F32 = jnp.float32
NT = (((1,), (1,)), ((), ()))


def dot(a, b):
    return jnp.dot(a, b, preferred_element_type=F32)


def dot_nt(a, b):
    return lax.dot_general(a, b, NT, preferred_element_type=F32)


def any_spec():
    return pl.BlockSpec(memory_space=pl.ANY)


def params(*semantics):
    return pltpu.CompilerParams(
        dimension_semantics=semantics if semantics else None, vmem_limit_bytes=VMEM
    )


def cost(flops, nbytes, trans=0):
    return pl.CostEstimate(flops=flops, bytes_accessed=nbytes, transcendentals=trans)

def layer_norm_parts(rows):
    center = jnp.mean(rows, axis=-1, keepdims=True)
    centered = rows - center
    spread = jnp.mean(centered * centered, axis=-1, keepdims=True)
    inverse = lax.rsqrt(spread + 1e-05)
    return centered * inverse, inverse


def layer_norm_back(grad, normal, inverse):
    mean_grad = jnp.mean(grad, axis=-1, keepdims=True)
    mean_both = jnp.mean(grad * normal, axis=-1, keepdims=True)
    return (grad - mean_grad - normal * mean_both) * inverse


def add_rows(ref, values):
    ref[...] += jnp.sum(values, axis=0, keepdims=True)


def zero_first(*refs):
    @pl.when(pl.program_id(0) == 0)
    def _():
        for ref in refs:
            ref[...] = jnp.zeros_like(ref)


def call(body, grid, spot, arrays, specs, weights, outs, out_specs, scratch=(), estimate=None):
    flat = [piece for pieces, _, _ in weights for piece in pieces]
    counts = [len(pieces) for pieces, _, _ in weights]
    n_arrays, n_flat, n_weights = len(arrays), len(flat), len(weights)
    n_outs = len(outs) if isinstance(outs, tuple) else 1

    def kernel(spot_ref, *refs):
        ins = refs[:n_arrays]
        piece_refs = refs[n_arrays : n_arrays + n_flat]
        out_refs = refs[n_arrays + n_flat : n_arrays + n_flat + n_outs]
        rest = refs[n_arrays + n_flat + n_outs :]
        held = rest[:n_weights]
        sems = rest[n_weights : 2 * n_weights]
        extra = rest[2 * n_weights :]

        if n_weights:

            @pl.when(pl.program_id(0) == 0)
            def _():
                copies, start = [], 0
                for (_, places, _), count, target, sem in zip(weights, counts, held, sems):
                    for index in range(count):
                        source, at = places[index](spot_ref, piece_refs[start + index])
                        copies.append(
                            pltpu.make_async_copy(source, target.at[at], sem.at[index])
                        )
                    start += count
                for copy in copies:
                    copy.start()
                for copy in copies:
                    copy.wait()

        body(spot_ref, *ins, *held, *out_refs, *extra)

    scratch_shapes = (
        [pltpu.VMEM(shape, BF) for _, _, shape in weights]
        + [pltpu.SemaphoreType.DMA((count,)) for count in counts]
        + list(scratch)
    )
    return pl.pallas_call(
        kernel,
        out_shape=outs,
        grid_spec=pltpu.PrefetchScalarGridSpec(
            num_scalar_prefetch=1,
            grid=grid,
            in_specs=list(specs) + [any_spec()] * n_flat,
            out_specs=out_specs,
            scratch_shapes=scratch_shapes,
        ),
        compiler_params=params(*(["arbitrary"] * len(grid))),
        cost_estimate=estimate,
    )(spot, *arrays, *flat)


def row(width, tile=TILE):
    return pl.BlockSpec((tile, width), lambda i, s: (i, 0))


def fixed(*shape):
    return pl.BlockSpec(shape, lambda *_: (0,) * len(shape))


def shape(dims, dtype):
    return jax.ShapeDtypeStruct(dims, dtype)


def project_qkv(spot, tokens, w_qkv, qkv_bias):
    count, width = tokens.shape
    wide = w_qkv[2][0]

    def body(spot_ref, x_ref, bias_ref, w_ref, out_ref):
        for start in range(0, wide, width):
            part = slice(start, start + width)
            out_ref[:, part] = (dot_nt(x_ref[...], w_ref[part, :]) + bias_ref[:, part]).astype(BF)

    return call(
        body, (count // TILE,), spot, (tokens, qkv_bias), (row(width), fixed(1, wide)), [w_qkv],
        shape((count, wide), BF), row(wide),
        estimate=cost(2 * count * width * wide, 2 * (count * width + wide * width + count * wide)),
    )


def lane_masks(dtype):
    lane = lax.broadcasted_iota(jnp.int32, (1, PAIR), 1)
    return [(lane // HD == head) for head in range(2)]


def attend_forward(qkv, segment_column, segment_row):
    count, wide = qkv.shape
    width = wide // 3
    pairs = width // PAIR
    blocks = count // BLOCK

    def body(q_ref, k_ref, v_ref, column_ref, row_ref, out_ref, lse_ref):
        visible = column_ref[...] == row_ref[0]
        query, key = q_ref[...] * BF(1.0 / math.sqrt(HD)), k_ref[...]
        value_turned = v_ref[...].T
        parts = []
        for head, lanes in enumerate(lane_masks(BF)):
            scores = dot_nt(key, jnp.where(lanes, query, BF(0)))
            scores = jnp.where(visible, scores, -1e30)
            highest = jnp.max(scores, axis=0, keepdims=True)
            exponent = jnp.exp(scores - highest)
            total = jnp.sum(exponent, axis=0, keepdims=True)
            part = dot(value_turned[head * HD : (head + 1) * HD], exponent.astype(BF))
            parts.append(part / total)
            lse_ref[0, 0, head : head + 1, :] = highest + jnp.log(total)
        out_ref[...] = jnp.concatenate(parts, axis=0).T.astype(BF)

    flops = 4 * blocks * HEADS * BLOCK * BLOCK * HD
    return pl.pallas_call(
        body,
        out_shape=(shape((count, width), BF), shape((blocks, pairs, 2, BLOCK), F32)),
        grid=(blocks, pairs),
        in_specs=[
            pl.BlockSpec((BLOCK, PAIR), lambda b, p: (b, p)),
            pl.BlockSpec((BLOCK, PAIR), lambda b, p: (b, pairs + p)),
            pl.BlockSpec((BLOCK, PAIR), lambda b, p: (b, 2 * pairs + p)),
            pl.BlockSpec((BLOCK, 1), lambda b, p: (b, 0)),
            pl.BlockSpec((1, 1, BLOCK), lambda b, p: (b, 0, 0)),
        ],
        out_specs=(
            pl.BlockSpec((BLOCK, PAIR), lambda b, p: (b, p)),
            pl.BlockSpec((1, 1, 2, BLOCK), lambda b, p: (b, p, 0, 0)),
        ),
        compiler_params=params("arbitrary", "arbitrary"),
        cost_estimate=cost(4 * flops, 8 * count * width, blocks * HEADS * BLOCK * BLOCK),
    )(qkv, qkv, qkv, segment_column, segment_row)


def attend_backward(qkv, segment_column, segment_row, lse, context, d_context):
    count, wide = qkv.shape
    width = wide // 3
    pairs = width // PAIR
    blocks = count // BLOCK
    factor = 1.0 / math.sqrt(HD)

    def body(q_ref, k_ref, v_ref, o_ref, do_ref, column_ref, row_ref, lse_ref,
             dq_ref, dk_ref, dv_ref, sum_q_ref, sum_v_ref):
        visible = column_ref[...] == row_ref[0]
        query, key, value = q_ref[...] * BF(factor), k_ref[...], v_ref[...]
        d_out = do_ref[...]
        key_turned = key.T
        product = (d_out.astype(F32) * o_ref[...].astype(F32)).T
        masks = lane_masks(BF)
        d_query, d_key, d_value = [], [], []
        for head, lanes in enumerate(masks):
            inside = slice(head * HD, (head + 1) * HD)
            delta = jnp.sum(product[inside], axis=0, keepdims=True)
            scores = dot_nt(key, jnp.where(lanes, query, BF(0)))
            scores = jnp.where(visible, scores - lse_ref[0, 0, head : head + 1, :], -1e30)
            prob = jnp.exp(scores)
            d_prob = dot_nt(value, jnp.where(lanes, d_out, BF(0)))
            d_score = (prob * (d_prob - delta)).astype(BF)
            d_value.append(dot(prob.astype(BF), d_out))
            d_key.append(dot(d_score, query))
            d_query.append(dot(key_turned[inside], d_score) * factor)
        dq = jnp.concatenate(d_query, axis=0).T.astype(BF)
        dk = jnp.where(masks[0], d_key[0], d_key[1]).astype(BF)
        dv = jnp.where(masks[0], d_value[0], d_value[1]).astype(BF)
        dq_ref[...] = dq
        dk_ref[...] = dk
        dv_ref[...] = dv
        sum_q_ref[0] = jnp.sum(dq.astype(F32), axis=0, keepdims=True)
        sum_v_ref[0] = jnp.sum(dv.astype(F32), axis=0, keepdims=True)

    tile = pl.BlockSpec((BLOCK, PAIR), lambda b, p: (b, p))
    flops = 10 * blocks * HEADS * BLOCK * BLOCK * HD
    return pl.pallas_call(
        body,
        out_shape=(shape((count, width), BF),) * 3 + (shape((blocks, 1, width), F32),) * 2,
        grid=(blocks, pairs),
        in_specs=[
            tile,
            pl.BlockSpec((BLOCK, PAIR), lambda b, p: (b, pairs + p)),
            pl.BlockSpec((BLOCK, PAIR), lambda b, p: (b, 2 * pairs + p)),
            tile,
            tile,
            pl.BlockSpec((BLOCK, 1), lambda b, p: (b, 0)),
            pl.BlockSpec((1, 1, BLOCK), lambda b, p: (b, 0, 0)),
            pl.BlockSpec((1, 1, 2, BLOCK), lambda b, p: (b, p, 0, 0)),
        ],
        out_specs=(tile,) * 3 + (pl.BlockSpec((1, 1, PAIR), lambda b, p: (b, 0, p)),) * 2,
        compiler_params=params("arbitrary", "arbitrary"),
        cost_estimate=cost(4 * flops, 16 * count * width, blocks * HEADS * BLOCK * BLOCK),
    )(qkv, qkv, qkv, context, d_context, segment_column, segment_row, lse)


def project_out(spot, context, tokens, w_out, biases, gains):
    count, width = tokens.shape

    def body(spot_ref, c_ref, x_ref, bias_ref, gain_ref, w_ref, normal_ref, inverse_ref, low_ref):
        resid = x_ref[...].astype(F32) + (dot_nt(c_ref[...], w_ref[...]) + bias_ref[2:3])
        normal, inverse = layer_norm_parts(resid)
        normal_ref[...] = normal
        inverse_ref[...] = inverse
        low_ref[...] = (normal * gain_ref[0:1] + bias_ref[3:4]).astype(BF)

    return call(
        body, (count // TILE,), spot, (context, tokens, biases, gains),
        (row(width), row(width), fixed(*biases.shape), fixed(*gains.shape)), [w_out],
        (shape((count, width), F32), shape((count, 1), F32), shape((count, width), BF)),
        (row(width), row(1), row(width)),
        estimate=cost(2 * count * width * width, 10 * count * width),
    )


def ffn_in(spot, normed_low, w_in, in_bias):
    count, width = normed_low.shape
    wide = w_in[2][1]

    def body(spot_ref, x_ref, bias_ref, w_ref, hidden_ref, slope_ref):
        for start in range(0, wide, width):
            part = slice(start, start + width)
            pre = dot(x_ref[...], w_ref[:, part]) + bias_ref[:, part]
            cdf = 0.5 + 0.5 * lax.erf(pre * (1.0 / math.sqrt(2.0)))
            hidden_ref[:, part] = (pre * cdf).astype(BF)
            density = jnp.exp(pre * pre * -0.5) * (1.0 / math.sqrt(2.0 * math.pi))
            slope_ref[:, part] = (cdf + pre * density).astype(BF)

    return call(
        body, (count // TILE,), spot, (normed_low, in_bias), (row(width), fixed(1, wide)), [w_in],
        (shape((count, wide), BF),) * 2, (row(wide),) * 2,
        estimate=cost(2 * count * width * wide, 4 * count * wide, 2 * count * wide),
    )


def ffn_out(spot, hidden, normal_one, out_grad, w_back, biases, gains):
    count, width = normal_one.shape
    wide = hidden.shape[1]

    def body(spot_ref, h_ref, n_ref, g_ref, bias_ref, gain_ref, w_ref,
             out_ref, d_two_ref, d_low_ref, sums_ref):
        zero_first(sums_ref)
        normed_one = n_ref[...] * gain_ref[0:1] + bias_ref[3:4]
        resid = normed_one + (dot_nt(h_ref[...], w_ref[...]) + bias_ref[4:5])
        normal, inverse = layer_norm_parts(resid)
        out_ref[...] = (normal * gain_ref[1:2] + bias_ref[5:6]).astype(BF)
        grad = g_ref[...].astype(F32)
        d_two = layer_norm_back(grad * gain_ref[1:2], normal, inverse)
        d_low = d_two.astype(BF)
        d_two_ref[...] = d_two
        d_low_ref[...] = d_low
        add_rows(sums_ref.at[0:1], grad * normal)
        add_rows(sums_ref.at[1:2], grad)
        add_rows(sums_ref.at[2:3], d_low.astype(F32))

    return call(
        body, (count // TILE,), spot, (hidden, normal_one, out_grad, biases, gains),
        (row(wide), row(width), row(width), fixed(*biases.shape), fixed(*gains.shape)), [w_back],
        (shape((count, width), BF), shape((count, width), F32), shape((count, width), BF),
         shape((8, width), F32)),
        (row(width), row(width), row(width), fixed(8, width)),
        estimate=cost(2 * count * width * wide, 2 * count * wide + 14 * count * width),
    )


def ffn_backward(spot, d_low, d_two, slope, normal_one, inverse_one, w_back, w_in, w_out, gains):
    count, width = normal_one.shape
    wide = slope.shape[1]

    def body(spot_ref, dl_ref, d2_ref, s_ref, n_ref, i_ref, gain_ref, wb_ref, wi_ref, wo_ref,
             d_pre_ref, d_one_ref, d_attn_ref, d_context_ref, sums_ref, hidden_sum_ref):
        zero_first(sums_ref, hidden_sum_ref)
        for start in range(0, wide, width):
            part = slice(start, start + width)
            d_hidden = dot(dl_ref[...], wb_ref[:, part])
            d_pre = (d_hidden * s_ref[:, part].astype(F32)).astype(BF)
            d_pre_ref[:, part] = d_pre
            add_rows(hidden_sum_ref.at[:, part], d_pre.astype(F32))
        d_normed = d2_ref[...] + dot_nt(d_pre_ref[...], wi_ref[...])
        normal = n_ref[...]
        d_one = layer_norm_back(d_normed * gain_ref[0:1], normal, i_ref[...])
        d_attn = d_one.astype(BF)
        d_one_ref[...] = d_one
        d_attn_ref[...] = d_attn
        d_context_ref[...] = dot(d_attn, wo_ref[...]).astype(BF)
        add_rows(sums_ref.at[0:1], d_normed * normal)
        add_rows(sums_ref.at[1:2], d_normed)
        add_rows(sums_ref.at[2:3], d_attn.astype(F32))

    return call(
        body, (count // TILE,), spot, (d_low, d_two, slope, normal_one, inverse_one, gains),
        (row(width), row(width), row(wide), row(width), row(1), fixed(*gains.shape)),
        [w_back, w_in, w_out],
        (shape((count, wide), BF), shape((count, width), F32), shape((count, width), BF),
         shape((count, width), BF), shape((8, width), F32), shape((1, wide), F32)),
        (row(wide), row(width), row(width), row(width), fixed(8, width), fixed(1, wide)),
        estimate=cost(2 * count * width * (2 * wide + width), 4 * count * wide + 18 * count * width),
    )


def tokens_backward(spot, d_one, d_query, d_key, d_value, w_qkv):
    count, width = d_one.shape

    def body(spot_ref, d1_ref, q_ref, k_ref, v_ref, w_ref, out_ref):
        total = d1_ref[...] + dot(q_ref[...], w_ref[0:width, :])
        total += dot(k_ref[...], w_ref[width : 2 * width, :])
        total += dot(v_ref[...], w_ref[2 * width : 3 * width, :])
        out_ref[...] = total.astype(BF)

    return call(
        body, (count // TILE,), spot, (d_one, d_query, d_key, d_value), (row(width),) * 4, [w_qkv],
        shape((count, width), BF), row(width),
        estimate=cost(6 * count * width * width, 12 * count * width),
    )


def gradient(spot, lefts, right, tile, blocks, block_shape):
    count, columns = right.shape
    width = lefts[0].shape[1]
    total = width * len(lefts)
    steps = columns // tile
    n_left = len(lefts)
    left_specs = [fixed(count, width)] * n_left
    right_spec = pl.BlockSpec((count, tile), lambda i, s: (0, i))
    estimate = cost(2 * count * total * columns, 2 * (count * (total + columns) + total * columns))

    def turn(left_refs, turned):
        @pl.when(pl.program_id(0) == 0)
        def _():
            for index, ref in enumerate(left_refs):
                turned[index * width : (index + 1) * width, :] = ref[...].T

    if blocks is None:

        def plain(spot_ref, *refs):
            left_refs, right_ref, out_ref, turned = refs[:n_left], *refs[n_left:]
            turn(left_refs, turned)
            out_ref[...] = dot(turned[...], right_ref[...]).astype(BF)

        return call(
            plain, (steps,), spot, (*lefts, right), (*left_specs, right_spec), [],
            shape((total, columns), BF), pl.BlockSpec((total, tile), lambda i, s: (0, i)),
            [pltpu.VMEM((total, count), BF)], estimate,
        )

    rows, cols = block_shape
    per_step = 32 // steps

    def placed(spot_ref, *refs):
        left_refs, right_ref, near_ref, far_ref, turned, held, sems = refs[:n_left], *refs[n_left:]
        step = pl.program_id(0)
        turn(left_refs, turned)
        for index in range(n_left):
            part = slice(index * width, (index + 1) * width)
            held[step, part, :] = dot(turned[part, :], right_ref[...]).astype(BF)
        for index, (row_at, column_at, x, core, z, y) in enumerate(blocks(step)):
            source = held.at[step, pl.ds(row_at, rows), pl.ds(column_at, cols)]
            sem = sems.at[step * per_step + index]
            where = (x ^ spot_ref[0], y ^ spot_ref[3], (z - spot_ref[2]) & 3)
            mine = (core ^ spot_ref[1]) == 0

            @pl.when(mine)
            def _():
                pltpu.make_async_copy(source, near_ref.at[where], sem).start()

            @pl.when(jnp.logical_not(mine))
            def _():
                pltpu.make_async_copy(source, far_ref.at[where], sem).start()

        @pl.when(step == steps - 1)
        def _():
            for index in range(32):
                source = held.at[0, pl.ds(0, rows), pl.ds(0, cols)]
                pltpu.make_async_copy(source, near_ref.at[0, 0, 0], sems.at[index]).wait()

    return call(
        placed, (steps,), spot, (*lefts, right), (*left_specs, right_spec), [],
        (shape((2, 2, 4, rows, cols), BF),) * 2, (any_spec(),) * 2,
        [pltpu.VMEM((total, count), BF), pltpu.VMEM((steps, total, tile), BF),
         pltpu.SemaphoreType.DMA((32,))],
        estimate,
    )


def swap(value, axis):
    return lax.ppermute(value, axis, [(0, 1), (1, 0)])


def rotate(value, distance):
    return lax.ppermute(value, "z", [(i, (i + distance) % 4) for i in range(4)])


def gather(piece):
    near = [piece] + [rotate(piece, distance) for distance in (1, 2, 3)]
    along_x = [swap(item, "x") for item in near]
    along_y = [swap(item, "y") for item in near]
    across = [swap(item, "x") for item in along_y[:2]] + [swap(item, "y") for item in along_x[2:]]
    pieces = {}
    for z in range(4):
        for x, y, item in ((0, 0, near), (1, 0, along_x), (0, 1, along_y), (1, 1, across)):
            pieces[0, x, y, z] = item[z]
            pieces[1, x, y, z] = swap(item[z], "core")
    return pieces


def widen(value):
    return value.astype(F32)


def reduce_pieces(near, far):
    sums = (widen(near) + widen(swap(far, "core"))).astype(BF)
    from_x = swap(sums[1, 1, :2], "x")
    from_y = swap(sums[1, 1, 2:], "y")
    along_y = jnp.concatenate([(widen(sums[0, 1, :2]) + widen(from_x)).astype(BF), sums[0, 1, 2:]])
    along_x = jnp.concatenate([sums[1, 0, :2], (widen(sums[1, 0, 2:]) + widen(from_y)).astype(BF)])
    column = widen(sums[0, 0]) + widen(swap(along_x, "x")) + widen(swap(along_y, "y"))
    column = column.astype(BF)
    total = widen(column[0])
    for distance in (1, 2, 3):
        total += widen(rotate(column[distance], distance))
    return total


def chip_of(spot_ref, x, y, z):
    depth = (spot_ref[2] - z) & 3
    return spot_ref[0] ^ x, 2 * depth + (spot_ref[3] ^ y)


def weight_of(pieces, source_rows, place, dims):
    start, rows, cols = source_rows
    arrays, places = [], []
    for (core, x, y, z), piece in pieces.items():

        def at(spot_ref, ref, core=core, x=x, y=y, z=z):
            own_x, f = chip_of(spot_ref, x, y, z)
            row_at, column_at = place(own_x, spot_ref[1] ^ core, f)
            return (
                ref.at[pl.ds(start, rows), :],
                (
                    pl.ds(pl.multiple_of(row_at, 16), rows),
                    pl.ds(pl.multiple_of(column_at, 128), cols),
                ),
            )

        arrays.append(piece)
        places.append(at)
    return arrays, places, dims


def whole_weight(array):
    def at(spot_ref, ref):
        return ref, (pl.ds(0, array.shape[0]), pl.ds(0, array.shape[1]))

    return [array], [at], array.shape


def small_vectors(shards, axes):
    biases, in_bias, gains = shards
    own = jnp.concatenate([biases.reshape(-1), in_bias, gains.reshape(-1)])
    every = lax.all_gather(own, axes, axis=0, tiled=False).astype(F32)
    devices = every.shape[0]
    first, second = biases.size, biases.size + in_bias.size
    return (
        every[:, :first].reshape(devices, 6, -1).transpose(1, 0, 2).reshape(6, -1),
        every[:, first:second].reshape(1, -1),
        every[:, second:].reshape(devices, 2, -1).transpose(1, 0, 2).reshape(2, -1),
    )


def spread_small(bias_total, hidden_total, gain_total, axes, devices):
    parts = jnp.concatenate(
        [
            bias_total.reshape(6, devices, -1).transpose(1, 0, 2).reshape(devices, -1),
            hidden_total.reshape(devices, -1),
            gain_total.reshape(2, devices, -1).transpose(1, 0, 2).reshape(devices, -1),
        ],
        axis=1,
    )
    own = lax.psum_scatter(parts.astype(BF), axes, scatter_dimension=0, tiled=True)
    own = own.astype(F32).reshape(-1)
    first = bias_total.size // devices
    second = first + hidden_total.size // devices
    return own[:first].reshape(6, -1), own[first:second], own[second:].reshape(2, -1)


def on_device(sizes, tokens, segment_ids, w_qkv, w_out, w_in, w_back, biases, in_bias, gains, out_grad):
    axes = ("x", "core", "z", "y")
    dp_axes, fsdp_axes = ("x", "core"), ("z", "y")
    devices = math.prod(sizes)
    by_permute = sizes == (2, 2, 4, 2)
    count, width = tokens.shape
    wide = w_back.shape[0] * sizes[0] * sizes[1]
    spot = jnp.stack([lax.axis_index(axis) for axis in axes]).astype(jnp.int32)
    core = spot[1]

    if by_permute:
        qkv_cols, out_cols = w_qkv.shape[1], w_out.shape[1]
        in_rows, in_cols = w_in.shape
        back_rows, back_cols = w_back.shape
        half_q, half_o = qkv_cols // 2, out_cols // 2

        def paired(turned):
            half = turned.shape[0] // 2
            first, second = turned[:half], turned[half:]
            mine = jnp.where(core == 0, first, second)
            other = swap(jnp.where(core == 0, second, first), "core")
            return jnp.where(
                core == 0,
                jnp.concatenate([mine, other], axis=1),
                jnp.concatenate([other, mine], axis=1),
            )

        qkv_pieces = gather(paired(w_qkv.T))
        in_pieces = gather(jnp.concatenate([w_in, paired(w_out.T)], axis=0))
        back_pieces = gather(w_back.T)
        pair_cols = 2 * w_qkv.shape[0]
        qkv_weight = weight_of(
            qkv_pieces, (0, half_q, pair_cols),
            lambda x, c, f: (f * qkv_cols + c * half_q, x * pair_cols), (3 * width, width),
        )
        in_weight = weight_of(
            in_pieces, (0, in_rows, in_cols),
            lambda x, c, f: ((2 * x + c) * in_rows, f * in_cols), (width, wide),
        )
        out_weight = weight_of(
            in_pieces, (in_rows, half_o, pair_cols),
            lambda x, c, f: (f * out_cols + c * half_o, x * pair_cols), (width, width),
        )
        back_weight = weight_of(
            back_pieces, (0, back_cols, back_rows),
            lambda x, c, f: (f * back_cols, (2 * x + c) * back_rows), (width, wide),
        )

        def back_blocks(step):
            return [(f * back_cols, 0, step >> 1, step & 1, f >> 1, f & 1) for f in range(8)]

        def in_blocks(step):
            return [
                ((2 * x + c) * in_rows, y * in_cols, x, c, step, y)
                for x in range(2) for c in range(2) for y in range(2)
            ]

        def out_blocks(step):
            return [
                (f * out_cols + c * half_o, 0, step, c, f >> 1, f & 1)
                for f in range(8) for c in range(2)
            ]

        def qkv_blocks(step):
            return [
                (f * qkv_cols + c * half_q, 0, step, c, f >> 1, f & 1)
                for f in range(8) for c in range(2)
            ]

        plans = {
            "back": (back_rows, back_blocks, (back_cols, back_rows)),
            "in": (2 * in_cols, in_blocks, (in_rows, in_cols)),
            "out": (pair_cols, out_blocks, (half_o, pair_cols)),
            "qkv": (pair_cols, qkv_blocks, (half_q, pair_cols)),
        }
    else:

        def full(shard):
            return lax.all_gather(
                lax.all_gather(shard, fsdp_axes, axis=1, tiled=True), dp_axes, axis=0, tiled=True
            )

        qkv_weight = whole_weight(full(w_qkv).T)
        out_weight = whole_weight(full(w_out).T)
        in_weight = whole_weight(full(w_in))
        back_weight = whole_weight(full(w_back).T)
        plans = {name: (width // 2, None, None) for name in ("back", "in", "out", "qkv")}

    bias_values, hidden_bias, gain_values = small_vectors((biases, in_bias, gains), axes)
    qkv_bias = jnp.concatenate(
        [bias_values[0:1], jnp.zeros((1, width), F32), bias_values[1:2]], axis=1
    )
    segment_column = segment_ids.reshape(count, 1)
    segment_row = segment_ids.reshape(count // BLOCK, 1, BLOCK)

    qkv = project_qkv(spot, tokens, qkv_weight, qkv_bias)
    context, lse = attend_forward(qkv, segment_column, segment_row)
    normal_one, inverse_one, normed_low = project_out(
        spot, context, tokens, out_weight, bias_values, gain_values
    )
    hidden, slope = ffn_in(spot, normed_low, in_weight, hidden_bias)
    layer_out, d_two, d_low, sums_two = ffn_out(
        spot, hidden, normal_one, out_grad, back_weight, bias_values, gain_values
    )
    grad_back = gradient(spot, [d_low], hidden, *plans["back"])
    d_pre, d_one, d_attn, d_context, sums_one, hidden_sum = ffn_backward(
        spot, d_low, d_two, slope, normal_one, inverse_one, back_weight, in_weight, out_weight,
        gain_values,
    )
    grad_in = gradient(spot, [normed_low], d_pre, *plans["in"])
    grad_out = gradient(spot, [d_attn], context, *plans["out"])
    d_query, d_key, d_value, sum_query, sum_value = attend_backward(
        qkv, segment_column, segment_row, lse, context, d_context
    )
    grad_qkv = gradient(spot, [d_query, d_key, d_value], tokens, *plans["qkv"])
    tokens_grad = tokens_backward(spot, d_one, d_query, d_key, d_value, qkv_weight)

    bias_total = jnp.stack(
        [
            jnp.sum(sum_query, axis=(0, 1)), jnp.sum(sum_value, axis=(0, 1)), sums_one[2],
            sums_one[1], sums_two[2], sums_two[1],
        ]
    )
    gain_total = jnp.stack([sums_one[0], sums_two[0]])
    own_bias, own_hidden, own_gain = spread_small(
        bias_total, hidden_sum[0], gain_total, axes, devices
    )

    if by_permute:

        def unpaired(sums):
            half = sums.shape[1] // 2
            left, right = sums[:, :half], sums[:, half:]
            mine = jnp.where(core == 0, left, right)
            other = swap(jnp.where(core == 0, right, left).astype(BF), "core").astype(F32)
            return jnp.where(
                core == 0,
                jnp.concatenate([mine, other], axis=0),
                jnp.concatenate([other, mine], axis=0),
            )

        own_back = reduce_pieces(*grad_back).T
        own_in = reduce_pieces(*grad_in)
        own_out = unpaired(reduce_pieces(*grad_out)).T
        own_qkv = unpaired(reduce_pieces(*grad_qkv)).T
    else:

        def scattered(total):
            part = lax.psum_scatter(total, dp_axes, scatter_dimension=0, tiled=True)
            part = lax.psum_scatter(part, fsdp_axes, scatter_dimension=1, tiled=True)
            return part.astype(F32)

        own_back = scattered(grad_back.T)
        own_in = scattered(grad_in)
        own_out = scattered(grad_out.T)
        own_qkv = scattered(grad_qkv.T)
    return (
        layer_out, tokens_grad, own_qkv, own_out, own_in, own_back, own_bias, own_hidden, own_gain,
    )


def solution(mesh):
    dp, fsdp = mesh.devices.shape
    sizes = (dp // 2, 2, fsdp // 2, 2)
    split = Mesh(mesh.devices.reshape(sizes), ("x", "core", "z", "y"))
    outer, inner = ("x", "core"), ("z", "y")
    every = outer + inner
    rows = P(every, None)
    weight = P(outer, inner)
    vectors = P(None, every)

    def placed(*arrays):
        return on_device(sizes, *arrays)

    return jax.shard_map(
        placed,
        mesh=split,
        in_specs=(rows, rows, weight, weight, weight, weight, vectors, P(every), vectors, rows),
        out_specs=(rows, rows, weight, weight, weight, weight, vectors, P(every), vectors),
        check_vma=False,
    )
```

```python
import math

import jax
import jax.numpy as jnp
from jax import lax
from jax.experimental import pallas as pl
from jax.experimental.pallas import tpu as pltpu
from jax.sharding import Mesh, PartitionSpec as P

HEADS = 12
HD = 64
BLOCK = 512
PAIR = 2 * HD
TILE = 256
VMEM = 58 * 1024 * 1024
BF = jnp.bfloat16
F32 = jnp.float32
NT = (((1,), (1,)), ((), ()))


def dot(a, b):
    return jnp.dot(a, b, preferred_element_type=F32)


def dot_nt(a, b):
    return lax.dot_general(a, b, NT, preferred_element_type=F32)


def any_spec():
    return pl.BlockSpec(memory_space=pl.ANY)


def params(*semantics):
    return pltpu.CompilerParams(
        dimension_semantics=semantics if semantics else None, vmem_limit_bytes=VMEM
    )


def cost(flops, nbytes, trans=0):
    return pl.CostEstimate(flops=flops, bytes_accessed=nbytes, transcendentals=trans)

def layer_norm_parts(rows):
    center = jnp.mean(rows, axis=-1, keepdims=True)
    centered = rows - center
    spread = jnp.mean(centered * centered, axis=-1, keepdims=True)
    inverse = lax.rsqrt(spread + 1e-05)
    return centered * inverse, inverse


def layer_norm_back(grad, normal, inverse):
    mean_grad = jnp.mean(grad, axis=-1, keepdims=True)
    mean_both = jnp.mean(grad * normal, axis=-1, keepdims=True)
    return (grad - mean_grad - normal * mean_both) * inverse


def add_rows(ref, values):
    ref[...] += jnp.sum(values, axis=0, keepdims=True)


def zero_first(*refs):
    @pl.when(pl.program_id(0) == 0)
    def _():
        for ref in refs:
            ref[...] = jnp.zeros_like(ref)


def call(body, grid, spot, arrays, specs, weights, outs, out_specs, scratch=(), estimate=None):
    flat = [piece for pieces, _, _ in weights for piece in pieces]
    counts = [len(pieces) for pieces, _, _ in weights]
    n_arrays, n_flat, n_weights = len(arrays), len(flat), len(weights)
    n_outs = len(outs) if isinstance(outs, tuple) else 1

    def kernel(spot_ref, *refs):
        ins = refs[:n_arrays]
        piece_refs = refs[n_arrays : n_arrays + n_flat]
        out_refs = refs[n_arrays + n_flat : n_arrays + n_flat + n_outs]
        rest = refs[n_arrays + n_flat + n_outs :]
        held = rest[:n_weights]
        sems = rest[n_weights : 2 * n_weights]
        extra = rest[2 * n_weights :]

        if n_weights:

            @pl.when(pl.program_id(0) == 0)
            def _():
                copies, start = [], 0
                for (_, places, _), count, target, sem in zip(weights, counts, held, sems):
                    number = 0
                    for index in range(count):
                        for source, at in places[index](spot_ref, piece_refs[start + index]):
                            copies.append(
                                pltpu.make_async_copy(source, target.at[at], sem.at[number])
                            )
                            number += 1
                    start += count
                for copy in copies:
                    copy.start()
                for copy in copies:
                    copy.wait()

        body(spot_ref, *ins, *held, *out_refs, *extra)

    scratch_shapes = (
        [pltpu.VMEM(shape, BF) for _, _, shape in weights]
        + [pltpu.SemaphoreType.DMA((8 * count,)) for count in counts]
        + list(scratch)
    )
    return pl.pallas_call(
        kernel,
        out_shape=outs,
        grid_spec=pltpu.PrefetchScalarGridSpec(
            num_scalar_prefetch=1,
            grid=grid,
            in_specs=list(specs) + [any_spec()] * n_flat,
            out_specs=out_specs,
            scratch_shapes=scratch_shapes,
        ),
        compiler_params=params(*(["arbitrary"] * len(grid))),
        cost_estimate=estimate,
    )(spot, *arrays, *flat)


def row(width, tile=TILE):
    return pl.BlockSpec((tile, width), lambda i, s: (i, 0))


def fixed(*shape):
    return pl.BlockSpec(shape, lambda *_: (0,) * len(shape))


def shape(dims, dtype):
    return jax.ShapeDtypeStruct(dims, dtype)


def project_qkv(spot, tokens, w_qkv, qkv_bias):
    count, width = tokens.shape
    wide = w_qkv[2][0]

    def body(spot_ref, x_ref, bias_ref, w_ref, out_ref):
        for start in range(0, wide, width):
            part = slice(start, start + width)
            out_ref[:, part] = (dot_nt(x_ref[...], w_ref[part, :]) + bias_ref[:, part]).astype(BF)

    return call(
        body, (count // TILE,), spot, (tokens, qkv_bias), (row(width), fixed(1, wide)), [w_qkv],
        shape((count, wide), BF), row(wide),
        estimate=cost(2 * count * width * wide, 2 * (count * width + wide * width + count * wide)),
    )


def lane_masks(dtype):
    lane = lax.broadcasted_iota(jnp.int32, (1, PAIR), 1)
    return [(lane // HD == head) for head in range(2)]


def attend_forward(qkv, segment_column, segment_row):
    count, wide = qkv.shape
    width = wide // 3
    pairs = width // PAIR
    blocks = count // BLOCK

    def body(q_ref, k_ref, v_ref, column_ref, row_ref, out_ref, lse_ref):
        visible = column_ref[...] == row_ref[0]
        query, key = q_ref[...] * BF(1.0 / math.sqrt(HD)), k_ref[...]
        value_turned = v_ref[...].T
        parts = []
        for head, lanes in enumerate(lane_masks(BF)):
            scores = dot_nt(key, jnp.where(lanes, query, BF(0)))
            scores = jnp.where(visible, scores, -1e30)
            highest = jnp.max(scores, axis=0, keepdims=True)
            exponent = jnp.exp(scores - highest)
            total = jnp.sum(exponent, axis=0, keepdims=True)
            part = dot(value_turned[head * HD : (head + 1) * HD], exponent.astype(BF))
            parts.append(part / total)
            lse_ref[0, 0, head : head + 1, :] = highest + jnp.log(total)
        out_ref[...] = jnp.concatenate(parts, axis=0).T.astype(BF)

    flops = 4 * blocks * HEADS * BLOCK * BLOCK * HD
    return pl.pallas_call(
        body,
        out_shape=(shape((count, width), BF), shape((blocks, pairs, 2, BLOCK), F32)),
        grid=(blocks, pairs),
        in_specs=[
            pl.BlockSpec((BLOCK, PAIR), lambda b, p: (b, p)),
            pl.BlockSpec((BLOCK, PAIR), lambda b, p: (b, pairs + p)),
            pl.BlockSpec((BLOCK, PAIR), lambda b, p: (b, 2 * pairs + p)),
            pl.BlockSpec((BLOCK, 1), lambda b, p: (b, 0)),
            pl.BlockSpec((1, 1, BLOCK), lambda b, p: (b, 0, 0)),
        ],
        out_specs=(
            pl.BlockSpec((BLOCK, PAIR), lambda b, p: (b, p)),
            pl.BlockSpec((1, 1, 2, BLOCK), lambda b, p: (b, p, 0, 0)),
        ),
        compiler_params=params("arbitrary", "arbitrary"),
        cost_estimate=cost(4 * flops, 8 * count * width, blocks * HEADS * BLOCK * BLOCK),
    )(qkv, qkv, qkv, segment_column, segment_row)


def attend_backward(qkv, segment_column, segment_row, lse, context, d_context):
    count, wide = qkv.shape
    width = wide // 3
    pairs = width // PAIR
    blocks = count // BLOCK
    factor = 1.0 / math.sqrt(HD)

    def body(q_ref, k_ref, v_ref, o_ref, do_ref, column_ref, row_ref, lse_ref,
             dq_ref, dk_ref, dv_ref, sum_q_ref, sum_v_ref):
        visible = column_ref[...] == row_ref[0]
        query, key, value = q_ref[...] * BF(factor), k_ref[...], v_ref[...]
        d_out = do_ref[...]
        key_turned = key.T
        product = (d_out.astype(F32) * o_ref[...].astype(F32)).T
        masks = lane_masks(BF)
        d_query, d_key, d_value = [], [], []
        for head, lanes in enumerate(masks):
            inside = slice(head * HD, (head + 1) * HD)
            delta = jnp.sum(product[inside], axis=0, keepdims=True)
            scores = dot_nt(key, jnp.where(lanes, query, BF(0)))
            scores = jnp.where(visible, scores - lse_ref[0, 0, head : head + 1, :], -1e30)
            prob = jnp.exp(scores)
            d_prob = dot_nt(value, jnp.where(lanes, d_out, BF(0)))
            d_score = (prob * (d_prob - delta)).astype(BF)
            d_value.append(dot(prob.astype(BF), d_out))
            d_key.append(dot(d_score, query))
            d_query.append(dot(key_turned[inside], d_score) * factor)
        dq = jnp.concatenate(d_query, axis=0).T.astype(BF)
        dk = jnp.where(masks[0], d_key[0], d_key[1]).astype(BF)
        dv = jnp.where(masks[0], d_value[0], d_value[1]).astype(BF)
        dq_ref[...] = dq
        dk_ref[...] = dk
        dv_ref[...] = dv
        sum_q_ref[0] = jnp.sum(dq.astype(F32), axis=0, keepdims=True)
        sum_v_ref[0] = jnp.sum(dv.astype(F32), axis=0, keepdims=True)

    tile = pl.BlockSpec((BLOCK, PAIR), lambda b, p: (b, p))
    flops = 10 * blocks * HEADS * BLOCK * BLOCK * HD
    return pl.pallas_call(
        body,
        out_shape=(shape((count, width), BF),) * 3 + (shape((blocks, 1, width), F32),) * 2,
        grid=(blocks, pairs),
        in_specs=[
            tile,
            pl.BlockSpec((BLOCK, PAIR), lambda b, p: (b, pairs + p)),
            pl.BlockSpec((BLOCK, PAIR), lambda b, p: (b, 2 * pairs + p)),
            tile,
            tile,
            pl.BlockSpec((BLOCK, 1), lambda b, p: (b, 0)),
            pl.BlockSpec((1, 1, BLOCK), lambda b, p: (b, 0, 0)),
            pl.BlockSpec((1, 1, 2, BLOCK), lambda b, p: (b, p, 0, 0)),
        ],
        out_specs=(tile,) * 3 + (pl.BlockSpec((1, 1, PAIR), lambda b, p: (b, 0, p)),) * 2,
        compiler_params=params("arbitrary", "arbitrary"),
        cost_estimate=cost(4 * flops, 16 * count * width, blocks * HEADS * BLOCK * BLOCK),
    )(qkv, qkv, qkv, context, d_context, segment_column, segment_row, lse)


def project_out(spot, context, tokens, w_out, biases, gains):
    count, width = tokens.shape

    def body(spot_ref, c_ref, x_ref, bias_ref, gain_ref, w_ref, normal_ref, inverse_ref, low_ref):
        resid = x_ref[...].astype(F32) + (dot_nt(c_ref[...], w_ref[...]) + bias_ref[2:3])
        normal, inverse = layer_norm_parts(resid)
        normal_ref[...] = normal
        inverse_ref[...] = inverse
        low_ref[...] = (normal * gain_ref[0:1] + bias_ref[3:4]).astype(BF)

    return call(
        body, (count // TILE,), spot, (context, tokens, biases, gains),
        (row(width), row(width), fixed(*biases.shape), fixed(*gains.shape)), [w_out],
        (shape((count, width), F32), shape((count, 1), F32), shape((count, width), BF)),
        (row(width), row(1), row(width)),
        estimate=cost(2 * count * width * width, 10 * count * width),
    )


def ffn_in(spot, normed_low, w_in, in_bias):
    count, width = normed_low.shape
    wide = w_in[2][1]

    def body(spot_ref, x_ref, bias_ref, w_ref, hidden_ref, slope_ref):
        for start in range(0, wide, width):
            part = slice(start, start + width)
            pre = dot(x_ref[...], w_ref[:, part]) + bias_ref[:, part]
            cdf = 0.5 + 0.5 * lax.erf(pre * (1.0 / math.sqrt(2.0)))
            hidden_ref[:, part] = (pre * cdf).astype(BF)
            density = jnp.exp(pre * pre * -0.5) * (1.0 / math.sqrt(2.0 * math.pi))
            slope_ref[:, part] = (cdf + pre * density).astype(BF)

    return call(
        body, (count // TILE,), spot, (normed_low, in_bias), (row(width), fixed(1, wide)), [w_in],
        (shape((count, wide), BF),) * 2, (row(wide),) * 2,
        estimate=cost(2 * count * width * wide, 4 * count * wide, 2 * count * wide),
    )


def ffn_out(spot, hidden, normal_one, out_grad, w_back, biases, gains):
    count, width = normal_one.shape
    wide = hidden.shape[1]

    def body(spot_ref, h_ref, n_ref, g_ref, bias_ref, gain_ref, w_ref,
             out_ref, d_two_ref, d_low_ref, sums_ref):
        zero_first(sums_ref)
        normed_one = n_ref[...] * gain_ref[0:1] + bias_ref[3:4]
        resid = normed_one + (dot_nt(h_ref[...], w_ref[...]) + bias_ref[4:5])
        normal, inverse = layer_norm_parts(resid)
        out_ref[...] = (normal * gain_ref[1:2] + bias_ref[5:6]).astype(BF)
        grad = g_ref[...].astype(F32)
        d_two = layer_norm_back(grad * gain_ref[1:2], normal, inverse)
        d_low = d_two.astype(BF)
        d_two_ref[...] = d_two
        d_low_ref[...] = d_low
        add_rows(sums_ref.at[0:1], grad * normal)
        add_rows(sums_ref.at[1:2], grad)
        add_rows(sums_ref.at[2:3], d_low.astype(F32))

    return call(
        body, (count // TILE,), spot, (hidden, normal_one, out_grad, biases, gains),
        (row(wide), row(width), row(width), fixed(*biases.shape), fixed(*gains.shape)), [w_back],
        (shape((count, width), BF), shape((count, width), F32), shape((count, width), BF),
         shape((8, width), F32)),
        (row(width), row(width), row(width), fixed(8, width)),
        estimate=cost(2 * count * width * wide, 2 * count * wide + 14 * count * width),
    )


def ffn_backward(spot, d_low, d_two, slope, normal_one, inverse_one, w_back, w_in, w_out, gains):
    count, width = normal_one.shape
    wide = slope.shape[1]

    def body(spot_ref, dl_ref, d2_ref, s_ref, n_ref, i_ref, gain_ref, wb_ref, wi_ref, wo_ref,
             d_pre_ref, d_one_ref, d_attn_ref, d_context_ref, sums_ref, hidden_sum_ref):
        zero_first(sums_ref, hidden_sum_ref)
        for start in range(0, wide, width):
            part = slice(start, start + width)
            d_hidden = dot(dl_ref[...], wb_ref[:, part])
            d_pre = (d_hidden * s_ref[:, part].astype(F32)).astype(BF)
            d_pre_ref[:, part] = d_pre
            add_rows(hidden_sum_ref.at[:, part], d_pre.astype(F32))
        d_normed = d2_ref[...] + dot_nt(d_pre_ref[...], wi_ref[...])
        normal = n_ref[...]
        d_one = layer_norm_back(d_normed * gain_ref[0:1], normal, i_ref[...])
        d_attn = d_one.astype(BF)
        d_one_ref[...] = d_one
        d_attn_ref[...] = d_attn
        d_context_ref[...] = dot(d_attn, wo_ref[...]).astype(BF)
        add_rows(sums_ref.at[0:1], d_normed * normal)
        add_rows(sums_ref.at[1:2], d_normed)
        add_rows(sums_ref.at[2:3], d_attn.astype(F32))

    return call(
        body, (count // TILE,), spot, (d_low, d_two, slope, normal_one, inverse_one, gains),
        (row(width), row(width), row(wide), row(width), row(1), fixed(*gains.shape)),
        [w_back, w_in, w_out],
        (shape((count, wide), BF), shape((count, width), F32), shape((count, width), BF),
         shape((count, width), BF), shape((8, width), F32), shape((1, wide), F32)),
        (row(wide), row(width), row(width), row(width), fixed(8, width), fixed(1, wide)),
        estimate=cost(2 * count * width * (2 * wide + width), 4 * count * wide + 18 * count * width),
    )


def tokens_backward(spot, d_one, d_query, d_key, d_value, w_qkv):
    count, width = d_one.shape

    def body(spot_ref, d1_ref, q_ref, k_ref, v_ref, w_ref, out_ref):
        total = d1_ref[...] + dot(q_ref[...], w_ref[0:width, :])
        total += dot(k_ref[...], w_ref[width : 2 * width, :])
        total += dot(v_ref[...], w_ref[2 * width : 3 * width, :])
        out_ref[...] = total.astype(BF)

    return call(
        body, (count // TILE,), spot, (d_one, d_query, d_key, d_value), (row(width),) * 4, [w_qkv],
        shape((count, width), BF), row(width),
        estimate=cost(6 * count * width * width, 12 * count * width),
    )


def gradient(spot, lefts, right, tile, blocks, block_shape):
    count, columns = right.shape
    width = lefts[0].shape[1]
    total = width * len(lefts)
    steps = columns // tile
    n_left = len(lefts)
    left_specs = [fixed(count, width)] * n_left
    right_spec = pl.BlockSpec((count, tile), lambda i, s: (0, i))
    estimate = cost(2 * count * total * columns, 2 * (count * (total + columns) + total * columns))

    def turn(left_refs, turned):
        @pl.when(pl.program_id(0) == 0)
        def _():
            for index, ref in enumerate(left_refs):
                turned[index * width : (index + 1) * width, :] = ref[...].T

    if blocks is None:

        def plain(spot_ref, *refs):
            left_refs, right_ref, out_ref, turned = refs[:n_left], *refs[n_left:]
            turn(left_refs, turned)
            out_ref[...] = dot(turned[...], right_ref[...]).astype(BF)

        return call(
            plain, (steps,), spot, (*lefts, right), (*left_specs, right_spec), [],
            shape((total, columns), BF), pl.BlockSpec((total, tile), lambda i, s: (0, i)),
            [pltpu.VMEM((total, count), BF)], estimate,
        )

    rows, cols = block_shape
    per_step = 32 // steps

    def placed(spot_ref, *refs):
        left_refs, right_ref, near_ref, far_ref, turned, held, sems = refs[:n_left], *refs[n_left:]
        step = pl.program_id(0)
        turn(left_refs, turned)
        for index in range(n_left):
            part = slice(index * width, (index + 1) * width)
            held[step, part, :] = dot(turned[part, :], right_ref[...]).astype(BF)
        for index, (row_at, column_at, x, core, z, y) in enumerate(blocks(step)):
            source = held.at[step, pl.ds(row_at, rows), pl.ds(column_at, cols)]
            sem = sems.at[step * per_step + index]
            far_x, far_y = x ^ spot_ref[0], y ^ spot_ref[3]
            first = far_x + core * (far_y - far_x)
            where = (z ^ spot_ref[2]) + 4 * first + 8 * (far_x + far_y - first)
            mine = (core ^ spot_ref[1]) == 0

            @pl.when(mine)
            def _():
                pltpu.make_async_copy(source, near_ref.at[where], sem).start()

            @pl.when(jnp.logical_not(mine))
            def _():
                pltpu.make_async_copy(source, far_ref.at[where], sem).start()

        @pl.when(step == steps - 1)
        def _():
            for index in range(32):
                source = held.at[0, pl.ds(0, rows), pl.ds(0, cols)]
                pltpu.make_async_copy(source, near_ref.at[0], sems.at[index]).wait()

    return call(
        placed, (steps,), spot, (*lefts, right), (*left_specs, right_spec), [],
        (shape((16, rows, cols), BF),) * 2, (any_spec(),) * 2,
        [pltpu.VMEM((total, count), BF), pltpu.VMEM((steps, total, tile), BF),
         pltpu.SemaphoreType.DMA((32,))],
        estimate,
    )


def widen(value):
    return value.astype(F32)


def exchange(value, stage):
    axes = ("x", "core", "z", "y")
    pairs = []
    for source in range(32):
        x, core, z, y = source >> 4, (source >> 3) & 1, (source >> 1) & 3, source & 1
        if stage < 2:
            z ^= 1 << stage
        elif stage == 4:
            core ^= 1
        elif (stage == 2) == (core == 0):
            x ^= 1
        else:
            y ^= 1
        pairs.append((source, 16 * x + 8 * core + 2 * z + y))
    return lax.ppermute(value, axes, pairs)


def gather(piece):
    held = piece[None]
    for stage in range(3):
        held = jnp.concatenate([held, exchange(held, stage)])
    across = exchange(held, 3)
    return [held, across, exchange(held, 4), exchange(across, 4)]


def reduce_pieces(near, far, kind=BF):
    terms = [near, exchange(far, 4)]
    size = near.shape[0]
    for stage in (3, 2, 1, 0):
        size //= 2
        upper = sum(widen(term[size : 2 * size]) for term in terms).astype(kind)
        terms = [term[:size] for term in terms] + [exchange(upper, stage)]
    return sum(widen(term[0]) for term in terms)


def slot_source(spot, core, slot):
    first, second = (slot >> 2) & 1, slot >> 3
    x = spot[0] ^ (first + core * (second - first))
    y = spot[3] ^ (second + core * (first - second))
    return x, 2 * (spot[2] ^ (slot & 3)) + y


def weight_of(arrays, source_rows, place, dims):
    start, rows, cols = source_rows
    pieces, places = [], []
    for position, array in enumerate(arrays):
        pieces.append(array)

        def at(spot_ref, ref, position=position):
            core = spot_ref[1] ^ (position >> 1)
            for index in range(8):
                x, f = slot_source(spot_ref, core, index + 8 * (position & 1))
                row_at, column_at = place(x, core, f)
                yield (
                    ref.at[index, pl.ds(start, rows), :],
                    (
                        pl.ds(pl.multiple_of(row_at, 16), rows),
                        pl.ds(pl.multiple_of(column_at, 128), cols),
                    ),
                )

        places.append(at)
    return pieces, places, dims


def whole_weight(array):
    def at(spot_ref, ref):
        yield ref, (pl.ds(0, array.shape[0]), pl.ds(0, array.shape[1]))

    return [array], [at], array.shape


def device_slots(spot):
    device = lax.broadcasted_iota(jnp.int32, (32, 32), 0)
    slot = lax.broadcasted_iota(jnp.int32, (32, 32), 1)
    core = spot[1] ^ (slot >> 4)
    x, f = slot_source(spot, core, slot & 15)
    return (device == 16 * x + 8 * core + f).astype(F32)


def small_vectors(every, shards):
    biases, in_bias, gains = shards
    devices = every.shape[0]
    first, second = biases.size, biases.size + in_bias.size
    third = second + gains.size
    return (
        every[:, :first].reshape(devices, 6, -1).transpose(1, 0, 2).reshape(6, -1),
        every[:, first:second].reshape(1, -1),
        every[:, second:third].reshape(devices, 2, -1).transpose(1, 0, 2).reshape(2, -1),
    )


def small_parts(bias_total, hidden_total, gain_total, devices):
    return jnp.concatenate(
        [
            bias_total.reshape(6, devices, -1).transpose(1, 0, 2).reshape(devices, -1),
            hidden_total.reshape(devices, -1),
            gain_total.reshape(2, devices, -1).transpose(1, 0, 2).reshape(devices, -1),
        ],
        axis=1,
    )


def on_device(sizes, tokens, segment_ids, w_qkv, w_out, w_in, w_back, biases, in_bias, gains, out_grad):
    axes = ("x", "core", "z", "y")
    dp_axes, fsdp_axes = ("x", "core"), ("z", "y")
    devices = math.prod(sizes)
    by_permute = sizes == (2, 2, 4, 2)
    count, width = tokens.shape
    wide = w_back.shape[0] * sizes[0] * sizes[1]
    spot = jnp.stack([lax.axis_index(axis) for axis in axes]).astype(jnp.int32)
    core = spot[1]

    if by_permute:
        qkv_cols, out_cols = w_qkv.shape[1], w_out.shape[1]
        in_rows, in_cols = w_in.shape
        back_rows, back_cols = w_back.shape
        half_q, half_o = qkv_cols // 2, out_cols // 2

        def paired(turned):
            half = turned.shape[0] // 2
            first, second = turned[:half], turned[half:]
            mine = jnp.where(core == 0, first, second)
            other = exchange(jnp.where(core == 0, second, first), 4)
            return jnp.where(
                core == 0,
                jnp.concatenate([mine, other], axis=1),
                jnp.concatenate([other, mine], axis=1),
            )

        qkv_pieces = gather(paired(w_qkv.T))
        in_pieces = gather(jnp.concatenate([w_in, paired(w_out.T)], axis=0))
        back_pieces = gather(w_back.T)
        pair_cols = 2 * w_qkv.shape[0]
        qkv_weight = weight_of(
            qkv_pieces, (0, half_q, pair_cols),
            lambda x, c, f: (f * qkv_cols + c * half_q, x * pair_cols), (3 * width, width),
        )
        in_weight = weight_of(
            in_pieces, (0, in_rows, in_cols),
            lambda x, c, f: ((2 * x + c) * in_rows, f * in_cols), (width, wide),
        )
        out_weight = weight_of(
            in_pieces, (in_rows, half_o, pair_cols),
            lambda x, c, f: (f * out_cols + c * half_o, x * pair_cols), (width, width),
        )
        back_weight = weight_of(
            back_pieces, (0, back_cols, back_rows),
            lambda x, c, f: (f * back_cols, (2 * x + c) * back_rows), (width, wide),
        )

        def back_blocks(step):
            return [(f * back_cols, 0, step >> 1, step & 1, f >> 1, f & 1) for f in range(8)]

        def in_blocks(step):
            return [
                ((2 * x + c) * in_rows, y * in_cols, x, c, step, y)
                for x in range(2) for c in range(2) for y in range(2)
            ]

        def out_blocks(step):
            return [
                (f * out_cols + c * half_o, 0, step, c, f >> 1, f & 1)
                for f in range(8) for c in range(2)
            ]

        def qkv_blocks(step):
            return [
                (f * qkv_cols + c * half_q, 0, step, c, f >> 1, f & 1)
                for f in range(8) for c in range(2)
            ]

        plans = {
            "back": (back_rows, back_blocks, (back_cols, back_rows)),
            "in": (2 * in_cols, in_blocks, (in_rows, in_cols)),
            "out": (pair_cols, out_blocks, (half_o, pair_cols)),
            "qkv": (pair_cols, qkv_blocks, (half_q, pair_cols)),
        }
    else:

        def full(shard):
            return lax.all_gather(
                lax.all_gather(shard, fsdp_axes, axis=1, tiled=True), dp_axes, axis=0, tiled=True
            )

        qkv_weight = whole_weight(full(w_qkv).T)
        out_weight = whole_weight(full(w_out).T)
        in_weight = whole_weight(full(w_in))
        back_weight = whole_weight(full(w_back).T)
        plans = {name: (width // 2, None, None) for name in ("back", "in", "out", "qkv")}

    shards = (biases, in_bias, gains)
    own_small = jnp.concatenate([biases.reshape(-1), in_bias, gains.reshape(-1)])
    if by_permute:
        slots = device_slots(spot)
        own_small = jnp.pad(own_small, (0, 1024 - own_small.size)).reshape(8, 128)
        arrived = widen(jnp.concatenate(gather(own_small))).reshape(32, 1024)
        every = jnp.dot(slots, arrived, precision=lax.Precision.HIGHEST)
    else:
        every = widen(lax.all_gather(own_small, axes, axis=0, tiled=False))
    bias_values, hidden_bias, gain_values = small_vectors(every, shards)
    qkv_bias = jnp.concatenate(
        [bias_values[0:1], jnp.zeros((1, width), F32), bias_values[1:2]], axis=1
    )
    segment_column = segment_ids.reshape(count, 1)
    segment_row = segment_ids.reshape(count // BLOCK, 1, BLOCK)

    qkv = project_qkv(spot, tokens, qkv_weight, qkv_bias)
    context, lse = attend_forward(qkv, segment_column, segment_row)
    normal_one, inverse_one, normed_low = project_out(
        spot, context, tokens, out_weight, bias_values, gain_values
    )
    hidden, slope = ffn_in(spot, normed_low, in_weight, hidden_bias)
    layer_out, d_two, d_low, sums_two = ffn_out(
        spot, hidden, normal_one, out_grad, back_weight, bias_values, gain_values
    )
    grad_back = gradient(spot, [d_low], hidden, *plans["back"])
    d_pre, d_one, d_attn, d_context, sums_one, hidden_sum = ffn_backward(
        spot, d_low, d_two, slope, normal_one, inverse_one, back_weight, in_weight, out_weight,
        gain_values,
    )
    grad_in = gradient(spot, [normed_low], d_pre, *plans["in"])
    grad_out = gradient(spot, [d_attn], context, *plans["out"])
    d_query, d_key, d_value, sum_query, sum_value = attend_backward(
        qkv, segment_column, segment_row, lse, context, d_context
    )
    grad_qkv = gradient(spot, [d_query, d_key, d_value], tokens, *plans["qkv"])
    tokens_grad = tokens_backward(spot, d_one, d_query, d_key, d_value, qkv_weight)

    bias_total = jnp.stack(
        [
            jnp.sum(sum_query, axis=(0, 1)), jnp.sum(sum_value, axis=(0, 1)), sums_one[2],
            sums_one[1], sums_two[2], sums_two[1],
        ]
    )
    gain_total = jnp.stack([sums_one[0], sums_two[0]])
    small = small_parts(bias_total, hidden_sum[0], gain_total, devices)
    if by_permute:

        def unpaired(sums):
            half = sums.shape[1] // 2
            left, right = sums[:, :half], sums[:, half:]
            mine = jnp.where(core == 0, left, right)
            other = widen(exchange(jnp.where(core == 0, right, left).astype(BF), 4))
            return jnp.where(
                core == 0,
                jnp.concatenate([mine, other], axis=0),
                jnp.concatenate([other, mine], axis=0),
            )

        own_back = reduce_pieces(*grad_back).T
        own_in = reduce_pieces(*grad_in)
        own_out = unpaired(reduce_pieces(*grad_out)).T
        own_qkv = unpaired(reduce_pieces(*grad_qkv)).T
        small = jnp.dot(slots.T, small, precision=lax.Precision.HIGHEST)
        small = jnp.pad(small, ((0, 0), (0, 1024 - small.shape[1]))).reshape(32, 8, 128)
        small = reduce_pieces(small[:16], small[16:], F32).reshape(-1)
    else:

        def scattered(total):
            part = lax.psum_scatter(total, dp_axes, scatter_dimension=0, tiled=True)
            part = lax.psum_scatter(part, fsdp_axes, scatter_dimension=1, tiled=True)
            return part.astype(F32)

        own_back = scattered(grad_back.T)
        own_in = scattered(grad_in)
        own_out = scattered(grad_out.T)
        own_qkv = scattered(grad_qkv.T)
        small = lax.psum_scatter(small.astype(BF), axes, scatter_dimension=0, tiled=True)
        small = widen(small).reshape(-1)
    first, second = biases.size, biases.size + in_bias.size
    own_bias = small[:first].reshape(biases.shape)
    own_hidden = small[first:second]
    own_gain = small[second : second + gains.size].reshape(gains.shape)
    return (
        layer_out, tokens_grad, own_qkv, own_out, own_in, own_back, own_bias, own_hidden, own_gain,
    )


def solution(mesh):
    dp, fsdp = mesh.devices.shape
    sizes = (dp // 2, 2, fsdp // 2, 2)
    split = Mesh(mesh.devices.reshape(sizes), ("x", "core", "z", "y"))
    outer, inner = ("x", "core"), ("z", "y")
    every = outer + inner
    rows = P(every, None)
    weight = P(outer, inner)
    vectors = P(None, every)

    def placed(*arrays):
        return on_device(sizes, *arrays)

    return jax.shard_map(
        placed,
        mesh=split,
        in_specs=(rows, rows, weight, weight, weight, weight, vectors, P(every), vectors, rows),
        out_specs=(rows, rows, weight, weight, weight, weight, vectors, P(every), vectors),
        check_vma=False,
    )
```

```python
import math

import jax
import jax.numpy as jnp
from jax import lax
from jax.experimental import pallas as pl
from jax.experimental.pallas import tpu as pltpu
from jax.sharding import Mesh, PartitionSpec as P

HEADS = 12
HD = 64
BLOCK = 512
PAIR = 2 * HD
TILE = 256
VMEM = 58 * 1024 * 1024
BF = jnp.bfloat16
F32 = jnp.float32
NT = (((1,), (1,)), ((), ()))


def dot(a, b):
    return jnp.dot(a, b, preferred_element_type=F32)


def dot_nt(a, b):
    return lax.dot_general(a, b, NT, preferred_element_type=F32)


def any_spec():
    return pl.BlockSpec(memory_space=pl.ANY)


def params(*semantics):
    return pltpu.CompilerParams(
        dimension_semantics=semantics if semantics else None, vmem_limit_bytes=VMEM
    )


def cost(flops, nbytes, trans=0):
    return pl.CostEstimate(flops=flops, bytes_accessed=nbytes, transcendentals=trans)

def layer_norm_parts(rows):
    center = jnp.mean(rows, axis=-1, keepdims=True)
    centered = rows - center
    spread = jnp.mean(centered * centered, axis=-1, keepdims=True)
    inverse = lax.rsqrt(spread + 1e-05)
    return centered * inverse, inverse


def layer_norm_back(grad, normal, inverse):
    mean_grad = jnp.mean(grad, axis=-1, keepdims=True)
    mean_both = jnp.mean(grad * normal, axis=-1, keepdims=True)
    return (grad - mean_grad - normal * mean_both) * inverse


def add_rows(ref, values):
    ref[...] += jnp.sum(values, axis=0, keepdims=True)


def zero_first(*refs):
    @pl.when(pl.program_id(0) == 0)
    def _():
        for ref in refs:
            ref[...] = jnp.zeros_like(ref)


def call(
    body, grid, spot, arrays, specs, weights, outs, out_specs, scratch=(), estimate=None, aliases=()
):
    flat = [piece for pieces, _, _ in weights for piece in pieces]
    counts = [len(pieces) for pieces, _, _ in weights]
    n_arrays, n_flat, n_weights = len(arrays), len(flat), len(weights)
    n_outs = len(outs) if isinstance(outs, tuple) else 1

    def kernel(spot_ref, *refs):
        ins = refs[:n_arrays]
        piece_refs = refs[n_arrays : n_arrays + n_flat]
        out_refs = refs[n_arrays + n_flat : n_arrays + n_flat + n_outs]
        rest = refs[n_arrays + n_flat + n_outs :]
        held = rest[:n_weights]
        sems = rest[n_weights : 2 * n_weights]
        extra = rest[2 * n_weights :]

        if n_weights:

            @pl.when(pl.program_id(0) == 0)
            def _():
                copies, start = [], 0
                for (_, places, _), count, target, sem in zip(weights, counts, held, sems):
                    number = 0
                    for index in range(count):
                        for source, at in places[index](spot_ref, piece_refs[start + index]):
                            copies.append(
                                pltpu.make_async_copy(source, target.at[at], sem.at[number])
                            )
                            number += 1
                    start += count
                for copy in copies:
                    copy.start()
                for copy in copies:
                    copy.wait()

        body(spot_ref, *ins, *held, *out_refs, *extra)

    scratch_shapes = (
        [pltpu.VMEM(shape, BF) for _, _, shape in weights]
        + [pltpu.SemaphoreType.DMA((8 * count,)) for count in counts]
        + list(scratch)
    )
    return pl.pallas_call(
        kernel,
        out_shape=outs,
        grid_spec=pltpu.PrefetchScalarGridSpec(
            num_scalar_prefetch=1,
            grid=grid,
            in_specs=list(specs) + [any_spec()] * n_flat,
            out_specs=out_specs,
            scratch_shapes=scratch_shapes,
        ),
        compiler_params=params(*(["arbitrary"] * len(grid))),
        cost_estimate=estimate,
        input_output_aliases=dict(aliases),
    )(spot, *arrays, *flat)


def row(width, tile=TILE):
    return pl.BlockSpec((tile, width), lambda i, s: (i, 0))


def fixed(*shape):
    return pl.BlockSpec(shape, lambda *_: (0,) * len(shape))


def shape(dims, dtype):
    return jax.ShapeDtypeStruct(dims, dtype)


def project_qkv(spot, tokens, w_qkv, qkv_bias):
    count, width = tokens.shape
    wide = w_qkv[2][0]

    def body(spot_ref, x_ref, bias_ref, w_ref, out_ref):
        for start in range(0, wide, width):
            part = slice(start, start + width)
            out_ref[:, part] = (dot_nt(x_ref[...], w_ref[part, :]) + bias_ref[:, part]).astype(BF)

    return call(
        body, (count // TILE,), spot, (tokens, qkv_bias), (row(width), fixed(1, wide)), [w_qkv],
        shape((count, wide), BF), row(wide),
        estimate=cost(2 * count * width * wide, 2 * (count * width + wide * width + count * wide)),
    )


def lane_masks(dtype):
    lane = lax.broadcasted_iota(jnp.int32, (1, PAIR), 1)
    return [(lane // HD == head) for head in range(2)]


def attend_forward(block, qkv, segment_column, segment_row, into=None):
    count, wide = qkv.shape
    width = wide // 3
    pairs = width // PAIR
    blocks = count // BLOCK

    def body(q_ref, k_ref, v_ref, column_ref, row_ref, *refs):
        out_ref, lse_ref = refs[-2:]
        visible = column_ref[...] == row_ref[0]
        query, key = q_ref[...] * BF(1.0 / math.sqrt(HD)), k_ref[...]
        value_turned = v_ref[...].T
        parts = []
        for head, lanes in enumerate(lane_masks(BF)):
            scores = dot_nt(key, jnp.where(lanes, query, BF(0)))
            scores = jnp.where(visible, scores, -1e30)
            highest = jnp.max(scores, axis=0, keepdims=True)
            exponent = jnp.exp(scores - highest)
            total = jnp.sum(exponent, axis=0, keepdims=True)
            part = dot(value_turned[head * HD : (head + 1) * HD], exponent.astype(BF))
            parts.append(part / total)
            lse_ref[0, 0, head : head + 1, :] = highest + jnp.log(total)
        out_ref[...] = jnp.concatenate(parts, axis=0).T.astype(BF)

    flops = 4 * HEADS * BLOCK * BLOCK * HD
    given = () if into is None else into
    return pl.pallas_call(
        body,
        out_shape=(shape((count, width), BF), shape((blocks, pairs, 2, BLOCK), F32)),
        grid=(pairs,),
        in_specs=[
            pl.BlockSpec((BLOCK, PAIR), lambda p: (block, p)),
            pl.BlockSpec((BLOCK, PAIR), lambda p: (block, pairs + p)),
            pl.BlockSpec((BLOCK, PAIR), lambda p: (block, 2 * pairs + p)),
            pl.BlockSpec((BLOCK, 1), lambda p: (block, 0)),
            pl.BlockSpec((1, 1, BLOCK), lambda p: (block, 0, 0)),
        ]
        + [any_spec()] * len(given),
        out_specs=(
            pl.BlockSpec((BLOCK, PAIR), lambda p: (block, p)),
            pl.BlockSpec((1, 1, 2, BLOCK), lambda p: (block, p, 0, 0)),
        ),
        compiler_params=params("arbitrary"),
        cost_estimate=cost(4 * flops, 4 * count * width, HEADS * BLOCK * BLOCK),
        input_output_aliases={5 + index: index for index in range(len(given))},
    )(qkv, qkv, qkv, segment_column, segment_row, *given)


def attend_backward(block, qkv, segment_column, segment_row, lse, context, d_context, into=None):
    count, wide = qkv.shape
    width = wide // 3
    pairs = width // PAIR
    factor = 1.0 / math.sqrt(HD)

    def body(q_ref, k_ref, v_ref, o_ref, do_ref, column_ref, row_ref, lse_ref, *refs):
        dq_ref, dk_ref, dv_ref, sum_q_ref, sum_v_ref = refs[-5:]
        visible = column_ref[...] == row_ref[0]
        query, key, value = q_ref[...] * BF(factor), k_ref[...], v_ref[...]
        d_out = do_ref[...]
        key_turned = key.T
        product = (d_out.astype(F32) * o_ref[...].astype(F32)).T
        masks = lane_masks(BF)
        d_query, d_key, d_value = [], [], []
        for head, lanes in enumerate(masks):
            inside = slice(head * HD, (head + 1) * HD)
            delta = jnp.sum(product[inside], axis=0, keepdims=True)
            scores = dot_nt(key, jnp.where(lanes, query, BF(0)))
            scores = jnp.where(visible, scores - lse_ref[0, 0, head : head + 1, :], -1e30)
            prob = jnp.exp(scores)
            d_prob = dot_nt(value, jnp.where(lanes, d_out, BF(0)))
            d_score = (prob * (d_prob - delta)).astype(BF)
            d_value.append(dot(prob.astype(BF), d_out))
            d_key.append(dot(d_score, query))
            d_query.append(dot(key_turned[inside], d_score) * factor)
        dq = jnp.concatenate(d_query, axis=0).T.astype(BF)
        dk = jnp.where(masks[0], d_key[0], d_key[1]).astype(BF)
        dv = jnp.where(masks[0], d_value[0], d_value[1]).astype(BF)
        dq_ref[...] = dq
        dk_ref[...] = dk
        dv_ref[...] = dv
        sum_q_ref[...] = jnp.sum(dq.astype(F32), axis=0, keepdims=True)
        sum_v_ref[...] = jnp.sum(dv.astype(F32), axis=0, keepdims=True)

    tile = pl.BlockSpec((BLOCK, PAIR), lambda p: (block, p))
    flops = 10 * HEADS * BLOCK * BLOCK * HD
    given = () if into is None else into
    return pl.pallas_call(
        body,
        out_shape=(shape((count, width), BF),) * 3 + (shape((1, width), F32),) * 2,
        grid=(pairs,),
        in_specs=[
            tile,
            pl.BlockSpec((BLOCK, PAIR), lambda p: (block, pairs + p)),
            pl.BlockSpec((BLOCK, PAIR), lambda p: (block, 2 * pairs + p)),
            tile,
            tile,
            pl.BlockSpec((BLOCK, 1), lambda p: (block, 0)),
            pl.BlockSpec((1, 1, BLOCK), lambda p: (block, 0, 0)),
            pl.BlockSpec((1, 1, 2, BLOCK), lambda p: (block, p, 0, 0)),
        ]
        + [any_spec()] * len(given),
        out_specs=(tile,) * 3 + (pl.BlockSpec((1, PAIR), lambda p: (0, p)),) * 2,
        compiler_params=params("arbitrary"),
        cost_estimate=cost(4 * flops, 8 * count * width, HEADS * BLOCK * BLOCK),
        input_output_aliases={8 + index: index for index in range(len(given))},
    )(qkv, qkv, qkv, context, d_context, segment_column, segment_row, lse, *given)


def project_out(spot, context, tokens, w_out, biases, gains):
    count, width = tokens.shape

    def body(spot_ref, c_ref, x_ref, bias_ref, gain_ref, w_ref, normal_ref, inverse_ref, low_ref):
        resid = x_ref[...].astype(F32) + (dot_nt(c_ref[...], w_ref[...]) + bias_ref[2:3])
        normal, inverse = layer_norm_parts(resid)
        normal_ref[...] = normal
        inverse_ref[...] = inverse
        low_ref[...] = (normal * gain_ref[0:1] + bias_ref[3:4]).astype(BF)

    return call(
        body, (count // TILE,), spot, (context, tokens, biases, gains),
        (row(width), row(width), fixed(*biases.shape), fixed(*gains.shape)), [w_out],
        (shape((count, width), F32), shape((count, 1), F32), shape((count, width), BF)),
        (row(width), row(1), row(width)),
        estimate=cost(2 * count * width * width, 10 * count * width),
    )


def ffn_in(spot, normed_low, w_in, in_bias):
    count, width = normed_low.shape
    wide = w_in[2][1]

    def body(spot_ref, x_ref, bias_ref, w_ref, hidden_ref, slope_ref):
        for start in range(0, wide, width):
            part = slice(start, start + width)
            pre = dot(x_ref[...], w_ref[:, part]) + bias_ref[:, part]
            cdf = 0.5 + 0.5 * lax.erf(pre * (1.0 / math.sqrt(2.0)))
            hidden_ref[:, part] = (pre * cdf).astype(BF)
            density = jnp.exp(pre * pre * -0.5) * (1.0 / math.sqrt(2.0 * math.pi))
            slope_ref[:, part] = (cdf + pre * density).astype(BF)

    return call(
        body, (count // TILE,), spot, (normed_low, in_bias), (row(width), fixed(1, wide)), [w_in],
        (shape((count, wide), BF),) * 2, (row(wide),) * 2,
        estimate=cost(2 * count * width * wide, 4 * count * wide, 2 * count * wide),
    )


def ffn_out(spot, hidden, normal_one, out_grad, w_back, biases, gains):
    count, width = normal_one.shape
    wide = hidden.shape[1]

    def body(spot_ref, h_ref, n_ref, g_ref, bias_ref, gain_ref, w_ref,
             out_ref, d_two_ref, d_low_ref, sums_ref):
        zero_first(sums_ref)
        normed_one = n_ref[...] * gain_ref[0:1] + bias_ref[3:4]
        resid = normed_one + (dot_nt(h_ref[...], w_ref[...]) + bias_ref[4:5])
        normal, inverse = layer_norm_parts(resid)
        out_ref[...] = (normal * gain_ref[1:2] + bias_ref[5:6]).astype(BF)
        grad = g_ref[...].astype(F32)
        d_two = layer_norm_back(grad * gain_ref[1:2], normal, inverse)
        d_low = d_two.astype(BF)
        d_two_ref[...] = d_two
        d_low_ref[...] = d_low
        add_rows(sums_ref.at[0:1], grad * normal)
        add_rows(sums_ref.at[1:2], grad)
        add_rows(sums_ref.at[2:3], d_low.astype(F32))

    return call(
        body, (count // TILE,), spot, (hidden, normal_one, out_grad, biases, gains),
        (row(wide), row(width), row(width), fixed(*biases.shape), fixed(*gains.shape)), [w_back],
        (shape((count, width), BF), shape((count, width), F32), shape((count, width), BF),
         shape((8, width), F32)),
        (row(width), row(width), row(width), fixed(8, width)),
        estimate=cost(2 * count * width * wide, 2 * count * wide + 14 * count * width),
    )


def hidden_backward(spot, d_low, slope, w_back):
    count, width = d_low.shape
    wide = slope.shape[1]

    def body(spot_ref, dl_ref, s_ref, wb_ref, d_pre_ref, hidden_sum_ref):
        zero_first(hidden_sum_ref)
        for start in range(0, wide, width):
            part = slice(start, start + width)
            d_hidden = dot(dl_ref[...], wb_ref[:, part])
            d_pre = (d_hidden * s_ref[:, part].astype(F32)).astype(BF)
            d_pre_ref[:, part] = d_pre
            add_rows(hidden_sum_ref.at[:, part], d_pre.astype(F32))

    return call(
        body, (count // TILE,), spot, (d_low, slope), (row(width), row(wide)), [w_back],
        (shape((count, wide), BF), shape((1, wide), F32)), (row(wide), fixed(1, wide)),
        estimate=cost(2 * count * width * wide, 4 * count * wide),
    )


def normed_backward(spot, d_pre, d_two, normal_one, inverse_one, w_in, w_out, gains):
    count, width = normal_one.shape
    wide = d_pre.shape[1]

    def body(spot_ref, p_ref, d2_ref, n_ref, i_ref, gain_ref, wi_ref, wo_ref,
             d_one_ref, d_attn_ref, d_context_ref, sums_ref):
        zero_first(sums_ref)
        d_normed = d2_ref[...] + dot_nt(p_ref[...], wi_ref[...])
        normal = n_ref[...]
        d_one = layer_norm_back(d_normed * gain_ref[0:1], normal, i_ref[...])
        d_attn = d_one.astype(BF)
        d_one_ref[...] = d_one
        d_attn_ref[...] = d_attn
        d_context_ref[...] = dot(d_attn, wo_ref[...]).astype(BF)
        add_rows(sums_ref.at[0:1], d_normed * normal)
        add_rows(sums_ref.at[1:2], d_normed)
        add_rows(sums_ref.at[2:3], d_attn.astype(F32))

    return call(
        body, (count // TILE,), spot, (d_pre, d_two, normal_one, inverse_one, gains),
        (row(wide), row(width), row(width), row(1), fixed(*gains.shape)), [w_in, w_out],
        (shape((count, width), F32), shape((count, width), BF), shape((count, width), BF),
         shape((8, width), F32)),
        (row(width), row(width), row(width), fixed(8, width)),
        estimate=cost(2 * count * width * (wide + width), 2 * count * wide + 18 * count * width),
    )


def tokens_backward(spot, d_one, d_query, d_key, d_value, w_qkv):
    count, width = d_one.shape

    def body(spot_ref, d1_ref, q_ref, k_ref, v_ref, w_ref, out_ref):
        total = d1_ref[...] + dot(q_ref[...], w_ref[0:width, :])
        total += dot(k_ref[...], w_ref[width : 2 * width, :])
        total += dot(v_ref[...], w_ref[2 * width : 3 * width, :])
        out_ref[...] = total.astype(BF)

    return call(
        body, (count // TILE,), spot, (d_one, d_query, d_key, d_value), (row(width),) * 4, [w_qkv],
        shape((count, width), BF), row(width),
        estimate=cost(6 * count * width * width, 12 * count * width),
    )


def gradient(spot, lefts, right, tile, blocks, block_shape, slot_rows=None, base=0, into=None):
    count, columns = right.shape
    width = lefts[0].shape[1]
    total = width * len(lefts)
    steps = columns // tile
    n_left = len(lefts)
    left_specs = [fixed(count, width)] * n_left
    right_spec = pl.BlockSpec((count, tile), lambda i, s: (0, i))
    estimate = cost(2 * count * total * columns, 2 * (count * (total + columns) + total * columns))

    def turn(left_refs, turned):
        @pl.when(pl.program_id(0) == 0)
        def _():
            for index, ref in enumerate(left_refs):
                turned[index * width : (index + 1) * width, :] = ref[...].T

    if blocks is None:

        def plain(spot_ref, *refs):
            left_refs, right_ref, out_ref, turned = refs[:n_left], *refs[n_left:]
            turn(left_refs, turned)
            out_ref[...] = dot(turned[...], right_ref[...]).astype(BF)

        return call(
            plain, (steps,), spot, (*lefts, right), (*left_specs, right_spec), [],
            shape((total, columns), BF), pl.BlockSpec((total, tile), lambda i, s: (0, i)),
            [pltpu.VMEM((total, count), BF)], estimate,
        )

    rows, cols = block_shape
    slot_rows = slot_rows or rows
    given = () if into is None else into
    per_step = 32 // steps
    here = pl.ds(base, rows)

    def placed(spot_ref, *refs):
        left_refs, right_ref = refs[:n_left], refs[n_left]
        near_ref, far_ref, turned, held, sems = refs[-5:]
        step = pl.program_id(0)
        turn(left_refs, turned)
        for index in range(n_left):
            part = slice(index * width, (index + 1) * width)
            held[step, part, :] = dot(turned[part, :], right_ref[...]).astype(BF)
        for index, (row_at, column_at, x, core, z, y) in enumerate(blocks(step)):
            source = held.at[step, pl.ds(row_at, rows), pl.ds(column_at, cols)]
            sem = sems.at[step * per_step + index]
            far_x, far_y = x ^ spot_ref[0], y ^ spot_ref[3]
            first = far_x + core * (far_y - far_x)
            where = (z ^ spot_ref[2]) + 4 * first + 8 * (far_x + far_y - first)
            mine = (core ^ spot_ref[1]) == 0

            @pl.when(mine)
            def _():
                pltpu.make_async_copy(source, near_ref.at[where, here], sem).start()

            @pl.when(jnp.logical_not(mine))
            def _():
                pltpu.make_async_copy(source, far_ref.at[where, here], sem).start()

        @pl.when(step == steps - 1)
        def _():
            for index in range(32):
                source = held.at[0, pl.ds(0, rows), pl.ds(0, cols)]
                pltpu.make_async_copy(source, near_ref.at[0, here], sems.at[index]).wait()

    return call(
        placed, (steps,), spot, (*lefts, right, *given),
        (*left_specs, right_spec) + (any_spec(),) * len(given), [],
        (shape((16, slot_rows, cols), BF),) * 2, (any_spec(),) * 2,
        [pltpu.VMEM((total, count), BF), pltpu.VMEM((steps, total, tile), BF),
         pltpu.SemaphoreType.DMA((32,))],
        estimate, {n_left + 2 + index: index for index in range(len(given))},
    )


def widen(value):
    return value.astype(F32)


def exchange(value, stage):
    axes = ("x", "core", "z", "y")
    pairs = []
    for source in range(32):
        x, core, z, y = source >> 4, (source >> 3) & 1, (source >> 1) & 3, source & 1
        if stage < 2:
            z ^= 1 << stage
        elif stage == 4:
            core ^= 1
        elif (stage == 2) == (core == 0):
            x ^= 1
        else:
            y ^= 1
        pairs.append((source, 16 * x + 8 * core + 2 * z + y))
    return lax.ppermute(value, axes, pairs)


class Gather:
    def __init__(self, piece):
        self.state = (piece[None],)
        self.stage = 0

    def step(self):
        if self.stage < 4:
            held = self.state[0] if self.stage == 0 else jnp.concatenate(self.state)
            self.state = (held, exchange(held, self.stage))
        else:
            self.state += tuple(exchange(held, 4) for held in self.state)
        self.stage += 1


class Reduce:
    def __init__(self, near, far, kind=BF):
        self.state = [near, far]
        self.stage = 4
        self.kind = kind

    def step(self):
        if self.stage == 4:
            self.state = [self.state[0], exchange(self.state[1], 4)]
        else:
            size = self.state[0].shape[0] // 2
            upper = sum(widen(term[size:]) for term in self.state).astype(self.kind)
            self.state = [term[:size] for term in self.state] + [exchange(upper, self.stage)]
        self.stage -= 1

    def result(self):
        return sum(widen(term[0]) for term in self.state)


def sync(values, *tracks):
    values, states = lax.optimization_barrier((values, [track.state for track in tracks]))
    for track, state in zip(tracks, states):
        track.state = state
    return values


def step(*tracks):
    for track in tracks:
        track.step()


def slot_source(spot, core, slot):
    first, second = (slot >> 2) & 1, slot >> 3
    x = spot[0] ^ (first + core * (second - first))
    y = spot[3] ^ (second + core * (first - second))
    return x, 2 * (spot[2] ^ (slot & 3)) + y


def weight_of(arrays, source_rows, place, dims):
    start, rows, cols = source_rows
    pieces, places = [], []
    for position, array in enumerate(arrays):
        pieces.append(array)

        def at(spot_ref, ref, position=position):
            core = spot_ref[1] ^ (position >> 1)
            for index in range(8):
                x, f = slot_source(spot_ref, core, index + 8 * (position & 1))
                row_at, column_at = place(x, core, f)
                yield (
                    ref.at[index, pl.ds(start, rows), :],
                    (
                        pl.ds(pl.multiple_of(row_at, 16), rows),
                        pl.ds(pl.multiple_of(column_at, 128), cols),
                    ),
                )

        places.append(at)
    return pieces, places, dims


def whole_weight(array):
    def at(spot_ref, ref):
        yield ref, (pl.ds(0, array.shape[0]), pl.ds(0, array.shape[1]))

    return [array], [at], array.shape


def device_slots(spot):
    device = lax.broadcasted_iota(jnp.int32, (32, 32), 0)
    slot = lax.broadcasted_iota(jnp.int32, (32, 32), 1)
    core = spot[1] ^ (slot >> 4)
    x, f = slot_source(spot, core, slot & 15)
    return (device == 16 * x + 8 * core + f).astype(F32)


def small_vectors(every, shards):
    biases, in_bias, gains = shards
    devices = every.shape[0]
    first, second = biases.size, biases.size + in_bias.size
    third = second + gains.size
    return (
        every[:, :first].reshape(devices, 6, -1).transpose(1, 0, 2).reshape(6, -1),
        every[:, first:second].reshape(1, -1),
        every[:, second:third].reshape(devices, 2, -1).transpose(1, 0, 2).reshape(2, -1),
    )


def small_parts(bias_total, hidden_total, gain_total, devices):
    return jnp.concatenate(
        [
            bias_total.reshape(6, devices, -1).transpose(1, 0, 2).reshape(devices, -1),
            hidden_total.reshape(devices, -1),
            gain_total.reshape(2, devices, -1).transpose(1, 0, 2).reshape(devices, -1),
        ],
        axis=1,
    )


def on_device(sizes, tokens, segment_ids, w_qkv, w_out, w_in, w_back, biases, in_bias, gains, out_grad):
    axes = ("x", "core", "z", "y")
    dp_axes, fsdp_axes = ("x", "core"), ("z", "y")
    devices = math.prod(sizes)
    by_permute = sizes == (2, 2, 4, 2)
    count, width = tokens.shape
    wide = w_back.shape[0] * sizes[0] * sizes[1]
    blocks = range(count // BLOCK)
    spot = jnp.stack([lax.axis_index(axis) for axis in axes]).astype(jnp.int32)
    core = spot[1]
    shards = (biases, in_bias, gains)
    own_small = jnp.concatenate([biases.reshape(-1), in_bias, gains.reshape(-1)])
    segment_column = segment_ids.reshape(count, 1)
    segment_row = segment_ids.reshape(count // BLOCK, 1, BLOCK)

    qkv_cols, out_cols = w_qkv.shape[1], w_out.shape[1]
    pair_cols = 2 * w_qkv.shape[0]
    in_rows, in_cols = w_in.shape
    back_rows, back_cols = w_back.shape
    half_q, half_o = qkv_cols // 2, out_cols // 2

    if by_permute:

        def paired(turned):
            half = turned.shape[0] // 2
            first, second = turned[:half], turned[half:]
            mine = jnp.where(core == 0, first, second)
            other = exchange(jnp.where(core == 0, second, first), 4)
            return jnp.where(
                core == 0,
                jnp.concatenate([mine, other], axis=1),
                jnp.concatenate([other, mine], axis=1),
            )

        slots = device_slots(spot)
        to_qkv = Gather(paired(w_qkv.T))
        to_in = Gather(jnp.concatenate([w_in, paired(w_out.T)], axis=0))
        to_back = Gather(w_back.T)
        to_small = Gather(jnp.pad(own_small, (0, 1024 - own_small.size)).reshape(8, 128))
        tracks = (to_qkv, to_small, to_in, to_back)
        step(to_qkv, to_small)
        sync((), *tracks)
        step(to_qkv, to_small)
        sync((), *tracks)
        step(to_qkv, to_small, to_in)
        sync((), *tracks)
        step(to_qkv, to_small, to_in)
        sync((), *tracks)
        step(to_qkv, to_small, to_in, to_back)
        tokens, segment_column = sync((tokens, segment_column), *tracks)
        qkv_weight = weight_of(
            to_qkv.state, (0, half_q, pair_cols),
            lambda x, c, f: (f * qkv_cols + c * half_q, x * pair_cols), (3 * width, width),
        )
        arrived = widen(jnp.concatenate(to_small.state)).reshape(32, 1024)
        every = jnp.dot(slots, arrived, precision=lax.Precision.HIGHEST)

        def back_blocks(index):
            return [(f * back_cols, 0, index >> 1, index & 1, f >> 1, f & 1) for f in range(8)]

        def in_blocks(index):
            return [
                ((2 * x + c) * in_rows, y * in_cols, x, c, index, y)
                for x in range(2) for c in range(2) for y in range(2)
            ]

        def out_blocks(index):
            return [
                (f * out_cols + c * half_o, 0, index, c, f >> 1, f & 1)
                for f in range(8) for c in range(2)
            ]

        def qkv_blocks(index):
            return [
                (f * qkv_cols + c * half_q, 0, index, c, f >> 1, f & 1)
                for f in range(8) for c in range(2)
            ]

        plans = {
            "back": (back_rows, back_blocks, (back_cols, back_rows)),
            "in": (2 * in_cols, in_blocks, (in_rows, in_cols), in_rows + half_o),
            "out": (pair_cols, out_blocks, (half_o, pair_cols), in_rows + half_o, in_rows),
            "qkv": (pair_cols, qkv_blocks, (half_q, pair_cols)),
        }
    else:

        def full(shard):
            return lax.all_gather(
                lax.all_gather(shard, fsdp_axes, axis=1, tiled=True), dp_axes, axis=0, tiled=True
            )

        qkv_weight = whole_weight(full(w_qkv).T)
        out_weight = whole_weight(full(w_out).T)
        in_weight = whole_weight(full(w_in))
        back_weight = whole_weight(full(w_back).T)
        every = widen(lax.all_gather(own_small, axes, axis=0, tiled=False))
        plans = {name: (width // 2, None, None) for name in ("back", "in", "out", "qkv")}
        tracks = ()

    bias_values, hidden_bias, gain_values = small_vectors(every, shards)
    qkv_bias = jnp.concatenate(
        [bias_values[0:1], jnp.zeros((1, width), F32), bias_values[1:2]], axis=1
    )

    if by_permute:
        step(to_in)
    qkv = project_qkv(spot, tokens, qkv_weight, qkv_bias)
    if by_permute:
        qkv = sync(qkv, to_back)
        step(to_back)
    attended = None
    for block in blocks:
        attended = attend_forward(block, qkv, segment_column, segment_row, attended)
        if by_permute and block == 0:
            attended = sync(attended, to_in, to_back)
            step(to_in, to_back)
    context, lse = attended
    if by_permute:
        context = sync(context, to_in, to_back)
        step(to_back)
        in_weight = weight_of(
            to_in.state, (0, in_rows, in_cols),
            lambda x, c, f: ((2 * x + c) * in_rows, f * in_cols), (width, wide),
        )
        out_weight = weight_of(
            to_in.state, (in_rows, half_o, pair_cols),
            lambda x, c, f: (f * out_cols + c * half_o, x * pair_cols), (width, width),
        )
    normal_one, inverse_one, normed_low = project_out(
        spot, context, tokens, out_weight, bias_values, gain_values
    )
    if by_permute:
        normed_low = sync(normed_low, to_back)
        step(to_back)
    hidden, slope = ffn_in(spot, normed_low, in_weight, hidden_bias)
    if by_permute:
        hidden = sync(hidden, to_back)
        back_weight = weight_of(
            to_back.state, (0, back_cols, back_rows),
            lambda x, c, f: (f * back_cols, (2 * x + c) * back_rows), (width, wide),
        )
    layer_out, d_two, d_low, sums_two = ffn_out(
        spot, hidden, normal_one, out_grad, back_weight, bias_values, gain_values
    )
    grad_back = gradient(spot, [d_low], hidden, *plans["back"])
    if by_permute:
        from_back = Reduce(*grad_back)
        d_low = sync(d_low, from_back)
        step(from_back)
    d_pre, hidden_sum = hidden_backward(spot, d_low, slope, back_weight)
    if by_permute:
        d_pre = sync(d_pre, from_back)
        step(from_back)
    d_one, d_attn, d_context, sums_one = normed_backward(
        spot, d_pre, d_two, normal_one, inverse_one, in_weight, out_weight, gain_values
    )
    if by_permute:
        d_pre, d_attn = sync((d_pre, d_attn), from_back)
        step(from_back)
    grad_in = gradient(spot, [normed_low], d_pre, *plans["in"])
    if by_permute:
        grad_in = gradient(spot, [d_attn], context, *plans["out"], into=grad_in)
        from_in = Reduce(*grad_in)
        d_context = sync(d_context, from_back, from_in)
        step(from_back, from_in)
    else:
        grad_out = gradient(spot, [d_attn], context, *plans["out"])
    attended, sums_query, sums_value = None, [], []
    for block in blocks:
        *attended, sum_query, sum_value = attend_backward(
            block, qkv, segment_column, segment_row, lse, context, d_context, attended
        )
        sums_query.append(sum_query)
        sums_value.append(sum_value)
        if by_permute:
            attended = sync(attended, from_back, from_in)
            if block == 0:
                step(from_back, from_in)
            else:
                step(from_in)
    grad_qkv = gradient(spot, attended, tokens, *plans["qkv"])
    if by_permute:
        from_qkv = Reduce(*grad_qkv)
        d_one = sync(d_one, from_in, from_qkv)
        step(from_in, from_qkv)
    tokens_grad = tokens_backward(spot, d_one, *attended, qkv_weight)

    bias_total = jnp.concatenate(
        [sum(sums_query), sum(sums_value), sums_one[2:3], sums_one[1:2], sums_two[2:3], sums_two[1:2]]
    )
    gain_total = jnp.concatenate([sums_one[0:1], sums_two[0:1]])
    small = small_parts(bias_total, hidden_sum[0], gain_total, devices)

    if by_permute:

        def unpaired(sums):
            half = sums.shape[1] // 2
            left, right = sums[:, :half], sums[:, half:]
            mine = jnp.where(core == 0, left, right)
            other = widen(exchange(jnp.where(core == 0, right, left).astype(BF), 4))
            return jnp.where(
                core == 0,
                jnp.concatenate([mine, other], axis=0),
                jnp.concatenate([other, mine], axis=0),
            )

        small = jnp.dot(slots.T, small, precision=lax.Precision.HIGHEST)
        small = jnp.pad(small, ((0, 0), (0, 1024 - small.shape[1]))).reshape(32, 8, 128)
        from_small = Reduce(small[:16], small[16:], F32)
        step(from_small)
        tokens_grad = sync(tokens_grad, from_in, from_qkv, from_small)
        step(from_in, from_qkv, from_small)
        for _ in range(3):
            sync((), from_qkv, from_small)
            step(from_qkv, from_small)
        own_back = from_back.result().T
        sums_in = from_in.result()
        own_in = sums_in[:in_rows]
        own_out = unpaired(sums_in[in_rows:]).T
        own_qkv = unpaired(from_qkv.result()).T
        small = from_small.result().reshape(-1)
    else:

        def scattered(total):
            part = lax.psum_scatter(total, dp_axes, scatter_dimension=0, tiled=True)
            part = lax.psum_scatter(part, fsdp_axes, scatter_dimension=1, tiled=True)
            return widen(part)

        own_back = scattered(grad_back.T)
        own_in = scattered(grad_in)
        own_out = scattered(grad_out.T)
        own_qkv = scattered(grad_qkv.T)
        small = lax.psum_scatter(small.astype(BF), axes, scatter_dimension=0, tiled=True)
        small = widen(small).reshape(-1)
    first, second = biases.size, biases.size + in_bias.size
    own_bias = small[:first].reshape(biases.shape)
    own_hidden = small[first:second]
    own_gain = small[second : second + gains.size].reshape(gains.shape)
    return (
        layer_out, tokens_grad, own_qkv, own_out, own_in, own_back, own_bias, own_hidden, own_gain,
    )


def solution(mesh):
    dp, fsdp = mesh.devices.shape
    sizes = (dp // 2, 2, fsdp // 2, 2)
    split = Mesh(mesh.devices.reshape(sizes), ("x", "core", "z", "y"))
    outer, inner = ("x", "core"), ("z", "y")
    every = outer + inner
    rows = P(every, None)
    weight = P(outer, inner)
    vectors = P(None, every)

    def placed(*arrays):
        return on_device(sizes, *arrays)

    return jax.shard_map(
        placed,
        mesh=split,
        in_specs=(rows, rows, weight, weight, weight, weight, vectors, P(every), vectors, rows),
        out_specs=(rows, rows, weight, weight, weight, weight, vectors, P(every), vectors),
        check_vma=False,
    )
```

```python
import math

import jax
import jax.numpy as jnp
from jax import lax
from jax.experimental import pallas as pl
from jax.experimental.pallas import tpu as pltpu
from jax.sharding import Mesh, PartitionSpec as P

HEADS = 12
HD = 64
BLOCK = 512
PAIR = 2 * HD
TILE = 256
VMEM = 58 * 1024 * 1024
BF = jnp.bfloat16
F32 = jnp.float32
NT = (((1,), (1,)), ((), ()))


def dot(a, b):
    return jnp.dot(a, b, preferred_element_type=F32)


def dot_nt(a, b):
    return lax.dot_general(a, b, NT, preferred_element_type=F32)


def any_spec():
    return pl.BlockSpec(memory_space=pl.ANY)


def params(*semantics):
    return pltpu.CompilerParams(
        dimension_semantics=semantics if semantics else None, vmem_limit_bytes=VMEM
    )


def cost(flops, nbytes, trans=0):
    return pl.CostEstimate(flops=flops, bytes_accessed=nbytes, transcendentals=trans)

def layer_norm_parts(rows):
    center = jnp.mean(rows, axis=-1, keepdims=True)
    centered = rows - center
    spread = jnp.mean(centered * centered, axis=-1, keepdims=True)
    inverse = lax.rsqrt(spread + 1e-05)
    return centered * inverse, inverse


def layer_norm_back(grad, normal, inverse):
    mean_grad = jnp.mean(grad, axis=-1, keepdims=True)
    mean_both = jnp.mean(grad * normal, axis=-1, keepdims=True)
    return (grad - mean_grad - normal * mean_both) * inverse


def add_rows(ref, values):
    ref[...] += jnp.sum(values, axis=0, keepdims=True)


def zero_first(*refs):
    @pl.when(pl.program_id(0) == 0)
    def _():
        for ref in refs:
            ref[...] = jnp.zeros_like(ref)


def call(
    body, grid, spot, arrays, specs, weights, outs, out_specs, scratch=(), estimate=None, aliases=()
):
    flat = [piece for pieces, _, _ in weights for piece in pieces]
    counts = [len(pieces) for pieces, _, _ in weights]
    n_arrays, n_flat, n_weights = len(arrays), len(flat), len(weights)
    n_outs = len(outs) if isinstance(outs, tuple) else 1

    def kernel(spot_ref, *refs):
        ins = refs[:n_arrays]
        piece_refs = refs[n_arrays : n_arrays + n_flat]
        out_refs = refs[n_arrays + n_flat : n_arrays + n_flat + n_outs]
        rest = refs[n_arrays + n_flat + n_outs :]
        held = rest[:n_weights]
        sems = rest[n_weights : 2 * n_weights]
        extra = rest[2 * n_weights :]
        first = pl.program_id(0) == 0

        def copies(number):
            start = sum(counts[:number])
            found = []
            for index in range(counts[number]):
                place = weights[number][1][index]
                for source, at in place(spot_ref, piece_refs[start + index]):
                    found.append(
                        pltpu.make_async_copy(
                            source, held[number].at[at], sems[number].at[len(found)]
                        )
                    )
            return found

        @pl.when(first)
        def _():
            for number in range(n_weights):
                for copy in copies(number):
                    copy.start()

        def ready(number):
            def wait():
                @pl.when(first)
                def _():
                    for copy in copies(number):
                        copy.wait()

                return held[number]

            return wait

        body(spot_ref, *ins, *[ready(number) for number in range(n_weights)], *out_refs, *extra)

    scratch_shapes = (
        [pltpu.VMEM(shape, BF) for _, _, shape in weights]
        + [pltpu.SemaphoreType.DMA((8 * count,)) for count in counts]
        + list(scratch)
    )
    return pl.pallas_call(
        kernel,
        out_shape=outs,
        grid_spec=pltpu.PrefetchScalarGridSpec(
            num_scalar_prefetch=1,
            grid=grid,
            in_specs=list(specs) + [any_spec()] * n_flat,
            out_specs=out_specs,
            scratch_shapes=scratch_shapes,
        ),
        compiler_params=params(*(["arbitrary"] * len(grid))),
        cost_estimate=estimate,
        input_output_aliases=dict(aliases),
    )(spot, *arrays, *flat)


def row(width, tile=TILE):
    return pl.BlockSpec((tile, width), lambda i, s: (i, 0))


def fixed(*shape):
    return pl.BlockSpec(shape, lambda *_: (0,) * len(shape))


def shape(dims, dtype):
    return jax.ShapeDtypeStruct(dims, dtype)


def project_qkv(spot, tokens, w_qkv, qkv_bias):
    count, width = tokens.shape
    wide = w_qkv[2][0]

    def body(spot_ref, x_ref, bias_ref, w_ready, out_ref):
        w_ref = w_ready()
        for start in range(0, wide, width):
            part = slice(start, start + width)
            out_ref[:, part] = (dot_nt(x_ref[...], w_ref[part, :]) + bias_ref[:, part]).astype(BF)

    return call(
        body, (count // TILE,), spot, (tokens, qkv_bias), (row(width), fixed(1, wide)), [w_qkv],
        shape((count, wide), BF), row(wide),
        estimate=cost(2 * count * width * wide, 2 * (count * width + wide * width + count * wide)),
    )


def lane_masks():
    lane = lax.broadcasted_iota(jnp.int32, (1, PAIR), 1)
    return [(lane // HD == head) for head in range(2)]


def same_segment(row_ref):
    numbers = row_ref[0].astype(F32)
    column = jnp.broadcast_to(numbers, (128, BLOCK)).T[:, 0:1]
    return column == numbers


def attend_forward(block, qkv, segment_row, into=None):
    count, wide = qkv.shape
    width = wide // 3
    pairs = width // PAIR
    blocks = count // BLOCK

    def body(q_ref, k_ref, v_ref, row_ref, *refs):
        out_ref, lse_ref = refs[-2:]
        visible = same_segment(row_ref)
        query, key = q_ref[...] * BF(1.0 / math.sqrt(HD)), k_ref[...]
        value_turned = v_ref[...].T
        parts = []
        for head, lanes in enumerate(lane_masks()):
            scores = dot_nt(key, jnp.where(lanes, query, BF(0)))
            scores = jnp.where(visible, scores, -1e30)
            highest = jnp.max(scores, axis=0, keepdims=True)
            exponent = jnp.exp(scores - highest)
            total = jnp.sum(exponent, axis=0, keepdims=True)
            part = dot(value_turned[head * HD : (head + 1) * HD], exponent.astype(BF))
            parts.append(part / total)
            lse_ref[0, 0, head : head + 1, :] = highest + jnp.log(total)
        out_ref[...] = jnp.concatenate(parts, axis=0).T.astype(BF)

    flops = 4 * HEADS * BLOCK * BLOCK * HD
    given = () if into is None else into
    return pl.pallas_call(
        body,
        out_shape=(shape((count, width), BF), shape((blocks, pairs, 2, BLOCK), F32)),
        grid=(pairs,),
        in_specs=[
            pl.BlockSpec((BLOCK, PAIR), lambda p: (block, p)),
            pl.BlockSpec((BLOCK, PAIR), lambda p: (block, pairs + p)),
            pl.BlockSpec((BLOCK, PAIR), lambda p: (block, 2 * pairs + p)),
            pl.BlockSpec((1, 1, BLOCK), lambda p: (block, 0, 0)),
        ]
        + [any_spec()] * len(given),
        out_specs=(
            pl.BlockSpec((BLOCK, PAIR), lambda p: (block, p)),
            pl.BlockSpec((1, 1, 2, BLOCK), lambda p: (block, p, 0, 0)),
        ),
        compiler_params=params("arbitrary"),
        cost_estimate=cost(4 * flops, 4 * count * width, HEADS * BLOCK * BLOCK),
        input_output_aliases={4 + index: index for index in range(len(given))},
    )(qkv, qkv, qkv, segment_row, *given)


def attend_backward(block, qkv, segment_row, lse, context, d_context, into=None):
    count, wide = qkv.shape
    width = wide // 3
    pairs = width // PAIR
    factor = 1.0 / math.sqrt(HD)

    def body(q_ref, k_ref, v_ref, o_ref, do_ref, row_ref, lse_ref, *refs):
        dq_ref, dk_ref, dv_ref, sum_q_ref, sum_v_ref = refs[-5:]
        visible = same_segment(row_ref)
        query, key, value = q_ref[...] * BF(factor), k_ref[...], v_ref[...]
        d_out = do_ref[...]
        key_turned = key.T
        product = (d_out.astype(F32) * o_ref[...].astype(F32)).T
        masks = lane_masks()
        d_query, d_key, d_value = [], [], []
        for head, lanes in enumerate(masks):
            inside = slice(head * HD, (head + 1) * HD)
            delta = jnp.sum(product[inside], axis=0, keepdims=True)
            scores = dot_nt(key, jnp.where(lanes, query, BF(0)))
            scores = jnp.where(visible, scores - lse_ref[0, 0, head : head + 1, :], -1e30)
            prob = jnp.exp(scores)
            d_prob = dot_nt(value, jnp.where(lanes, d_out, BF(0)))
            d_score = (prob * (d_prob - delta)).astype(BF)
            d_value.append(dot(prob.astype(BF), d_out))
            d_key.append(dot(d_score, query))
            d_query.append(dot(key_turned[inside], d_score) * factor)
        dq = jnp.concatenate(d_query, axis=0).T.astype(BF)
        dk = jnp.where(masks[0], d_key[0], d_key[1]).astype(BF)
        dv = jnp.where(masks[0], d_value[0], d_value[1]).astype(BF)
        dq_ref[...] = dq
        dk_ref[...] = dk
        dv_ref[...] = dv
        sum_q_ref[...] = jnp.sum(dq.astype(F32), axis=0, keepdims=True)
        sum_v_ref[...] = jnp.sum(dv.astype(F32), axis=0, keepdims=True)

    tile = pl.BlockSpec((BLOCK, PAIR), lambda p: (block, p))
    flops = 10 * HEADS * BLOCK * BLOCK * HD
    given = () if into is None else into
    return pl.pallas_call(
        body,
        out_shape=(shape((count, width), BF),) * 3 + (shape((1, width), F32),) * 2,
        grid=(pairs,),
        in_specs=[
            tile,
            pl.BlockSpec((BLOCK, PAIR), lambda p: (block, pairs + p)),
            pl.BlockSpec((BLOCK, PAIR), lambda p: (block, 2 * pairs + p)),
            tile,
            tile,
            pl.BlockSpec((1, 1, BLOCK), lambda p: (block, 0, 0)),
            pl.BlockSpec((1, 1, 2, BLOCK), lambda p: (block, p, 0, 0)),
        ]
        + [any_spec()] * len(given),
        out_specs=(tile,) * 3 + (pl.BlockSpec((1, PAIR), lambda p: (0, p)),) * 2,
        compiler_params=params("arbitrary"),
        cost_estimate=cost(4 * flops, 8 * count * width, HEADS * BLOCK * BLOCK),
        input_output_aliases={7 + index: index for index in range(len(given))},
    )(qkv, qkv, qkv, context, d_context, segment_row, lse, *given)


def emit(plan, step, held, spot_ref, out_refs, sems):
    tile, blocks, (rows, cols), _, base = plan
    if blocks is None:
        target = out_refs[0].at[:, pl.ds(pl.multiple_of(step * tile, tile), tile)]
        pltpu.make_async_copy(held.at[step], target, sems.at[step]).start()
        return
    listed = blocks(step)
    for index, (row_at, column_at, x, core, z, y) in enumerate(listed):
        source = held.at[step, pl.ds(row_at, rows), pl.ds(column_at, cols)]
        sem = sems.at[step * len(listed) + index]
        far_x, far_y = x ^ spot_ref[0], y ^ spot_ref[3]
        first = far_x + core * (far_y - far_x)
        slot = (z ^ spot_ref[2]) + 4 * first + 8 * (far_x + far_y - first)
        mine = (core ^ spot_ref[1]) == 0

        @pl.when(mine)
        def _():
            pltpu.make_async_copy(source, out_refs[0].at[slot, pl.ds(base, rows)], sem).start()

        @pl.when(jnp.logical_not(mine))
        def _():
            pltpu.make_async_copy(source, out_refs[1].at[slot, pl.ds(base, rows)], sem).start()


def emitted(plan, steps, held, out_refs, sems):
    tile, blocks, (rows, cols), _, base = plan
    if blocks is None:
        for step in range(steps):
            target = out_refs[0].at[:, pl.ds(step * tile, tile)]
            pltpu.make_async_copy(held.at[step], target, sems.at[step]).wait()
        return
    for index in range(32):
        source = held.at[0, pl.ds(0, rows), pl.ds(0, cols)]
        pltpu.make_async_copy(source, out_refs[0].at[0, pl.ds(base, rows)], sems.at[index]).wait()


def emit_shapes(plan, total, columns):
    _, blocks, (rows, cols), slot_rows, _ = plan
    if blocks is None:
        return (shape((total, columns), BF),)
    return (shape((16, slot_rows, cols), BF),) * 2


def clamped(width, last, tile=TILE):
    return pl.BlockSpec((tile, width), lambda i, s: (jnp.minimum(i, last), 0))


def forward_rows(
    spot, context, tokens, out_grad, w_out, w_in, w_back, biases, in_bias, gains, plan
):
    count, width = tokens.shape
    wide = w_in[2][1]
    steps = count // TILE
    tile = plan[0]
    columns = wide // tile
    shapes = emit_shapes(plan, width, wide)

    def body(spot_ref, c_ref, x_ref, g_ref, bias_ref, hidden_bias_ref, gain_ref,
             wo_ready, wi_ready, wb_ready,
             normal_ref, inverse_ref, low_ref, slope_ref, out_ref, d_two_ref, d_low_ref, sums_ref,
             *refs):
        grads, (hidden, d_rows, turned, held, sems) = refs[: len(shapes)], refs[len(shapes) :]
        index = pl.program_id(0)
        zero_first(sums_ref)

        @pl.when(index < steps)
        def _():
            here = pl.ds(pl.multiple_of(index * TILE, TILE), TILE)
            w_ref = wo_ready()
            resid = x_ref[...].astype(F32) + (dot_nt(c_ref[...], w_ref[...]) + bias_ref[2:3])
            normal, inverse = layer_norm_parts(resid)
            normal_ref[...] = normal
            inverse_ref[...] = jnp.broadcast_to(inverse, inverse_ref.shape)
            normed = normal * gain_ref[0:1] + bias_ref[3:4]
            low_ref[...] = normed.astype(BF)
            w_ref = wi_ready()
            for start in range(0, wide, width):
                part = slice(start, start + width)
                pre = dot(low_ref[...], w_ref[:, part]) + hidden_bias_ref[:, part]
                cdf = 0.5 + 0.5 * lax.erf(pre * (1.0 / math.sqrt(2.0)))
                hidden[here, part] = (pre * cdf).astype(BF)
                density = jnp.exp(pre * pre * -0.5) * (1.0 / math.sqrt(2.0 * math.pi))
                slope_ref[:, part] = (cdf + pre * density).astype(BF)
            w_ref = wb_ready()
            resid = normal_ref[...] * gain_ref[0:1] + bias_ref[3:4]
            resid += dot_nt(hidden[here, :], w_ref[...]) + bias_ref[4:5]
            normal, inverse = layer_norm_parts(resid)
            out_ref[...] = (normal * gain_ref[1:2] + bias_ref[5:6]).astype(BF)
            grad = g_ref[...].astype(F32)
            d_two = layer_norm_back(grad * gain_ref[1:2], normal, inverse)
            d_low = d_two.astype(BF)
            d_two_ref[...] = d_two
            d_low_ref[...] = d_low
            d_rows[here, :] = d_low
            add_rows(sums_ref.at[0:1], grad * normal)
            add_rows(sums_ref.at[1:2], grad)
            add_rows(sums_ref.at[2:3], d_low.astype(F32))

        @pl.when(index == steps)
        def _():
            turned[...] = d_rows[...].T

        @pl.when(index >= steps)
        def _():
            column = index - steps
            at = pl.ds(pl.multiple_of(column * tile, tile), tile)
            held[column] = dot(turned[...], hidden[:, at]).astype(BF)
            emit(plan, column, held, spot_ref, grads, sems)

        @pl.when(index == steps + columns - 1)
        def _():
            emitted(plan, columns, held, grads, sems)

    last = steps - 1
    rows = lambda wide_: clamped(wide_, last)
    return call(
        body, (steps + columns,), spot, (context, tokens, out_grad, biases, in_bias, gains),
        (rows(width), rows(width), rows(width), fixed(*biases.shape), fixed(1, wide),
         fixed(*gains.shape)),
        [w_out, w_in, w_back],
        (shape((count, width), F32), shape((count, 128), F32), shape((count, width), BF),
         shape((count, wide), BF), shape((count, width), BF), shape((count, width), F32),
         shape((count, width), BF), shape((8, width), F32), *shapes),
        (rows(width), rows(128), rows(width), rows(wide), rows(width), rows(width), rows(width),
         fixed(8, width), *[any_spec()] * len(shapes)),
        [pltpu.VMEM((count, wide), BF), pltpu.VMEM((count, width), BF),
         pltpu.VMEM((width, count), BF), pltpu.VMEM((columns, width, tile), BF),
         pltpu.SemaphoreType.DMA((32,))],
        cost(2 * count * width * (3 * wide + width), 20 * count * width + 2 * count * wide),
    )


def backward_rows(
    spot, d_low, slope, d_two, normal_one, inverse_one, normed_low, context, w_back, w_in, w_out,
    gains, plan_in, plan_out,
):
    count, width = d_two.shape
    wide = slope.shape[1]
    steps = count // TILE
    tile_in, tile_out = plan_in[0], plan_out[0]
    columns_in, columns_out = wide // tile_in, width // tile_out
    shared = plan_in[1] is not None
    shapes = emit_shapes(plan_in, width, wide)
    if not shared:
        shapes += emit_shapes(plan_out, width, width)

    def body(spot_ref, dl_ref, s_ref, d2_ref, n_ref, i_ref, low_ref, c_ref, gain_ref,
             wb_ready, wi_ready, wo_ready,
             d_one_ref, d_context_ref, sums_ref, hidden_sum_ref, *refs):
        grads = refs[: len(shapes)]
        d_pre, d_attn, turned, held_in, held_out, sems_in, sems_out = refs[len(shapes) :]
        grads_in, grads_out = (grads, grads) if shared else (grads[:1], grads[1:])
        index = pl.program_id(0)
        zero_first(sums_ref, hidden_sum_ref)

        @pl.when(index < steps)
        def _():
            here = pl.ds(pl.multiple_of(index * TILE, TILE), TILE)
            w_ref = wb_ready()
            for start in range(0, wide, width):
                part = slice(start, start + width)
                d_hidden = dot(dl_ref[...], w_ref[:, part])
                piece = (d_hidden * s_ref[:, part].astype(F32)).astype(BF)
                d_pre[here, part] = piece
                add_rows(hidden_sum_ref.at[:, part], piece.astype(F32))
            w_ref = wi_ready()
            d_normed = d2_ref[...] + dot_nt(d_pre[here, :], w_ref[...])
            normal = n_ref[...]
            d_one = layer_norm_back(d_normed * gain_ref[0:1], normal, i_ref[:, 0:1])
            low = d_one.astype(BF)
            d_one_ref[...] = d_one
            d_attn[here, :] = low
            d_context_ref[...] = dot(low, wo_ready()[...]).astype(BF)
            add_rows(sums_ref.at[0:1], d_normed * normal)
            add_rows(sums_ref.at[1:2], d_normed)
            add_rows(sums_ref.at[2:3], low.astype(F32))

        @pl.when(index == steps)
        def _():
            turned[...] = low_ref[...].T

        @pl.when(jnp.logical_and(index >= steps, index < steps + columns_in))
        def _():
            column = index - steps
            at = pl.ds(pl.multiple_of(column * tile_in, tile_in), tile_in)
            held_in[column] = dot(turned[...], d_pre[:, at]).astype(BF)
            emit(plan_in, column, held_in, spot_ref, grads_in, sems_in)

        @pl.when(index == steps + columns_in)
        def _():
            turned[...] = d_attn[...].T

        @pl.when(index >= steps + columns_in)
        def _():
            column = index - steps - columns_in
            held_out[column] = dot(turned[...], c_ref[...]).astype(BF)
            emit(plan_out, column, held_out, spot_ref, grads_out, sems_out)

        @pl.when(index == steps + columns_in + columns_out - 1)
        def _():
            emitted(plan_in, columns_in, held_in, grads_in, sems_in)
            emitted(plan_out, columns_out, held_out, grads_out, sems_out)

    last, before = steps - 1, steps + columns_in
    rows = lambda wide_: clamped(wide_, last)
    return call(
        body, (steps + columns_in + columns_out,), spot,
        (d_low, slope, d_two, normal_one, inverse_one, normed_low, context, gains),
        (rows(width), rows(wide), rows(width), rows(width), rows(128), fixed(count, width),
         pl.BlockSpec((count, tile_out), lambda i, s: (0, jnp.maximum(i - before, 0))),
         fixed(*gains.shape)),
        [w_back, w_in, w_out],
        (shape((count, width), F32), shape((count, width), BF), shape((8, width), F32),
         shape((1, wide), F32), *shapes),
        (rows(width), rows(width), fixed(8, width), fixed(1, wide), *[any_spec()] * len(shapes)),
        [pltpu.VMEM((count, wide), BF), pltpu.VMEM((count, width), BF),
         pltpu.VMEM((width, count), BF), pltpu.VMEM((columns_in, width, tile_in), BF),
         pltpu.VMEM((columns_out, width, tile_out), BF),
         pltpu.SemaphoreType.DMA((32,)), pltpu.SemaphoreType.DMA((32,))],
        cost(2 * count * width * (3 * wide + 2 * width), 18 * count * width + 2 * count * wide),
    )


def tokens_backward(spot, d_one, d_query, d_key, d_value, w_qkv):
    count, width = d_one.shape

    def body(spot_ref, d1_ref, q_ref, k_ref, v_ref, w_ready, out_ref):
        w_ref = w_ready()
        total = d1_ref[...] + dot(q_ref[...], w_ref[0:width, :])
        total += dot(k_ref[...], w_ref[width : 2 * width, :])
        total += dot(v_ref[...], w_ref[2 * width : 3 * width, :])
        out_ref[...] = total.astype(BF)

    return call(
        body, (count // TILE,), spot, (d_one, d_query, d_key, d_value), (row(width),) * 4, [w_qkv],
        shape((count, width), BF), row(width),
        estimate=cost(6 * count * width * width, 12 * count * width),
    )


def gradient(spot, lefts, right, plan):
    count, columns = right.shape
    width = lefts[0].shape[1]
    total = width * len(lefts)
    tile = plan[0]
    steps = columns // tile
    n_left = len(lefts)
    shapes = emit_shapes(plan, total, columns)

    def body(spot_ref, *refs):
        left_refs, right_ref = refs[:n_left], refs[n_left]
        grads = refs[n_left + 1 : n_left + 1 + len(shapes)]
        turned, held, sems = refs[-3:]
        step = pl.program_id(0)

        @pl.when(step == 0)
        def _():
            for index, ref in enumerate(left_refs):
                turned[index * width : (index + 1) * width, :] = ref[...].T

        for index in range(n_left):
            part = slice(index * width, (index + 1) * width)
            held[step, part, :] = dot(turned[part, :], right_ref[...]).astype(BF)
        emit(plan, step, held, spot_ref, grads, sems)

        @pl.when(step == steps - 1)
        def _():
            emitted(plan, steps, held, grads, sems)

    return call(
        body, (steps,), spot, (*lefts, right),
        (*[fixed(count, width)] * n_left, pl.BlockSpec((count, tile), lambda i, s: (0, i))), [],
        shapes, (any_spec(),) * len(shapes),
        [pltpu.VMEM((total, count), BF), pltpu.VMEM((steps, total, tile), BF),
         pltpu.SemaphoreType.DMA((32,))],
        cost(2 * count * total * columns, 2 * (count * (total + columns) + total * columns)),
    )


def widen(value):
    return value.astype(F32)


def exchange(value, stage):
    axes = ("x", "core", "z", "y")
    pairs = []
    for source in range(32):
        x, core, z, y = source >> 4, (source >> 3) & 1, (source >> 1) & 3, source & 1
        if stage < 2:
            z ^= 1 << stage
        elif stage == 4:
            core ^= 1
        elif (stage == 2) == (core == 0):
            x ^= 1
        else:
            y ^= 1
        pairs.append((source, 16 * x + 8 * core + 2 * z + y))
    return lax.ppermute(value, axes, pairs)


class Gather:
    def __init__(self, piece):
        self.state = (piece[None],)
        self.stage = 0

    def step(self):
        if self.stage < 4:
            held = self.state[0] if self.stage == 0 else jnp.concatenate(self.state)
            self.state = (held, exchange(held, self.stage))
        else:
            self.state += tuple(exchange(held, 4) for held in self.state)
        self.stage += 1


class Reduce:
    def __init__(self, near, far, kind=BF):
        self.state = [near, far]
        self.stage = 4
        self.kind = kind

    def step(self):
        if self.stage == 4:
            self.state = [self.state[0], exchange(self.state[1], 4)]
        else:
            size = self.state[0].shape[0] // 2
            upper = sum(widen(term[size:]) for term in self.state).astype(self.kind)
            self.state = [term[:size] for term in self.state] + [exchange(upper, self.stage)]
        self.stage -= 1

    def result(self):
        return sum(widen(term[0]) for term in self.state)


def sync(values, *tracks):
    values, states = lax.optimization_barrier((values, [track.state for track in tracks]))
    for track, state in zip(tracks, states):
        track.state = state
    return values


def step(*tracks):
    for track in tracks:
        track.step()


def slot_source(spot, core, slot):
    first, second = (slot >> 2) & 1, slot >> 3
    x = spot[0] ^ (first + core * (second - first))
    y = spot[3] ^ (second + core * (first - second))
    return x, 2 * (spot[2] ^ (slot & 3)) + y


def weight_of(arrays, source_rows, place, dims):
    start, rows, cols = source_rows
    pieces, places = [], []
    for position, array in enumerate(arrays):
        pieces.append(array)

        def at(spot_ref, ref, position=position):
            core = spot_ref[1] ^ (position >> 1)
            for index in range(8):
                x, f = slot_source(spot_ref, core, index + 8 * (position & 1))
                row_at, column_at = place(x, core, f)
                yield (
                    ref.at[index, pl.ds(start, rows), :],
                    (
                        pl.ds(pl.multiple_of(row_at, 16), rows),
                        pl.ds(pl.multiple_of(column_at, 128), cols),
                    ),
                )

        places.append(at)
    return pieces, places, dims


def whole_weight(array):
    def at(spot_ref, ref):
        yield ref, (pl.ds(0, array.shape[0]), pl.ds(0, array.shape[1]))

    return [array], [at], array.shape


def device_slots(spot):
    device = lax.broadcasted_iota(jnp.int32, (32, 32), 0)
    slot = lax.broadcasted_iota(jnp.int32, (32, 32), 1)
    core = spot[1] ^ (slot >> 4)
    x, f = slot_source(spot, core, slot & 15)
    return (device == 16 * x + 8 * core + f).astype(F32)


def small_vectors(every, shards):
    biases, in_bias, gains = shards
    devices = every.shape[0]
    first, second = biases.size, biases.size + in_bias.size
    third = second + gains.size
    return (
        every[:, :first].reshape(devices, 6, -1).transpose(1, 0, 2).reshape(6, -1),
        every[:, first:second].reshape(1, -1),
        every[:, second:third].reshape(devices, 2, -1).transpose(1, 0, 2).reshape(2, -1),
    )


def small_parts(bias_total, hidden_total, gain_total, devices):
    return jnp.concatenate(
        [
            bias_total.reshape(6, devices, -1).transpose(1, 0, 2).reshape(devices, -1),
            hidden_total.reshape(devices, -1),
            gain_total.reshape(2, devices, -1).transpose(1, 0, 2).reshape(devices, -1),
        ],
        axis=1,
    )


def on_device(sizes, tokens, segment_ids, w_qkv, w_out, w_in, w_back, biases, in_bias, gains, out_grad):
    axes = ("x", "core", "z", "y")
    dp_axes, fsdp_axes = ("x", "core"), ("z", "y")
    devices = math.prod(sizes)
    by_permute = sizes == (2, 2, 4, 2)
    count, width = tokens.shape
    wide = w_back.shape[0] * sizes[0] * sizes[1]
    blocks = range(count // BLOCK)
    spot = jnp.stack([lax.axis_index(axis) for axis in axes]).astype(jnp.int32)
    core = spot[1]
    shards = (biases, in_bias, gains)
    own_small = jnp.concatenate([biases.reshape(-1), in_bias, gains.reshape(-1)])
    segment_row = segment_ids.reshape(count // BLOCK, 1, BLOCK)

    qkv_cols, out_cols = w_qkv.shape[1], w_out.shape[1]
    pair_cols = 2 * w_qkv.shape[0]
    in_rows, in_cols = w_in.shape
    back_rows, back_cols = w_back.shape
    half_q, half_o = qkv_cols // 2, out_cols // 2

    if by_permute:

        def paired(turned):
            half = turned.shape[0] // 2
            first, second = turned[:half], turned[half:]
            mine = jnp.where(core == 0, first, second)
            other = exchange(jnp.where(core == 0, second, first), 4)
            return jnp.where(
                core == 0,
                jnp.concatenate([mine, other], axis=1),
                jnp.concatenate([other, mine], axis=1),
            )

        slots = device_slots(spot)
        to_qkv = Gather(paired(w_qkv.T))
        to_in = Gather(jnp.concatenate([w_in, paired(w_out.T)], axis=0))
        to_back = Gather(w_back.T)
        to_small = Gather(jnp.pad(own_small, (0, 1024 - own_small.size)).reshape(8, 128))
        tracks = (to_qkv, to_small, to_in, to_back)
        step(to_qkv, to_small)
        sync((), *tracks)
        step(to_qkv, to_small)
        sync((), *tracks)
        step(to_qkv, to_small, to_in)
        sync((), *tracks)
        step(to_qkv, to_small, to_in)
        sync((), *tracks)
        step(to_qkv, to_small, to_in, to_back)
        tokens = sync(tokens, *tracks)
        qkv_weight = weight_of(
            to_qkv.state, (0, half_q, pair_cols),
            lambda x, c, f: (f * qkv_cols + c * half_q, x * pair_cols), (3 * width, width),
        )
        arrived = widen(jnp.concatenate(to_small.state)).reshape(32, 1024)
        every = jnp.dot(slots, arrived, precision=lax.Precision.HIGHEST)

        def back_blocks(index):
            return [(f * back_cols, 0, index >> 1, index & 1, f >> 1, f & 1) for f in range(8)]

        def in_blocks(index):
            return [
                ((2 * x + c) * in_rows, y * in_cols, x, c, index, y)
                for x in range(2) for c in range(2) for y in range(2)
            ]

        def out_blocks(index):
            return [
                (f * out_cols + c * half_o, 0, index, c, f >> 1, f & 1)
                for f in range(8) for c in range(2)
            ]

        def qkv_blocks(index):
            return [
                (f * qkv_cols + c * half_q, 0, index, c, f >> 1, f & 1)
                for f in range(8) for c in range(2)
            ]

        plans = {
            "back": (back_rows, back_blocks, (back_cols, back_rows), back_cols, 0),
            "in": (2 * in_cols, in_blocks, (in_rows, in_cols), in_rows + half_o, 0),
            "out": (pair_cols, out_blocks, (half_o, pair_cols), in_rows + half_o, in_rows),
            "qkv": (pair_cols, qkv_blocks, (half_q, pair_cols), half_q, 0),
        }
    else:

        def full(shard):
            return lax.all_gather(
                lax.all_gather(shard, fsdp_axes, axis=1, tiled=True), dp_axes, axis=0, tiled=True
            )

        qkv_weight = whole_weight(full(w_qkv).T)
        out_weight = whole_weight(full(w_out).T)
        in_weight = whole_weight(full(w_in))
        back_weight = whole_weight(full(w_back).T)
        every = widen(lax.all_gather(own_small, axes, axis=0, tiled=False))
        plans = {name: (width // 2, None, (0, 0), 0, 0) for name in ("back", "in", "out", "qkv")}
        tracks = ()

    bias_values, hidden_bias, gain_values = small_vectors(every, shards)
    qkv_bias = jnp.concatenate(
        [bias_values[0:1], jnp.zeros((1, width), F32), bias_values[1:2]], axis=1
    )

    if by_permute:
        step(to_in)
    qkv = project_qkv(spot, tokens, qkv_weight, qkv_bias)
    if by_permute:
        qkv = sync(qkv, to_back)
        step(to_back)
    attended = None
    for block in blocks:
        attended = attend_forward(block, qkv, segment_row, attended)
        if by_permute and block == 0:
            attended = sync(attended, to_in, to_back)
            step(to_in, to_back)
    context, lse = attended
    if by_permute:
        context = sync(context, to_in, to_back)
        step(to_back)
        context = sync(context, to_back)
        step(to_back)
        in_weight = weight_of(
            to_in.state, (0, in_rows, in_cols),
            lambda x, c, f: ((2 * x + c) * in_rows, f * in_cols), (width, wide),
        )
        out_weight = weight_of(
            to_in.state, (in_rows, half_o, pair_cols),
            lambda x, c, f: (f * out_cols + c * half_o, x * pair_cols), (width, width),
        )
        back_weight = weight_of(
            to_back.state, (0, back_cols, back_rows),
            lambda x, c, f: (f * back_cols, (2 * x + c) * back_rows), (width, wide),
        )
    (normal_one, inverse_one, normed_low, slope, layer_out, d_two, d_low, sums_two,
     *grad_back) = forward_rows(
        spot, context, tokens, out_grad, out_weight, in_weight, back_weight, bias_values,
        hidden_bias, gain_values, plans["back"],
    )
    if by_permute:
        from_back = Reduce(*grad_back)
        d_low = sync(d_low, from_back)
        step(from_back)
    d_one, d_context, sums_one, hidden_sum, *grads_in = backward_rows(
        spot, d_low, slope, d_two, normal_one, inverse_one, normed_low, context, back_weight,
        in_weight, out_weight, gain_values, plans["in"], plans["out"],
    )
    if by_permute:
        from_in = Reduce(*grads_in)
        d_context = sync(d_context, from_back, from_in)
        step(from_back, from_in)
    else:
        grad_in, grad_out = grads_in
        grad_back, = grad_back
    attended, sums_query, sums_value = None, [], []
    for block in blocks:
        *attended, sum_query, sum_value = attend_backward(
            block, qkv, segment_row, lse, context, d_context, attended
        )
        sums_query.append(sum_query)
        sums_value.append(sum_value)
        if by_permute:
            attended = sync(attended, from_back, from_in)
            step(from_back, from_in)
    grad_qkv = gradient(spot, attended, tokens, plans["qkv"])
    if by_permute:
        from_qkv = Reduce(*grad_qkv)
        d_one = sync(d_one, from_back, from_in, from_qkv)
        step(from_back, from_in, from_qkv)
    else:
        grad_qkv, = grad_qkv
    tokens_grad = tokens_backward(spot, d_one, *attended, qkv_weight)

    bias_total = jnp.concatenate(
        [sum(sums_query), sum(sums_value), sums_one[2:3], sums_one[1:2], sums_two[2:3], sums_two[1:2]]
    )
    gain_total = jnp.concatenate([sums_one[0:1], sums_two[0:1]])
    small = small_parts(bias_total, hidden_sum[0], gain_total, devices)

    if by_permute:

        def unpaired(sums):
            half = sums.shape[1] // 2
            left, right = sums[:, :half], sums[:, half:]
            mine = jnp.where(core == 0, left, right)
            other = widen(exchange(jnp.where(core == 0, right, left).astype(BF), 4))
            return jnp.where(
                core == 0,
                jnp.concatenate([mine, other], axis=0),
                jnp.concatenate([other, mine], axis=0),
            )

        small = jnp.dot(slots.T, small, precision=lax.Precision.HIGHEST)
        small = jnp.pad(small, ((0, 0), (0, 1024 - small.shape[1]))).reshape(32, 8, 128)
        from_small = Reduce(small[:16], small[16:], F32)
        step(from_small)
        tokens_grad = sync(tokens_grad, from_in, from_qkv, from_small)
        step(from_in, from_qkv, from_small)
        for _ in range(3):
            sync((), from_qkv, from_small)
            step(from_qkv, from_small)
        own_back = from_back.result().T
        sums_in = from_in.result()
        own_in = sums_in[:in_rows]
        own_out = unpaired(sums_in[in_rows:]).T
        own_qkv = unpaired(from_qkv.result()).T
        small = from_small.result().reshape(-1)
    else:

        def scattered(total):
            part = lax.psum_scatter(total, dp_axes, scatter_dimension=0, tiled=True)
            part = lax.psum_scatter(part, fsdp_axes, scatter_dimension=1, tiled=True)
            return widen(part)

        own_back = scattered(grad_back.T)
        own_in = scattered(grad_in)
        own_out = scattered(grad_out.T)
        own_qkv = scattered(grad_qkv.T)
        small = lax.psum_scatter(small.astype(BF), axes, scatter_dimension=0, tiled=True)
        small = widen(small).reshape(-1)
    first, second = biases.size, biases.size + in_bias.size
    own_bias = small[:first].reshape(biases.shape)
    own_hidden = small[first:second]
    own_gain = small[second : second + gains.size].reshape(gains.shape)
    return (
        layer_out, tokens_grad, own_qkv, own_out, own_in, own_back, own_bias, own_hidden, own_gain,
    )


def solution(mesh):
    dp, fsdp = mesh.devices.shape
    sizes = (dp // 2, 2, fsdp // 2, 2)
    split = Mesh(mesh.devices.reshape(sizes), ("x", "core", "z", "y"))
    outer, inner = ("x", "core"), ("z", "y")
    every = outer + inner
    rows = P(every, None)
    weight = P(outer, inner)
    vectors = P(None, every)

    def placed(*arrays):
        return on_device(sizes, *arrays)

    return jax.shard_map(
        placed,
        mesh=split,
        in_specs=(rows, rows, weight, weight, weight, weight, vectors, P(every), vectors, rows),
        out_specs=(rows, rows, weight, weight, weight, weight, vectors, P(every), vectors),
        check_vma=False,
    )
```

```python
import math

import jax
import jax.numpy as jnp
from jax import lax
from jax.experimental import pallas as pl
from jax.experimental.pallas import tpu as pltpu
from jax.sharding import Mesh, PartitionSpec as P

HEADS = 12
HD = 64
BLOCK = 512
PAIR = 2 * HD
TILE = 256
VMEM = 58 * 1024 * 1024
BF = jnp.bfloat16
F32 = jnp.float32
Z1, Z2, FIRST, SECOND, CORE, Z3 = range(6)
NT = (((1,), (1,)), ((), ()))


def dot(a, b):
    return jnp.dot(a, b, preferred_element_type=F32)


def dot_nt(a, b):
    return lax.dot_general(a, b, NT, preferred_element_type=F32)


def any_spec():
    return pl.BlockSpec(memory_space=pl.ANY)


def params(*semantics):
    return pltpu.CompilerParams(
        dimension_semantics=semantics if semantics else None, vmem_limit_bytes=VMEM
    )


def cost(flops, nbytes, trans=0):
    return pl.CostEstimate(flops=flops, bytes_accessed=nbytes, transcendentals=trans)

def layer_norm_parts(rows):
    center = jnp.mean(rows, axis=-1, keepdims=True)
    centered = rows - center
    spread = jnp.mean(centered * centered, axis=-1, keepdims=True)
    inverse = lax.rsqrt(spread + 1e-05)
    return centered * inverse, inverse


def layer_norm_back(grad, normal, inverse):
    mean_grad = jnp.mean(grad, axis=-1, keepdims=True)
    mean_both = jnp.mean(grad * normal, axis=-1, keepdims=True)
    return (grad - mean_grad - normal * mean_both) * inverse


def add_rows(ref, values):
    ref[...] += jnp.sum(values, axis=0, keepdims=True)


def zero_first(*refs):
    @pl.when(pl.program_id(0) == 0)
    def _():
        for ref in refs:
            ref[...] = jnp.zeros_like(ref)


def call(
    body, grid, spot, arrays, specs, weights, outs, out_specs, scratch=(), estimate=None, aliases=()
):
    flat = [piece for pieces, _, _ in weights for piece in pieces]
    counts = [len(pieces) for pieces, _, _ in weights]
    n_arrays, n_flat, n_weights = len(arrays), len(flat), len(weights)
    n_outs = len(outs) if isinstance(outs, tuple) else 1

    def kernel(spot_ref, *refs):
        ins = refs[:n_arrays]
        piece_refs = refs[n_arrays : n_arrays + n_flat]
        out_refs = refs[n_arrays + n_flat : n_arrays + n_flat + n_outs]
        rest = refs[n_arrays + n_flat + n_outs :]
        held = rest[:n_weights]
        sems = rest[n_weights : 2 * n_weights]
        extra = rest[2 * n_weights :]
        first = pl.program_id(0) == 0

        def copies(number):
            start = sum(counts[:number])
            found = []
            for index in range(counts[number]):
                place = weights[number][1][index]
                for source, at in place(spot_ref, piece_refs[start + index]):
                    found.append(
                        pltpu.make_async_copy(
                            source, held[number].at[at], sems[number].at[len(found)]
                        )
                    )
            return found

        @pl.when(first)
        def _():
            for number in range(n_weights):
                for copy in copies(number):
                    copy.start()

        def ready(number):
            def wait():
                @pl.when(first)
                def _():
                    for copy in copies(number):
                        copy.wait()

                return held[number]

            return wait

        body(spot_ref, *ins, *[ready(number) for number in range(n_weights)], *out_refs, *extra)

    scratch_shapes = (
        [pltpu.VMEM(shape, BF) for _, _, shape in weights]
        + [pltpu.SemaphoreType.DMA((4 * count,)) for count in counts]
        + list(scratch)
    )
    return pl.pallas_call(
        kernel,
        out_shape=outs,
        grid_spec=pltpu.PrefetchScalarGridSpec(
            num_scalar_prefetch=1,
            grid=grid,
            in_specs=list(specs) + [any_spec()] * n_flat,
            out_specs=out_specs,
            scratch_shapes=scratch_shapes,
        ),
        compiler_params=params(*(["arbitrary"] * len(grid))),
        cost_estimate=estimate,
        input_output_aliases=dict(aliases),
    )(spot, *arrays, *flat)


def row(width, tile=TILE):
    return pl.BlockSpec((tile, width), lambda i, s: (i, 0))


def fixed(*shape):
    return pl.BlockSpec(shape, lambda *_: (0,) * len(shape))


def shape(dims, dtype):
    return jax.ShapeDtypeStruct(dims, dtype)


def project_qkv(spot, tokens, w_qkv, qkv_bias):
    count, width = tokens.shape
    wide = w_qkv[2][0]

    def body(spot_ref, x_ref, bias_ref, w_ready, out_ref):
        w_ref = w_ready()
        for start in range(0, wide, width):
            part = slice(start, start + width)
            out_ref[:, part] = (dot_nt(x_ref[...], w_ref[part, :]) + bias_ref[:, part]).astype(BF)

    return call(
        body, (count // TILE,), spot, (tokens, qkv_bias), (row(width), fixed(1, wide)), [w_qkv],
        shape((count, wide), BF), row(wide),
        estimate=cost(2 * count * width * wide, 2 * (count * width + wide * width + count * wide)),
    )


def lane_masks():
    lane = lax.broadcasted_iota(jnp.int32, (1, PAIR), 1)
    return [(lane // HD == head) for head in range(2)]


def same_segment(row_ref):
    numbers = row_ref[0].astype(F32)
    column = jnp.broadcast_to(numbers, (128, BLOCK)).T[:, 0:1]
    return column == numbers


def attend_forward(block, qkv, segment_row, into=None):
    count, wide = qkv.shape
    width = wide // 3
    pairs = width // PAIR
    blocks = count // BLOCK

    def body(q_ref, k_ref, v_ref, row_ref, *refs):
        out_ref, lse_ref = refs[-2:]
        visible = same_segment(row_ref)
        query, key = q_ref[...] * BF(1.0 / math.sqrt(HD)), k_ref[...]
        value_turned = v_ref[...].T
        parts = []
        for head, lanes in enumerate(lane_masks()):
            scores = dot_nt(key, jnp.where(lanes, query, BF(0)))
            scores = jnp.where(visible, scores, -1e30)
            highest = jnp.max(scores, axis=0, keepdims=True)
            exponent = jnp.exp(scores - highest)
            total = jnp.sum(exponent, axis=0, keepdims=True)
            part = dot(value_turned[head * HD : (head + 1) * HD], exponent.astype(BF))
            parts.append(part / total)
            lse_ref[0, 0, head : head + 1, :] = highest + jnp.log(total)
        out_ref[...] = jnp.concatenate(parts, axis=0).T.astype(BF)

    flops = 4 * HEADS * BLOCK * BLOCK * HD
    given = () if into is None else into
    return pl.pallas_call(
        body,
        out_shape=(shape((count, width), BF), shape((blocks, pairs, 2, BLOCK), F32)),
        grid=(pairs,),
        in_specs=[
            pl.BlockSpec((BLOCK, PAIR), lambda p: (block, p)),
            pl.BlockSpec((BLOCK, PAIR), lambda p: (block, pairs + p)),
            pl.BlockSpec((BLOCK, PAIR), lambda p: (block, 2 * pairs + p)),
            pl.BlockSpec((1, 1, BLOCK), lambda p: (block, 0, 0)),
        ]
        + [any_spec()] * len(given),
        out_specs=(
            pl.BlockSpec((BLOCK, PAIR), lambda p: (block, p)),
            pl.BlockSpec((1, 1, 2, BLOCK), lambda p: (block, p, 0, 0)),
        ),
        compiler_params=params("arbitrary"),
        cost_estimate=cost(4 * flops, 4 * count * width, HEADS * BLOCK * BLOCK),
        input_output_aliases={4 + index: index for index in range(len(given))},
    )(qkv, qkv, qkv, segment_row, *given)


def attend_backward(block, qkv, segment_row, lse, context, d_context, into=None):
    count, wide = qkv.shape
    width = wide // 3
    pairs = width // PAIR
    factor = 1.0 / math.sqrt(HD)

    def body(q_ref, k_ref, v_ref, o_ref, do_ref, row_ref, lse_ref, *refs):
        dq_ref, dk_ref, dv_ref, sum_q_ref, sum_v_ref = refs[-5:]
        visible = same_segment(row_ref)
        query, key, value = q_ref[...] * BF(factor), k_ref[...], v_ref[...]
        d_out = do_ref[...]
        key_turned = key.T
        product = (d_out.astype(F32) * o_ref[...].astype(F32)).T
        masks = lane_masks()
        d_query, d_key, d_value = [], [], []
        for head, lanes in enumerate(masks):
            inside = slice(head * HD, (head + 1) * HD)
            delta = jnp.sum(product[inside], axis=0, keepdims=True)
            scores = dot_nt(key, jnp.where(lanes, query, BF(0)))
            scores = jnp.where(visible, scores - lse_ref[0, 0, head : head + 1, :], -1e30)
            prob = jnp.exp(scores)
            d_prob = dot_nt(value, jnp.where(lanes, d_out, BF(0)))
            d_score = (prob * (d_prob - delta)).astype(BF)
            d_value.append(dot(prob.astype(BF), d_out))
            d_key.append(dot(d_score, query))
            d_query.append(dot(key_turned[inside], d_score) * factor)
        dq = jnp.concatenate(d_query, axis=0).T.astype(BF)
        dk = jnp.where(masks[0], d_key[0], d_key[1]).astype(BF)
        dv = jnp.where(masks[0], d_value[0], d_value[1]).astype(BF)
        dq_ref[...] = dq
        dk_ref[...] = dk
        dv_ref[...] = dv
        sum_q_ref[...] = jnp.sum(dq.astype(F32), axis=0, keepdims=True)
        sum_v_ref[...] = jnp.sum(dv.astype(F32), axis=0, keepdims=True)

    tile = pl.BlockSpec((BLOCK, PAIR), lambda p: (block, p))
    flops = 10 * HEADS * BLOCK * BLOCK * HD
    given = () if into is None else into
    return pl.pallas_call(
        body,
        out_shape=(shape((count, width), BF),) * 3 + (shape((1, width), F32),) * 2,
        grid=(pairs,),
        in_specs=[
            tile,
            pl.BlockSpec((BLOCK, PAIR), lambda p: (block, pairs + p)),
            pl.BlockSpec((BLOCK, PAIR), lambda p: (block, 2 * pairs + p)),
            tile,
            tile,
            pl.BlockSpec((1, 1, BLOCK), lambda p: (block, 0, 0)),
            pl.BlockSpec((1, 1, 2, BLOCK), lambda p: (block, p, 0, 0)),
        ]
        + [any_spec()] * len(given),
        out_specs=(tile,) * 3 + (pl.BlockSpec((1, PAIR), lambda p: (0, p)),) * 2,
        compiler_params=params("arbitrary"),
        cost_estimate=cost(4 * flops, 8 * count * width, HEADS * BLOCK * BLOCK),
        input_output_aliases={7 + index: index for index in range(len(given))},
    )(qkv, qkv, qkv, context, d_context, segment_row, lse, *given)


def emit(plan, step, held, spot_ref, out_refs, sems):
    tile, blocks, (rows, cols), _, base = plan
    if blocks is None:
        target = out_refs[0].at[:, pl.ds(pl.multiple_of(step * tile, tile), tile)]
        pltpu.make_async_copy(held.at[step], target, sems.at[step]).start()
        return
    listed = blocks(step)
    for index, (row_at, column_at, x, core, z, y) in enumerate(listed):
        source = held.at[step, pl.ds(row_at, rows), pl.ds(column_at, cols)]
        sem = sems.at[step * len(listed) + index]
        far_x, far_y = x ^ spot_ref[0], y ^ spot_ref[3]
        first = far_x + core * (far_y - far_x)
        depth = z ^ spot_ref[2]
        slot = (depth & 1) + 2 * first + 4 * (far_x + far_y - first) + 8 * (depth >> 1)
        mine = (core ^ spot_ref[1]) == 0

        @pl.when(mine)
        def _():
            pltpu.make_async_copy(source, out_refs[0].at[slot, pl.ds(base, rows)], sem).start()

        @pl.when(jnp.logical_not(mine))
        def _():
            pltpu.make_async_copy(source, out_refs[1].at[slot, pl.ds(base, rows)], sem).start()


def emitted(plan, steps, held, out_refs, sems):
    tile, blocks, (rows, cols), _, base = plan
    if blocks is None:
        for step in range(steps):
            target = out_refs[0].at[:, pl.ds(step * tile, tile)]
            pltpu.make_async_copy(held.at[step], target, sems.at[step]).wait()
        return
    for index in range(32):
        source = held.at[0, pl.ds(0, rows), pl.ds(0, cols)]
        pltpu.make_async_copy(source, out_refs[0].at[0, pl.ds(base, rows)], sems.at[index]).wait()


def emit_shapes(plan, total, columns):
    _, blocks, (rows, cols), slot_rows, _ = plan
    if blocks is None:
        return (shape((total, columns), BF),)
    return (shape((16, slot_rows, cols), BF),) * 2


def clamped(width, last, tile=TILE):
    return pl.BlockSpec((tile, width), lambda i, s: (jnp.minimum(i, last), 0))


def project_out(spot, context, tokens, w_out, biases, gains):
    count, width = tokens.shape

    def body(spot_ref, c_ref, x_ref, bias_ref, gain_ref, w_ready, normal_ref, inverse_ref, low_ref):
        w_ref = w_ready()
        resid = x_ref[...].astype(F32) + (dot_nt(c_ref[...], w_ref[...]) + bias_ref[2:3])
        normal, inverse = layer_norm_parts(resid)
        normal_ref[...] = normal
        inverse_ref[...] = jnp.broadcast_to(inverse, inverse_ref.shape)
        low_ref[...] = (normal * gain_ref[0:1] + bias_ref[3:4]).astype(BF)

    return call(
        body, (count // TILE,), spot, (context, tokens, biases, gains),
        (row(width), row(width), fixed(*biases.shape), fixed(*gains.shape)), [w_out],
        (shape((count, width), F32), shape((count, 128), F32), shape((count, width), BF)),
        (row(width), row(128), row(width)),
        estimate=cost(2 * count * width * width, 10 * count * width),
    )


def ffn_in(spot, normed_low, w_in, in_bias):
    count, width = normed_low.shape
    wide = w_in[2][1]

    def body(spot_ref, x_ref, bias_ref, w_ready, hidden_ref, slope_ref):
        w_ref = w_ready()
        for start in range(0, wide, width):
            part = slice(start, start + width)
            pre = dot(x_ref[...], w_ref[:, part]) + bias_ref[:, part]
            cdf = 0.5 + 0.5 * lax.erf(pre * (1.0 / math.sqrt(2.0)))
            hidden_ref[:, part] = (pre * cdf).astype(BF)
            density = jnp.exp(pre * pre * -0.5) * (1.0 / math.sqrt(2.0 * math.pi))
            slope_ref[:, part] = (cdf + pre * density).astype(BF)

    return call(
        body, (count // TILE,), spot, (normed_low, in_bias), (row(width), fixed(1, wide)), [w_in],
        (shape((count, wide), BF),) * 2, (row(wide),) * 2,
        estimate=cost(2 * count * width * wide, 4 * count * wide, 2 * count * wide),
    )


def forward_rows(spot, hidden, normal_one, out_grad, w_back, biases, gains, plan):
    count, width = out_grad.shape
    wide = hidden.shape[1]
    steps = count // TILE
    tile = plan[0]
    columns = wide // tile
    shapes = emit_shapes(plan, width, wide)

    def body(spot_ref, h_ref, n_ref, g_ref, bias_ref, gain_ref, wb_ready,
             out_ref, d_two_ref, d_low_ref, sums_ref, *refs):
        grads, (kept, d_rows, turned, held, sems) = refs[: len(shapes)], refs[len(shapes) :]
        index = pl.program_id(0)
        zero_first(sums_ref)

        @pl.when(index < steps)
        def _():
            here = pl.ds(pl.multiple_of(index * TILE, TILE), TILE)
            kept[here, :] = h_ref[...]
            resid = n_ref[...] * gain_ref[0:1] + bias_ref[3:4]
            w_ref = wb_ready()
            resid += dot_nt(h_ref[...], w_ref[...]) + bias_ref[4:5]
            normal, inverse = layer_norm_parts(resid)
            out_ref[...] = (normal * gain_ref[1:2] + bias_ref[5:6]).astype(BF)
            grad = g_ref[...].astype(F32)
            d_two = layer_norm_back(grad * gain_ref[1:2], normal, inverse)
            d_low = d_two.astype(BF)
            d_two_ref[...] = d_two
            d_low_ref[...] = d_low
            d_rows[here, :] = d_low
            add_rows(sums_ref.at[0:1], grad * normal)
            add_rows(sums_ref.at[1:2], grad)
            add_rows(sums_ref.at[2:3], d_low.astype(F32))

        @pl.when(index == steps)
        def _():
            turned[...] = d_rows[...].T

        @pl.when(index >= steps)
        def _():
            column = index - steps
            at = pl.ds(pl.multiple_of(column * tile, tile), tile)
            held[column] = dot(turned[...], kept[:, at]).astype(BF)
            emit(plan, column, held, spot_ref, grads, sems)

        @pl.when(index == steps + columns - 1)
        def _():
            emitted(plan, columns, held, grads, sems)

    last = steps - 1
    rows = lambda wide_: clamped(wide_, last)
    return call(
        body, (steps + columns,), spot, (hidden, normal_one, out_grad, biases, gains),
        (rows(wide), rows(width), rows(width), fixed(*biases.shape), fixed(*gains.shape)),
        [w_back],
        (shape((count, width), BF), shape((count, width), F32), shape((count, width), BF),
         shape((8, width), F32), *shapes),
        (rows(width), rows(width), rows(width), fixed(8, width), *[any_spec()] * len(shapes)),
        [pltpu.VMEM((count, wide), BF), pltpu.VMEM((count, width), BF),
         pltpu.VMEM((width, count), BF), pltpu.VMEM((columns, width, tile), BF),
         pltpu.SemaphoreType.DMA((32,))],
        cost(4 * count * width * wide, 14 * count * width + 4 * count * wide),
    )


def backward_rows(
    spot, d_low, slope, d_two, normal_one, inverse_one, normed_low, context, w_back, w_in, w_out,
    gains, plan_in, plan_out,
):
    count, width = d_two.shape
    wide = slope.shape[1]
    steps = count // TILE
    tile_in, tile_out = plan_in[0], plan_out[0]
    columns_in, columns_out = wide // tile_in, width // tile_out
    shared = plan_in[1] is not None
    shapes = emit_shapes(plan_in, width, wide)
    if not shared:
        shapes += emit_shapes(plan_out, width, width)

    def body(spot_ref, dl_ref, s_ref, d2_ref, n_ref, i_ref, low_ref, c_ref, gain_ref,
             wb_ready, wi_ready, wo_ready,
             d_one_ref, d_context_ref, sums_ref, hidden_sum_ref, *refs):
        grads = refs[: len(shapes)]
        d_pre, d_attn, turned, held_in, held_out, sems_in, sems_out = refs[len(shapes) :]
        grads_in, grads_out = (grads, grads) if shared else (grads[:1], grads[1:])
        index = pl.program_id(0)
        zero_first(sums_ref, hidden_sum_ref)

        @pl.when(index < steps)
        def _():
            here = pl.ds(pl.multiple_of(index * TILE, TILE), TILE)
            w_ref = wb_ready()
            for start in range(0, wide, width):
                part = slice(start, start + width)
                d_hidden = dot(dl_ref[...], w_ref[:, part])
                piece = (d_hidden * s_ref[:, part].astype(F32)).astype(BF)
                d_pre[here, part] = piece
                add_rows(hidden_sum_ref.at[:, part], piece.astype(F32))
            w_ref = wi_ready()
            d_normed = d2_ref[...] + dot_nt(d_pre[here, :], w_ref[...])
            normal = n_ref[...]
            d_one = layer_norm_back(d_normed * gain_ref[0:1], normal, i_ref[:, 0:1])
            low = d_one.astype(BF)
            d_one_ref[...] = d_one
            d_attn[here, :] = low
            d_context_ref[...] = dot(low, wo_ready()[...]).astype(BF)
            add_rows(sums_ref.at[0:1], d_normed * normal)
            add_rows(sums_ref.at[1:2], d_normed)
            add_rows(sums_ref.at[2:3], low.astype(F32))

        @pl.when(index == steps)
        def _():
            turned[...] = low_ref[...].T

        @pl.when(jnp.logical_and(index >= steps, index < steps + columns_in))
        def _():
            column = index - steps
            at = pl.ds(pl.multiple_of(column * tile_in, tile_in), tile_in)
            held_in[column] = dot(turned[...], d_pre[:, at]).astype(BF)
            emit(plan_in, column, held_in, spot_ref, grads_in, sems_in)

        @pl.when(index == steps + columns_in)
        def _():
            turned[...] = d_attn[...].T

        @pl.when(index >= steps + columns_in)
        def _():
            column = index - steps - columns_in
            held_out[column] = dot(turned[...], c_ref[...]).astype(BF)
            emit(plan_out, column, held_out, spot_ref, grads_out, sems_out)

        @pl.when(index == steps + columns_in + columns_out - 1)
        def _():
            emitted(plan_in, columns_in, held_in, grads_in, sems_in)
            emitted(plan_out, columns_out, held_out, grads_out, sems_out)

    last, before = steps - 1, steps + columns_in
    rows = lambda wide_: clamped(wide_, last)
    return call(
        body, (steps + columns_in + columns_out,), spot,
        (d_low, slope, d_two, normal_one, inverse_one, normed_low, context, gains),
        (rows(width), rows(wide), rows(width), rows(width), rows(128), fixed(count, width),
         pl.BlockSpec((count, tile_out), lambda i, s: (0, jnp.maximum(i - before, 0))),
         fixed(*gains.shape)),
        [w_back, w_in, w_out],
        (shape((count, width), F32), shape((count, width), BF), shape((8, width), F32),
         shape((1, wide), F32), *shapes),
        (rows(width), rows(width), fixed(8, width), fixed(1, wide), *[any_spec()] * len(shapes)),
        [pltpu.VMEM((count, wide), BF), pltpu.VMEM((count, width), BF),
         pltpu.VMEM((width, count), BF), pltpu.VMEM((columns_in, width, tile_in), BF),
         pltpu.VMEM((columns_out, width, tile_out), BF),
         pltpu.SemaphoreType.DMA((32,)), pltpu.SemaphoreType.DMA((32,))],
        cost(2 * count * width * (3 * wide + 2 * width), 18 * count * width + 2 * count * wide),
    )


def tokens_backward(spot, d_one, d_query, d_key, d_value, w_qkv):
    count, width = d_one.shape

    def body(spot_ref, d1_ref, q_ref, k_ref, v_ref, w_ready, out_ref):
        w_ref = w_ready()
        total = d1_ref[...] + dot(q_ref[...], w_ref[0:width, :])
        total += dot(k_ref[...], w_ref[width : 2 * width, :])
        total += dot(v_ref[...], w_ref[2 * width : 3 * width, :])
        out_ref[...] = total.astype(BF)

    return call(
        body, (count // TILE,), spot, (d_one, d_query, d_key, d_value), (row(width),) * 4, [w_qkv],
        shape((count, width), BF), row(width),
        estimate=cost(6 * count * width * width, 12 * count * width),
    )


def gradient(spot, lefts, right, plan):
    count, columns = right.shape
    width = lefts[0].shape[1]
    total = width * len(lefts)
    tile = plan[0]
    steps = columns // tile
    n_left = len(lefts)
    shapes = emit_shapes(plan, total, columns)

    def body(spot_ref, *refs):
        left_refs, right_ref = refs[:n_left], refs[n_left]
        grads = refs[n_left + 1 : n_left + 1 + len(shapes)]
        turned, held, sems = refs[-3:]
        step = pl.program_id(0)

        @pl.when(step == 0)
        def _():
            for index, ref in enumerate(left_refs):
                turned[index * width : (index + 1) * width, :] = ref[...].T

        for index in range(n_left):
            part = slice(index * width, (index + 1) * width)
            held[step, part, :] = dot(turned[part, :], right_ref[...]).astype(BF)
        emit(plan, step, held, spot_ref, grads, sems)

        @pl.when(step == steps - 1)
        def _():
            emitted(plan, steps, held, grads, sems)

    return call(
        body, (steps,), spot, (*lefts, right),
        (*[fixed(count, width)] * n_left, pl.BlockSpec((count, tile), lambda i, s: (0, i))), [],
        shapes, (any_spec(),) * len(shapes),
        [pltpu.VMEM((total, count), BF), pltpu.VMEM((steps, total, tile), BF),
         pltpu.SemaphoreType.DMA((32,))],
        cost(2 * count * total * columns, 2 * (count * (total + columns) + total * columns)),
    )


def widen(value):
    return value.astype(F32)


def exchange(value, stage):
    axes = ("x", "core", "z", "y")
    pairs = []
    for source in range(32):
        x, core, z, y = source >> 4, (source >> 3) & 1, (source >> 1) & 3, source & 1
        if stage in (Z1, Z2, Z3):
            z ^= {Z1: 1, Z2: 2, Z3: 3}[stage]
        elif stage == CORE:
            core ^= 1
        elif (stage == FIRST) == (core == 0):
            x ^= 1
        else:
            y ^= 1
        pairs.append((source, 16 * x + 8 * core + 2 * z + y))
    return lax.ppermute(value, axes, pairs)


def join(*parts):
    return jnp.concatenate(parts)


class Track:
    def __init__(self, **held):
        self.held = held

    def go(self, *names):
        for name in names:
            getattr(self, name)()


class Gather(Track):
    def __init__(self, piece):
        super().__init__(own=piece[None])

    def z1(self):
        self.held["z1"] = exchange(self.held["own"], Z1)

    def z2(self):
        self.held["near"] = join(self.held["own"], self.held["z1"])
        self.held["z2"] = exchange(self.held["near"], Z2)

    def first_a(self):
        self.held["first_a"] = exchange(self.held["near"], FIRST)

    def first_b(self):
        self.held["first_b"] = exchange(self.held["z2"], FIRST)

    def second_a(self):
        self.held["a"] = join(self.held["near"], self.held["first_a"])
        self.held["second_a"] = exchange(self.held["a"], SECOND)

    def second_b(self):
        self.held["b"] = join(self.held["z2"], self.held["first_b"])
        self.held["second_b"] = exchange(self.held["b"], SECOND)

    def core_a(self):
        self.held["core_a"] = exchange(self.held["a"], CORE)
        self.held["cross_a"] = exchange(self.held["second_a"], CORE)

    def core_b(self):
        self.held["core_b"] = exchange(self.held["b"], CORE)
        self.held["cross_b"] = exchange(self.held["second_b"], CORE)

    def result(self):
        names = ("a", "second_a", "b", "second_b", "core_a", "cross_a", "core_b", "cross_b")
        return [self.held[name] for name in names]


class Reduce(Track):
    def core(self):
        self.held["core"] = exchange(self.held["far"], CORE)

    def sum(self, start, stop, *others):
        total = widen(self.held["near"][start:stop]) + widen(self.held["core"][start:stop])
        for name, at in others:
            total += widen(self.held[name][at : at + stop - start])
        return total

    def second_b(self):
        self.held["second_b"] = exchange(self.sum(12, 16).astype(BF), SECOND)

    def second_a(self):
        self.held["second_a"] = exchange(self.sum(4, 8).astype(BF), SECOND)

    def first_b(self):
        self.held["first_b"] = exchange(self.sum(10, 12, ("second_b", 2)).astype(BF), FIRST)

    def first_a(self):
        self.held["first_a"] = exchange(self.sum(2, 4, ("second_a", 2)).astype(BF), FIRST)

    def z2(self):
        total = self.sum(8, 10, ("second_b", 0), ("first_b", 0))
        self.held["z2"] = exchange(total.astype(BF), Z2)

    def z1(self):
        total = self.sum(1, 2, ("second_a", 1), ("first_a", 1), ("z2", 1))
        self.held["z1"] = exchange(total.astype(BF), Z1)

    def direct_b(self):
        two = self.sum(8, 9, ("second_b", 0), ("first_b", 0))
        three = self.sum(9, 10, ("second_b", 1), ("first_b", 1))
        self.held["z2"] = exchange(two.astype(BF), Z2)
        self.held["z3"] = exchange(three.astype(BF), Z3)

    def direct_a(self):
        total = self.sum(1, 2, ("second_a", 1), ("first_a", 1))
        self.held["z1"] = exchange(total.astype(BF), Z1)

    def result(self):
        names = [name for name in ("second_a", "first_a", "z1", "z2", "z3") if name in self.held]
        return self.sum(0, 1, *[(name, 0) for name in names])[0]


class SmallGather(Track):
    def __init__(self, piece):
        super().__init__(all=piece[None])

    def step(self, stage):
        self.held["all"] = join(self.held["all"], exchange(self.held["all"], stage))


class SmallReduce(Track):
    def __init__(self, slots):
        super().__init__(all=slots)

    def step(self, stage):
        half = self.held["all"].shape[0] // 2
        self.held["all"] = self.held["all"][:half] + exchange(self.held["all"][half:], stage)


def sync(values, *waits):
    held = [{name: track.held[name] for name in names} for track, *names in waits]
    values, held = lax.optimization_barrier((values, held))
    for (track, *_), found in zip(waits, held):
        track.held.update(found)
    return values


def source_of(spot, core, first, second, depth):
    x = spot[0] ^ (first + core * (second - first))
    y = spot[3] ^ (second + core * (first - second))
    return x, 2 * (spot[2] ^ depth) + y


def weight_of(arrays, source_rows, place, dims):
    start, rows, cols = source_rows
    pieces, places = [], []
    for position, array in enumerate(arrays):
        pieces.append(array)

        def at(spot_ref, ref, position=position):
            core = spot_ref[1] ^ (position >> 2)
            for index in range(4):
                depth = 2 * ((position >> 1) & 1) + (index & 1)
                x, f = source_of(spot_ref, core, index >> 1, position & 1, depth)
                row_at, column_at = place(x, core, f)
                yield (
                    ref.at[index, pl.ds(start, rows), :],
                    (
                        pl.ds(pl.multiple_of(row_at, 16), rows),
                        pl.ds(pl.multiple_of(column_at, 128), cols),
                    ),
                )

        places.append(at)
    return pieces, places, dims


def whole_weight(array):
    def at(spot_ref, ref):
        yield ref, (pl.ds(0, array.shape[0]), pl.ds(0, array.shape[1]))

    return [array], [at], array.shape


def device_slots(spot):
    device = lax.broadcasted_iota(jnp.int32, (32, 32), 0)
    slot = lax.broadcasted_iota(jnp.int32, (32, 32), 1)
    core = spot[1] ^ (slot >> 4)
    x, f = source_of(spot, core, (slot >> 2) & 1, (slot >> 3) & 1, slot & 3)
    return (device == 16 * x + 8 * core + f).astype(F32)


def small_vectors(every, shards):
    biases, in_bias, gains = shards
    devices = every.shape[0]
    first, second = biases.size, biases.size + in_bias.size
    third = second + gains.size
    return (
        every[:, :first].reshape(devices, 6, -1).transpose(1, 0, 2).reshape(6, -1),
        every[:, first:second].reshape(1, -1),
        every[:, second:third].reshape(devices, 2, -1).transpose(1, 0, 2).reshape(2, -1),
    )


def small_parts(bias_total, hidden_total, gain_total, devices):
    return jnp.concatenate(
        [
            bias_total.reshape(6, devices, -1).transpose(1, 0, 2).reshape(devices, -1),
            hidden_total.reshape(devices, -1),
            gain_total.reshape(2, devices, -1).transpose(1, 0, 2).reshape(devices, -1),
        ],
        axis=1,
    )


def on_device(sizes, tokens, segment_ids, w_qkv, w_out, w_in, w_back, biases, in_bias, gains, out_grad):
    axes = ("x", "core", "z", "y")
    dp_axes, fsdp_axes = ("x", "core"), ("z", "y")
    devices = math.prod(sizes)
    by_permute = sizes == (2, 2, 4, 2)
    count, width = tokens.shape
    wide = w_back.shape[0] * sizes[0] * sizes[1]
    blocks = range(count // BLOCK)
    spot = jnp.stack([lax.axis_index(axis) for axis in axes]).astype(jnp.int32)
    core = spot[1]
    shards = (biases, in_bias, gains)
    own_small = jnp.concatenate([biases.reshape(-1), in_bias, gains.reshape(-1)])
    segment_row = segment_ids.reshape(count // BLOCK, 1, BLOCK)

    qkv_cols, out_cols = w_qkv.shape[1], w_out.shape[1]
    pair_cols = 2 * w_qkv.shape[0]
    in_rows, in_cols = w_in.shape
    back_rows, back_cols = w_back.shape
    half_q, half_o = qkv_cols // 2, out_cols // 2

    if by_permute:

        def paired(turned):
            half = turned.shape[0] // 2
            first, second = turned[:half], turned[half:]
            mine = jnp.where(core == 0, first, second)
            other = exchange(jnp.where(core == 0, second, first), CORE)
            return jnp.where(
                core == 0,
                jnp.concatenate([mine, other], axis=1),
                jnp.concatenate([other, mine], axis=1),
            )

        slots = device_slots(spot)
        to_qkv = Gather(paired(w_qkv.T))
        to_in = Gather(jnp.concatenate([w_in, paired(w_out.T)], axis=0))
        to_back = Gather(w_back.T)
        padded = jnp.pad(own_small, (0, 1024 - own_small.size)).reshape(8, 128)
        to_small = SmallGather(padded)
        to_qkv.go("z1")
        to_small.step(Z1)
        sync((), (to_qkv, "z1"), (to_small, "all"), (to_in, "own"))
        to_qkv.go("z2", "first_a")
        to_in.go("z1")
        to_small.step(Z2)
        sync((), (to_qkv, "first_a"), (to_small, "all"))
        to_qkv.go("second_a")
        to_small.step(FIRST)
        sync((), (to_qkv, "z2"), (to_in, "z1"), (to_small, "all"))
        to_qkv.go("first_b")
        to_in.go("z2")
        to_small.step(SECOND)
        sync((), (to_qkv, "first_b", "second_a"), (to_small, "all"))
        to_qkv.go("second_b", "core_a")
        to_small.step(CORE)
        sync((), (to_qkv, "second_b"), (to_in, "near"), (to_back, "own"))
        to_qkv.go("core_b")
        to_in.go("first_a")
        to_back.go("z1")
        tokens = sync(tokens, (to_qkv, "core_a", "cross_a", "core_b", "cross_b"))
        qkv_weight = weight_of(
            to_qkv.result(), (0, half_q, pair_cols),
            lambda x, c, f: (f * qkv_cols + c * half_q, x * pair_cols), (3 * width, width),
        )
        arrived = widen(to_small.held["all"]).reshape(32, 1024)
        every = jnp.dot(slots, arrived, precision=lax.Precision.HIGHEST)

        def back_blocks(index):
            return [(f * back_cols, 0, index >> 1, index & 1, f >> 1, f & 1) for f in range(8)]

        def in_blocks(index):
            return [
                ((2 * x + c) * in_rows, y * in_cols, x, c, index, y)
                for x in range(2) for c in range(2) for y in range(2)
            ]

        def out_blocks(index):
            return [
                (f * out_cols + c * half_o, 0, index, c, f >> 1, f & 1)
                for f in range(8) for c in range(2)
            ]

        def qkv_blocks(index):
            return [
                (f * qkv_cols + c * half_q, 0, index, c, f >> 1, f & 1)
                for f in range(8) for c in range(2)
            ]

        plans = {
            "back": (back_rows, back_blocks, (back_cols, back_rows), back_cols, 0),
            "in": (2 * in_cols, in_blocks, (in_rows, in_cols), in_rows + half_o, 0),
            "out": (pair_cols, out_blocks, (half_o, pair_cols), in_rows + half_o, in_rows),
            "qkv": (pair_cols, qkv_blocks, (half_q, pair_cols), half_q, 0),
        }
    else:

        def full(shard):
            return lax.all_gather(
                lax.all_gather(shard, fsdp_axes, axis=1, tiled=True), dp_axes, axis=0, tiled=True
            )

        qkv_weight = whole_weight(full(w_qkv).T)
        out_weight = whole_weight(full(w_out).T)
        in_weight = whole_weight(full(w_in))
        back_weight = whole_weight(full(w_back).T)
        every = widen(lax.all_gather(own_small, axes, axis=0, tiled=False))
        plans = {name: (width // 2, None, (0, 0), 0, 0) for name in ("back", "in", "out", "qkv")}

    bias_values, hidden_bias, gain_values = small_vectors(every, shards)
    qkv_bias = jnp.concatenate(
        [bias_values[0:1], jnp.zeros((1, width), F32), bias_values[1:2]], axis=1
    )

    qkv = project_qkv(spot, tokens, qkv_weight, qkv_bias)
    if by_permute:
        qkv = sync(qkv, (to_in, "first_a", "z2"), (to_back, "z1"))
        to_in.go("second_a", "first_b")
        to_back.go("z2")
    attended = None
    for block in blocks:
        attended = attend_forward(block, qkv, segment_row, attended)
        if by_permute and block == 0:
            attended = sync(attended, (to_in, "second_a", "first_b"), (to_back, "near"))
            to_in.go("second_b", "core_a")
            to_back.go("first_a")
    context, lse = attended
    if by_permute:
        context = sync(context, (to_in, "second_b"), (to_back, "first_a", "z2"))
        to_in.go("core_b")
        to_back.go("second_a", "first_b")
        context = sync(context, (to_in, "core_a", "cross_a", "core_b", "cross_b"))
        in_weight = weight_of(
            to_in.result(), (0, in_rows, in_cols),
            lambda x, c, f: ((2 * x + c) * in_rows, f * in_cols), (width, wide),
        )
        out_weight = weight_of(
            to_in.result(), (in_rows, half_o, pair_cols),
            lambda x, c, f: (f * out_cols + c * half_o, x * pair_cols), (width, width),
        )
    normal_one, inverse_one, normed_low = project_out(
        spot, context, tokens, out_weight, bias_values, gain_values
    )
    if by_permute:
        normed_low = sync(normed_low, (to_back, "second_a", "first_b"))
        to_back.go("second_b", "core_a")
    hidden, slope = ffn_in(spot, normed_low, in_weight, hidden_bias)
    if by_permute:
        hidden = sync(hidden, (to_back, "second_b"))
        to_back.go("core_b")
        back_weight = weight_of(
            to_back.result(), (0, back_cols, back_rows),
            lambda x, c, f: (f * back_cols, (2 * x + c) * back_rows), (width, wide),
        )
    layer_out, d_two, d_low, sums_two, *grad_back = forward_rows(
        spot, hidden, normal_one, out_grad, back_weight, bias_values, gain_values, plans["back"]
    )
    if by_permute:
        from_back = Reduce(near=grad_back[0], far=grad_back[1])
        d_low = sync(d_low, (from_back, "far"))
        from_back.go("core")
    d_one, d_context, sums_one, hidden_sum, *grads_in = backward_rows(
        spot, d_low, slope, d_two, normal_one, inverse_one, normed_low, context, back_weight,
        in_weight, out_weight, gain_values, plans["in"], plans["out"],
    )
    if by_permute:
        from_in = Reduce(near=grads_in[0], far=grads_in[1])
        d_context = sync(d_context, (from_back, "core"), (from_in, "far"))
        from_back.go("second_b", "second_a")
        from_in.go("core")
    else:
        grad_in, grad_out = grads_in
        grad_back, = grad_back
    attended, sums_query, sums_value = None, [], []
    for block in blocks:
        *attended, sum_query, sum_value = attend_backward(
            block, qkv, segment_row, lse, context, d_context, attended
        )
        sums_query.append(sum_query)
        sums_value.append(sum_value)
        if by_permute and block == 0:
            attended = sync(attended, (from_back, "second_a", "second_b"), (from_in, "core"))
            from_back.go("first_b", "first_a")
            from_in.go("second_b")
        elif by_permute:
            attended = sync(attended, (from_back, "first_a", "first_b"), (from_in, "second_b"))
            from_back.go("z2")
            from_in.go("second_a", "first_b")
    grad_qkv = gradient(spot, attended, tokens, plans["qkv"])
    sums_query, sums_value = sum(sums_query), sum(sums_value)
    if by_permute:
        from_qkv = Reduce(near=grad_qkv[0], far=grad_qkv[1])
        sums_query, sums_value = sync(
            (sums_query, sums_value), (from_qkv, "far"), (from_back, "z2"),
            (from_in, "second_a", "first_b"),
        )
        from_qkv.go("core")
        from_back.go("z1")
        from_in.go("first_a", "z2")
    else:
        grad_qkv, = grad_qkv

    bias_total = jnp.concatenate(
        [sums_query, sums_value, sums_one[2:3], sums_one[1:2], sums_two[2:3], sums_two[1:2]]
    )
    gain_total = jnp.concatenate([sums_one[0:1], sums_two[0:1]])
    small = small_parts(bias_total, hidden_sum[0], gain_total, devices)

    if by_permute:

        def unpaired(sums):
            half = sums.shape[1] // 2
            left, right = sums[:, :half], sums[:, half:]
            mine = jnp.where(core == 0, left, right)
            other = widen(exchange(jnp.where(core == 0, right, left).astype(BF), CORE))
            return jnp.where(
                core == 0,
                jnp.concatenate([mine, other], axis=0),
                jnp.concatenate([other, mine], axis=0),
            )

        small = jnp.dot(slots.T, small, precision=lax.Precision.HIGHEST)
        small = jnp.pad(small, ((0, 0), (0, 1024 - small.shape[1]))).reshape(32, 8, 128)
        from_small = SmallReduce(small)
        d_one = sync(d_one, (from_qkv, "core"), (from_small, "all"))
        from_qkv.go("second_b", "second_a")
        from_small.step(CORE)
        tokens_grad = tokens_backward(spot, d_one, *attended, qkv_weight)
        tokens_grad = sync(
            tokens_grad, (from_qkv, "second_a", "second_b"), (from_small, "all"),
            (from_in, "first_a", "z2"),
        )
        from_qkv.go("first_b", "first_a")
        from_small.step(SECOND)
        from_in.go("z1")
        sync((), (from_qkv, "first_b", "first_a"), (from_small, "all"))
        from_qkv.go("direct_b", "direct_a")
        from_small.step(FIRST)
        from_small.step(Z2)
        from_small.step(Z1)
        own_back = from_back.result().T
        sums_in = from_in.result()
        own_in = sums_in[:in_rows]
        own_out = unpaired(sums_in[in_rows:]).T
        own_qkv = unpaired(from_qkv.result()).T
        small = from_small.held["all"].reshape(-1)
    else:

        def scattered(total):
            part = lax.psum_scatter(total, dp_axes, scatter_dimension=0, tiled=True)
            part = lax.psum_scatter(part, fsdp_axes, scatter_dimension=1, tiled=True)
            return widen(part)

        tokens_grad = tokens_backward(spot, d_one, *attended, qkv_weight)
        own_back = scattered(grad_back.T)
        own_in = scattered(grad_in)
        own_out = scattered(grad_out.T)
        own_qkv = scattered(grad_qkv.T)
        small = lax.psum_scatter(small.astype(BF), axes, scatter_dimension=0, tiled=True)
        small = widen(small).reshape(-1)
    first, second = biases.size, biases.size + in_bias.size
    own_bias = small[:first].reshape(biases.shape)
    own_hidden = small[first:second]
    own_gain = small[second : second + gains.size].reshape(gains.shape)
    return (
        layer_out, tokens_grad, own_qkv, own_out, own_in, own_back, own_bias, own_hidden, own_gain,
    )


def solution(mesh):
    dp, fsdp = mesh.devices.shape
    sizes = (dp // 2, 2, fsdp // 2, 2)
    split = Mesh(mesh.devices.reshape(sizes), ("x", "core", "z", "y"))
    outer, inner = ("x", "core"), ("z", "y")
    every = outer + inner
    rows = P(every, None)
    weight = P(outer, inner)
    vectors = P(None, every)

    def placed(*arrays):
        return on_device(sizes, *arrays)

    return jax.shard_map(
        placed,
        mesh=split,
        in_specs=(rows, rows, weight, weight, weight, weight, vectors, P(every), vectors, rows),
        out_specs=(rows, rows, weight, weight, weight, weight, vectors, P(every), vectors),
        check_vma=False,
    )
```

```python
import math

import jax
import jax.numpy as jnp
from jax import lax
from jax.experimental import pallas as pl
from jax.experimental.pallas import tpu as pltpu
from jax.sharding import Mesh, PartitionSpec as P

HEADS = 12
HD = 64
BLOCK = 512
PAIR = 2 * HD
TILE = 256
VMEM = 58 * 1024 * 1024
BF = jnp.bfloat16
F32 = jnp.float32
Z1, Z2, FIRST, SECOND, CORE, Z3 = range(6)
NT = (((1,), (1,)), ((), ()))


def dot(a, b):
    return jnp.dot(a, b, preferred_element_type=F32)


def dot_nt(a, b):
    return lax.dot_general(a, b, NT, preferred_element_type=F32)


def any_spec():
    return pl.BlockSpec(memory_space=pl.ANY)


def params(*semantics):
    return pltpu.CompilerParams(
        dimension_semantics=semantics if semantics else None, vmem_limit_bytes=VMEM
    )


def cost(flops, nbytes, trans=0):
    return pl.CostEstimate(flops=flops, bytes_accessed=nbytes, transcendentals=trans)

def layer_norm_parts(rows):
    center = jnp.mean(rows, axis=-1, keepdims=True)
    centered = rows - center
    spread = jnp.mean(centered * centered, axis=-1, keepdims=True)
    inverse = lax.rsqrt(spread + 1e-05)
    return centered * inverse, inverse


def layer_norm_back(grad, normal, inverse):
    mean_grad = jnp.mean(grad, axis=-1, keepdims=True)
    mean_both = jnp.mean(grad * normal, axis=-1, keepdims=True)
    return (grad - mean_grad - normal * mean_both) * inverse


def add_rows(ref, values):
    ref[...] += jnp.sum(values, axis=0, keepdims=True)


def zero_first(*refs):
    @pl.when(pl.program_id(0) == 0)
    def _():
        for ref in refs:
            ref[...] = jnp.zeros_like(ref)


def call(
    body, grid, spot, arrays, specs, weights, outs, out_specs, scratch=(), estimate=None, aliases=()
):
    flat = [piece for pieces, _, _ in weights for piece in pieces]
    counts = [len(pieces) for pieces, _, _ in weights]
    n_arrays, n_flat, n_weights = len(arrays), len(flat), len(weights)
    n_outs = len(outs) if isinstance(outs, tuple) else 1

    def kernel(spot_ref, *refs):
        ins = refs[:n_arrays]
        piece_refs = refs[n_arrays : n_arrays + n_flat]
        out_refs = refs[n_arrays + n_flat : n_arrays + n_flat + n_outs]
        rest = refs[n_arrays + n_flat + n_outs :]
        held = rest[:n_weights]
        sems = rest[n_weights : 2 * n_weights]
        extra = rest[2 * n_weights :]
        first = pl.program_id(0) == 0

        def copies(number):
            start = sum(counts[:number])
            found = []
            for index in range(counts[number]):
                place = weights[number][1][index]
                for source, at in place(spot_ref, piece_refs[start + index]):
                    found.append(
                        pltpu.make_async_copy(
                            source, held[number].at[at], sems[number].at[len(found)]
                        )
                    )
            return found

        @pl.when(first)
        def _():
            for number in range(n_weights):
                for copy in copies(number):
                    copy.start()

        def ready(number):
            def wait():
                @pl.when(first)
                def _():
                    for copy in copies(number):
                        copy.wait()

                return held[number]

            return wait

        body(spot_ref, *ins, *[ready(number) for number in range(n_weights)], *out_refs, *extra)

    scratch_shapes = (
        [pltpu.VMEM(shape, BF) for _, _, shape in weights]
        + [pltpu.SemaphoreType.DMA((32,)) for _ in counts]
        + list(scratch)
    )
    return pl.pallas_call(
        kernel,
        out_shape=outs,
        grid_spec=pltpu.PrefetchScalarGridSpec(
            num_scalar_prefetch=1,
            grid=grid,
            in_specs=list(specs) + [any_spec()] * n_flat,
            out_specs=out_specs,
            scratch_shapes=scratch_shapes,
        ),
        compiler_params=params(*(["arbitrary"] * len(grid))),
        cost_estimate=estimate,
        input_output_aliases=dict(aliases),
    )(spot, *arrays, *flat)


def row(width, tile=TILE):
    return pl.BlockSpec((tile, width), lambda i, s: (i, 0))


def fixed(*shape):
    return pl.BlockSpec(shape, lambda *_: (0,) * len(shape))


def shape(dims, dtype):
    return jax.ShapeDtypeStruct(dims, dtype)


def project_qkv(spot, tokens, w_qkv, qkv_bias):
    count, width = tokens.shape
    wide = w_qkv[2][0]

    def body(spot_ref, x_ref, bias_ref, w_ready, out_ref):
        w_ref = w_ready()
        for start in range(0, wide, width):
            part = slice(start, start + width)
            out_ref[:, part] = (dot_nt(x_ref[...], w_ref[part, :]) + bias_ref[:, part]).astype(BF)

    return call(
        body, (count // TILE,), spot, (tokens, qkv_bias), (row(width), fixed(1, wide)), [w_qkv],
        shape((count, wide), BF), row(wide),
        estimate=cost(2 * count * width * wide, 2 * (count * width + wide * width + count * wide)),
    )


def lane_masks():
    lane = lax.broadcasted_iota(jnp.int32, (1, PAIR), 1)
    return [(lane // HD == head) for head in range(2)]


def same_segment(row_ref):
    numbers = row_ref[0].astype(F32)
    column = jnp.broadcast_to(numbers, (128, BLOCK)).T[:, 0:1]
    return column == numbers


def attend_forward(block, qkv, segment_row, into=None):
    count, wide = qkv.shape
    width = wide // 3
    pairs = width // PAIR
    blocks = count // BLOCK

    def body(q_ref, k_ref, v_ref, row_ref, *refs):
        out_ref, lse_ref = refs[-2:]
        visible = same_segment(row_ref)
        query, key = q_ref[...] * BF(1.0 / math.sqrt(HD)), k_ref[...]
        value_turned = v_ref[...].T
        parts = []
        for head, lanes in enumerate(lane_masks()):
            scores = dot_nt(key, jnp.where(lanes, query, BF(0)))
            scores = jnp.where(visible, scores, -1e30)
            highest = jnp.max(scores, axis=0, keepdims=True)
            exponent = jnp.exp(scores - highest)
            total = jnp.sum(exponent, axis=0, keepdims=True)
            part = dot(value_turned[head * HD : (head + 1) * HD], exponent.astype(BF))
            parts.append(part / total)
            lse_ref[0, 0, head : head + 1, :] = highest + jnp.log(total)
        out_ref[...] = jnp.concatenate(parts, axis=0).T.astype(BF)

    flops = 4 * HEADS * BLOCK * BLOCK * HD
    given = () if into is None else into
    return pl.pallas_call(
        body,
        out_shape=(shape((count, width), BF), shape((blocks, pairs, 2, BLOCK), F32)),
        grid=(pairs,),
        in_specs=[
            pl.BlockSpec((BLOCK, PAIR), lambda p: (block, p)),
            pl.BlockSpec((BLOCK, PAIR), lambda p: (block, pairs + p)),
            pl.BlockSpec((BLOCK, PAIR), lambda p: (block, 2 * pairs + p)),
            pl.BlockSpec((1, 1, BLOCK), lambda p: (block, 0, 0)),
        ]
        + [any_spec()] * len(given),
        out_specs=(
            pl.BlockSpec((BLOCK, PAIR), lambda p: (block, p)),
            pl.BlockSpec((1, 1, 2, BLOCK), lambda p: (block, p, 0, 0)),
        ),
        compiler_params=params("arbitrary"),
        cost_estimate=cost(4 * flops, 4 * count * width, HEADS * BLOCK * BLOCK),
        input_output_aliases={4 + index: index for index in range(len(given))},
    )(qkv, qkv, qkv, segment_row, *given)


def attend_backward(block, qkv, segment_row, lse, context, d_context, into=None):
    count, wide = qkv.shape
    width = wide // 3
    pairs = width // PAIR
    factor = 1.0 / math.sqrt(HD)

    def body(q_ref, k_ref, v_ref, o_ref, do_ref, row_ref, lse_ref, *refs):
        dq_ref, dk_ref, dv_ref, sum_q_ref, sum_v_ref = refs[-5:]
        visible = same_segment(row_ref)
        query, key, value = q_ref[...] * BF(factor), k_ref[...], v_ref[...]
        d_out = do_ref[...]
        key_turned = key.T
        product = (d_out.astype(F32) * o_ref[...].astype(F32)).T
        masks = lane_masks()
        d_query, d_key, d_value = [], [], []
        for head, lanes in enumerate(masks):
            inside = slice(head * HD, (head + 1) * HD)
            delta = jnp.sum(product[inside], axis=0, keepdims=True)
            scores = dot_nt(key, jnp.where(lanes, query, BF(0)))
            scores = jnp.where(visible, scores - lse_ref[0, 0, head : head + 1, :], -1e30)
            prob = jnp.exp(scores)
            d_prob = dot_nt(value, jnp.where(lanes, d_out, BF(0)))
            d_score = (prob * (d_prob - delta)).astype(BF)
            d_value.append(dot(prob.astype(BF), d_out))
            d_key.append(dot(d_score, query))
            d_query.append(dot(key_turned[inside], d_score) * factor)
        dq = jnp.concatenate(d_query, axis=0).T.astype(BF)
        dk = jnp.where(masks[0], d_key[0], d_key[1]).astype(BF)
        dv = jnp.where(masks[0], d_value[0], d_value[1]).astype(BF)
        dq_ref[...] = dq
        dk_ref[...] = dk
        dv_ref[...] = dv
        sum_q_ref[...] = jnp.sum(dq.astype(F32), axis=0, keepdims=True)
        sum_v_ref[...] = jnp.sum(dv.astype(F32), axis=0, keepdims=True)

    tile = pl.BlockSpec((BLOCK, PAIR), lambda p: (block, p))
    flops = 10 * HEADS * BLOCK * BLOCK * HD
    given = () if into is None else into
    return pl.pallas_call(
        body,
        out_shape=(shape((count, width), BF),) * 3 + (shape((1, width), F32),) * 2,
        grid=(pairs,),
        in_specs=[
            tile,
            pl.BlockSpec((BLOCK, PAIR), lambda p: (block, pairs + p)),
            pl.BlockSpec((BLOCK, PAIR), lambda p: (block, 2 * pairs + p)),
            tile,
            tile,
            pl.BlockSpec((1, 1, BLOCK), lambda p: (block, 0, 0)),
            pl.BlockSpec((1, 1, 2, BLOCK), lambda p: (block, p, 0, 0)),
        ]
        + [any_spec()] * len(given),
        out_specs=(tile,) * 3 + (pl.BlockSpec((1, PAIR), lambda p: (0, p)),) * 2,
        compiler_params=params("arbitrary"),
        cost_estimate=cost(4 * flops, 8 * count * width, HEADS * BLOCK * BLOCK),
        input_output_aliases={7 + index: index for index in range(len(given))},
    )(qkv, qkv, qkv, context, d_context, segment_row, lse, *given)


def emit(plan, step, held, spot_ref, out_refs, sems):
    tile, blocks, (rows, cols), _, base = plan
    if blocks is None:
        target = out_refs[0].at[:, pl.ds(pl.multiple_of(step * tile, tile), tile)]
        pltpu.make_async_copy(held.at[step], target, sems.at[step]).start()
        return
    listed = blocks(step)
    for index, (row_at, column_at, x, core, z, y) in enumerate(listed):
        source = held.at[step, pl.ds(row_at, rows), pl.ds(column_at, cols)]
        sem = sems.at[step * len(listed) + index]
        far_x, far_y = x ^ spot_ref[0], y ^ spot_ref[3]
        first = far_x + core * (far_y - far_x)
        depth = z ^ spot_ref[2]
        slot = (depth & 1) + 2 * first + 4 * (far_x + far_y - first) + 8 * (depth >> 1)
        mine = (core ^ spot_ref[1]) == 0

        @pl.when(mine)
        def _():
            pltpu.make_async_copy(source, out_refs[0].at[slot, pl.ds(base, rows)], sem).start()

        @pl.when(jnp.logical_not(mine))
        def _():
            pltpu.make_async_copy(source, out_refs[1].at[slot, pl.ds(base, rows)], sem).start()


def emitted(plan, steps, held, out_refs, sems):
    tile, blocks, (rows, cols), _, base = plan
    if blocks is None:
        for step in range(steps):
            target = out_refs[0].at[:, pl.ds(step * tile, tile)]
            pltpu.make_async_copy(held.at[step], target, sems.at[step]).wait()
        return
    for index in range(32):
        source = held.at[0, pl.ds(0, rows), pl.ds(0, cols)]
        pltpu.make_async_copy(source, out_refs[0].at[0, pl.ds(base, rows)], sems.at[index]).wait()


def emit_shapes(plan, total, columns):
    _, blocks, (rows, cols), slot_rows, _ = plan
    if blocks is None:
        return (shape((total, columns), BF),)
    return (shape((16, slot_rows, cols), BF),) * 2


def clamped(width, last, tile=TILE):
    return pl.BlockSpec((tile, width), lambda i, s: (jnp.minimum(i, last), 0))


def project_out(spot, context, tokens, w_out, biases, gains):
    count, width = tokens.shape

    def body(spot_ref, c_ref, x_ref, bias_ref, gain_ref, w_ready, normal_ref, inverse_ref, low_ref):
        w_ref = w_ready()
        resid = x_ref[...].astype(F32) + (dot_nt(c_ref[...], w_ref[...]) + bias_ref[2:3])
        normal, inverse = layer_norm_parts(resid)
        normal_ref[...] = normal
        inverse_ref[...] = jnp.broadcast_to(inverse, inverse_ref.shape)
        low_ref[...] = (normal * gain_ref[0:1] + bias_ref[3:4]).astype(BF)

    return call(
        body, (count // TILE,), spot, (context, tokens, biases, gains),
        (row(width), row(width), fixed(*biases.shape), fixed(*gains.shape)), [w_out],
        (shape((count, width), F32), shape((count, 128), F32), shape((count, width), BF)),
        (row(width), row(128), row(width)),
        estimate=cost(2 * count * width * width, 10 * count * width),
    )


def ffn_in(spot, normed_low, w_in, in_bias):
    count, width = normed_low.shape
    wide = w_in[2][1]

    def body(spot_ref, x_ref, bias_ref, w_ready, hidden_ref, slope_ref):
        w_ref = w_ready()
        for start in range(0, wide, width):
            part = slice(start, start + width)
            pre = dot(x_ref[...], w_ref[:, part]) + bias_ref[:, part]
            cdf = 0.5 + 0.5 * lax.erf(pre * (1.0 / math.sqrt(2.0)))
            hidden_ref[:, part] = (pre * cdf).astype(BF)
            density = jnp.exp(pre * pre * -0.5) * (1.0 / math.sqrt(2.0 * math.pi))
            slope_ref[:, part] = (cdf + pre * density).astype(BF)

    return call(
        body, (count // TILE,), spot, (normed_low, in_bias), (row(width), fixed(1, wide)), [w_in],
        (shape((count, wide), BF),) * 2, (row(wide),) * 2,
        estimate=cost(2 * count * width * wide, 4 * count * wide, 2 * count * wide),
    )


def forward_rows(spot, hidden, normal_one, out_grad, w_back, biases, gains, plan):
    count, width = out_grad.shape
    wide = hidden.shape[1]
    steps = count // TILE
    tile = plan[0]
    columns = wide // tile
    shapes = emit_shapes(plan, width, wide)

    def body(spot_ref, h_ref, n_ref, g_ref, bias_ref, gain_ref, wb_ready,
             out_ref, d_two_ref, d_low_ref, sums_ref, *refs):
        grads, (kept, d_rows, turned, held, sems) = refs[: len(shapes)], refs[len(shapes) :]
        index = pl.program_id(0)
        zero_first(sums_ref)

        @pl.when(index < steps)
        def _():
            here = pl.ds(pl.multiple_of(index * TILE, TILE), TILE)
            kept[here, :] = h_ref[...]
            resid = n_ref[...] * gain_ref[0:1] + bias_ref[3:4]
            w_ref = wb_ready()
            resid += dot_nt(h_ref[...], w_ref[...]) + bias_ref[4:5]
            normal, inverse = layer_norm_parts(resid)
            out_ref[...] = (normal * gain_ref[1:2] + bias_ref[5:6]).astype(BF)
            grad = g_ref[...].astype(F32)
            d_two = layer_norm_back(grad * gain_ref[1:2], normal, inverse)
            d_low = d_two.astype(BF)
            d_two_ref[...] = d_two
            d_low_ref[...] = d_low
            d_rows[here, :] = d_low
            add_rows(sums_ref.at[0:1], grad * normal)
            add_rows(sums_ref.at[1:2], grad)
            add_rows(sums_ref.at[2:3], d_low.astype(F32))

        @pl.when(index == steps)
        def _():
            turned[...] = d_rows[...].T

        @pl.when(index >= steps)
        def _():
            column = index - steps
            at = pl.ds(pl.multiple_of(column * tile, tile), tile)
            held[column] = dot(turned[...], kept[:, at]).astype(BF)
            emit(plan, column, held, spot_ref, grads, sems)

        @pl.when(index == steps + columns - 1)
        def _():
            emitted(plan, columns, held, grads, sems)

    last = steps - 1
    rows = lambda wide_: clamped(wide_, last)
    return call(
        body, (steps + columns,), spot, (hidden, normal_one, out_grad, biases, gains),
        (rows(wide), rows(width), rows(width), fixed(*biases.shape), fixed(*gains.shape)),
        [w_back],
        (shape((count, width), BF), shape((count, width), F32), shape((count, width), BF),
         shape((8, width), F32), *shapes),
        (rows(width), rows(width), rows(width), fixed(8, width), *[any_spec()] * len(shapes)),
        [pltpu.VMEM((count, wide), BF), pltpu.VMEM((count, width), BF),
         pltpu.VMEM((width, count), BF), pltpu.VMEM((columns, width, tile), BF),
         pltpu.SemaphoreType.DMA((32,))],
        cost(4 * count * width * wide, 14 * count * width + 4 * count * wide),
    )


def backward_rows(
    spot, d_low, slope, d_two, normal_one, inverse_one, normed_low, context, w_back, w_in, w_out,
    gains, plan_in, plan_out,
):
    count, width = d_two.shape
    wide = slope.shape[1]
    steps = count // TILE
    tile_in, tile_out = plan_in[0], plan_out[0]
    columns_in, columns_out = wide // tile_in, width // tile_out
    shared = plan_in[1] is not None
    shapes = emit_shapes(plan_in, width, wide)
    if not shared:
        shapes += emit_shapes(plan_out, width, width)

    def body(spot_ref, dl_ref, s_ref, d2_ref, n_ref, i_ref, low_ref, c_ref, gain_ref,
             wb_ready, wi_ready, wo_ready,
             d_one_ref, d_context_ref, sums_ref, hidden_sum_ref, *refs):
        grads = refs[: len(shapes)]
        d_pre, d_attn, turned, held_in, held_out, sems_in, sems_out = refs[len(shapes) :]
        grads_in, grads_out = (grads, grads) if shared else (grads[:1], grads[1:])
        index = pl.program_id(0)
        zero_first(sums_ref, hidden_sum_ref)

        @pl.when(index < steps)
        def _():
            here = pl.ds(pl.multiple_of(index * TILE, TILE), TILE)
            w_ref = wb_ready()
            for start in range(0, wide, width):
                part = slice(start, start + width)
                d_hidden = dot(dl_ref[...], w_ref[:, part])
                piece = (d_hidden * s_ref[:, part].astype(F32)).astype(BF)
                d_pre[here, part] = piece
                add_rows(hidden_sum_ref.at[:, part], piece.astype(F32))
            w_ref = wi_ready()
            d_normed = d2_ref[...] + dot_nt(d_pre[here, :], w_ref[...])
            normal = n_ref[...]
            d_one = layer_norm_back(d_normed * gain_ref[0:1], normal, i_ref[:, 0:1])
            low = d_one.astype(BF)
            d_one_ref[...] = d_one
            d_attn[here, :] = low
            d_context_ref[...] = dot(low, wo_ready()[...]).astype(BF)
            add_rows(sums_ref.at[0:1], d_normed * normal)
            add_rows(sums_ref.at[1:2], d_normed)
            add_rows(sums_ref.at[2:3], low.astype(F32))

        @pl.when(index == steps)
        def _():
            turned[...] = low_ref[...].T

        @pl.when(jnp.logical_and(index >= steps, index < steps + columns_in))
        def _():
            column = index - steps
            at = pl.ds(pl.multiple_of(column * tile_in, tile_in), tile_in)
            held_in[column] = dot(turned[...], d_pre[:, at]).astype(BF)
            emit(plan_in, column, held_in, spot_ref, grads_in, sems_in)

        @pl.when(index == steps + columns_in)
        def _():
            turned[...] = d_attn[...].T

        @pl.when(index >= steps + columns_in)
        def _():
            column = index - steps - columns_in
            held_out[column] = dot(turned[...], c_ref[...]).astype(BF)
            emit(plan_out, column, held_out, spot_ref, grads_out, sems_out)

        @pl.when(index == steps + columns_in + columns_out - 1)
        def _():
            emitted(plan_in, columns_in, held_in, grads_in, sems_in)
            emitted(plan_out, columns_out, held_out, grads_out, sems_out)

    last, before = steps - 1, steps + columns_in
    rows = lambda wide_: clamped(wide_, last)
    return call(
        body, (steps + columns_in + columns_out,), spot,
        (d_low, slope, d_two, normal_one, inverse_one, normed_low, context, gains),
        (rows(width), rows(wide), rows(width), rows(width), rows(128), fixed(count, width),
         pl.BlockSpec((count, tile_out), lambda i, s: (0, jnp.maximum(i - before, 0))),
         fixed(*gains.shape)),
        [w_back, w_in, w_out],
        (shape((count, width), F32), shape((count, width), BF), shape((8, width), F32),
         shape((1, wide), F32), *shapes),
        (rows(width), rows(width), fixed(8, width), fixed(1, wide), *[any_spec()] * len(shapes)),
        [pltpu.VMEM((count, wide), BF), pltpu.VMEM((count, width), BF),
         pltpu.VMEM((width, count), BF), pltpu.VMEM((columns_in, width, tile_in), BF),
         pltpu.VMEM((columns_out, width, tile_out), BF),
         pltpu.SemaphoreType.DMA((32,)), pltpu.SemaphoreType.DMA((32,))],
        cost(2 * count * width * (3 * wide + 2 * width), 18 * count * width + 2 * count * wide),
    )


def tokens_backward(spot, d_one, d_query, d_key, d_value, w_qkv):
    count, width = d_one.shape

    def body(spot_ref, d1_ref, q_ref, k_ref, v_ref, w_ready, out_ref):
        w_ref = w_ready()
        total = d1_ref[...] + dot(q_ref[...], w_ref[0:width, :])
        total += dot(k_ref[...], w_ref[width : 2 * width, :])
        total += dot(v_ref[...], w_ref[2 * width : 3 * width, :])
        out_ref[...] = total.astype(BF)

    return call(
        body, (count // TILE,), spot, (d_one, d_query, d_key, d_value), (row(width),) * 4, [w_qkv],
        shape((count, width), BF), row(width),
        estimate=cost(6 * count * width * width, 12 * count * width),
    )


def gradient(spot, lefts, right, plan):
    count, columns = right.shape
    width = lefts[0].shape[1]
    total = width * len(lefts)
    tile = plan[0]
    steps = columns // tile
    n_left = len(lefts)
    shapes = emit_shapes(plan, total, columns)

    def body(spot_ref, *refs):
        left_refs, right_ref = refs[:n_left], refs[n_left]
        grads = refs[n_left + 1 : n_left + 1 + len(shapes)]
        turned, held, sems = refs[-3:]
        step = pl.program_id(0)

        @pl.when(step == 0)
        def _():
            for index, ref in enumerate(left_refs):
                turned[index * width : (index + 1) * width, :] = ref[...].T

        for index in range(n_left):
            part = slice(index * width, (index + 1) * width)
            held[step, part, :] = dot(turned[part, :], right_ref[...]).astype(BF)
        emit(plan, step, held, spot_ref, grads, sems)

        @pl.when(step == steps - 1)
        def _():
            emitted(plan, steps, held, grads, sems)

    return call(
        body, (steps,), spot, (*lefts, right),
        (*[fixed(count, width)] * n_left, pl.BlockSpec((count, tile), lambda i, s: (0, i))), [],
        shapes, (any_spec(),) * len(shapes),
        [pltpu.VMEM((total, count), BF), pltpu.VMEM((steps, total, tile), BF),
         pltpu.SemaphoreType.DMA((32,))],
        cost(2 * count * total * columns, 2 * (count * (total + columns) + total * columns)),
    )


def widen(value):
    return value.astype(F32)


def exchange(value, stage):
    axes = ("x", "core", "z", "y")
    pairs = []
    for source in range(32):
        x, core, z, y = source >> 4, (source >> 3) & 1, (source >> 1) & 3, source & 1
        if stage in (Z1, Z2, Z3):
            z ^= {Z1: 1, Z2: 2, Z3: 3}[stage]
        elif stage == CORE:
            core ^= 1
        elif (stage == FIRST) == (core == 0):
            x ^= 1
        else:
            y ^= 1
        pairs.append((source, 16 * x + 8 * core + 2 * z + y))
    return lax.ppermute(value, axes, pairs)


class Parcel:
    def __init__(self, array, origins=((0, 0, 0, 0),)):
        self.array = array
        self.origins = tuple(origins)

    def moved(self, stage):
        def change(origin):
            core, second, first, depth = origin
            return {
                Z1: (core, second, first, depth ^ 1),
                Z2: (core, second, first, depth ^ 2),
                FIRST: (core, second, first ^ 1, depth),
                SECOND: (core, second ^ 1, first, depth),
                CORE: (core ^ 1, second, first, depth),
            }[stage]

        return Parcel(exchange(self.array, stage), [change(origin) for origin in self.origins])

    def __add__(self, other):
        return Parcel(jnp.concatenate([self.array, other.array]), self.origins + other.origins)


def sync(values, *parcels):
    values, arrays = lax.optimization_barrier((values, [parcel.array for parcel in parcels]))
    for parcel, array in zip(parcels, arrays):
        parcel.array = array
    return values


class Reduce:
    def __init__(self, near, far):
        self.near, self.far = near, Parcel(far)

    def send_core(self):
        self.core = Parcel(exchange(self.far.array, CORE))

    def sum(self, start, stop, *others):
        total = widen(self.near[start:stop]) + widen(self.core.array[start:stop])
        for parcel, at in others:
            total += widen(parcel.array[at : at + stop - start])
        return total

    def send(self, stage, start, stop, *others):
        return Parcel(exchange(self.sum(start, stop, *others).astype(BF), stage))

    def send_second_b(self):
        self.second_b = self.send(SECOND, 12, 16)

    def send_second_a(self):
        self.second_a = self.send(SECOND, 4, 8)

    def send_first_b(self):
        self.first_b = self.send(FIRST, 10, 12, (self.second_b, 2))

    def send_first_a(self):
        self.first_a = self.send(FIRST, 2, 4, (self.second_a, 2))

    def send_z2(self):
        self.z2 = self.send(Z2, 8, 10, (self.second_b, 0), (self.first_b, 0))

    def send_z1(self):
        self.z1 = self.send(Z1, 1, 2, (self.second_a, 1), (self.first_a, 1), (self.z2, 1))
        self.last = (self.z2, self.z1)

    def send_direct_b(self):
        self.z2 = self.send(Z2, 8, 9, (self.second_b, 0), (self.first_b, 0))
        self.z3 = self.send(Z3, 9, 10, (self.second_b, 1), (self.first_b, 1))

    def send_direct_a(self):
        self.z1 = self.send(Z1, 1, 2, (self.second_a, 1), (self.first_a, 1))
        self.last = (self.z1, self.z2, self.z3)

    def result(self):
        others = (self.second_a, self.first_a) + self.last
        return self.sum(0, 1, *[(parcel, 0) for parcel in others])[0]


def source_of(spot, origin):
    away, second, first, depth = origin
    core = spot[1] ^ away
    x = spot[0] ^ (first + core * (second - first))
    y = spot[3] ^ (second + core * (first - second))
    return core, x, 2 * (spot[2] ^ depth) + y


def weight_of(parcels, source_rows, place, dims):
    start, rows, cols = source_rows
    pieces, places = [], []
    for parcel in parcels:
        pieces.append(parcel.array)

        def at(spot_ref, ref, origins=parcel.origins):
            for index, origin in enumerate(origins):
                core, x, f = source_of(spot_ref, origin)
                row_at, column_at = place(x, core, f)
                yield (
                    ref.at[index, pl.ds(start, rows), :],
                    (
                        pl.ds(pl.multiple_of(row_at, 16), rows),
                        pl.ds(pl.multiple_of(column_at, 128), cols),
                    ),
                )

        places.append(at)
    return pieces, places, dims


def whole_weight(array):
    def at(spot_ref, ref):
        yield ref, (pl.ds(0, array.shape[0]), pl.ds(0, array.shape[1]))

    return [array], [at], array.shape


def device_slots(spot, origins):
    device = lax.broadcasted_iota(jnp.int32, (len(origins), len(origins)), 0)
    owners = []
    for origin in origins:
        core, x, f = source_of(spot, origin)
        owners.append(16 * x + 8 * core + f)
    return (device == jnp.stack(owners)[None, :]).astype(F32)


def small_vectors(every, shards):
    biases, in_bias, gains = shards
    devices = every.shape[0]
    first, second = biases.size, biases.size + in_bias.size
    third = second + gains.size
    return (
        every[:, :first].reshape(devices, 6, -1).transpose(1, 0, 2).reshape(6, -1),
        every[:, first:second].reshape(1, -1),
        every[:, second:third].reshape(devices, 2, -1).transpose(1, 0, 2).reshape(2, -1),
    )


def on_device(sizes, tokens, segment_ids, w_qkv, w_out, w_in, w_back, biases, in_bias, gains, out_grad):
    axes = ("x", "core", "z", "y")
    dp_axes, fsdp_axes = ("x", "core"), ("z", "y")
    devices = math.prod(sizes)
    by_permute = sizes == (2, 2, 4, 2)
    count, width = tokens.shape
    wide = w_back.shape[0] * sizes[0] * sizes[1]
    blocks = range(count // BLOCK)
    spot = jnp.stack([lax.axis_index(axis) for axis in axes]).astype(jnp.int32)
    core = spot[1]
    shards = (biases, in_bias, gains)
    segment_row = segment_ids.reshape(count // BLOCK, 1, BLOCK)

    qkv_cols, out_cols = w_qkv.shape[1], w_out.shape[1]
    pair_cols = 2 * w_qkv.shape[0]
    in_rows, in_cols = w_in.shape
    back_rows, back_cols = w_back.shape
    half_q, half_o = qkv_cols // 2, out_cols // 2

    if by_permute:

        def paired(turned):
            half = turned.shape[0] // 2
            first, second = turned[:half], turned[half:]
            mine = jnp.where(core == 0, first, second)
            other = exchange(jnp.where(core == 0, second, first), CORE)
            return jnp.where(
                core == 0,
                jnp.concatenate([mine, other], axis=1),
                jnp.concatenate([other, mine], axis=1),
            )

        to_qkv = Parcel(paired(w_qkv.T)[None])
        qkv_z1 = to_qkv.moved(Z1)
        to_small, to_in, w_back = sync((shards, (w_in, w_out), w_back), qkv_z1)
        biases, in_bias, gains = to_small
        own_small = jnp.concatenate([biases.reshape(-1), in_bias, gains.reshape(-1)])
        to_small = Parcel(jnp.pad(own_small, (0, 1024 - own_small.size)).reshape(1, 8, 128))
        to_in = Parcel(jnp.concatenate([to_in[0], paired(to_in[1].T)], axis=0)[None])
        to_back = Parcel(w_back.T[None])
        qkv_near = to_qkv + qkv_z1
        qkv_z2 = qkv_near.moved(Z2)
        qkv_first_a = qkv_near.moved(FIRST)
        to_small += to_small.moved(Z1)
        sync((), qkv_first_a, to_small)
        qkv_a = qkv_near + qkv_first_a
        qkv_second_a = qkv_a.moved(SECOND)
        in_z1 = to_in.moved(Z1)
        to_small += to_small.moved(Z2)
        sync((), qkv_z2, in_z1, to_small)
        qkv_first_b = qkv_z2.moved(FIRST)
        to_in += in_z1
        in_z2 = to_in.moved(Z2)
        to_small += to_small.moved(FIRST)
        sync((), qkv_first_b, qkv_second_a, to_small)
        qkv_b = qkv_z2 + qkv_first_b
        qkv_second_b = qkv_b.moved(SECOND)
        qkv_core_a = qkv_a.moved(CORE), qkv_second_a.moved(CORE)
        to_small += to_small.moved(SECOND)
        sync((), qkv_second_b, to_small, to_back, in_z2)
        qkv_core_b = qkv_b.moved(CORE), qkv_second_b.moved(CORE)
        to_small += to_small.moved(CORE)
        to_in += in_z2
        in_first = to_in.moved(FIRST)
        back_z1 = to_back.moved(Z1)
        tokens = sync(tokens, *qkv_core_a, *qkv_core_b)
        qkv_parcels = (
            qkv_a, qkv_second_a, qkv_b, qkv_second_b, *qkv_core_a, *qkv_core_b
        )
        qkv_weight = weight_of(
            qkv_parcels, (0, half_q, pair_cols),
            lambda x, c, f: (f * qkv_cols + c * half_q, x * pair_cols), (3 * width, width),
        )
        slots = device_slots(spot, to_small.origins)
        arrived = widen(to_small.array).reshape(32, 1024)
        every = jnp.dot(slots, arrived, precision=lax.Precision.HIGHEST)

        def back_blocks(index):
            return [(f * back_cols, 0, index >> 1, index & 1, f >> 1, f & 1) for f in range(8)]

        def in_blocks(index):
            return [
                ((2 * x + c) * in_rows, y * in_cols, x, c, index, y)
                for x in range(2) for c in range(2) for y in range(2)
            ]

        def out_blocks(index):
            return [
                (f * out_cols + c * half_o, 0, index, c, f >> 1, f & 1)
                for f in range(8) for c in range(2)
            ]

        def qkv_blocks(index):
            return [
                (f * qkv_cols + c * half_q, 0, index, c, f >> 1, f & 1)
                for f in range(8) for c in range(2)
            ]

        plans = {
            "back": (back_rows, back_blocks, (back_cols, back_rows), back_cols, 0),
            "in": (2 * in_cols, in_blocks, (in_rows, in_cols), in_rows + half_o, 0),
            "out": (pair_cols, out_blocks, (half_o, pair_cols), in_rows + half_o, in_rows),
            "qkv": (pair_cols, qkv_blocks, (half_q, pair_cols), half_q, 0),
        }
    else:

        def full(shard):
            return lax.all_gather(
                lax.all_gather(shard, fsdp_axes, axis=1, tiled=True), dp_axes, axis=0, tiled=True
            )

        qkv_weight = whole_weight(full(w_qkv).T)
        out_weight = whole_weight(full(w_out).T)
        in_weight = whole_weight(full(w_in))
        back_weight = whole_weight(full(w_back).T)
        own_small = jnp.concatenate([biases.reshape(-1), in_bias, gains.reshape(-1)])
        every = widen(lax.all_gather(own_small, axes, axis=0, tiled=False))
        plans = {name: (width // 2, None, (0, 0), 0, 0) for name in ("back", "in", "out", "qkv")}

    bias_values, hidden_bias, gain_values = small_vectors(every, shards)
    qkv_bias = jnp.concatenate(
        [bias_values[0:1], jnp.zeros((1, width), F32), bias_values[1:2]], axis=1
    )

    qkv = project_qkv(spot, tokens, qkv_weight, qkv_bias)
    if by_permute:
        qkv = sync(qkv, in_first, back_z1)
        to_in += in_first
        in_second = to_in.moved(SECOND)
        to_back += back_z1
        back_z2 = to_back.moved(Z2)
    attended = None
    for block in blocks:
        attended = attend_forward(block, qkv, segment_row, attended)
        if by_permute and block == 0:
            attended = sync(attended, back_z2)
            in_core = to_in.moved(CORE)
            to_back += back_z2
            back_first = to_back.moved(FIRST)
    context, lse = attended
    if by_permute:
        context = sync(context, in_second, in_core, back_first)
        in_cross = in_second.moved(CORE)
        to_back += back_first
        back_second = to_back.moved(SECOND)
        context = sync(context, in_cross)
        in_parcels = (to_in, in_second, in_core, in_cross)
        in_weight = weight_of(
            in_parcels, (0, in_rows, in_cols),
            lambda x, c, f: ((2 * x + c) * in_rows, f * in_cols), (width, wide),
        )
        out_weight = weight_of(
            in_parcels, (in_rows, half_o, pair_cols),
            lambda x, c, f: (f * out_cols + c * half_o, x * pair_cols), (width, width),
        )
    normal_one, inverse_one, normed_low = project_out(
        spot, context, tokens, out_weight, bias_values, gain_values
    )
    if by_permute:
        normed_low = sync(normed_low, back_second)
        back_core, back_cross = to_back.moved(CORE), back_second.moved(CORE)
    hidden, slope = ffn_in(spot, normed_low, in_weight, hidden_bias)
    if by_permute:
        hidden = sync(hidden, back_core, back_cross)
        back_weight = weight_of(
            (to_back, back_second, back_core, back_cross), (0, back_cols, back_rows),
            lambda x, c, f: (f * back_cols, (2 * x + c) * back_rows), (width, wide),
        )
    layer_out, d_two, d_low, sums_two, *grad_back = forward_rows(
        spot, hidden, normal_one, out_grad, back_weight, bias_values, gain_values, plans["back"]
    )
    if by_permute:
        from_back = Reduce(*grad_back)
        d_low = sync(d_low, from_back.far)
        from_back.send_core()
    d_one, d_context, sums_one, hidden_sum, *grads_in = backward_rows(
        spot, d_low, slope, d_two, normal_one, inverse_one, normed_low, context, back_weight,
        in_weight, out_weight, gain_values, plans["in"], plans["out"],
    )
    if by_permute:
        from_in = Reduce(*grads_in)
        d_context = sync(d_context, from_back.core, from_in.far)
        from_back.send_second_b()
        from_back.send_second_a()
        from_in.send_core()
    else:
        grad_in, grad_out = grads_in
        grad_back, = grad_back
    attended, sums = None, [sums_two, sums_one, hidden_sum.reshape(-1, width)]
    for block in blocks:
        *attended, sum_query, sum_value = attend_backward(
            block, qkv, segment_row, lse, context, d_context, attended
        )
        sums += [sum_query, sum_value]
        if by_permute and block == 0:
            attended = sync(attended, from_back.second_a, from_back.second_b, from_in.core)
            from_back.send_first_b()
            from_back.send_first_a()
            from_in.send_second_b()
        elif by_permute:
            attended = sync(attended, from_back.first_a, from_back.first_b, from_in.second_b)
            from_back.send_z2()
            from_in.send_second_a()
            from_in.send_first_b()
    grad_qkv = gradient(spot, attended, tokens, plans["qkv"])
    small = jnp.concatenate(sums)
    if by_permute:
        from_qkv = Reduce(*grad_qkv)
        small = sync(
            small, from_qkv.far, from_back.z2, from_in.second_a, from_in.first_b
        )
        from_qkv.send_core()
        from_back.send_z1()
        from_in.send_first_a()
        from_in.send_z2()
        to_small = Parcel(small)
        small_sent = to_small.moved(CORE)
        d_one = sync(d_one, from_qkv.core, small_sent)
        from_qkv.send_second_b()
        from_qkv.send_second_a()
        small = small + small_sent.array
        small_sent = Parcel(small).moved(SECOND)
    else:
        grad_qkv, = grad_qkv
    tokens_grad = tokens_backward(spot, d_one, *attended, qkv_weight)

    if by_permute:

        def unpaired(sums):
            half = sums.shape[1] // 2
            left, right = sums[:, :half], sums[:, half:]
            mine = jnp.where(core == 0, left, right)
            other = widen(exchange(jnp.where(core == 0, right, left).astype(BF), CORE))
            return jnp.where(
                core == 0,
                jnp.concatenate([mine, other], axis=0),
                jnp.concatenate([other, mine], axis=0),
            )

        tokens_grad = sync(
            tokens_grad, from_qkv.second_b, from_qkv.second_a, small_sent, from_in.first_a,
            from_in.z2, from_back.z1,
        )
        from_qkv.send_first_b()
        from_qkv.send_first_a()
        from_in.send_z1()
        small = small + small_sent.array
        small_sent = Parcel(small).moved(FIRST)
        sync((), from_qkv.first_b, from_qkv.first_a, small_sent)
        from_qkv.send_direct_b()
        from_qkv.send_direct_a()
        small = small + small_sent.array
        small_sent = Parcel(small).moved(Z1)
        small = small + small_sent.array
        small_sent = Parcel(small).moved(Z2)
        small = small + small_sent.array
        sums_in = from_in.result()
        own_back = from_back.result().T
        own_in = sums_in[:in_rows]
        own_out = unpaired(sums_in[in_rows:]).T
        own_qkv = unpaired(from_qkv.result()).T
    else:

        def scattered(total):
            part = lax.psum_scatter(total, dp_axes, scatter_dimension=0, tiled=True)
            part = lax.psum_scatter(part, fsdp_axes, scatter_dimension=1, tiled=True)
            return widen(part)

        own_back = scattered(grad_back.T)
        own_in = scattered(grad_in)
        own_out = scattered(grad_out.T)
        own_qkv = scattered(grad_qkv.T)
        small = lax.psum(small, axes)
    device = lax.axis_index(axes)
    queries = small[20:22] + small[22:24]
    bias_total = jnp.concatenate([queries, small[10:11], small[9:10], small[2:3], small[1:2]])
    gain_total = jnp.concatenate([small[8:9], small[0:1]])
    own_bias = lax.dynamic_slice_in_dim(bias_total, device * biases.shape[1], biases.shape[1], 1)
    own_gain = lax.dynamic_slice_in_dim(gain_total, device * gains.shape[1], gains.shape[1], 1)
    own_hidden = lax.dynamic_slice_in_dim(
        small[16:20].reshape(-1), device * in_bias.shape[0], in_bias.shape[0], 0
    )
    return (
        layer_out, tokens_grad, own_qkv, own_out, own_in, own_back, own_bias, own_hidden, own_gain,
    )


def solution(mesh):
    dp, fsdp = mesh.devices.shape
    sizes = (dp // 2, 2, fsdp // 2, 2)
    split = Mesh(mesh.devices.reshape(sizes), ("x", "core", "z", "y"))
    outer, inner = ("x", "core"), ("z", "y")
    every = outer + inner
    rows = P(every, None)
    weight = P(outer, inner)
    vectors = P(None, every)

    def placed(*arrays):
        return on_device(sizes, *arrays)

    return jax.shard_map(
        placed,
        mesh=split,
        in_specs=(rows, rows, weight, weight, weight, weight, vectors, P(every), vectors, rows),
        out_specs=(rows, rows, weight, weight, weight, weight, vectors, P(every), vectors),
        check_vma=False,
    )
```

```python
import math

import jax
import jax.numpy as jnp
from jax import lax
from jax.experimental import pallas as pl
from jax.experimental.pallas import tpu as pltpu
from jax.sharding import Mesh, PartitionSpec as P

HEADS = 12
HD = 64
BLOCK = 512
PAIR = 2 * HD
TILE = 256
VMEM = 58 * 1024 * 1024
BF = jnp.bfloat16
F32 = jnp.float32
Z1, Z2, FIRST, SECOND, CORE, Z3 = range(6)
HIDDEN_SUM, QUERY_SUM = 16, 20
NT = (((1,), (1,)), ((), ()))


def dot(a, b):
    return jnp.dot(a, b, preferred_element_type=F32)


def dot_nt(a, b):
    return lax.dot_general(a, b, NT, preferred_element_type=F32)


def any_spec():
    return pl.BlockSpec(memory_space=pl.ANY)


def params(*semantics):
    return pltpu.CompilerParams(
        dimension_semantics=semantics if semantics else None, vmem_limit_bytes=VMEM
    )


def cost(flops, nbytes, trans=0):
    return pl.CostEstimate(flops=flops, bytes_accessed=nbytes, transcendentals=trans)

def layer_norm_parts(rows):
    center = jnp.mean(rows, axis=-1, keepdims=True)
    centered = rows - center
    spread = jnp.mean(centered * centered, axis=-1, keepdims=True)
    inverse = lax.rsqrt(spread + 1e-05)
    return centered * inverse, inverse


def layer_norm_back(grad, normal, inverse):
    mean_grad = jnp.mean(grad, axis=-1, keepdims=True)
    mean_both = jnp.mean(grad * normal, axis=-1, keepdims=True)
    return (grad - mean_grad - normal * mean_both) * inverse


def add_rows(ref, values):
    ref[...] += jnp.sum(values, axis=0, keepdims=True)


def zero_first(*refs):
    @pl.when(pl.program_id(0) == 0)
    def _():
        for ref in refs:
            ref[...] = jnp.zeros_like(ref)


def call(
    body, grid, spot, arrays, specs, weights, outs, out_specs, scratch=(), estimate=None, aliases=()
):
    flat = [piece for pieces, _, _ in weights for piece in pieces]
    counts = [len(pieces) for pieces, _, _ in weights]
    n_arrays, n_flat, n_weights = len(arrays), len(flat), len(weights)
    n_outs = len(outs) if isinstance(outs, tuple) else 1

    def kernel(spot_ref, *refs):
        ins = refs[:n_arrays]
        piece_refs = refs[n_arrays : n_arrays + n_flat]
        out_refs = refs[n_arrays + n_flat : n_arrays + n_flat + n_outs]
        rest = refs[n_arrays + n_flat + n_outs :]
        held = rest[:n_weights]
        sems = rest[n_weights : 2 * n_weights]
        extra = rest[2 * n_weights :]
        first = pl.program_id(0) == 0

        def copies(number):
            start = sum(counts[:number])
            found = []
            for index in range(counts[number]):
                place = weights[number][1][index]
                for source, at in place(spot_ref, piece_refs[start + index]):
                    found.append(
                        pltpu.make_async_copy(
                            source, held[number].at[at], sems[number].at[len(found)]
                        )
                    )
            return found

        @pl.when(first)
        def _():
            for number in range(n_weights):
                for copy in copies(number):
                    copy.start()

        def ready(number):
            def wait():
                @pl.when(first)
                def _():
                    for copy in copies(number):
                        copy.wait()

                return held[number]

            return wait

        body(spot_ref, *ins, *[ready(number) for number in range(n_weights)], *out_refs, *extra)

    scratch_shapes = (
        [pltpu.VMEM(shape, BF) for _, _, shape in weights]
        + [pltpu.SemaphoreType.DMA((32,)) for _ in counts]
        + list(scratch)
    )
    return pl.pallas_call(
        kernel,
        out_shape=outs,
        grid_spec=pltpu.PrefetchScalarGridSpec(
            num_scalar_prefetch=1,
            grid=grid,
            in_specs=list(specs) + [any_spec()] * n_flat,
            out_specs=out_specs,
            scratch_shapes=scratch_shapes,
        ),
        compiler_params=params(*(["arbitrary"] * len(grid))),
        cost_estimate=estimate,
        input_output_aliases=dict(aliases),
    )(spot, *arrays, *flat)


def row(width, tile=TILE):
    return pl.BlockSpec((tile, width), lambda i, s: (i, 0))


def fixed(*shape):
    return pl.BlockSpec(shape, lambda *_: (0,) * len(shape))


def shape(dims, dtype):
    return jax.ShapeDtypeStruct(dims, dtype)


def project_qkv(spot, tokens, w_qkv, qkv_bias):
    count, width = tokens.shape
    wide = w_qkv[2][0]

    def body(spot_ref, x_ref, bias_ref, w_ready, out_ref):
        w_ref = w_ready()
        for start in range(0, wide, width):
            part = slice(start, start + width)
            out_ref[:, part] = (dot_nt(x_ref[...], w_ref[part, :]) + bias_ref[:, part]).astype(BF)

    return call(
        body, (count // TILE,), spot, (tokens, qkv_bias), (row(width), fixed(1, wide)), [w_qkv],
        shape((count, wide), BF), row(wide),
        estimate=cost(2 * count * width * wide, 2 * (count * width + wide * width + count * wide)),
    )


def lane_masks():
    lane = lax.broadcasted_iota(jnp.int32, (1, PAIR), 1)
    return [(lane // HD == head) for head in range(2)]


def same_segment(row_ref):
    numbers = row_ref[0].astype(F32)
    column = jnp.broadcast_to(numbers, (128, BLOCK)).T[:, 0:1]
    return column == numbers


def attend_forward(block, qkv, segment_row, into=None):
    count, wide = qkv.shape
    width = wide // 3
    pairs = width // PAIR
    blocks = count // BLOCK

    def body(q_ref, k_ref, v_ref, row_ref, *refs):
        out_ref, lse_ref = refs[-2:]
        visible = same_segment(row_ref)
        query, key = q_ref[...] * BF(1.0 / math.sqrt(HD)), k_ref[...]
        value_turned = v_ref[...].T
        parts = []
        for head, lanes in enumerate(lane_masks()):
            scores = dot_nt(key, jnp.where(lanes, query, BF(0)))
            scores = jnp.where(visible, scores, -1e30)
            highest = jnp.max(scores, axis=0, keepdims=True)
            exponent = jnp.exp(scores - highest)
            total = jnp.sum(exponent, axis=0, keepdims=True)
            part = dot(value_turned[head * HD : (head + 1) * HD], exponent.astype(BF))
            parts.append(part / total)
            lse_ref[0, 0, head : head + 1, :] = highest + jnp.log(total)
        out_ref[...] = jnp.concatenate(parts, axis=0).T.astype(BF)

    flops = 4 * HEADS * BLOCK * BLOCK * HD
    given = () if into is None else into
    return pl.pallas_call(
        body,
        out_shape=(shape((count, width), BF), shape((blocks, pairs, 2, BLOCK), F32)),
        grid=(pairs,),
        in_specs=[
            pl.BlockSpec((BLOCK, PAIR), lambda p: (block, p)),
            pl.BlockSpec((BLOCK, PAIR), lambda p: (block, pairs + p)),
            pl.BlockSpec((BLOCK, PAIR), lambda p: (block, 2 * pairs + p)),
            pl.BlockSpec((1, 1, BLOCK), lambda p: (block, 0, 0)),
        ]
        + [any_spec()] * len(given),
        out_specs=(
            pl.BlockSpec((BLOCK, PAIR), lambda p: (block, p)),
            pl.BlockSpec((1, 1, 2, BLOCK), lambda p: (block, p, 0, 0)),
        ),
        compiler_params=params("arbitrary"),
        cost_estimate=cost(4 * flops, 4 * count * width, HEADS * BLOCK * BLOCK),
        input_output_aliases={4 + index: index for index in range(len(given))},
    )(qkv, qkv, qkv, segment_row, *given)


def attend_backward(block, qkv, segment_row, lse, context, d_context, sums, into=None):
    count, wide = qkv.shape
    width = wide // 3
    pairs = width // PAIR
    factor = 1.0 / math.sqrt(HD)

    def body(q_ref, k_ref, v_ref, o_ref, do_ref, row_ref, lse_ref, given_ref, *refs):
        dq_ref, dk_ref, dv_ref, sums_ref = refs[-4:]

        @pl.when(pl.program_id(0) == 0)
        def _():
            sums_ref[...] = given_ref[...]

        visible = same_segment(row_ref)
        query, key, value = q_ref[...] * BF(factor), k_ref[...], v_ref[...]
        d_out = do_ref[...]
        key_turned = key.T
        product = (d_out.astype(F32) * o_ref[...].astype(F32)).T
        masks = lane_masks()
        d_query, d_key, d_value = [], [], []
        for head, lanes in enumerate(masks):
            inside = slice(head * HD, (head + 1) * HD)
            delta = jnp.sum(product[inside], axis=0, keepdims=True)
            scores = dot_nt(key, jnp.where(lanes, query, BF(0)))
            scores = jnp.where(visible, scores - lse_ref[0, 0, head : head + 1, :], -1e30)
            prob = jnp.exp(scores)
            d_prob = dot_nt(value, jnp.where(lanes, d_out, BF(0)))
            d_score = (prob * (d_prob - delta)).astype(BF)
            d_value.append(dot(prob.astype(BF), d_out))
            d_key.append(dot(d_score, query))
            d_query.append(dot(key_turned[inside], d_score) * factor)
        dq = jnp.concatenate(d_query, axis=0).T.astype(BF)
        dk = jnp.where(masks[0], d_key[0], d_key[1]).astype(BF)
        dv = jnp.where(masks[0], d_value[0], d_value[1]).astype(BF)
        dq_ref[...] = dq
        dk_ref[...] = dk
        dv_ref[...] = dv
        here = pl.ds(pl.multiple_of(pl.program_id(0) * PAIR, PAIR), PAIR)
        add_rows(sums_ref.at[QUERY_SUM : QUERY_SUM + 1, here], dq.astype(F32))
        add_rows(sums_ref.at[QUERY_SUM + 1 : QUERY_SUM + 2, here], dv.astype(F32))

    tile = pl.BlockSpec((BLOCK, PAIR), lambda p: (block, p))
    flops = 10 * HEADS * BLOCK * BLOCK * HD
    given = () if into is None else into
    return pl.pallas_call(
        body,
        out_shape=(shape((count, width), BF),) * 3 + (shape((24, width), F32),),
        grid=(pairs,),
        in_specs=[
            tile,
            pl.BlockSpec((BLOCK, PAIR), lambda p: (block, pairs + p)),
            pl.BlockSpec((BLOCK, PAIR), lambda p: (block, 2 * pairs + p)),
            tile,
            tile,
            pl.BlockSpec((1, 1, BLOCK), lambda p: (block, 0, 0)),
            pl.BlockSpec((1, 1, 2, BLOCK), lambda p: (block, p, 0, 0)),
            fixed(24, width),
        ]
        + [any_spec()] * len(given),
        out_specs=(tile,) * 3 + (fixed(24, width),),
        compiler_params=params("arbitrary"),
        cost_estimate=cost(4 * flops, 8 * count * width, HEADS * BLOCK * BLOCK),
        input_output_aliases={8 + index: index for index in range(len(given))},
    )(qkv, qkv, qkv, context, d_context, segment_row, lse, sums, *given)


def emit(plan, step, held, spot_ref, out_refs, sems):
    tile, blocks, (rows, cols), _, base = plan
    if blocks is None:
        target = out_refs[0].at[:, pl.ds(pl.multiple_of(step * tile, tile), tile)]
        pltpu.make_async_copy(held.at[step], target, sems.at[step]).start()
        return
    listed = blocks(step)
    for index, (row_at, column_at, x, core, z, y) in enumerate(listed):
        source = held.at[step, pl.ds(row_at, rows), pl.ds(column_at, cols)]
        sem = sems.at[step * len(listed) + index]
        far_x, far_y = x ^ spot_ref[0], y ^ spot_ref[3]
        first = far_x + core * (far_y - far_x)
        depth = z ^ spot_ref[2]
        slot = (depth & 1) + 2 * first + 4 * (far_x + far_y - first) + 8 * (depth >> 1)
        mine = (core ^ spot_ref[1]) == 0

        @pl.when(mine)
        def _():
            pltpu.make_async_copy(source, out_refs[0].at[slot, pl.ds(base, rows)], sem).start()

        @pl.when(jnp.logical_not(mine))
        def _():
            pltpu.make_async_copy(source, out_refs[1].at[slot, pl.ds(base, rows)], sem).start()


def emitted(plan, steps, held, out_refs, sems):
    tile, blocks, (rows, cols), _, base = plan
    if blocks is None:
        for step in range(steps):
            target = out_refs[0].at[:, pl.ds(step * tile, tile)]
            pltpu.make_async_copy(held.at[step], target, sems.at[step]).wait()
        return
    for index in range(32):
        source = held.at[0, pl.ds(0, rows), pl.ds(0, cols)]
        pltpu.make_async_copy(source, out_refs[0].at[0, pl.ds(base, rows)], sems.at[index]).wait()


def emit_shapes(plan, total, columns):
    _, blocks, (rows, cols), slot_rows, _ = plan
    if blocks is None:
        return (shape((total, columns), BF),)
    return (shape((16, slot_rows, cols), BF),) * 2


def clamped(width, last, tile=TILE):
    return pl.BlockSpec((tile, width), lambda i, s: (jnp.minimum(i, last), 0))


def project_out(spot, context, tokens, w_out, biases, gains):
    count, width = tokens.shape

    def body(spot_ref, c_ref, x_ref, bias_ref, gain_ref, w_ready, normal_ref, inverse_ref, low_ref):
        w_ref = w_ready()
        resid = x_ref[...].astype(F32) + (dot_nt(c_ref[...], w_ref[...]) + bias_ref[2:3])
        normal, inverse = layer_norm_parts(resid)
        normal_ref[...] = normal
        inverse_ref[...] = jnp.broadcast_to(inverse, inverse_ref.shape)
        low_ref[...] = (normal * gain_ref[0:1] + bias_ref[3:4]).astype(BF)

    return call(
        body, (count // TILE,), spot, (context, tokens, biases, gains),
        (row(width), row(width), fixed(*biases.shape), fixed(*gains.shape)), [w_out],
        (shape((count, width), F32), shape((count, 128), F32), shape((count, width), BF)),
        (row(width), row(128), row(width)),
        estimate=cost(2 * count * width * width, 10 * count * width),
    )


def ffn_in(spot, normed_low, w_in, in_bias):
    count, width = normed_low.shape
    wide = w_in[2][1]

    def body(spot_ref, x_ref, bias_ref, w_ready, hidden_ref, slope_ref):
        w_ref = w_ready()
        for start in range(0, wide, width):
            part = slice(start, start + width)
            pre = dot(x_ref[...], w_ref[:, part]) + bias_ref[:, part]
            cdf = 0.5 + 0.5 * lax.erf(pre * (1.0 / math.sqrt(2.0)))
            hidden_ref[:, part] = (pre * cdf).astype(BF)
            density = jnp.exp(pre * pre * -0.5) * (1.0 / math.sqrt(2.0 * math.pi))
            slope_ref[:, part] = (cdf + pre * density).astype(BF)

    return call(
        body, (count // TILE,), spot, (normed_low, in_bias), (row(width), fixed(1, wide)), [w_in],
        (shape((count, wide), BF),) * 2, (row(wide),) * 2,
        estimate=cost(2 * count * width * wide, 4 * count * wide, 2 * count * wide),
    )


def forward_rows(spot, hidden, normal_one, out_grad, w_back, biases, gains, plan):
    count, width = out_grad.shape
    wide = hidden.shape[1]
    steps = count // TILE
    tile = plan[0]
    columns = wide // tile
    shapes = emit_shapes(plan, width, wide)

    def body(spot_ref, h_ref, n_ref, g_ref, bias_ref, gain_ref, wb_ready,
             out_ref, d_two_ref, d_low_ref, sums_ref, *refs):
        grads, (kept, d_rows, turned, held, sems) = refs[: len(shapes)], refs[len(shapes) :]
        index = pl.program_id(0)
        zero_first(sums_ref)

        @pl.when(index < steps)
        def _():
            here = pl.ds(pl.multiple_of(index * TILE, TILE), TILE)
            kept[here, :] = h_ref[...]
            resid = n_ref[...] * gain_ref[0:1] + bias_ref[3:4]
            w_ref = wb_ready()
            resid += dot_nt(h_ref[...], w_ref[...]) + bias_ref[4:5]
            normal, inverse = layer_norm_parts(resid)
            out_ref[...] = (normal * gain_ref[1:2] + bias_ref[5:6]).astype(BF)
            grad = g_ref[...].astype(F32)
            d_two = layer_norm_back(grad * gain_ref[1:2], normal, inverse)
            d_low = d_two.astype(BF)
            d_two_ref[...] = d_two
            d_low_ref[...] = d_low
            d_rows[here, :] = d_low
            add_rows(sums_ref.at[0:1], grad * normal)
            add_rows(sums_ref.at[1:2], grad)
            add_rows(sums_ref.at[2:3], d_low.astype(F32))

        @pl.when(index == steps)
        def _():
            turned[...] = d_rows[...].T

        @pl.when(index >= steps)
        def _():
            column = index - steps
            at = pl.ds(pl.multiple_of(column * tile, tile), tile)
            held[column] = dot(turned[...], kept[:, at]).astype(BF)
            emit(plan, column, held, spot_ref, grads, sems)

        @pl.when(index == steps + columns - 1)
        def _():
            emitted(plan, columns, held, grads, sems)

    last = steps - 1
    rows = lambda wide_: clamped(wide_, last)
    return call(
        body, (steps + columns,), spot, (hidden, normal_one, out_grad, biases, gains),
        (rows(wide), rows(width), rows(width), fixed(*biases.shape), fixed(*gains.shape)),
        [w_back],
        (shape((count, width), BF), shape((count, width), F32), shape((count, width), BF),
         shape((8, width), F32), *shapes),
        (rows(width), rows(width), rows(width), fixed(8, width), *[any_spec()] * len(shapes)),
        [pltpu.VMEM((count, wide), BF), pltpu.VMEM((count, width), BF),
         pltpu.VMEM((width, count), BF), pltpu.VMEM((columns, width, tile), BF),
         pltpu.SemaphoreType.DMA((32,))],
        cost(4 * count * width * wide, 14 * count * width + 4 * count * wide),
    )


def backward_rows(
    spot, d_low, slope, d_two, normal_one, inverse_one, normed_low, context, sums_two, w_back, w_in,
    w_out, gains, plan_in, plan_out,
):
    count, width = d_two.shape
    wide = slope.shape[1]
    steps = count // TILE
    tile_in, tile_out = plan_in[0], plan_out[0]
    columns_in, columns_out = wide // tile_in, width // tile_out
    shared = plan_in[1] is not None
    shapes = emit_shapes(plan_in, width, wide)
    if not shared:
        shapes += emit_shapes(plan_out, width, width)

    def body(spot_ref, dl_ref, s_ref, d2_ref, n_ref, i_ref, low_ref, c_ref, two_ref, gain_ref,
             wb_ready, wi_ready, wo_ready, d_one_ref, d_context_ref, sums_ref, *refs):
        grads = refs[: len(shapes)]
        d_pre, d_attn, turned, held_in, held_out, sems_in, sems_out = refs[len(shapes) :]
        grads_in, grads_out = (grads, grads) if shared else (grads[:1], grads[1:])
        index = pl.program_id(0)

        @pl.when(index == 0)
        def _():
            sums_ref[...] = jnp.zeros_like(sums_ref)
            sums_ref[0:8, :] = two_ref[...]

        @pl.when(index < steps)
        def _():
            here = pl.ds(pl.multiple_of(index * TILE, TILE), TILE)
            w_ref = wb_ready()
            for start in range(0, wide, width):
                part = slice(start, start + width)
                d_hidden = dot(dl_ref[...], w_ref[:, part])
                piece = (d_hidden * s_ref[:, part].astype(F32)).astype(BF)
                d_pre[here, part] = piece
                at = HIDDEN_SUM + start // width
                add_rows(sums_ref.at[at : at + 1], piece.astype(F32))
            w_ref = wi_ready()
            d_normed = d2_ref[...] + dot_nt(d_pre[here, :], w_ref[...])
            normal = n_ref[...]
            d_one = layer_norm_back(d_normed * gain_ref[0:1], normal, i_ref[:, 0:1])
            low = d_one.astype(BF)
            d_one_ref[...] = d_one
            d_attn[here, :] = low
            d_context_ref[...] = dot(low, wo_ready()[...]).astype(BF)
            add_rows(sums_ref.at[8:9], d_normed * normal)
            add_rows(sums_ref.at[9:10], d_normed)
            add_rows(sums_ref.at[10:11], low.astype(F32))

        @pl.when(index == steps)
        def _():
            turned[...] = low_ref[...].T

        @pl.when(jnp.logical_and(index >= steps, index < steps + columns_in))
        def _():
            column = index - steps
            at = pl.ds(pl.multiple_of(column * tile_in, tile_in), tile_in)
            held_in[column] = dot(turned[...], d_pre[:, at]).astype(BF)
            emit(plan_in, column, held_in, spot_ref, grads_in, sems_in)

        @pl.when(index == steps + columns_in)
        def _():
            turned[...] = d_attn[...].T

        @pl.when(index >= steps + columns_in)
        def _():
            column = index - steps - columns_in
            held_out[column] = dot(turned[...], c_ref[...]).astype(BF)
            emit(plan_out, column, held_out, spot_ref, grads_out, sems_out)

        @pl.when(index == steps + columns_in + columns_out - 1)
        def _():
            emitted(plan_in, columns_in, held_in, grads_in, sems_in)
            emitted(plan_out, columns_out, held_out, grads_out, sems_out)

    last, before = steps - 1, steps + columns_in
    rows = lambda wide_: clamped(wide_, last)
    return call(
        body, (steps + columns_in + columns_out,), spot,
        (d_low, slope, d_two, normal_one, inverse_one, normed_low, context, sums_two, gains),
        (rows(width), rows(wide), rows(width), rows(width), rows(128), fixed(count, width),
         pl.BlockSpec((count, tile_out), lambda i, s: (0, jnp.maximum(i - before, 0))),
         fixed(8, width), fixed(*gains.shape)),
        [w_back, w_in, w_out],
        (shape((count, width), F32), shape((count, width), BF), shape((24, width), F32), *shapes),
        (rows(width), rows(width), fixed(24, width), *[any_spec()] * len(shapes)),
        [pltpu.VMEM((count, wide), BF), pltpu.VMEM((count, width), BF),
         pltpu.VMEM((width, count), BF), pltpu.VMEM((columns_in, width, tile_in), BF),
         pltpu.VMEM((columns_out, width, tile_out), BF),
         pltpu.SemaphoreType.DMA((32,)), pltpu.SemaphoreType.DMA((32,))],
        cost(2 * count * width * (3 * wide + 2 * width), 18 * count * width + 2 * count * wide),
    )


def tokens_backward(spot, d_one, d_query, d_key, d_value, w_qkv):
    count, width = d_one.shape

    def body(spot_ref, d1_ref, q_ref, k_ref, v_ref, w_ready, out_ref):
        w_ref = w_ready()
        total = d1_ref[...] + dot(q_ref[...], w_ref[0:width, :])
        total += dot(k_ref[...], w_ref[width : 2 * width, :])
        total += dot(v_ref[...], w_ref[2 * width : 3 * width, :])
        out_ref[...] = total.astype(BF)

    return call(
        body, (count // TILE,), spot, (d_one, d_query, d_key, d_value), (row(width),) * 4, [w_qkv],
        shape((count, width), BF), row(width),
        estimate=cost(6 * count * width * width, 12 * count * width),
    )


def gradient(spot, lefts, right, plan):
    count, columns = right.shape
    width = lefts[0].shape[1]
    total = width * len(lefts)
    tile = plan[0]
    steps = columns // tile
    n_left = len(lefts)
    shapes = emit_shapes(plan, total, columns)

    def body(spot_ref, *refs):
        left_refs, right_ref = refs[:n_left], refs[n_left]
        grads = refs[n_left + 1 : n_left + 1 + len(shapes)]
        turned, held, sems = refs[-3:]
        step = pl.program_id(0)

        @pl.when(step == 0)
        def _():
            for index, ref in enumerate(left_refs):
                turned[index * width : (index + 1) * width, :] = ref[...].T

        for index in range(n_left):
            part = slice(index * width, (index + 1) * width)
            held[step, part, :] = dot(turned[part, :], right_ref[...]).astype(BF)
        emit(plan, step, held, spot_ref, grads, sems)

        @pl.when(step == steps - 1)
        def _():
            emitted(plan, steps, held, grads, sems)

    return call(
        body, (steps,), spot, (*lefts, right),
        (*[fixed(count, width)] * n_left, pl.BlockSpec((count, tile), lambda i, s: (0, i))), [],
        shapes, (any_spec(),) * len(shapes),
        [pltpu.VMEM((total, count), BF), pltpu.VMEM((steps, total, tile), BF),
         pltpu.SemaphoreType.DMA((32,))],
        cost(2 * count * total * columns, 2 * (count * (total + columns) + total * columns)),
    )


def widen(value):
    return value.astype(F32)


def exchange(value, stage):
    axes = ("x", "core", "z", "y")
    pairs = []
    for source in range(32):
        x, core, z, y = source >> 4, (source >> 3) & 1, (source >> 1) & 3, source & 1
        if stage in (Z1, Z2, Z3):
            z ^= {Z1: 1, Z2: 2, Z3: 3}[stage]
        elif stage == CORE:
            core ^= 1
        elif (stage == FIRST) == (core == 0):
            x ^= 1
        else:
            y ^= 1
        pairs.append((source, 16 * x + 8 * core + 2 * z + y))
    return lax.ppermute(value, axes, pairs)


class Parcel:
    def __init__(self, array, origins=((0, 0, 0, 0),)):
        self.array = array
        self.origins = tuple(origins)

    def moved(self, stage):
        def change(origin):
            core, second, first, depth = origin
            along_first = stage == (SECOND if core else FIRST)
            along_second = stage == (FIRST if core else SECOND)
            return (
                core ^ (stage == CORE),
                second ^ along_second,
                first ^ along_first,
                depth ^ {Z1: 1, Z2: 2}.get(stage, 0),
            )

        return Parcel(exchange(self.array, stage), [change(origin) for origin in self.origins])

    def __add__(self, other):
        return Parcel(jnp.concatenate([self.array, other.array]), self.origins + other.origins)


def sync(values, *parcels):
    values, arrays = lax.optimization_barrier((values, [parcel.array for parcel in parcels]))
    for parcel, array in zip(parcels, arrays):
        parcel.array = array
    return values


class Reduce:
    def __init__(self, near, far):
        self.near, self.far = near, Parcel(far)

    def send_core(self):
        self.core = Parcel(exchange(self.far.array, CORE))

    def sum(self, start, stop, *others):
        total = widen(self.near[start:stop]) + widen(self.core.array[start:stop])
        for parcel, at in others:
            total += widen(parcel.array[at : at + stop - start])
        return total

    def send(self, stage, start, stop, *others):
        return Parcel(exchange(self.sum(start, stop, *others).astype(BF), stage))

    def send_second_b(self):
        self.second_b = self.send(SECOND, 12, 16)

    def send_second_a(self):
        self.second_a = self.send(SECOND, 4, 8)

    def send_first_b(self):
        self.first_b = self.send(FIRST, 10, 12, (self.second_b, 2))

    def send_first_a(self):
        self.first_a = self.send(FIRST, 2, 4, (self.second_a, 2))

    def send_z2(self):
        self.z2 = self.send(Z2, 8, 10, (self.second_b, 0), (self.first_b, 0))

    def send_z1(self):
        self.z1 = self.send(Z1, 1, 2, (self.second_a, 1), (self.first_a, 1), (self.z2, 1))
        self.last = (self.z2, self.z1)

    def send_direct_b(self):
        self.z2 = self.send(Z2, 8, 9, (self.second_b, 0), (self.first_b, 0))
        self.z3 = self.send(Z3, 9, 10, (self.second_b, 1), (self.first_b, 1))

    def send_direct_a(self):
        self.z1 = self.send(Z1, 1, 2, (self.second_a, 1), (self.first_a, 1))
        self.last = (self.z1, self.z2, self.z3)

    def result(self):
        others = (self.second_a, self.first_a) + self.last
        return self.sum(0, 1, *[(parcel, 0) for parcel in others])[0]


def source_of(spot, origin):
    away, second, first, depth = origin
    core = spot[1] ^ away
    x = spot[0] ^ (first + core * (second - first))
    y = spot[3] ^ (second + core * (first - second))
    return core, x, 2 * (spot[2] ^ depth) + y


def weight_of(parcels, source_rows, place, dims):
    start, rows, cols = source_rows
    pieces, places = [], []
    for parcel in parcels:
        pieces.append(parcel.array)

        def at(spot_ref, ref, origins=parcel.origins):
            for index, origin in enumerate(origins):
                core, x, f = source_of(spot_ref, origin)
                row_at, column_at = place(x, core, f)
                yield (
                    ref.at[index, pl.ds(start, rows), :],
                    (
                        pl.ds(pl.multiple_of(row_at, 16), rows),
                        pl.ds(pl.multiple_of(column_at, 128), cols),
                    ),
                )

        places.append(at)
    return pieces, places, dims


def whole_weight(array):
    def at(spot_ref, ref):
        yield ref, (pl.ds(0, array.shape[0]), pl.ds(0, array.shape[1]))

    return [array], [at], array.shape


def device_slots(spot, origins):
    device = lax.broadcasted_iota(jnp.int32, (len(origins), len(origins)), 0)
    owners = []
    for origin in origins:
        core, x, f = source_of(spot, origin)
        owners.append(16 * x + 8 * core + f)
    return (device == jnp.stack(owners)[None, :]).astype(F32)


def small_vectors(every, shards):
    biases, in_bias, gains = shards
    devices = every.shape[0]
    first, second = biases.size, biases.size + in_bias.size
    third = second + gains.size
    return (
        every[:, :first].reshape(devices, 6, -1).transpose(1, 0, 2).reshape(6, -1),
        every[:, first:second].reshape(1, -1),
        every[:, second:third].reshape(devices, 2, -1).transpose(1, 0, 2).reshape(2, -1),
    )


def on_device(sizes, tokens, segment_ids, w_qkv, w_out, w_in, w_back, biases, in_bias, gains, out_grad):
    axes = ("x", "core", "z", "y")
    dp_axes, fsdp_axes = ("x", "core"), ("z", "y")
    devices = math.prod(sizes)
    by_permute = sizes == (2, 2, 4, 2)
    count, width = tokens.shape
    wide = w_back.shape[0] * sizes[0] * sizes[1]
    blocks = range(count // BLOCK)
    spot = jnp.stack([lax.axis_index(axis) for axis in axes]).astype(jnp.int32)
    core = spot[1]
    shards = (biases, in_bias, gains)
    segment_row = segment_ids.reshape(count // BLOCK, 1, BLOCK)

    qkv_cols, out_cols = w_qkv.shape[1], w_out.shape[1]
    pair_cols = 2 * w_qkv.shape[0]
    in_rows, in_cols = w_in.shape
    back_rows, back_cols = w_back.shape
    half_q, half_o = qkv_cols // 2, out_cols // 2

    if by_permute:

        def paired(turned):
            half = turned.shape[0] // 2
            first, second = turned[:half], turned[half:]
            mine = jnp.where(core == 0, first, second)
            other = exchange(jnp.where(core == 0, second, first), CORE)
            return jnp.where(
                core == 0,
                jnp.concatenate([mine, other], axis=1),
                jnp.concatenate([other, mine], axis=1),
            )

        to_qkv = Parcel(paired(w_qkv.T)[None])
        qkv_z1 = to_qkv.moved(Z1)
        own_vectors, w_in = sync(((biases, in_bias, gains), w_in), to_qkv)
        own_small = jnp.concatenate([part.reshape(-1) for part in own_vectors])
        to_small = Parcel(jnp.pad(own_small, (0, 1024 - own_small.size)).reshape(1, 8, 128))
        to_small += to_small.moved(CORE)
        w_in, w_out, w_back = sync((w_in, w_out, w_back), qkv_z1, to_small)
        qkv_near = to_qkv + qkv_z1
        qkv_z2 = qkv_near.moved(Z2)
        qkv_first_a = qkv_near.moved(FIRST)
        to_small += to_small.moved(FIRST)
        to_in = Parcel(jnp.concatenate([w_in, paired(w_out.T)], axis=0)[None])
        to_back = Parcel(w_back.T[None])
        sync((), qkv_first_a, to_small, to_in)
        qkv_a = qkv_near + qkv_first_a
        qkv_second_a = qkv_a.moved(SECOND)
        in_z1 = to_in.moved(Z1)
        to_small += to_small.moved(SECOND)
        sync((), qkv_z2)
        qkv_first_b = qkv_z2.moved(FIRST)
        sync((), qkv_z2, to_small)
        to_small += to_small.moved(Z1)
        sync((), qkv_first_b, to_small)
        qkv_b = qkv_z2 + qkv_first_b
        qkv_second_b = qkv_b.moved(SECOND)
        to_small += to_small.moved(Z2)
        sync((), qkv_first_b, qkv_second_a, to_small, in_z1)
        qkv_core_a = qkv_a.moved(CORE), qkv_second_a.moved(CORE)
        in_near = to_in + in_z1
        in_z2 = in_near.moved(Z2)
        sync((), qkv_second_b, in_near, to_back)
        qkv_core_b = qkv_b.moved(CORE), qkv_second_b.moved(CORE)
        in_first_a = in_near.moved(FIRST)
        back_z1 = to_back.moved(Z1)
        tokens = sync(tokens, *qkv_core_a, *qkv_core_b)
        qkv_parcels = (
            qkv_a, qkv_second_a, qkv_b, qkv_second_b, *qkv_core_a, *qkv_core_b
        )
        qkv_weight = weight_of(
            qkv_parcels, (0, half_q, pair_cols),
            lambda x, c, f: (f * qkv_cols + c * half_q, x * pair_cols), (3 * width, width),
        )
        slots = device_slots(spot, to_small.origins)
        arrived = widen(to_small.array).reshape(32, 1024)
        every = jnp.dot(slots, arrived, precision=lax.Precision.HIGHEST)

        def back_blocks(index):
            return [(f * back_cols, 0, index >> 1, index & 1, f >> 1, f & 1) for f in range(8)]

        def in_blocks(index):
            return [
                ((2 * x + c) * in_rows, y * in_cols, x, c, index, y)
                for x in range(2) for c in range(2) for y in range(2)
            ]

        def out_blocks(index):
            return [
                (f * out_cols + c * half_o, 0, index, c, f >> 1, f & 1)
                for f in range(8) for c in range(2)
            ]

        def qkv_blocks(index):
            return [
                (f * qkv_cols + c * half_q, 0, index, c, f >> 1, f & 1)
                for f in range(8) for c in range(2)
            ]

        plans = {
            "back": (back_rows, back_blocks, (back_cols, back_rows), back_cols, 0),
            "in": (2 * in_cols, in_blocks, (in_rows, in_cols), in_rows + half_o, 0),
            "out": (pair_cols, out_blocks, (half_o, pair_cols), in_rows + half_o, in_rows),
            "qkv": (pair_cols, qkv_blocks, (half_q, pair_cols), half_q, 0),
        }
    else:

        def full(shard):
            return lax.all_gather(
                lax.all_gather(shard, fsdp_axes, axis=1, tiled=True), dp_axes, axis=0, tiled=True
            )

        qkv_weight = whole_weight(full(w_qkv).T)
        out_weight = whole_weight(full(w_out).T)
        in_weight = whole_weight(full(w_in))
        back_weight = whole_weight(full(w_back).T)
        own_small = jnp.concatenate([biases.reshape(-1), in_bias, gains.reshape(-1)])
        every = widen(lax.all_gather(own_small, axes, axis=0, tiled=False))
        plans = {name: (width // 2, None, (0, 0), 0, 0) for name in ("back", "in", "out", "qkv")}

    bias_values, hidden_bias, gain_values = small_vectors(every, shards)
    qkv_bias = jnp.concatenate(
        [bias_values[0:1], jnp.zeros((1, width), F32), bias_values[1:2]], axis=1
    )

    qkv = project_qkv(spot, tokens, qkv_weight, qkv_bias)
    if by_permute:
        qkv = sync(qkv, in_first_a, in_z2, back_z1)
        in_a = in_near + in_first_a
        in_second_a = in_a.moved(SECOND)
        in_first_b = in_z2.moved(FIRST)
        back_near = to_back + back_z1
        back_z2 = back_near.moved(Z2)
    attended = None
    for block in blocks:
        attended = attend_forward(block, qkv, segment_row, attended)
        if by_permute and block == 0:
            attended = sync(attended, in_second_a, in_first_b)
            in_b = in_z2 + in_first_b
            in_second_b = in_b.moved(SECOND)
            in_core = in_a.moved(CORE), in_second_a.moved(CORE), in_b.moved(CORE)
            back_first_a = back_near.moved(FIRST)
    context, lse = attended
    if by_permute:
        context = sync(context, in_second_b, *in_core, back_first_a, back_z2)
        in_cross = in_second_b.moved(CORE)
        back_a = back_near + back_first_a
        back_second_a = back_a.moved(SECOND)
        back_first_b = back_z2.moved(FIRST)
        context = sync(context, in_cross)
        in_parcels = (in_a, in_second_a, in_b, in_second_b, *in_core, in_cross)
        in_weight = weight_of(
            in_parcels, (0, in_rows, in_cols),
            lambda x, c, f: ((2 * x + c) * in_rows, f * in_cols), (width, wide),
        )
        out_weight = weight_of(
            in_parcels, (in_rows, half_o, pair_cols),
            lambda x, c, f: (f * out_cols + c * half_o, x * pair_cols), (width, width),
        )
    normal_one, inverse_one, normed_low = project_out(
        spot, context, tokens, out_weight, bias_values, gain_values
    )
    if by_permute:
        normed_low = sync(normed_low, back_second_a, back_first_b)
        back_b = back_z2 + back_first_b
        back_second_b = back_b.moved(SECOND)
        back_core = back_a.moved(CORE), back_second_a.moved(CORE), back_b.moved(CORE)
    hidden, slope = ffn_in(spot, normed_low, in_weight, hidden_bias)
    if by_permute:
        hidden = sync(hidden, back_second_b, *back_core)
        back_cross = back_second_b.moved(CORE)
        back_weight = weight_of(
            (back_a, back_second_a, back_b, back_second_b, *back_core, back_cross),
            (0, back_cols, back_rows),
            lambda x, c, f: (f * back_cols, (2 * x + c) * back_rows), (width, wide),
        )
    layer_out, d_two, d_low, sums_two, *grad_back = forward_rows(
        spot, hidden, normal_one, out_grad, back_weight, bias_values, gain_values, plans["back"]
    )
    if by_permute:
        from_back = Reduce(*grad_back)
        d_low = sync(d_low, from_back.far)
        from_back.send_core()
    d_one, d_context, small, *grads_in = backward_rows(
        spot, d_low, slope, d_two, normal_one, inverse_one, normed_low, context, sums_two,
        back_weight, in_weight, out_weight, gain_values, plans["in"], plans["out"],
    )
    if by_permute:
        from_in = Reduce(*grads_in)
        d_context = sync(d_context, from_back.core, from_in.far)
        from_back.send_second_b()
        from_back.send_second_a()
        from_in.send_core()
    else:
        grad_in, grad_out = grads_in
        grad_back, = grad_back
    attended = None
    for block in blocks:
        *attended, small = attend_backward(
            block, qkv, segment_row, lse, context, d_context, small, attended
        )
        if by_permute and block == 0:
            attended = sync(attended, from_back.second_a, from_back.second_b, from_in.core)
            from_back.send_first_b()
            from_back.send_first_a()
            from_in.send_second_b()
        elif by_permute:
            attended, small = sync(
                (attended, small), from_back.first_a, from_back.first_b, from_in.second_b
            )
            from_in.send_second_a()
            from_in.send_first_b()
            from_back.send_z2()
            small_sent = Parcel(small).moved(CORE)
    grad_qkv = gradient(spot, attended, tokens, plans["qkv"])
    if by_permute:
        from_qkv = Reduce(*grad_qkv)
        small = sync(small, from_qkv.far, small_sent, from_in.second_a, from_in.first_b)
        from_qkv.send_core()
        small = small + small_sent.array
        small_sent = Parcel(small).moved(Z1)
        from_in.send_z2()
        from_in.send_first_a()
        d_one = sync(d_one, from_qkv.core)
        from_qkv.send_second_b()
        from_qkv.send_second_a()
    else:
        grad_qkv, = grad_qkv
    tokens_grad = tokens_backward(spot, d_one, *attended, qkv_weight)

    if by_permute:

        def unpaired(sums):
            half = sums.shape[1] // 2
            left, right = sums[:, :half], sums[:, half:]
            mine = jnp.where(core == 0, left, right)
            other = widen(exchange(jnp.where(core == 0, right, left).astype(BF), CORE))
            return jnp.where(
                core == 0,
                jnp.concatenate([mine, other], axis=0),
                jnp.concatenate([other, mine], axis=0),
            )

        tokens_grad, small = sync((tokens_grad, small), from_qkv.second_b)
        from_qkv.send_first_b()
        small, = sync((small,), from_qkv.second_a, small_sent)
        from_qkv.send_first_a()
        small = small + small_sent.array
        small_sent = Parcel(small).moved(SECOND)
        small = sync(small, from_qkv.first_b, small_sent)
        from_qkv.send_direct_b()
        small = small + small_sent.array
        small_sent = Parcel(small).moved(FIRST)
        small = sync(small, from_qkv.first_a, small_sent, from_in.first_a, from_in.z2, from_back.z2)
        from_qkv.send_direct_a()
        small = small + small_sent.array
        small_sent = Parcel(small).moved(Z2)
        from_in.send_z1()
        from_back.send_z1()
        small = sync(small, small_sent, from_in.z1, from_back.z1)
        small = small + small_sent.array
        sums_in = from_in.result()
        own_back = from_back.result().T
        own_in = sums_in[:in_rows]
        own_out = unpaired(sums_in[in_rows:]).T
        own_qkv = unpaired(from_qkv.result()).T
    else:

        def scattered(total):
            part = lax.psum_scatter(total, dp_axes, scatter_dimension=0, tiled=True)
            part = lax.psum_scatter(part, fsdp_axes, scatter_dimension=1, tiled=True)
            return widen(part)

        own_back = scattered(grad_back.T)
        own_in = scattered(grad_in)
        own_out = scattered(grad_out.T)
        own_qkv = scattered(grad_qkv.T)
        small = lax.psum(small, axes)
    device = lax.axis_index(axes)
    queries = small[QUERY_SUM : QUERY_SUM + 2]
    bias_total = jnp.concatenate([queries, small[10:11], small[9:10], small[2:3], small[1:2]])
    gain_total = jnp.concatenate([small[8:9], small[0:1]])
    own_bias = lax.dynamic_slice_in_dim(bias_total, device * biases.shape[1], biases.shape[1], 1)
    own_gain = lax.dynamic_slice_in_dim(gain_total, device * gains.shape[1], gains.shape[1], 1)
    own_hidden = lax.dynamic_slice_in_dim(
        small[HIDDEN_SUM:QUERY_SUM].reshape(-1), device * in_bias.shape[0], in_bias.shape[0], 0
    )
    return (
        layer_out, tokens_grad, own_qkv, own_out, own_in, own_back, own_bias, own_hidden, own_gain,
    )


def solution(mesh):
    dp, fsdp = mesh.devices.shape
    sizes = (dp // 2, 2, fsdp // 2, 2)
    split = Mesh(mesh.devices.reshape(sizes), ("x", "core", "z", "y"))
    outer, inner = ("x", "core"), ("z", "y")
    every = outer + inner
    rows = P(every, None)
    weight = P(outer, inner)
    vectors = P(None, every)

    def placed(*arrays):
        return on_device(sizes, *arrays)

    return jax.shard_map(
        placed,
        mesh=split,
        in_specs=(rows, rows, weight, weight, weight, weight, vectors, P(every), vectors, rows),
        out_specs=(rows, rows, weight, weight, weight, weight, vectors, P(every), vectors),
        check_vma=False,
    )
```

```python
import math

import jax
import jax.numpy as jnp
from jax import lax
from jax.experimental import pallas as pl
from jax.experimental.pallas import tpu as pltpu
from jax.sharding import Mesh, PartitionSpec as P

HEADS = 12
HD = 64
BLOCK = 512
PAIR = 2 * HD
TILE = 256
VMEM = 58 * 1024 * 1024
BF = jnp.bfloat16
F32 = jnp.float32
Z1, Z2, FIRST, SECOND, CORE, Z3 = range(6)
HIDDEN_SUM, QUERY_SUM = 16, 20
NT = (((1,), (1,)), ((), ()))


def dot(a, b):
    return jnp.dot(a, b, preferred_element_type=F32)


def dot_nt(a, b):
    return lax.dot_general(a, b, NT, preferred_element_type=F32)


def any_spec():
    return pl.BlockSpec(memory_space=pl.ANY)


def params(*semantics):
    return pltpu.CompilerParams(
        dimension_semantics=semantics if semantics else None, vmem_limit_bytes=VMEM
    )


def cost(flops, nbytes, trans=0):
    return pl.CostEstimate(flops=flops, bytes_accessed=nbytes, transcendentals=trans)

def layer_norm_parts(rows):
    center = jnp.mean(rows, axis=-1, keepdims=True)
    centered = rows - center
    spread = jnp.mean(centered * centered, axis=-1, keepdims=True)
    inverse = lax.rsqrt(spread + 1e-05)
    return centered * inverse, inverse


def layer_norm_back(grad, normal, inverse):
    mean_grad = jnp.mean(grad, axis=-1, keepdims=True)
    mean_both = jnp.mean(grad * normal, axis=-1, keepdims=True)
    return (grad - mean_grad - normal * mean_both) * inverse


def add_rows(ref, values):
    ref[...] += jnp.sum(values, axis=0, keepdims=True)


def zero_first(*refs):
    @pl.when(pl.program_id(0) == 0)
    def _():
        for ref in refs:
            ref[...] = jnp.zeros_like(ref)


def call(
    body, grid, spot, arrays, specs, weights, outs, out_specs, scratch=(), estimate=None, aliases=()
):
    flat = [piece for pieces, _, _ in weights for piece in pieces]
    counts = [len(pieces) for pieces, _, _ in weights]
    n_arrays, n_flat, n_weights = len(arrays), len(flat), len(weights)
    n_outs = len(outs) if isinstance(outs, tuple) else 1

    def kernel(spot_ref, *refs):
        ins = refs[:n_arrays]
        piece_refs = refs[n_arrays : n_arrays + n_flat]
        out_refs = refs[n_arrays + n_flat : n_arrays + n_flat + n_outs]
        rest = refs[n_arrays + n_flat + n_outs :]
        held = rest[:n_weights]
        sems = rest[n_weights : 2 * n_weights]
        extra = rest[2 * n_weights :]
        first = pl.program_id(0) == 0

        def copies(number):
            start = sum(counts[:number])
            found = []
            for index in range(counts[number]):
                place = weights[number][1][index]
                for source, at in place(spot_ref, piece_refs[start + index]):
                    found.append(
                        pltpu.make_async_copy(
                            source, held[number].at[at], sems[number].at[len(found)]
                        )
                    )
            return found

        @pl.when(first)
        def _():
            for number in range(n_weights):
                for copy in copies(number):
                    copy.start()

        def ready(number):
            def wait():
                @pl.when(first)
                def _():
                    for copy in copies(number):
                        copy.wait()

                return held[number]

            return wait

        body(spot_ref, *ins, *[ready(number) for number in range(n_weights)], *out_refs, *extra)

    scratch_shapes = (
        [pltpu.VMEM(shape, BF) for _, _, shape in weights]
        + [pltpu.SemaphoreType.DMA((32,)) for _ in counts]
        + list(scratch)
    )
    return pl.pallas_call(
        kernel,
        out_shape=outs,
        grid_spec=pltpu.PrefetchScalarGridSpec(
            num_scalar_prefetch=1,
            grid=grid,
            in_specs=list(specs) + [any_spec()] * n_flat,
            out_specs=out_specs,
            scratch_shapes=scratch_shapes,
        ),
        compiler_params=params(*(["arbitrary"] * len(grid))),
        cost_estimate=estimate,
        input_output_aliases=dict(aliases),
    )(spot, *arrays, *flat)


def row(width, tile=TILE):
    return pl.BlockSpec((tile, width), lambda i, s: (i, 0))


def fixed(*shape):
    return pl.BlockSpec(shape, lambda *_: (0,) * len(shape))


def shape(dims, dtype):
    return jax.ShapeDtypeStruct(dims, dtype)


def project_qkv(spot, tokens, w_qkv, qkv_bias):
    count, width = tokens.shape
    wide = w_qkv[2][0]

    def body(spot_ref, x_ref, bias_ref, w_ready, out_ref):
        w_ref = w_ready()
        for start in range(0, wide, width):
            part = slice(start, start + width)
            out_ref[:, part] = (dot_nt(x_ref[...], w_ref[part, :]) + bias_ref[:, part]).astype(BF)

    return call(
        body, (count // TILE,), spot, (tokens, qkv_bias), (row(width), fixed(1, wide)), [w_qkv],
        shape((count, wide), BF), row(wide),
        estimate=cost(2 * count * width * wide, 2 * (count * width + wide * width + count * wide)),
    )


def lane_masks():
    lane = lax.broadcasted_iota(jnp.int32, (1, PAIR), 1)
    return [(lane // HD == head) for head in range(2)]


def same_segment(row_ref):
    numbers = row_ref[0].astype(F32)
    column = jnp.broadcast_to(numbers, (128, BLOCK)).T[:, 0:1]
    return column == numbers


def attend_forward(block, qkv, segment_row, into=None):
    count, wide = qkv.shape
    width = wide // 3
    pairs = width // PAIR
    blocks = count // BLOCK

    def body(q_ref, k_ref, v_ref, row_ref, *refs):
        out_ref, lse_ref = refs[-2:]
        visible = same_segment(row_ref)
        query, key = q_ref[...] * BF(1.0 / math.sqrt(HD)), k_ref[...]
        value_turned = v_ref[...].T
        parts = []
        for head, lanes in enumerate(lane_masks()):
            scores = dot_nt(key, jnp.where(lanes, query, BF(0)))
            scores = jnp.where(visible, scores, -1e30)
            highest = jnp.max(scores, axis=0, keepdims=True)
            exponent = jnp.exp(scores - highest)
            total = jnp.sum(exponent, axis=0, keepdims=True)
            part = dot(value_turned[head * HD : (head + 1) * HD], exponent.astype(BF))
            parts.append(part / total)
            lse_ref[0, 0, head : head + 1, :] = highest + jnp.log(total)
        out_ref[...] = jnp.concatenate(parts, axis=0).T.astype(BF)

    flops = 4 * HEADS * BLOCK * BLOCK * HD
    given = () if into is None else into
    return pl.pallas_call(
        body,
        out_shape=(shape((count, width), BF), shape((blocks, pairs, 2, BLOCK), F32)),
        grid=(pairs,),
        in_specs=[
            pl.BlockSpec((BLOCK, PAIR), lambda p: (block, p)),
            pl.BlockSpec((BLOCK, PAIR), lambda p: (block, pairs + p)),
            pl.BlockSpec((BLOCK, PAIR), lambda p: (block, 2 * pairs + p)),
            pl.BlockSpec((1, 1, BLOCK), lambda p: (block, 0, 0)),
        ]
        + [any_spec()] * len(given),
        out_specs=(
            pl.BlockSpec((BLOCK, PAIR), lambda p: (block, p)),
            pl.BlockSpec((1, 1, 2, BLOCK), lambda p: (block, p, 0, 0)),
        ),
        compiler_params=params("arbitrary"),
        cost_estimate=cost(4 * flops, 4 * count * width, HEADS * BLOCK * BLOCK),
        input_output_aliases={4 + index: index for index in range(len(given))},
    )(qkv, qkv, qkv, segment_row, *given)


def attend_backward(block, qkv, segment_row, lse, context, d_context, sums, into=None):
    count, wide = qkv.shape
    width = wide // 3
    pairs = width // PAIR
    factor = 1.0 / math.sqrt(HD)

    def body(q_ref, k_ref, v_ref, o_ref, do_ref, row_ref, lse_ref, given_ref, *refs):
        dq_ref, dk_ref, dv_ref, sums_ref = refs[-4:]

        @pl.when(pl.program_id(0) == 0)
        def _():
            sums_ref[...] = given_ref[...]

        visible = same_segment(row_ref)
        query, key, value = q_ref[...] * BF(factor), k_ref[...], v_ref[...]
        d_out = do_ref[...]
        key_turned = key.T
        product = (d_out.astype(F32) * o_ref[...].astype(F32)).T
        masks = lane_masks()
        d_query, d_key, d_value = [], [], []
        for head, lanes in enumerate(masks):
            inside = slice(head * HD, (head + 1) * HD)
            delta = jnp.sum(product[inside], axis=0, keepdims=True)
            scores = dot_nt(key, jnp.where(lanes, query, BF(0)))
            scores = jnp.where(visible, scores - lse_ref[0, 0, head : head + 1, :], -1e30)
            prob = jnp.exp(scores)
            d_prob = dot_nt(value, jnp.where(lanes, d_out, BF(0)))
            d_score = (prob * (d_prob - delta)).astype(BF)
            d_value.append(dot(prob.astype(BF), d_out))
            d_key.append(dot(d_score, query))
            d_query.append(dot(key_turned[inside], d_score) * factor)
        dq = jnp.concatenate(d_query, axis=0).T.astype(BF)
        dk = jnp.where(masks[0], d_key[0], d_key[1]).astype(BF)
        dv = jnp.where(masks[0], d_value[0], d_value[1]).astype(BF)
        dq_ref[...] = dq
        dk_ref[...] = dk
        dv_ref[...] = dv
        here = pl.ds(pl.multiple_of(pl.program_id(0) * PAIR, PAIR), PAIR)
        add_rows(sums_ref.at[QUERY_SUM : QUERY_SUM + 1, here], dq.astype(F32))
        add_rows(sums_ref.at[QUERY_SUM + 1 : QUERY_SUM + 2, here], dv.astype(F32))

    tile = pl.BlockSpec((BLOCK, PAIR), lambda p: (block, p))
    flops = 10 * HEADS * BLOCK * BLOCK * HD
    given = () if into is None else into
    return pl.pallas_call(
        body,
        out_shape=(shape((count, width), BF),) * 3 + (shape((24, width), F32),),
        grid=(pairs,),
        in_specs=[
            tile,
            pl.BlockSpec((BLOCK, PAIR), lambda p: (block, pairs + p)),
            pl.BlockSpec((BLOCK, PAIR), lambda p: (block, 2 * pairs + p)),
            tile,
            tile,
            pl.BlockSpec((1, 1, BLOCK), lambda p: (block, 0, 0)),
            pl.BlockSpec((1, 1, 2, BLOCK), lambda p: (block, p, 0, 0)),
            fixed(24, width),
        ]
        + [any_spec()] * len(given),
        out_specs=(tile,) * 3 + (fixed(24, width),),
        compiler_params=params("arbitrary"),
        cost_estimate=cost(4 * flops, 8 * count * width, HEADS * BLOCK * BLOCK),
        input_output_aliases={8 + index: index for index in range(len(given))},
    )(qkv, qkv, qkv, context, d_context, segment_row, lse, sums, *given)


def emit(plan, step, held, spot_ref, out_refs, sems):
    tile, blocks, (rows, cols), _, base = plan
    if blocks is None:
        target = out_refs[0].at[:, pl.ds(pl.multiple_of(step * tile, tile), tile)]
        pltpu.make_async_copy(held.at[step], target, sems.at[step]).start()
        return
    listed = blocks(step)
    for index, (row_at, column_at, x, core, z, y) in enumerate(listed):
        source = held.at[step, pl.ds(row_at, rows), pl.ds(column_at, cols)]
        sem = sems.at[step * len(listed) + index]
        far_x, far_y = x ^ spot_ref[0], y ^ spot_ref[3]
        first = far_x + core * (far_y - far_x)
        depth = z ^ spot_ref[2]
        slot = (depth & 1) + 2 * first + 4 * (far_x + far_y - first) + 8 * (depth >> 1)
        mine = (core ^ spot_ref[1]) == 0

        @pl.when(mine)
        def _():
            pltpu.make_async_copy(source, out_refs[0].at[slot, pl.ds(base, rows)], sem).start()

        @pl.when(jnp.logical_not(mine))
        def _():
            pltpu.make_async_copy(source, out_refs[1].at[slot, pl.ds(base, rows)], sem).start()


def emitted(plan, steps, held, out_refs, sems):
    tile, blocks, (rows, cols), _, base = plan
    if blocks is None:
        for step in range(steps):
            target = out_refs[0].at[:, pl.ds(step * tile, tile)]
            pltpu.make_async_copy(held.at[step], target, sems.at[step]).wait()
        return
    for index in range(32):
        source = held.at[0, pl.ds(0, rows), pl.ds(0, cols)]
        pltpu.make_async_copy(source, out_refs[0].at[0, pl.ds(base, rows)], sems.at[index]).wait()


def emit_shapes(plan, total, columns):
    _, blocks, (rows, cols), slot_rows, _ = plan
    if blocks is None:
        return (shape((total, columns), BF),)
    return (shape((16, slot_rows, cols), BF),) * 2


def clamped(width, last, tile=TILE):
    return pl.BlockSpec((tile, width), lambda i, s: (jnp.minimum(i, last), 0))


def project_out(spot, context, tokens, w_out, biases, gains):
    count, width = tokens.shape

    def body(spot_ref, c_ref, x_ref, bias_ref, gain_ref, w_ready, normal_ref, inverse_ref, low_ref):
        w_ref = w_ready()
        resid = x_ref[...].astype(F32) + (dot_nt(c_ref[...], w_ref[...]) + bias_ref[2:3])
        normal, inverse = layer_norm_parts(resid)
        normal_ref[...] = normal
        inverse_ref[...] = jnp.broadcast_to(inverse, inverse_ref.shape)
        low_ref[...] = (normal * gain_ref[0:1] + bias_ref[3:4]).astype(BF)

    return call(
        body, (count // TILE,), spot, (context, tokens, biases, gains),
        (row(width), row(width), fixed(*biases.shape), fixed(*gains.shape)), [w_out],
        (shape((count, width), F32), shape((count, 128), F32), shape((count, width), BF)),
        (row(width), row(128), row(width)),
        estimate=cost(2 * count * width * width, 10 * count * width),
    )


def ffn_in(spot, normed_low, w_in, in_bias):
    count, width = normed_low.shape
    wide = w_in[2][1]

    def body(spot_ref, x_ref, bias_ref, w_ready, hidden_ref, slope_ref):
        w_ref = w_ready()
        for start in range(0, wide, width):
            part = slice(start, start + width)
            pre = dot(x_ref[...], w_ref[:, part]) + bias_ref[:, part]
            cdf = 0.5 + 0.5 * lax.erf(pre * (1.0 / math.sqrt(2.0)))
            hidden_ref[:, part] = (pre * cdf).astype(BF)
            density = jnp.exp(pre * pre * -0.5) * (1.0 / math.sqrt(2.0 * math.pi))
            slope_ref[:, part] = (cdf + pre * density).astype(BF)

    return call(
        body, (count // TILE,), spot, (normed_low, in_bias), (row(width), fixed(1, wide)), [w_in],
        (shape((count, wide), BF),) * 2, (row(wide),) * 2,
        estimate=cost(2 * count * width * wide, 4 * count * wide, 2 * count * wide),
    )


def forward_rows(spot, hidden, normal_one, out_grad, w_back, biases, gains, plan):
    count, width = out_grad.shape
    wide = hidden.shape[1]
    steps = count // TILE
    tile = plan[0]
    columns = wide // tile
    shapes = emit_shapes(plan, width, wide)

    def body(spot_ref, h_ref, n_ref, g_ref, bias_ref, gain_ref, wb_ready,
             out_ref, d_two_ref, d_low_ref, sums_ref, *refs):
        grads, (kept, d_rows, turned, held, sems) = refs[: len(shapes)], refs[len(shapes) :]
        index = pl.program_id(0)
        zero_first(sums_ref)

        @pl.when(index < steps)
        def _():
            here = pl.ds(pl.multiple_of(index * TILE, TILE), TILE)
            kept[here, :] = h_ref[...]
            resid = n_ref[...] * gain_ref[0:1] + bias_ref[3:4]
            w_ref = wb_ready()
            resid += dot_nt(h_ref[...], w_ref[...]) + bias_ref[4:5]
            normal, inverse = layer_norm_parts(resid)
            out_ref[...] = (normal * gain_ref[1:2] + bias_ref[5:6]).astype(BF)
            grad = g_ref[...].astype(F32)
            d_two = layer_norm_back(grad * gain_ref[1:2], normal, inverse)
            d_low = d_two.astype(BF)
            d_two_ref[...] = d_two
            d_low_ref[...] = d_low
            d_rows[here, :] = d_low
            add_rows(sums_ref.at[0:1], grad * normal)
            add_rows(sums_ref.at[1:2], grad)
            add_rows(sums_ref.at[2:3], d_low.astype(F32))

        @pl.when(index == steps)
        def _():
            turned[...] = d_rows[...].T

        @pl.when(index >= steps)
        def _():
            column = index - steps
            at = pl.ds(pl.multiple_of(column * tile, tile), tile)
            held[column] = dot(turned[...], kept[:, at]).astype(BF)
            emit(plan, column, held, spot_ref, grads, sems)

        @pl.when(index == steps + columns - 1)
        def _():
            emitted(plan, columns, held, grads, sems)

    last = steps - 1
    rows = lambda wide_: clamped(wide_, last)
    return call(
        body, (steps + columns,), spot, (hidden, normal_one, out_grad, biases, gains),
        (rows(wide), rows(width), rows(width), fixed(*biases.shape), fixed(*gains.shape)),
        [w_back],
        (shape((count, width), BF), shape((count, width), F32), shape((count, width), BF),
         shape((8, width), F32), *shapes),
        (rows(width), rows(width), rows(width), fixed(8, width), *[any_spec()] * len(shapes)),
        [pltpu.VMEM((count, wide), BF), pltpu.VMEM((count, width), BF),
         pltpu.VMEM((width, count), BF), pltpu.VMEM((columns, width, tile), BF),
         pltpu.SemaphoreType.DMA((32,))],
        cost(4 * count * width * wide, 14 * count * width + 4 * count * wide),
    )


def backward_rows(
    spot, d_low, slope, d_two, normal_one, inverse_one, normed_low, context, sums_two, w_back, w_in,
    w_out, gains, plan_in, plan_out,
):
    count, width = d_two.shape
    wide = slope.shape[1]
    steps = count // TILE
    tile_in, tile_out = plan_in[0], plan_out[0]
    columns_in, columns_out = wide // tile_in, width // tile_out
    shared = plan_in[1] is not None
    shapes = emit_shapes(plan_in, width, wide)
    if not shared:
        shapes += emit_shapes(plan_out, width, width)

    def body(spot_ref, dl_ref, s_ref, d2_ref, n_ref, i_ref, low_ref, c_ref, two_ref, gain_ref,
             wb_ready, wi_ready, wo_ready, d_one_ref, d_context_ref, sums_ref, *refs):
        grads = refs[: len(shapes)]
        d_pre, d_attn, turned, held_in, held_out, sems_in, sems_out = refs[len(shapes) :]
        grads_in, grads_out = (grads, grads) if shared else (grads[:1], grads[1:])
        index = pl.program_id(0)

        @pl.when(index == 0)
        def _():
            sums_ref[...] = jnp.zeros_like(sums_ref)
            sums_ref[0:8, :] = two_ref[...]

        @pl.when(index < steps)
        def _():
            here = pl.ds(pl.multiple_of(index * TILE, TILE), TILE)
            w_ref = wb_ready()
            for start in range(0, wide, width):
                part = slice(start, start + width)
                d_hidden = dot(dl_ref[...], w_ref[:, part])
                piece = (d_hidden * s_ref[:, part].astype(F32)).astype(BF)
                d_pre[here, part] = piece
                at = HIDDEN_SUM + start // width
                add_rows(sums_ref.at[at : at + 1], piece.astype(F32))
            w_ref = wi_ready()
            d_normed = d2_ref[...] + dot_nt(d_pre[here, :], w_ref[...])
            normal = n_ref[...]
            d_one = layer_norm_back(d_normed * gain_ref[0:1], normal, i_ref[:, 0:1])
            low = d_one.astype(BF)
            d_one_ref[...] = d_one
            d_attn[here, :] = low
            d_context_ref[...] = dot(low, wo_ready()[...]).astype(BF)
            add_rows(sums_ref.at[8:9], d_normed * normal)
            add_rows(sums_ref.at[9:10], d_normed)
            add_rows(sums_ref.at[10:11], low.astype(F32))

        @pl.when(index == steps)
        def _():
            turned[...] = low_ref[...].T

        @pl.when(jnp.logical_and(index >= steps, index < steps + columns_in))
        def _():
            column = index - steps
            at = pl.ds(pl.multiple_of(column * tile_in, tile_in), tile_in)
            held_in[column] = dot(turned[...], d_pre[:, at]).astype(BF)
            emit(plan_in, column, held_in, spot_ref, grads_in, sems_in)

        @pl.when(index == steps + columns_in)
        def _():
            turned[...] = d_attn[...].T

        @pl.when(index >= steps + columns_in)
        def _():
            column = index - steps - columns_in
            held_out[column] = dot(turned[...], c_ref[...]).astype(BF)
            emit(plan_out, column, held_out, spot_ref, grads_out, sems_out)

        @pl.when(index == steps + columns_in + columns_out - 1)
        def _():
            emitted(plan_in, columns_in, held_in, grads_in, sems_in)
            emitted(plan_out, columns_out, held_out, grads_out, sems_out)

    last, before = steps - 1, steps + columns_in
    rows = lambda wide_: clamped(wide_, last)
    return call(
        body, (steps + columns_in + columns_out,), spot,
        (d_low, slope, d_two, normal_one, inverse_one, normed_low, context, sums_two, gains),
        (rows(width), rows(wide), rows(width), rows(width), rows(128), fixed(count, width),
         pl.BlockSpec((count, tile_out), lambda i, s: (0, jnp.maximum(i - before, 0))),
         fixed(8, width), fixed(*gains.shape)),
        [w_back, w_in, w_out],
        (shape((count, width), F32), shape((count, width), BF), shape((24, width), F32), *shapes),
        (rows(width), rows(width), fixed(24, width), *[any_spec()] * len(shapes)),
        [pltpu.VMEM((count, wide), BF), pltpu.VMEM((count, width), BF),
         pltpu.VMEM((width, count), BF), pltpu.VMEM((columns_in, width, tile_in), BF),
         pltpu.VMEM((columns_out, width, tile_out), BF),
         pltpu.SemaphoreType.DMA((32,)), pltpu.SemaphoreType.DMA((32,))],
        cost(2 * count * width * (3 * wide + 2 * width), 18 * count * width + 2 * count * wide),
    )


def tokens_backward(spot, d_one, d_query, d_key, d_value, w_qkv):
    count, width = d_one.shape

    def body(spot_ref, d1_ref, q_ref, k_ref, v_ref, w_ready, out_ref):
        w_ref = w_ready()
        total = d1_ref[...] + dot(q_ref[...], w_ref[0:width, :])
        total += dot(k_ref[...], w_ref[width : 2 * width, :])
        total += dot(v_ref[...], w_ref[2 * width : 3 * width, :])
        out_ref[...] = total.astype(BF)

    return call(
        body, (count // TILE,), spot, (d_one, d_query, d_key, d_value), (row(width),) * 4, [w_qkv],
        shape((count, width), BF), row(width),
        estimate=cost(6 * count * width * width, 12 * count * width),
    )


def gradient(spot, lefts, right, plan):
    count, columns = right.shape
    width = lefts[0].shape[1]
    total = width * len(lefts)
    tile = plan[0]
    steps = columns // tile
    n_left = len(lefts)
    shapes = emit_shapes(plan, total, columns)

    def body(spot_ref, *refs):
        left_refs, right_ref = refs[:n_left], refs[n_left]
        grads = refs[n_left + 1 : n_left + 1 + len(shapes)]
        turned, held, sems = refs[-3:]
        step = pl.program_id(0)

        @pl.when(step == 0)
        def _():
            for index, ref in enumerate(left_refs):
                turned[index * width : (index + 1) * width, :] = ref[...].T

        for index in range(n_left):
            part = slice(index * width, (index + 1) * width)
            held[step, part, :] = dot(turned[part, :], right_ref[...]).astype(BF)
        emit(plan, step, held, spot_ref, grads, sems)

        @pl.when(step == steps - 1)
        def _():
            emitted(plan, steps, held, grads, sems)

    return call(
        body, (steps,), spot, (*lefts, right),
        (*[fixed(count, width)] * n_left, pl.BlockSpec((count, tile), lambda i, s: (0, i))), [],
        shapes, (any_spec(),) * len(shapes),
        [pltpu.VMEM((total, count), BF), pltpu.VMEM((steps, total, tile), BF),
         pltpu.SemaphoreType.DMA((32,))],
        cost(2 * count * total * columns, 2 * (count * (total + columns) + total * columns)),
    )


def widen(value):
    return value.astype(F32)


def exchange(value, stage):
    axes = ("x", "core", "z", "y")
    pairs = []
    for source in range(32):
        x, core, z, y = source >> 4, (source >> 3) & 1, (source >> 1) & 3, source & 1
        if stage in (Z1, Z2, Z3):
            z ^= {Z1: 1, Z2: 2, Z3: 3}[stage]
        elif stage == CORE:
            core ^= 1
        elif (stage == FIRST) == (core == 0):
            x ^= 1
        else:
            y ^= 1
        pairs.append((source, 16 * x + 8 * core + 2 * z + y))
    return lax.ppermute(value, axes, pairs)


class Parcel:
    def __init__(self, array, origins=((0, 0, 0, 0),)):
        self.array = array
        self.origins = tuple(origins)

    def moved(self, stage):
        def change(origin):
            core, second, first, depth = origin
            along_first = stage == (SECOND if core else FIRST)
            along_second = stage == (FIRST if core else SECOND)
            return (
                core ^ (stage == CORE),
                second ^ along_second,
                first ^ along_first,
                depth ^ {Z1: 1, Z2: 2}.get(stage, 0),
            )

        return Parcel(exchange(self.array, stage), [change(origin) for origin in self.origins])

    def __add__(self, other):
        return Parcel(jnp.concatenate([self.array, other.array]), self.origins + other.origins)


def sync(values, *parcels):
    values, arrays = lax.optimization_barrier((values, [parcel.array for parcel in parcels]))
    for parcel, array in zip(parcels, arrays):
        parcel.array = array
    return values


class Reduce:
    def __init__(self, near, far):
        self.near, self.far = near, Parcel(far)

    def send_core(self):
        self.core = Parcel(exchange(self.far.array, CORE))

    def sum(self, start, stop, *others):
        total = widen(self.near[start:stop]) + widen(self.core.array[start:stop])
        for parcel, at in others:
            total += widen(parcel.array[at : at + stop - start])
        return total

    def send(self, stage, start, stop, *others):
        return Parcel(exchange(self.sum(start, stop, *others).astype(BF), stage))

    def send_second_b(self):
        self.second_b = self.send(SECOND, 12, 16)

    def send_second_a(self):
        self.second_a = self.send(SECOND, 4, 8)

    def send_first_b(self):
        self.first_b = self.send(FIRST, 10, 12, (self.second_b, 2))

    def send_first_a(self):
        self.first_a = self.send(FIRST, 2, 4, (self.second_a, 2))

    def send_z2(self):
        self.z2 = self.send(Z2, 8, 10, (self.second_b, 0), (self.first_b, 0))

    def send_z1(self):
        self.z1 = self.send(Z1, 1, 2, (self.second_a, 1), (self.first_a, 1), (self.z2, 1))
        self.last = (self.z2, self.z1)

    def send_direct_b(self):
        self.z2 = self.send(Z2, 8, 9, (self.second_b, 0), (self.first_b, 0))
        self.z3 = self.send(Z3, 9, 10, (self.second_b, 1), (self.first_b, 1))

    def send_direct_a(self):
        self.z1 = self.send(Z1, 1, 2, (self.second_a, 1), (self.first_a, 1))
        self.last = (self.z1, self.z2, self.z3)

    def result(self):
        others = (self.second_a, self.first_a) + self.last
        return self.sum(0, 1, *[(parcel, 0) for parcel in others])[0]


def source_of(spot, origin):
    away, second, first, depth = origin
    core = spot[1] ^ away
    x = spot[0] ^ (first + core * (second - first))
    y = spot[3] ^ (second + core * (first - second))
    return core, x, 2 * (spot[2] ^ depth) + y


def weight_of(parcels, source_rows, place, dims):
    start, rows, cols = source_rows
    pieces, places = [], []
    for parcel in parcels:
        pieces.append(parcel.array)

        def at(spot_ref, ref, origins=parcel.origins):
            for index, origin in enumerate(origins):
                core, x, f = source_of(spot_ref, origin)
                row_at, column_at = place(x, core, f)
                yield (
                    ref.at[index, pl.ds(start, rows), :],
                    (
                        pl.ds(pl.multiple_of(row_at, 16), rows),
                        pl.ds(pl.multiple_of(column_at, 128), cols),
                    ),
                )

        places.append(at)
    return pieces, places, dims


def whole_weight(array):
    def at(spot_ref, ref):
        yield ref, (pl.ds(0, array.shape[0]), pl.ds(0, array.shape[1]))

    return [array], [at], array.shape


def device_slots(spot, origins):
    device = lax.broadcasted_iota(jnp.int32, (len(origins), len(origins)), 0)
    owners = []
    for origin in origins:
        core, x, f = source_of(spot, origin)
        owners.append(16 * x + 8 * core + f)
    return (device == jnp.stack(owners)[None, :]).astype(F32)


def small_vectors(every, shards):
    biases, in_bias, gains = shards
    devices = every.shape[0]
    first, second = biases.size, biases.size + in_bias.size
    third = second + gains.size
    return (
        every[:, :first].reshape(devices, 6, -1).transpose(1, 0, 2).reshape(6, -1),
        every[:, first:second].reshape(1, -1),
        every[:, second:third].reshape(devices, 2, -1).transpose(1, 0, 2).reshape(2, -1),
    )


def on_device(sizes, tokens, segment_ids, w_qkv, w_out, w_in, w_back, biases, in_bias, gains, out_grad):
    axes = ("x", "core", "z", "y")
    dp_axes, fsdp_axes = ("x", "core"), ("z", "y")
    devices = math.prod(sizes)
    by_permute = sizes == (2, 2, 4, 2)
    count, width = tokens.shape
    wide = w_back.shape[0] * sizes[0] * sizes[1]
    blocks = range(count // BLOCK)
    spot = jnp.stack([lax.axis_index(axis) for axis in axes]).astype(jnp.int32)
    core = spot[1]
    shards = (biases, in_bias, gains)
    segment_row = segment_ids.reshape(count // BLOCK, 1, BLOCK)

    qkv_cols, out_cols = w_qkv.shape[1], w_out.shape[1]
    pair_cols = 2 * w_qkv.shape[0]
    in_rows, in_cols = w_in.shape
    back_rows, back_cols = w_back.shape
    half_q, half_o = qkv_cols // 2, out_cols // 2

    if by_permute:

        def paired(turned):
            half = turned.shape[0] // 2
            first, second = turned[:half], turned[half:]
            mine = jnp.where(core == 0, first, second)
            other = exchange(jnp.where(core == 0, second, first), CORE)
            return jnp.where(
                core == 0,
                jnp.concatenate([mine, other], axis=1),
                jnp.concatenate([other, mine], axis=1),
            )

        to_qkv = Parcel(paired(w_qkv.T)[None])
        qkv_z1 = to_qkv.moved(Z1)
        own_vectors, w_in = sync(((biases, in_bias, gains), w_in), to_qkv)
        own_small = jnp.concatenate([part.reshape(-1) for part in own_vectors])
        to_small = Parcel(jnp.pad(own_small, (0, 1024 - own_small.size)).reshape(1, 8, 128))
        to_small += to_small.moved(CORE)
        w_in, w_out, w_back = sync((w_in, w_out, w_back), qkv_z1, to_small)
        qkv_near = to_qkv + qkv_z1
        qkv_z2 = qkv_near.moved(Z2)
        qkv_first_a = qkv_near.moved(FIRST)
        to_small += to_small.moved(FIRST)
        to_in = Parcel(jnp.concatenate([w_in, paired(w_out.T)], axis=0)[None])
        to_back = Parcel(w_back.T[None])
        sync((), qkv_first_a, to_small, to_in)
        qkv_a = qkv_near + qkv_first_a
        qkv_second_a = qkv_a.moved(SECOND)
        in_z1 = to_in.moved(Z1)
        to_small += to_small.moved(SECOND)
        sync((), qkv_z2)
        qkv_first_b = qkv_z2.moved(FIRST)
        sync((), qkv_z2, to_small)
        to_small += to_small.moved(Z1)
        sync((), qkv_first_b, to_small)
        qkv_b = qkv_z2 + qkv_first_b
        qkv_second_b = qkv_b.moved(SECOND)
        to_small += to_small.moved(Z2)
        sync((), qkv_first_b, qkv_second_a, to_small, in_z1)
        qkv_core_a = qkv_a.moved(CORE), qkv_second_a.moved(CORE)
        in_near = to_in + in_z1
        in_z2 = in_near.moved(Z2)
        sync((), qkv_second_b, in_near, to_back)
        qkv_core_b = qkv_b.moved(CORE), qkv_second_b.moved(CORE)
        in_first_a = in_near.moved(FIRST)
        back_z1 = to_back.moved(Z1)
        tokens = sync(tokens, *qkv_core_a, *qkv_core_b)
        qkv_parcels = (
            qkv_a, qkv_second_a, qkv_b, qkv_second_b, *qkv_core_a, *qkv_core_b
        )
        qkv_weight = weight_of(
            qkv_parcels, (0, half_q, pair_cols),
            lambda x, c, f: (f * qkv_cols + c * half_q, x * pair_cols), (3 * width, width),
        )
        slots = device_slots(spot, to_small.origins)
        arrived = widen(to_small.array).reshape(32, 1024)
        every = jnp.dot(slots, arrived, precision=lax.Precision.HIGHEST)

        def back_blocks(index):
            return [(f * back_cols, 0, index >> 1, index & 1, f >> 1, f & 1) for f in range(8)]

        def in_blocks(index):
            return [
                ((2 * x + c) * in_rows, y * in_cols, x, c, index, y)
                for x in range(2) for c in range(2) for y in range(2)
            ]

        def out_blocks(index):
            return [
                (f * out_cols + c * half_o, 0, index, c, f >> 1, f & 1)
                for f in range(8) for c in range(2)
            ]

        def qkv_blocks(index):
            return [
                (f * qkv_cols + c * half_q, 0, index, c, f >> 1, f & 1)
                for f in range(8) for c in range(2)
            ]

        plans = {
            "back": (back_rows, back_blocks, (back_cols, back_rows), back_cols, 0),
            "in": (2 * in_cols, in_blocks, (in_rows, in_cols), in_rows + half_o, 0),
            "out": (pair_cols, out_blocks, (half_o, pair_cols), in_rows + half_o, in_rows),
            "qkv": (pair_cols, qkv_blocks, (half_q, pair_cols), half_q, 0),
        }
    else:

        def full(shard):
            return lax.all_gather(
                lax.all_gather(shard, fsdp_axes, axis=1, tiled=True), dp_axes, axis=0, tiled=True
            )

        qkv_weight = whole_weight(full(w_qkv).T)
        out_weight = whole_weight(full(w_out).T)
        in_weight = whole_weight(full(w_in))
        back_weight = whole_weight(full(w_back).T)
        own_small = jnp.concatenate([biases.reshape(-1), in_bias, gains.reshape(-1)])
        every = widen(lax.all_gather(own_small, axes, axis=0, tiled=False))
        plans = {name: (width // 2, None, (0, 0), 0, 0) for name in ("back", "in", "out", "qkv")}

    bias_values, hidden_bias, gain_values = small_vectors(every, shards)
    qkv_bias = jnp.concatenate(
        [bias_values[0:1], jnp.zeros((1, width), F32), bias_values[1:2]], axis=1
    )

    qkv = project_qkv(spot, tokens, qkv_weight, qkv_bias)
    if by_permute:
        qkv = sync(qkv, in_first_a, in_z2, back_z1)
        in_a = in_near + in_first_a
        in_second_a = in_a.moved(SECOND)
        in_first_b = in_z2.moved(FIRST)
        back_near = to_back + back_z1
        back_z2 = back_near.moved(Z2)
    attended = None
    for block in blocks:
        attended = attend_forward(block, qkv, segment_row, attended)
        if by_permute and block == 0:
            attended = sync(attended, in_second_a, in_first_b, back_z2)
            in_b = in_z2 + in_first_b
            in_second_b = in_b.moved(SECOND)
            in_core = in_a.moved(CORE), in_second_a.moved(CORE), in_b.moved(CORE)
            back_first_a = back_near.moved(FIRST)
    context, lse = attended
    if by_permute:
        context = sync(context, in_second_b, *in_core, back_first_a)
        in_cross = in_second_b.moved(CORE)
        back_a = back_near + back_first_a
        back_second_a = back_a.moved(SECOND)
        back_first_b = back_z2.moved(FIRST)
        context = sync(context, in_cross)
        in_parcels = (in_a, in_second_a, in_b, in_second_b, *in_core, in_cross)
        in_weight = weight_of(
            in_parcels, (0, in_rows, in_cols),
            lambda x, c, f: ((2 * x + c) * in_rows, f * in_cols), (width, wide),
        )
        out_weight = weight_of(
            in_parcels, (in_rows, half_o, pair_cols),
            lambda x, c, f: (f * out_cols + c * half_o, x * pair_cols), (width, width),
        )
    normal_one, inverse_one, normed_low = project_out(
        spot, context, tokens, out_weight, bias_values, gain_values
    )
    if by_permute:
        normed_low = sync(normed_low, back_second_a, back_first_b)
        back_b = back_z2 + back_first_b
        back_second_b = back_b.moved(SECOND)
        back_core = back_a.moved(CORE), back_second_a.moved(CORE), back_b.moved(CORE)
    hidden, slope = ffn_in(spot, normed_low, in_weight, hidden_bias)
    if by_permute:
        hidden = sync(hidden, back_second_b, *back_core)
        back_cross = back_second_b.moved(CORE)
        back_weight = weight_of(
            (back_a, back_second_a, back_b, back_second_b, *back_core, back_cross),
            (0, back_cols, back_rows),
            lambda x, c, f: (f * back_cols, (2 * x + c) * back_rows), (width, wide),
        )
    layer_out, d_two, d_low, sums_two, *grad_back = forward_rows(
        spot, hidden, normal_one, out_grad, back_weight, bias_values, gain_values, plans["back"]
    )
    if by_permute:
        from_back = Reduce(*grad_back)
        d_low = sync(d_low, from_back.far)
        from_back.send_core()
    d_one, d_context, small, *grads_in = backward_rows(
        spot, d_low, slope, d_two, normal_one, inverse_one, normed_low, context, sums_two,
        back_weight, in_weight, out_weight, gain_values, plans["in"], plans["out"],
    )
    if by_permute:
        from_in = Reduce(*grads_in)
        d_context = sync(d_context, from_back.core, from_in.far)
        from_back.send_second_b()
        from_back.send_second_a()
        from_in.send_core()
    else:
        grad_in, grad_out = grads_in
        grad_back, = grad_back
    attended = None
    for block in blocks:
        *attended, small = attend_backward(
            block, qkv, segment_row, lse, context, d_context, small, attended
        )
        if by_permute and block == 0:
            attended = sync(attended, from_back.second_a, from_back.second_b, from_in.core)
            from_back.send_first_b()
            from_back.send_first_a()
            from_in.send_second_b()
        elif by_permute:
            attended, small = sync(
                (attended, small), from_back.first_a, from_back.first_b, from_in.second_b
            )
            from_in.send_second_a()
            from_in.send_first_b()
            from_back.send_z2()
            small_sent = Parcel(small).moved(CORE)
    grad_qkv = gradient(spot, attended, tokens, plans["qkv"])
    if by_permute:
        from_qkv = Reduce(*grad_qkv)
        small = sync(small, from_qkv.far, small_sent, from_in.second_a, from_in.first_b)
        from_qkv.send_core()
        small = small + small_sent.array
        small_sent = Parcel(small).moved(Z1)
        from_in.send_z2()
        from_in.send_first_a()
        d_one = sync(d_one, from_qkv.core)
        from_qkv.send_second_b()
        from_qkv.send_second_a()
    else:
        grad_qkv, = grad_qkv
    tokens_grad = tokens_backward(spot, d_one, *attended, qkv_weight)

    if by_permute:

        def unpaired(sums):
            half = sums.shape[1] // 2
            left, right = sums[:, :half], sums[:, half:]
            mine = jnp.where(core == 0, left, right)
            other = widen(exchange(jnp.where(core == 0, right, left).astype(BF), CORE))
            return jnp.where(
                core == 0,
                jnp.concatenate([mine, other], axis=0),
                jnp.concatenate([other, mine], axis=0),
            )

        tokens_grad, small = sync((tokens_grad, small), from_qkv.second_b)
        from_qkv.send_first_b()
        small, = sync((small,), from_qkv.second_a, small_sent)
        from_qkv.send_first_a()
        small = small + small_sent.array
        small_sent = Parcel(small).moved(SECOND)
        small = sync(small, from_qkv.first_b, small_sent)
        from_qkv.send_direct_b()
        small = small + small_sent.array
        small_sent = Parcel(small).moved(FIRST)
        small = sync(small, from_qkv.first_a, small_sent, from_in.first_a, from_in.z2, from_back.z2)
        from_qkv.send_direct_a()
        small = small + small_sent.array
        small_sent = Parcel(small).moved(Z2)
        from_in.send_z1()
        from_back.send_z1()
        small = sync(small, small_sent, from_in.z1, from_back.z1)
        small = small + small_sent.array
        sums_in = from_in.result()
        own_back = from_back.result().T
        own_in = sums_in[:in_rows]
        own_out = unpaired(sums_in[in_rows:]).T
        own_qkv = unpaired(from_qkv.result()).T
    else:

        def scattered(total):
            part = lax.psum_scatter(total, dp_axes, scatter_dimension=0, tiled=True)
            part = lax.psum_scatter(part, fsdp_axes, scatter_dimension=1, tiled=True)
            return widen(part)

        own_back = scattered(grad_back.T)
        own_in = scattered(grad_in)
        own_out = scattered(grad_out.T)
        own_qkv = scattered(grad_qkv.T)
        small = lax.psum(small, axes)
    device = lax.axis_index(axes)
    queries = small[QUERY_SUM : QUERY_SUM + 2]
    bias_total = jnp.concatenate([queries, small[10:11], small[9:10], small[2:3], small[1:2]])
    gain_total = jnp.concatenate([small[8:9], small[0:1]])
    own_bias = lax.dynamic_slice_in_dim(bias_total, device * biases.shape[1], biases.shape[1], 1)
    own_gain = lax.dynamic_slice_in_dim(gain_total, device * gains.shape[1], gains.shape[1], 1)
    own_hidden = lax.dynamic_slice_in_dim(
        small[HIDDEN_SUM:QUERY_SUM].reshape(-1), device * in_bias.shape[0], in_bias.shape[0], 0
    )
    return (
        layer_out, tokens_grad, own_qkv, own_out, own_in, own_back, own_bias, own_hidden, own_gain,
    )


def solution(mesh):
    dp, fsdp = mesh.devices.shape
    sizes = (dp // 2, 2, fsdp // 2, 2)
    split = Mesh(mesh.devices.reshape(sizes), ("x", "core", "z", "y"))
    outer, inner = ("x", "core"), ("z", "y")
    every = outer + inner
    rows = P(every, None)
    weight = P(outer, inner)
    vectors = P(None, every)

    def placed(*arrays):
        return on_device(sizes, *arrays)

    return jax.shard_map(
        placed,
        mesh=split,
        in_specs=(rows, rows, weight, weight, weight, weight, vectors, P(every), vectors, rows),
        out_specs=(rows, rows, weight, weight, weight, weight, vectors, P(every), vectors),
        check_vma=False,
    )
```

```python
import math

import jax
import jax.numpy as jnp
from jax import lax
from jax.experimental import pallas as pl
from jax.experimental.pallas import tpu as pltpu
from jax.sharding import Mesh, PartitionSpec as P

HEADS = 12
HD = 64
BLOCK = 512
PAIR = 2 * HD
GROUP = 2
TILE = 256
VMEM = 58 * 1024 * 1024
BF = jnp.bfloat16
F32 = jnp.float32
Z1, Z2, FIRST, SECOND, CORE, Z3 = range(6)
HIDDEN_SUM, QUERY_SUM = 16, 20
NT = (((1,), (1,)), ((), ()))


def dot(a, b):
    return jnp.dot(a, b, preferred_element_type=F32)


def dot_nt(a, b):
    return lax.dot_general(a, b, NT, preferred_element_type=F32)


def any_spec():
    return pl.BlockSpec(memory_space=pl.ANY)


def params(*semantics):
    return pltpu.CompilerParams(
        dimension_semantics=semantics if semantics else None, vmem_limit_bytes=VMEM
    )


def cost(flops, nbytes, trans=0):
    return pl.CostEstimate(flops=flops, bytes_accessed=nbytes, transcendentals=trans)

def layer_norm_parts(rows):
    center = jnp.mean(rows, axis=-1, keepdims=True)
    centered = rows - center
    spread = jnp.mean(centered * centered, axis=-1, keepdims=True)
    inverse = lax.rsqrt(spread + 1e-05)
    return centered * inverse, inverse


def layer_norm_back(grad, normal, inverse):
    mean_grad = jnp.mean(grad, axis=-1, keepdims=True)
    mean_both = jnp.mean(grad * normal, axis=-1, keepdims=True)
    return (grad - mean_grad - normal * mean_both) * inverse


def add_rows(ref, values):
    ref[...] += jnp.sum(values, axis=0, keepdims=True)


def zero_first(*refs):
    @pl.when(pl.program_id(0) == 0)
    def _():
        for ref in refs:
            ref[...] = jnp.zeros_like(ref)


def call(
    body, grid, spot, arrays, specs, weights, outs, out_specs, scratch=(), estimate=None, aliases=()
):
    flat = [piece for pieces, _, _ in weights for piece in pieces]
    counts = [len(pieces) for pieces, _, _ in weights]
    n_arrays, n_flat, n_weights = len(arrays), len(flat), len(weights)
    n_outs = len(outs) if isinstance(outs, tuple) else 1

    def kernel(spot_ref, *refs):
        ins = refs[:n_arrays]
        piece_refs = refs[n_arrays : n_arrays + n_flat]
        out_refs = refs[n_arrays + n_flat : n_arrays + n_flat + n_outs]
        rest = refs[n_arrays + n_flat + n_outs :]
        held = rest[:n_weights]
        sems = rest[n_weights : 2 * n_weights]
        extra = rest[2 * n_weights :]
        first = pl.program_id(0) == 0

        def copies(number):
            start = sum(counts[:number])
            found = []
            for index in range(counts[number]):
                place = weights[number][1][index]
                for source, at in place(spot_ref, piece_refs[start + index]):
                    found.append(
                        pltpu.make_async_copy(
                            source, held[number].at[at], sems[number].at[len(found)]
                        )
                    )
            return found

        @pl.when(first)
        def _():
            for number in range(n_weights):
                for copy in copies(number):
                    copy.start()

        def ready(number):
            def wait():
                @pl.when(first)
                def _():
                    for copy in copies(number):
                        copy.wait()

                return held[number]

            return wait

        body(spot_ref, *ins, *[ready(number) for number in range(n_weights)], *out_refs, *extra)

    scratch_shapes = (
        [pltpu.VMEM(shape, BF) for _, _, shape in weights]
        + [pltpu.SemaphoreType.DMA((32,)) for _ in counts]
        + list(scratch)
    )
    return pl.pallas_call(
        kernel,
        out_shape=outs,
        grid_spec=pltpu.PrefetchScalarGridSpec(
            num_scalar_prefetch=1,
            grid=grid,
            in_specs=list(specs) + [any_spec()] * n_flat,
            out_specs=out_specs,
            scratch_shapes=scratch_shapes,
        ),
        compiler_params=params(*(["arbitrary"] * len(grid))),
        cost_estimate=estimate,
        input_output_aliases=dict(aliases),
    )(spot, *arrays, *flat)


def row(width, tile=TILE):
    return pl.BlockSpec((tile, width), lambda i, s: (i, 0))


def fixed(*shape):
    return pl.BlockSpec(shape, lambda *_: (0,) * len(shape))


def shape(dims, dtype):
    return jax.ShapeDtypeStruct(dims, dtype)


def project_qkv(spot, tokens, w_qkv, qkv_bias):
    count, width = tokens.shape
    wide = w_qkv[2][0]

    def body(spot_ref, x_ref, bias_ref, w_ready, out_ref):
        w_ref = w_ready()
        for start in range(0, wide, width):
            part = slice(start, start + width)
            out_ref[:, part] = (dot_nt(x_ref[...], w_ref[part, :]) + bias_ref[:, part]).astype(BF)

    return call(
        body, (count // TILE,), spot, (tokens, qkv_bias), (row(width), fixed(1, wide)), [w_qkv],
        shape((count, wide), BF), row(wide),
        estimate=cost(2 * count * width * wide, 2 * (count * width + wide * width + count * wide)),
    )


def lane_masks():
    lane = lax.broadcasted_iota(jnp.int32, (1, PAIR), 1)
    return [(lane // HD == head) for head in range(2)]


def same_segment(row_ref):
    numbers = row_ref[0].astype(F32)
    column = jnp.broadcast_to(numbers, (128, BLOCK)).T[:, 0:1]
    return column == numbers


def attend_forward(block, qkv, segment_row, into=None):
    count, wide = qkv.shape
    width = wide // 3
    pairs = width // PAIR
    steps = pairs // GROUP
    blocks = count // BLOCK

    def body(q_ref, k_ref, v_ref, row_ref, *refs):
        out_ref, lse_ref = refs[-2:]
        visible = same_segment(row_ref)
        for pair in range(GROUP):
            at = slice(pair * PAIR, (pair + 1) * PAIR)
            query, key = q_ref[:, at] * BF(1.0 / math.sqrt(HD)), k_ref[:, at]
            value_turned = v_ref[:, at].T
            parts = []
            for head, lanes in enumerate(lane_masks()):
                scores = dot_nt(key, jnp.where(lanes, query, BF(0)))
                scores = jnp.where(visible, scores, -1e30)
                highest = jnp.max(scores, axis=0, keepdims=True)
                exponent = jnp.exp(scores - highest)
                total = jnp.sum(exponent, axis=0, keepdims=True)
                part = dot(value_turned[head * HD : (head + 1) * HD], exponent.astype(BF))
                parts.append(part / total)
                lse_ref[0, pair, head : head + 1, :] = highest + jnp.log(total)
            out_ref[:, at] = jnp.concatenate(parts, axis=0).T.astype(BF)

    flops = 4 * HEADS * BLOCK * BLOCK * HD
    given = () if into is None else into
    return pl.pallas_call(
        body,
        out_shape=(shape((count, width), BF), shape((blocks, pairs, 2, BLOCK), F32)),
        grid=(steps,),
        in_specs=[
            pl.BlockSpec((BLOCK, GROUP * PAIR), lambda p: (block, p)),
            pl.BlockSpec((BLOCK, GROUP * PAIR), lambda p: (block, steps + p)),
            pl.BlockSpec((BLOCK, GROUP * PAIR), lambda p: (block, 2 * steps + p)),
            pl.BlockSpec((1, 1, BLOCK), lambda p: (block, 0, 0)),
        ]
        + [any_spec()] * len(given),
        out_specs=(
            pl.BlockSpec((BLOCK, GROUP * PAIR), lambda p: (block, p)),
            pl.BlockSpec((1, GROUP, 2, BLOCK), lambda p: (block, p, 0, 0)),
        ),
        compiler_params=params("arbitrary"),
        cost_estimate=cost(4 * flops, 4 * count * width, HEADS * BLOCK * BLOCK),
        input_output_aliases={4 + index: index for index in range(len(given))},
    )(qkv, qkv, qkv, segment_row, *given)


def attend_backward(block, qkv, segment_row, lse, context, d_context, sums, into=None):
    count, wide = qkv.shape
    width = wide // 3
    pairs = width // PAIR
    steps = pairs // GROUP
    factor = 1.0 / math.sqrt(HD)

    def body(q_ref, k_ref, v_ref, o_ref, do_ref, row_ref, lse_ref, given_ref, *refs):
        dq_ref, dk_ref, dv_ref, sums_ref = refs[-4:]

        @pl.when(pl.program_id(0) == 0)
        def _():
            sums_ref[...] = given_ref[...]

        visible = same_segment(row_ref)
        masks = lane_masks()
        for pair in range(GROUP):
            at = slice(pair * PAIR, (pair + 1) * PAIR)
            query, key, value = q_ref[:, at] * BF(factor), k_ref[:, at], v_ref[:, at]
            d_out = do_ref[:, at]
            key_turned = key.T
            product = (d_out.astype(F32) * o_ref[:, at].astype(F32)).T
            d_query, d_key, d_value = [], [], []
            for head, lanes in enumerate(masks):
                inside = slice(head * HD, (head + 1) * HD)
                delta = jnp.sum(product[inside], axis=0, keepdims=True)
                scores = dot_nt(key, jnp.where(lanes, query, BF(0)))
                scores -= lse_ref[0, pair, head : head + 1, :]
                prob = jnp.exp(jnp.where(visible, scores, -1e30))
                d_prob = dot_nt(value, jnp.where(lanes, d_out, BF(0)))
                d_score = (prob * (d_prob - delta)).astype(BF)
                d_value.append(dot(prob.astype(BF), d_out))
                d_key.append(dot(d_score, query))
                d_query.append(dot(key_turned[inside], d_score) * factor)
            dq = jnp.concatenate(d_query, axis=0).T.astype(BF)
            dk = jnp.where(masks[0], d_key[0], d_key[1]).astype(BF)
            dv = jnp.where(masks[0], d_value[0], d_value[1]).astype(BF)
            dq_ref[:, at] = dq
            dk_ref[:, at] = dk
            dv_ref[:, at] = dv
            lane = (pl.program_id(0) * GROUP + pair) * PAIR
            here = pl.ds(pl.multiple_of(lane, PAIR), PAIR)
            add_rows(sums_ref.at[QUERY_SUM : QUERY_SUM + 1, here], dq.astype(F32))
            add_rows(sums_ref.at[QUERY_SUM + 1 : QUERY_SUM + 2, here], dv.astype(F32))

    tile = pl.BlockSpec((BLOCK, GROUP * PAIR), lambda p: (block, p))
    flops = 10 * HEADS * BLOCK * BLOCK * HD
    given = () if into is None else into
    return pl.pallas_call(
        body,
        out_shape=(shape((count, width), BF),) * 3 + (shape((24, width), F32),),
        grid=(steps,),
        in_specs=[
            tile,
            pl.BlockSpec((BLOCK, GROUP * PAIR), lambda p: (block, steps + p)),
            pl.BlockSpec((BLOCK, GROUP * PAIR), lambda p: (block, 2 * steps + p)),
            tile,
            tile,
            pl.BlockSpec((1, 1, BLOCK), lambda p: (block, 0, 0)),
            pl.BlockSpec((1, GROUP, 2, BLOCK), lambda p: (block, p, 0, 0)),
            fixed(24, width),
        ]
        + [any_spec()] * len(given),
        out_specs=(tile,) * 3 + (fixed(24, width),),
        compiler_params=params("arbitrary"),
        cost_estimate=cost(4 * flops, 8 * count * width, HEADS * BLOCK * BLOCK),
        input_output_aliases={8 + index: index for index in range(len(given))},
    )(qkv, qkv, qkv, context, d_context, segment_row, lse, sums, *given)


def emit(plan, step, held, spot_ref, out_refs, sems):
    tile, blocks, (rows, cols), _, base = plan
    if blocks is None:
        target = out_refs[0].at[:, pl.ds(pl.multiple_of(step * tile, tile), tile)]
        pltpu.make_async_copy(held.at[step], target, sems.at[step]).start()
        return
    listed = blocks(step)
    for index, (row_at, column_at, x, core, z, y) in enumerate(listed):
        source = held.at[step, pl.ds(row_at, rows), pl.ds(column_at, cols)]
        sem = sems.at[step * len(listed) + index]
        far_x, far_y = x ^ spot_ref[0], y ^ spot_ref[3]
        first = far_x + core * (far_y - far_x)
        depth = z ^ spot_ref[2]
        slot = (depth & 1) + 2 * first + 4 * (far_x + far_y - first) + 8 * (depth >> 1)
        mine = (core ^ spot_ref[1]) == 0

        @pl.when(mine)
        def _():
            pltpu.make_async_copy(source, out_refs[0].at[slot, pl.ds(base, rows)], sem).start()

        @pl.when(jnp.logical_not(mine))
        def _():
            pltpu.make_async_copy(source, out_refs[1].at[slot, pl.ds(base, rows)], sem).start()


def emitted(plan, steps, held, out_refs, sems):
    tile, blocks, (rows, cols), _, base = plan
    if blocks is None:
        for step in range(steps):
            target = out_refs[0].at[:, pl.ds(step * tile, tile)]
            pltpu.make_async_copy(held.at[step], target, sems.at[step]).wait()
        return
    for index in range(32):
        source = held.at[0, pl.ds(0, rows), pl.ds(0, cols)]
        pltpu.make_async_copy(source, out_refs[0].at[0, pl.ds(base, rows)], sems.at[index]).wait()


def emit_shapes(plan, total, columns):
    _, blocks, (rows, cols), slot_rows, _ = plan
    if blocks is None:
        return (shape((total, columns), BF),)
    return (shape((16, slot_rows, cols), BF),) * 2


def clamped(width, last, tile=TILE):
    return pl.BlockSpec((tile, width), lambda i, s: (jnp.minimum(i, last), 0))


def project_out(spot, context, tokens, w_out, biases, gains):
    count, width = tokens.shape

    def body(spot_ref, c_ref, x_ref, bias_ref, gain_ref, w_ready, normal_ref, inverse_ref, low_ref):
        w_ref = w_ready()
        resid = x_ref[...].astype(F32) + (dot_nt(c_ref[...], w_ref[...]) + bias_ref[2:3])
        normal, inverse = layer_norm_parts(resid)
        normal_ref[...] = normal
        inverse_ref[...] = jnp.broadcast_to(inverse, inverse_ref.shape)
        low_ref[...] = (normal * gain_ref[0:1] + bias_ref[3:4]).astype(BF)

    return call(
        body, (count // TILE,), spot, (context, tokens, biases, gains),
        (row(width), row(width), fixed(*biases.shape), fixed(*gains.shape)), [w_out],
        (shape((count, width), F32), shape((count, 128), F32), shape((count, width), BF)),
        (row(width), row(128), row(width)),
        estimate=cost(2 * count * width * width, 10 * count * width),
    )


def ffn_in(spot, normed_low, w_in, in_bias):
    count, width = normed_low.shape
    wide = w_in[2][1]

    def body(spot_ref, x_ref, bias_ref, w_ready, hidden_ref, slope_ref):
        w_ref = w_ready()
        for start in range(0, wide, width):
            part = slice(start, start + width)
            pre = dot(x_ref[...], w_ref[:, part]) + bias_ref[:, part]
            cdf = 0.5 + 0.5 * lax.erf(pre * (1.0 / math.sqrt(2.0)))
            hidden_ref[:, part] = (pre * cdf).astype(BF)
            density = jnp.exp(pre * pre * -0.5) * (1.0 / math.sqrt(2.0 * math.pi))
            slope_ref[:, part] = (cdf + pre * density).astype(BF)

    return call(
        body, (count // TILE,), spot, (normed_low, in_bias), (row(width), fixed(1, wide)), [w_in],
        (shape((count, wide), BF),) * 2, (row(wide),) * 2,
        estimate=cost(2 * count * width * wide, 4 * count * wide, 2 * count * wide),
    )


def forward_rows(spot, hidden, normal_one, out_grad, w_back, biases, gains, plan):
    count, width = out_grad.shape
    wide = hidden.shape[1]
    steps = count // TILE
    tile = plan[0]
    columns = wide // tile
    shapes = emit_shapes(plan, width, wide)

    def body(spot_ref, h_ref, column_ref, n_ref, g_ref, bias_ref, gain_ref, wb_ready,
             out_ref, d_two_ref, d_low_ref, sums_ref, *refs):
        grads, (d_rows, turned, held, sems) = refs[: len(shapes)], refs[len(shapes) :]
        index = pl.program_id(0)
        zero_first(sums_ref)

        @pl.when(index < steps)
        def _():
            here = pl.ds(pl.multiple_of(index * TILE, TILE), TILE)
            resid = n_ref[...] * gain_ref[0:1] + bias_ref[3:4]
            w_ref = wb_ready()
            resid += dot_nt(h_ref[...], w_ref[...]) + bias_ref[4:5]
            normal, inverse = layer_norm_parts(resid)
            out_ref[...] = (normal * gain_ref[1:2] + bias_ref[5:6]).astype(BF)
            grad = g_ref[...].astype(F32)
            d_two = layer_norm_back(grad * gain_ref[1:2], normal, inverse)
            d_low = d_two.astype(BF)
            d_two_ref[...] = d_two
            d_low_ref[...] = d_low
            d_rows[here, :] = d_low
            add_rows(sums_ref.at[0:1], grad * normal)
            add_rows(sums_ref.at[1:2], grad)
            add_rows(sums_ref.at[2:3], d_low.astype(F32))

        @pl.when(index == steps)
        def _():
            turned[...] = d_rows[...].T

        @pl.when(index >= steps)
        def _():
            column = index - steps
            held[column] = dot(turned[...], column_ref[...]).astype(BF)
            emit(plan, column, held, spot_ref, grads, sems)

        @pl.when(index == steps + columns - 1)
        def _():
            emitted(plan, columns, held, grads, sems)

    last = steps - 1
    rows = lambda wide_: clamped(wide_, last)
    return call(
        body, (steps + columns,), spot, (hidden, hidden, normal_one, out_grad, biases, gains),
        (rows(wide), pl.BlockSpec((count, tile), lambda i, s: (0, jnp.maximum(i - steps, 0))),
         rows(width), rows(width), fixed(*biases.shape), fixed(*gains.shape)),
        [w_back],
        (shape((count, width), BF), shape((count, width), F32), shape((count, width), BF),
         shape((8, width), F32), *shapes),
        (rows(width), rows(width), rows(width), fixed(8, width), *[any_spec()] * len(shapes)),
        [pltpu.VMEM((count, width), BF),
         pltpu.VMEM((width, count), BF), pltpu.VMEM((columns, width, tile), BF),
         pltpu.SemaphoreType.DMA((32,))],
        cost(4 * count * width * wide, 14 * count * width + 4 * count * wide),
    )


def backward_rows(
    spot, d_low, slope, d_two, normal_one, inverse_one, normed_low, context, sums_two, w_back, w_in,
    w_out, gains, plan_in, plan_out,
):
    count, width = d_two.shape
    wide = slope.shape[1]
    steps = count // TILE
    tile_in, tile_out = plan_in[0], plan_out[0]
    columns_in, columns_out = wide // tile_in, width // tile_out
    shared = plan_in[1] is not None
    shapes = emit_shapes(plan_in, width, wide)
    if not shared:
        shapes += emit_shapes(plan_out, width, width)

    def body(spot_ref, dl_ref, s_ref, d2_ref, n_ref, i_ref, low_ref, c_ref, two_ref, gain_ref,
             wb_ready, wi_ready, wo_ready, d_one_ref, d_context_ref, sums_ref, *refs):
        grads = refs[: len(shapes)]
        d_pre, d_attn, turned, held_in, held_out, low_held, sems_in, sems_out, late = refs[
            len(shapes) :
        ]
        fetch_low = pltpu.make_async_copy(low_ref, low_held, late.at[0])
        grads_in, grads_out = (grads, grads) if shared else (grads[:1], grads[1:])
        index = pl.program_id(0)

        @pl.when(index == 0)
        def _():
            sums_ref[...] = jnp.zeros_like(sums_ref)
            sums_ref[0:8, :] = two_ref[...]
            fetch_low.start()

        @pl.when(index < steps)
        def _():
            here = pl.ds(pl.multiple_of(index * TILE, TILE), TILE)
            w_ref = wb_ready()
            pieces = []
            for start in range(0, wide, width):
                part = slice(start, start + width)
                d_hidden = dot(dl_ref[...], w_ref[:, part])
                piece = (d_hidden * s_ref[:, part].astype(F32)).astype(BF)
                d_pre[here, part] = piece
                pieces.append(piece)
                at = HIDDEN_SUM + start // width
                add_rows(sums_ref.at[at : at + 1], piece.astype(F32))
            w_ref = wi_ready()
            d_normed = d2_ref[...]
            for number, piece in enumerate(pieces):
                d_normed += dot_nt(piece, w_ref[:, number * width : (number + 1) * width])
            normal = n_ref[...]
            d_one = layer_norm_back(d_normed * gain_ref[0:1], normal, i_ref[:, 0:1])
            low = d_one.astype(BF)
            d_one_ref[...] = d_one
            d_attn[here, :] = low
            d_context_ref[...] = dot(low, wo_ready()[...]).astype(BF)
            add_rows(sums_ref.at[8:9], d_normed * normal)
            add_rows(sums_ref.at[9:10], d_normed)
            add_rows(sums_ref.at[10:11], low.astype(F32))

        @pl.when(index == steps)
        def _():
            fetch_low.wait()
            turned[...] = low_held[...].T

        @pl.when(jnp.logical_and(index >= steps, index < steps + columns_in))
        def _():
            column = index - steps
            at = pl.ds(pl.multiple_of(column * tile_in, tile_in), tile_in)
            held_in[column] = dot(turned[...], d_pre[:, at]).astype(BF)
            emit(plan_in, column, held_in, spot_ref, grads_in, sems_in)

        @pl.when(index == steps + columns_in)
        def _():
            turned[...] = d_attn[...].T

        @pl.when(index >= steps + columns_in)
        def _():
            column = index - steps - columns_in
            held_out[column] = dot(turned[...], c_ref[...]).astype(BF)
            emit(plan_out, column, held_out, spot_ref, grads_out, sems_out)

        @pl.when(index == steps + columns_in + columns_out - 1)
        def _():
            emitted(plan_in, columns_in, held_in, grads_in, sems_in)
            emitted(plan_out, columns_out, held_out, grads_out, sems_out)

    last, before = steps - 1, steps + columns_in
    rows = lambda wide_: clamped(wide_, last)
    return call(
        body, (steps + columns_in + columns_out,), spot,
        (d_low, slope, d_two, normal_one, inverse_one, normed_low, context, sums_two, gains),
        (rows(width), rows(wide), rows(width), rows(width), rows(128), any_spec(),
         pl.BlockSpec((count, tile_out), lambda i, s: (0, jnp.maximum(i - before, 0))),
         fixed(8, width), fixed(*gains.shape)),
        [w_back, w_in, w_out],
        (shape((count, width), F32), shape((count, width), BF), shape((24, width), F32), *shapes),
        (rows(width), rows(width), fixed(24, width), *[any_spec()] * len(shapes)),
        [pltpu.VMEM((count, wide), BF), pltpu.VMEM((count, width), BF),
         pltpu.VMEM((width, count), BF), pltpu.VMEM((columns_in, width, tile_in), BF),
         pltpu.VMEM((columns_out, width, tile_out), BF), pltpu.VMEM((count, width), BF),
         pltpu.SemaphoreType.DMA((32,)), pltpu.SemaphoreType.DMA((32,)),
         pltpu.SemaphoreType.DMA((1,))],
        cost(2 * count * width * (3 * wide + 2 * width), 18 * count * width + 2 * count * wide),
    )


def tokens_backward(spot, d_one, d_query, d_key, d_value, w_qkv):
    count, width = d_one.shape

    def body(spot_ref, d1_ref, q_ref, k_ref, v_ref, w_ready, out_ref):
        w_ref = w_ready()
        total = d1_ref[...] + dot(q_ref[...], w_ref[0:width, :])
        total += dot(k_ref[...], w_ref[width : 2 * width, :])
        total += dot(v_ref[...], w_ref[2 * width : 3 * width, :])
        out_ref[...] = total.astype(BF)

    return call(
        body, (count // TILE,), spot, (d_one, d_query, d_key, d_value), (row(width),) * 4, [w_qkv],
        shape((count, width), BF), row(width),
        estimate=cost(6 * count * width * width, 12 * count * width),
    )


def gradient(spot, lefts, right, plan):
    count, columns = right.shape
    width = lefts[0].shape[1]
    total = width * len(lefts)
    tile = plan[0]
    steps = columns // tile
    n_left = len(lefts)
    shapes = emit_shapes(plan, total, columns)

    def body(spot_ref, *refs):
        left_refs, right_ref = refs[:n_left], refs[n_left]
        grads = refs[n_left + 1 : n_left + 1 + len(shapes)]
        turned, held, sems = refs[-3:]
        step = pl.program_id(0)

        @pl.when(step == 0)
        def _():
            for index, ref in enumerate(left_refs):
                turned[index * width : (index + 1) * width, :] = ref[...].T

        for index in range(n_left):
            part = slice(index * width, (index + 1) * width)
            held[step, part, :] = dot(turned[part, :], right_ref[...]).astype(BF)
        emit(plan, step, held, spot_ref, grads, sems)

        @pl.when(step == steps - 1)
        def _():
            emitted(plan, steps, held, grads, sems)

    return call(
        body, (steps,), spot, (*lefts, right),
        (*[fixed(count, width)] * n_left, pl.BlockSpec((count, tile), lambda i, s: (0, i))), [],
        shapes, (any_spec(),) * len(shapes),
        [pltpu.VMEM((total, count), BF), pltpu.VMEM((steps, total, tile), BF),
         pltpu.SemaphoreType.DMA((32,))],
        cost(2 * count * total * columns, 2 * (count * (total + columns) + total * columns)),
    )


def widen(value):
    return value.astype(F32)


def exchange(value, stage):
    axes = ("x", "core", "z", "y")
    pairs = []
    for source in range(32):
        x, core, z, y = source >> 4, (source >> 3) & 1, (source >> 1) & 3, source & 1
        if stage in (Z1, Z2, Z3):
            z ^= {Z1: 1, Z2: 2, Z3: 3}[stage]
        elif stage == CORE:
            core ^= 1
        elif (stage == FIRST) == (core == 0):
            x ^= 1
        else:
            y ^= 1
        pairs.append((source, 16 * x + 8 * core + 2 * z + y))
    return lax.ppermute(value, axes, pairs)


class Parcel:
    def __init__(self, array, origins=((0, 0, 0, 0),)):
        self.array = array
        self.origins = tuple(origins)

    def moved(self, stage):
        def change(origin):
            core, second, first, depth = origin
            along_first = stage == (SECOND if core else FIRST)
            along_second = stage == (FIRST if core else SECOND)
            return (
                core ^ (stage == CORE),
                second ^ along_second,
                first ^ along_first,
                depth ^ {Z1: 1, Z2: 2}.get(stage, 0),
            )

        return Parcel(exchange(self.array, stage), [change(origin) for origin in self.origins])

    def __add__(self, other):
        return Parcel(jnp.concatenate([self.array, other.array]), self.origins + other.origins)


def sync(values, *parcels):
    values, arrays = lax.optimization_barrier((values, [parcel.array for parcel in parcels]))
    for parcel, array in zip(parcels, arrays):
        parcel.array = array
    return values


class Reduce:
    def __init__(self, near, far):
        self.near, self.far = near, Parcel(far)

    def send_core(self):
        self.core = Parcel(exchange(self.far.array, CORE))

    def sum(self, start, stop, *others):
        total = widen(self.near[start:stop]) + widen(self.core.array[start:stop])
        for parcel, at in others:
            total += widen(parcel.array[at : at + stop - start])
        return total

    def send(self, stage, start, stop, *others):
        return Parcel(exchange(self.sum(start, stop, *others).astype(BF), stage))

    def send_second_b(self):
        self.second_b = self.send(SECOND, 12, 16)

    def send_second_a(self):
        self.second_a = self.send(SECOND, 4, 8)

    def send_first_b(self):
        self.first_b = self.send(FIRST, 10, 12, (self.second_b, 2))

    def send_first_a(self):
        self.first_a = self.send(FIRST, 2, 4, (self.second_a, 2))

    def send_z2(self):
        self.z2 = self.send(Z2, 8, 10, (self.second_b, 0), (self.first_b, 0))

    def send_z1(self):
        self.z1 = self.send(Z1, 1, 2, (self.second_a, 1), (self.first_a, 1), (self.z2, 1))
        self.last = (self.z2, self.z1)

    def send_direct_b(self):
        self.z2 = self.send(Z2, 8, 9, (self.second_b, 0), (self.first_b, 0))
        self.z3 = self.send(Z3, 9, 10, (self.second_b, 1), (self.first_b, 1))

    def send_direct_a(self):
        self.z1 = self.send(Z1, 1, 2, (self.second_a, 1), (self.first_a, 1))
        self.last = (self.z1, self.z2, self.z3)

    def result(self):
        others = (self.second_a, self.first_a) + self.last
        return self.sum(0, 1, *[(parcel, 0) for parcel in others])[0]


def source_of(spot, origin):
    away, second, first, depth = origin
    core = spot[1] ^ away
    x = spot[0] ^ (first + core * (second - first))
    y = spot[3] ^ (second + core * (first - second))
    return core, x, 2 * (spot[2] ^ depth) + y


def weight_of(parcels, source_rows, place, dims):
    start, rows, cols = source_rows
    pieces, places = [], []
    for parcel in parcels:
        pieces.append(parcel.array)

        def at(spot_ref, ref, origins=parcel.origins):
            for index, origin in enumerate(origins):
                core, x, f = source_of(spot_ref, origin)
                row_at, column_at = place(x, core, f)
                yield (
                    ref.at[index, pl.ds(start, rows), :],
                    (
                        pl.ds(pl.multiple_of(row_at, 16), rows),
                        pl.ds(pl.multiple_of(column_at, 128), cols),
                    ),
                )

        places.append(at)
    return pieces, places, dims


def whole_weight(array):
    def at(spot_ref, ref):
        yield ref, (pl.ds(0, array.shape[0]), pl.ds(0, array.shape[1]))

    return [array], [at], array.shape


def device_slots(spot, origins):
    device = lax.broadcasted_iota(jnp.int32, (len(origins), len(origins)), 0)
    owners = []
    for origin in origins:
        core, x, f = source_of(spot, origin)
        owners.append(16 * x + 8 * core + f)
    return (device == jnp.stack(owners)[None, :]).astype(F32)


def small_vectors(every, shards):
    biases, in_bias, gains = shards
    devices = every.shape[0]
    first, second = biases.size, biases.size + in_bias.size
    third = second + gains.size
    return (
        every[:, :first].reshape(devices, 6, -1).transpose(1, 0, 2).reshape(6, -1),
        every[:, first:second].reshape(1, -1),
        every[:, second:third].reshape(devices, 2, -1).transpose(1, 0, 2).reshape(2, -1),
    )


def on_device(sizes, tokens, segment_ids, w_qkv, w_out, w_in, w_back, biases, in_bias, gains, out_grad):
    axes = ("x", "core", "z", "y")
    dp_axes, fsdp_axes = ("x", "core"), ("z", "y")
    devices = math.prod(sizes)
    by_permute = sizes == (2, 2, 4, 2)
    count, width = tokens.shape
    wide = w_back.shape[0] * sizes[0] * sizes[1]
    blocks = range(count // BLOCK)
    spot = jnp.stack([lax.axis_index(axis) for axis in axes]).astype(jnp.int32)
    core = spot[1]
    shards = (biases, in_bias, gains)
    segment_row = segment_ids.reshape(count // BLOCK, 1, BLOCK)

    qkv_cols, out_cols = w_qkv.shape[1], w_out.shape[1]
    pair_cols = 2 * w_qkv.shape[0]
    in_rows, in_cols = w_in.shape
    back_rows, back_cols = w_back.shape
    half_q, half_o = qkv_cols // 2, out_cols // 2

    if by_permute:

        def paired(turned):
            half = turned.shape[0] // 2
            first, second = turned[:half], turned[half:]
            mine = jnp.where(core == 0, first, second)
            other = exchange(jnp.where(core == 0, second, first), CORE)
            return jnp.where(
                core == 0,
                jnp.concatenate([mine, other], axis=1),
                jnp.concatenate([other, mine], axis=1),
            )

        to_qkv = Parcel(paired(w_qkv.T)[None])
        qkv_z1 = to_qkv.moved(Z1)
        own_vectors, w_in = sync(((biases, in_bias, gains), w_in), to_qkv)
        own_small = jnp.concatenate([part.reshape(-1) for part in own_vectors])
        to_small = Parcel(jnp.pad(own_small, (0, 1024 - own_small.size)).reshape(1, 8, 128))
        to_small += to_small.moved(CORE)
        w_in, w_out, w_back = sync((w_in, w_out, w_back), qkv_z1, to_small)
        qkv_near = to_qkv + qkv_z1
        qkv_z2 = qkv_near.moved(Z2)
        qkv_first_a = qkv_near.moved(FIRST)
        to_small += to_small.moved(FIRST)
        to_in = Parcel(jnp.concatenate([w_in, paired(w_out.T)], axis=0)[None])
        to_back = Parcel(w_back.T[None])
        sync((), qkv_first_a, to_small, to_in)
        qkv_a = qkv_near + qkv_first_a
        qkv_second_a = qkv_a.moved(SECOND)
        in_z1 = to_in.moved(Z1)
        to_small += to_small.moved(SECOND)
        sync((), qkv_z2)
        qkv_first_b = qkv_z2.moved(FIRST)
        sync((), qkv_z2, to_small)
        to_small += to_small.moved(Z1)
        sync((), qkv_first_b, to_small)
        qkv_b = qkv_z2 + qkv_first_b
        qkv_second_b = qkv_b.moved(SECOND)
        to_small += to_small.moved(Z2)
        sync((), qkv_first_b, qkv_second_a, to_small, in_z1)
        qkv_core_a = qkv_a.moved(CORE), qkv_second_a.moved(CORE)
        in_near = to_in + in_z1
        in_z2 = in_near.moved(Z2)
        sync((), qkv_second_b, in_near, to_back)
        qkv_core_b = qkv_b.moved(CORE), qkv_second_b.moved(CORE)
        in_first_a = in_near.moved(FIRST)
        back_z1 = to_back.moved(Z1)
        tokens = sync(tokens, *qkv_core_a, *qkv_core_b)
        qkv_parcels = (
            qkv_a, qkv_second_a, qkv_b, qkv_second_b, *qkv_core_a, *qkv_core_b
        )
        qkv_weight = weight_of(
            qkv_parcels, (0, half_q, pair_cols),
            lambda x, c, f: (f * qkv_cols + c * half_q, x * pair_cols), (3 * width, width),
        )
        slots = device_slots(spot, to_small.origins)
        arrived = widen(to_small.array).reshape(32, 1024)
        every = jnp.dot(slots, arrived, precision=lax.Precision.HIGHEST)

        def back_blocks(index):
            return [(f * back_cols, 0, index >> 1, index & 1, f >> 1, f & 1) for f in range(8)]

        def in_blocks(index):
            return [
                ((2 * x + c) * in_rows, y * in_cols, x, c, index, y)
                for x in range(2) for c in range(2) for y in range(2)
            ]

        def out_blocks(index):
            return [
                (f * out_cols + c * half_o, 0, index, c, f >> 1, f & 1)
                for f in range(8) for c in range(2)
            ]

        def qkv_blocks(index):
            return [
                (f * qkv_cols + c * half_q, 0, index, c, f >> 1, f & 1)
                for f in range(8) for c in range(2)
            ]

        plans = {
            "back": (back_rows, back_blocks, (back_cols, back_rows), back_cols, 0),
            "in": (2 * in_cols, in_blocks, (in_rows, in_cols), in_rows + half_o, 0),
            "out": (pair_cols, out_blocks, (half_o, pair_cols), in_rows + half_o, in_rows),
            "qkv": (pair_cols, qkv_blocks, (half_q, pair_cols), half_q, 0),
        }
    else:

        def full(shard):
            return lax.all_gather(
                lax.all_gather(shard, fsdp_axes, axis=1, tiled=True), dp_axes, axis=0, tiled=True
            )

        qkv_weight = whole_weight(full(w_qkv).T)
        out_weight = whole_weight(full(w_out).T)
        in_weight = whole_weight(full(w_in))
        back_weight = whole_weight(full(w_back).T)
        own_small = jnp.concatenate([biases.reshape(-1), in_bias, gains.reshape(-1)])
        every = widen(lax.all_gather(own_small, axes, axis=0, tiled=False))
        plans = {name: (width // 2, None, (0, 0), 0, 0) for name in ("back", "in", "out", "qkv")}

    bias_values, hidden_bias, gain_values = small_vectors(every, shards)
    qkv_bias = jnp.concatenate(
        [bias_values[0:1], jnp.zeros((1, width), F32), bias_values[1:2]], axis=1
    )

    qkv = project_qkv(spot, tokens, qkv_weight, qkv_bias)
    if by_permute:
        qkv = sync(qkv, in_first_a, in_z2, back_z1)
        in_a = in_near + in_first_a
        in_second_a = in_a.moved(SECOND)
        in_first_b = in_z2.moved(FIRST)
        back_near = to_back + back_z1
        back_z2 = back_near.moved(Z2)
    attended = None
    for block in blocks:
        attended = attend_forward(block, qkv, segment_row, attended)
        if by_permute and block == 0:
            attended = sync(attended, in_second_a, in_first_b, back_z2)
            in_b = in_z2 + in_first_b
            in_second_b = in_b.moved(SECOND)
            in_core = in_a.moved(CORE), in_second_a.moved(CORE), in_b.moved(CORE)
            back_first_a = back_near.moved(FIRST)
    context, lse = attended
    if by_permute:
        context = sync(context, in_second_b, *in_core, back_first_a)
        in_cross = in_second_b.moved(CORE)
        back_a = back_near + back_first_a
        back_second_a = back_a.moved(SECOND)
        back_first_b = back_z2.moved(FIRST)
        context = sync(context, in_cross)
        in_parcels = (in_a, in_second_a, in_b, in_second_b, *in_core, in_cross)
        in_weight = weight_of(
            in_parcels, (0, in_rows, in_cols),
            lambda x, c, f: ((2 * x + c) * in_rows, f * in_cols), (width, wide),
        )
        out_weight = weight_of(
            in_parcels, (in_rows, half_o, pair_cols),
            lambda x, c, f: (f * out_cols + c * half_o, x * pair_cols), (width, width),
        )
    normal_one, inverse_one, normed_low = project_out(
        spot, context, tokens, out_weight, bias_values, gain_values
    )
    if by_permute:
        normed_low = sync(normed_low, back_second_a, back_first_b)
        back_b = back_z2 + back_first_b
        back_second_b = back_b.moved(SECOND)
        back_core = back_a.moved(CORE), back_second_a.moved(CORE), back_b.moved(CORE)
    hidden, slope = ffn_in(spot, normed_low, in_weight, hidden_bias)
    if by_permute:
        hidden = sync(hidden, back_second_b, *back_core)
        back_cross = back_second_b.moved(CORE)
        back_weight = weight_of(
            (back_a, back_second_a, back_b, back_second_b, *back_core, back_cross),
            (0, back_cols, back_rows),
            lambda x, c, f: (f * back_cols, (2 * x + c) * back_rows), (width, wide),
        )
    layer_out, d_two, d_low, sums_two, *grad_back = forward_rows(
        spot, hidden, normal_one, out_grad, back_weight, bias_values, gain_values, plans["back"]
    )
    if by_permute:
        from_back = Reduce(*grad_back)
        d_low = sync(d_low, from_back.far)
        from_back.send_core()
    d_one, d_context, small, *grads_in = backward_rows(
        spot, d_low, slope, d_two, normal_one, inverse_one, normed_low, context, sums_two,
        back_weight, in_weight, out_weight, gain_values, plans["in"], plans["out"],
    )
    if by_permute:
        from_in = Reduce(*grads_in)
        d_context = sync(d_context, from_back.core, from_in.far)
        from_back.send_second_b()
        from_back.send_second_a()
        from_in.send_core()
    else:
        grad_in, grad_out = grads_in
        grad_back, = grad_back
    attended = None
    for block in blocks:
        *attended, small = attend_backward(
            block, qkv, segment_row, lse, context, d_context, small, attended
        )
        if by_permute and block == 0:
            attended = sync(attended, from_back.second_a, from_back.second_b, from_in.core)
            from_back.send_first_b()
            from_back.send_first_a()
            from_in.send_second_b()
        elif by_permute:
            attended, small = sync(
                (attended, small), from_back.first_a, from_back.first_b, from_in.second_b
            )
            from_in.send_second_a()
            from_in.send_first_b()
            from_back.send_z2()
            small_sent = Parcel(small).moved(CORE)
    grad_qkv = gradient(spot, attended, tokens, plans["qkv"])
    if by_permute:
        from_qkv = Reduce(*grad_qkv)
        small = sync(small, from_qkv.far, small_sent, from_in.second_a, from_in.first_b)
        from_qkv.send_core()
        small = small + small_sent.array
        small_sent = Parcel(small).moved(Z1)
        from_in.send_z2()
        d_one = sync(d_one, from_qkv.core)
        from_qkv.send_second_b()
        from_qkv.send_second_a()
    else:
        grad_qkv, = grad_qkv
    tokens_grad = tokens_backward(spot, d_one, *attended, qkv_weight)

    if by_permute:

        def unpaired(sums):
            half = sums.shape[1] // 2
            left, right = sums[:, :half], sums[:, half:]
            mine = jnp.where(core == 0, left, right)
            other = widen(exchange(jnp.where(core == 0, right, left).astype(BF), CORE))
            return jnp.where(
                core == 0,
                jnp.concatenate([mine, other], axis=0),
                jnp.concatenate([other, mine], axis=0),
            )

        tokens_grad, small = sync(
            (tokens_grad, small), from_qkv.second_b, from_qkv.second_a, small_sent, from_back.z2
        )
        from_qkv.send_first_b()
        from_qkv.send_first_a()
        from_in.send_first_a()
        from_back.send_z1()
        small = small + small_sent.array
        small_sent = Parcel(small).moved(SECOND)
        sync((), from_qkv.first_b)
        from_qkv.send_direct_b()
        small = sync(small, from_qkv.first_a)
        from_qkv.send_direct_a()
        small = sync(small, small_sent, from_in.first_a, from_in.z2)
        from_in.send_z1()
        small = small + small_sent.array
        small_sent = Parcel(small).moved(FIRST)
        small = sync(small, small_sent, from_back.z1)
        small = small + small_sent.array
        small_sent = Parcel(small).moved(Z2)
        small = sync(small, small_sent, from_in.z1)
        small = small + small_sent.array
        sums_in = from_in.result()
        own_back = from_back.result().T
        own_in = sums_in[:in_rows]
        own_out = unpaired(sums_in[in_rows:]).T
        own_qkv = unpaired(from_qkv.result()).T
    else:

        def scattered(total):
            part = lax.psum_scatter(total, dp_axes, scatter_dimension=0, tiled=True)
            part = lax.psum_scatter(part, fsdp_axes, scatter_dimension=1, tiled=True)
            return widen(part)

        own_back = scattered(grad_back.T)
        own_in = scattered(grad_in)
        own_out = scattered(grad_out.T)
        own_qkv = scattered(grad_qkv.T)
        small = lax.psum(small, axes)
    device = lax.axis_index(axes)
    queries = small[QUERY_SUM : QUERY_SUM + 2]
    bias_total = jnp.concatenate([queries, small[10:11], small[9:10], small[2:3], small[1:2]])
    gain_total = jnp.concatenate([small[8:9], small[0:1]])
    own_bias = lax.dynamic_slice_in_dim(bias_total, device * biases.shape[1], biases.shape[1], 1)
    own_gain = lax.dynamic_slice_in_dim(gain_total, device * gains.shape[1], gains.shape[1], 1)
    own_hidden = lax.dynamic_slice_in_dim(
        small[HIDDEN_SUM:QUERY_SUM].reshape(-1), device * in_bias.shape[0], in_bias.shape[0], 0
    )
    return (
        layer_out, tokens_grad, own_qkv, own_out, own_in, own_back, own_bias, own_hidden, own_gain,
    )


def solution(mesh):
    dp, fsdp = mesh.devices.shape
    sizes = (dp // 2, 2, fsdp // 2, 2)
    split = Mesh(mesh.devices.reshape(sizes), ("x", "core", "z", "y"))
    outer, inner = ("x", "core"), ("z", "y")
    every = outer + inner
    rows = P(every, None)
    weight = P(outer, inner)
    vectors = P(None, every)

    def placed(*arrays):
        return on_device(sizes, *arrays)

    return jax.shard_map(
        placed,
        mesh=split,
        in_specs=(rows, rows, weight, weight, weight, weight, vectors, P(every), vectors, rows),
        out_specs=(rows, rows, weight, weight, weight, weight, vectors, P(every), vectors),
        check_vma=False,
    )
```

```python
import math

import jax
import jax.numpy as jnp
from jax import lax
from jax.experimental import pallas as pl
from jax.experimental.pallas import tpu as pltpu
from jax.sharding import Mesh, PartitionSpec as P

HEADS = 12
HD = 64
BLOCK = 512
PAIR = 2 * HD
GROUP = 2
TILE = 256
VMEM = 58 * 1024 * 1024
BF = jnp.bfloat16
F32 = jnp.float32
Z1, Z2, FIRST, SECOND, CORE, Z3 = range(6)
HIDDEN_SUM, QUERY_SUM = 16, 20
NT = (((1,), (1,)), ((), ()))


def dot(a, b):
    return jnp.dot(a, b, preferred_element_type=F32)


def dot_nt(a, b):
    return lax.dot_general(a, b, NT, preferred_element_type=F32)


def any_spec():
    return pl.BlockSpec(memory_space=pl.ANY)


def params(*semantics):
    return pltpu.CompilerParams(
        dimension_semantics=semantics if semantics else None, vmem_limit_bytes=VMEM
    )


def cost(flops, nbytes, trans=0):
    return pl.CostEstimate(flops=flops, bytes_accessed=nbytes, transcendentals=trans)

def layer_norm_parts(rows):
    center = jnp.mean(rows, axis=-1, keepdims=True)
    centered = rows - center
    spread = jnp.mean(centered * centered, axis=-1, keepdims=True)
    inverse = lax.rsqrt(spread + 1e-05)
    return centered * inverse, inverse


def layer_norm_back(grad, normal, inverse):
    mean_grad = jnp.mean(grad, axis=-1, keepdims=True)
    mean_both = jnp.mean(grad * normal, axis=-1, keepdims=True)
    return (grad - mean_grad - normal * mean_both) * inverse


def add_rows(ref, values):
    ref[...] += jnp.sum(values, axis=0, keepdims=True)


def zero_first(*refs):
    @pl.when(pl.program_id(0) == 0)
    def _():
        for ref in refs:
            ref[...] = jnp.zeros_like(ref)


def call(
    body, grid, spot, arrays, specs, weights, outs, out_specs, scratch=(), estimate=None, aliases=()
):
    flat = [piece for pieces, _, _ in weights for piece in pieces]
    counts = [len(pieces) for pieces, _, _ in weights]
    n_arrays, n_flat, n_weights = len(arrays), len(flat), len(weights)
    n_outs = len(outs) if isinstance(outs, tuple) else 1

    def kernel(spot_ref, *refs):
        ins = refs[:n_arrays]
        piece_refs = refs[n_arrays : n_arrays + n_flat]
        out_refs = refs[n_arrays + n_flat : n_arrays + n_flat + n_outs]
        rest = refs[n_arrays + n_flat + n_outs :]
        held = rest[:n_weights]
        sems = rest[n_weights : 2 * n_weights]
        extra = rest[2 * n_weights :]
        first = pl.program_id(0) == 0

        def copies(number):
            start = sum(counts[:number])
            found = []
            for index in range(counts[number]):
                place = weights[number][1][index]
                for source, at in place(spot_ref, piece_refs[start + index]):
                    found.append(
                        pltpu.make_async_copy(
                            source, held[number].at[at], sems[number].at[len(found)]
                        )
                    )
            return found

        @pl.when(first)
        def _():
            for number in range(n_weights):
                for copy in copies(number):
                    copy.start()

        def ready(number):
            def wait():
                @pl.when(first)
                def _():
                    for copy in copies(number):
                        copy.wait()

                return held[number]

            return wait

        body(spot_ref, *ins, *[ready(number) for number in range(n_weights)], *out_refs, *extra)

    scratch_shapes = (
        [pltpu.VMEM(shape, BF) for _, _, shape in weights]
        + [pltpu.SemaphoreType.DMA((32,)) for _ in counts]
        + list(scratch)
    )
    return pl.pallas_call(
        kernel,
        out_shape=outs,
        grid_spec=pltpu.PrefetchScalarGridSpec(
            num_scalar_prefetch=1,
            grid=grid,
            in_specs=list(specs) + [any_spec()] * n_flat,
            out_specs=out_specs,
            scratch_shapes=scratch_shapes,
        ),
        compiler_params=params(*(["arbitrary"] * len(grid))),
        cost_estimate=estimate,
        input_output_aliases=dict(aliases),
    )(spot, *arrays, *flat)


def row(width, tile=TILE):
    return pl.BlockSpec((tile, width), lambda i, s: (i, 0))


def fixed(*shape):
    return pl.BlockSpec(shape, lambda *_: (0,) * len(shape))


def shape(dims, dtype):
    return jax.ShapeDtypeStruct(dims, dtype)


def project_qkv(spot, tokens, w_qkv, qkv_bias):
    count, width = tokens.shape
    wide = w_qkv[2][0]

    def body(spot_ref, x_ref, bias_ref, w_ready, out_ref):
        w_ref = w_ready()
        for start in range(0, wide, width):
            part = slice(start, start + width)
            out_ref[:, part] = (dot_nt(x_ref[...], w_ref[part, :]) + bias_ref[:, part]).astype(BF)

    return call(
        body, (count // TILE,), spot, (tokens, qkv_bias), (row(width), fixed(1, wide)), [w_qkv],
        shape((count, wide), BF), row(wide),
        estimate=cost(2 * count * width * wide, 2 * (count * width + wide * width + count * wide)),
    )


def lane_masks():
    lane = lax.broadcasted_iota(jnp.int32, (1, PAIR), 1)
    return [(lane // HD == head) for head in range(2)]


def same_segment(row_ref):
    numbers = row_ref[0].astype(F32)
    column = jnp.broadcast_to(numbers, (128, BLOCK)).T[:, 0:1]
    return column == numbers


def attend_forward(block, qkv, segment_row, into=None):
    count, wide = qkv.shape
    width = wide // 3
    pairs = width // PAIR
    steps = pairs // GROUP
    blocks = count // BLOCK

    def body(q_ref, k_ref, v_ref, row_ref, *refs):
        out_ref, lse_ref = refs[-2:]
        visible = same_segment(row_ref)
        for pair in range(GROUP):
            at = slice(pair * PAIR, (pair + 1) * PAIR)
            query, key = q_ref[:, at] * BF(1.0 / math.sqrt(HD)), k_ref[:, at]
            value_turned = v_ref[:, at].T
            parts = []
            for head, lanes in enumerate(lane_masks()):
                scores = dot_nt(key, jnp.where(lanes, query, BF(0)))
                scores = jnp.where(visible, scores, -1e30)
                highest = jnp.max(scores, axis=0, keepdims=True)
                exponent = jnp.exp(scores - highest)
                total = jnp.sum(exponent, axis=0, keepdims=True)
                part = dot(value_turned[head * HD : (head + 1) * HD], exponent.astype(BF))
                parts.append(part / total)
                lse_ref[0, pair, head : head + 1, :] = highest + jnp.log(total)
            out_ref[:, at] = jnp.concatenate(parts, axis=0).T.astype(BF)

    flops = 4 * HEADS * BLOCK * BLOCK * HD
    given = () if into is None else into
    return pl.pallas_call(
        body,
        out_shape=(shape((count, width), BF), shape((blocks, pairs, 2, BLOCK), F32)),
        grid=(steps,),
        in_specs=[
            pl.BlockSpec((BLOCK, GROUP * PAIR), lambda p: (block, p)),
            pl.BlockSpec((BLOCK, GROUP * PAIR), lambda p: (block, steps + p)),
            pl.BlockSpec((BLOCK, GROUP * PAIR), lambda p: (block, 2 * steps + p)),
            pl.BlockSpec((1, 1, BLOCK), lambda p: (block, 0, 0)),
        ]
        + [any_spec()] * len(given),
        out_specs=(
            pl.BlockSpec((BLOCK, GROUP * PAIR), lambda p: (block, p)),
            pl.BlockSpec((1, GROUP, 2, BLOCK), lambda p: (block, p, 0, 0)),
        ),
        compiler_params=params("arbitrary"),
        cost_estimate=cost(4 * flops, 4 * count * width, HEADS * BLOCK * BLOCK),
        input_output_aliases={4 + index: index for index in range(len(given))},
    )(qkv, qkv, qkv, segment_row, *given)


def attend_backward(block, qkv, segment_row, lse, context, d_context, sums, into=None):
    count, wide = qkv.shape
    width = wide // 3
    pairs = width // PAIR
    steps = pairs // GROUP
    factor = 1.0 / math.sqrt(HD)

    def body(q_ref, k_ref, v_ref, o_ref, do_ref, row_ref, lse_ref, given_ref, *refs):
        dq_ref, dk_ref, dv_ref, sums_ref = refs[-4:]

        @pl.when(pl.program_id(0) == 0)
        def _():
            sums_ref[...] = given_ref[...]

        visible = same_segment(row_ref)
        masks = lane_masks()
        for pair in range(GROUP):
            at = slice(pair * PAIR, (pair + 1) * PAIR)
            query, key, value = q_ref[:, at] * BF(factor), k_ref[:, at], v_ref[:, at]
            d_out = do_ref[:, at]
            key_turned = key.T
            product = (d_out.astype(F32) * o_ref[:, at].astype(F32)).T
            d_query, d_key, d_value = [], [], []
            for head, lanes in enumerate(masks):
                inside = slice(head * HD, (head + 1) * HD)
                delta = jnp.sum(product[inside], axis=0, keepdims=True)
                scores = dot_nt(key, jnp.where(lanes, query, BF(0)))
                scores -= lse_ref[0, pair, head : head + 1, :]
                prob = jnp.exp(jnp.where(visible, scores, -1e30))
                d_prob = dot_nt(value, jnp.where(lanes, d_out, BF(0)))
                d_score = (prob * (d_prob - delta)).astype(BF)
                d_value.append(dot(prob.astype(BF), d_out))
                d_key.append(dot(d_score, query))
                d_query.append(dot(key_turned[inside], d_score) * factor)
            dq = jnp.concatenate(d_query, axis=0).T.astype(BF)
            dk = jnp.where(masks[0], d_key[0], d_key[1]).astype(BF)
            dv = jnp.where(masks[0], d_value[0], d_value[1]).astype(BF)
            dq_ref[:, at] = dq
            dk_ref[:, at] = dk
            dv_ref[:, at] = dv
            lane = (pl.program_id(0) * GROUP + pair) * PAIR
            here = pl.ds(pl.multiple_of(lane, PAIR), PAIR)
            add_rows(sums_ref.at[QUERY_SUM : QUERY_SUM + 1, here], dq.astype(F32))
            add_rows(sums_ref.at[QUERY_SUM + 1 : QUERY_SUM + 2, here], dv.astype(F32))

    tile = pl.BlockSpec((BLOCK, GROUP * PAIR), lambda p: (block, p))
    flops = 10 * HEADS * BLOCK * BLOCK * HD
    given = () if into is None else into
    return pl.pallas_call(
        body,
        out_shape=(shape((count, width), BF),) * 3 + (shape((24, width), F32),),
        grid=(steps,),
        in_specs=[
            tile,
            pl.BlockSpec((BLOCK, GROUP * PAIR), lambda p: (block, steps + p)),
            pl.BlockSpec((BLOCK, GROUP * PAIR), lambda p: (block, 2 * steps + p)),
            tile,
            tile,
            pl.BlockSpec((1, 1, BLOCK), lambda p: (block, 0, 0)),
            pl.BlockSpec((1, GROUP, 2, BLOCK), lambda p: (block, p, 0, 0)),
            fixed(24, width),
        ]
        + [any_spec()] * len(given),
        out_specs=(tile,) * 3 + (fixed(24, width),),
        compiler_params=params("arbitrary"),
        cost_estimate=cost(4 * flops, 8 * count * width, HEADS * BLOCK * BLOCK),
        input_output_aliases={8 + index: index for index in range(len(given))},
    )(qkv, qkv, qkv, context, d_context, segment_row, lse, sums, *given)


def emit(plan, step, held, spot_ref, out_refs, sems):
    tile, blocks, (rows, cols), _, base = plan
    if blocks is None:
        target = out_refs[0].at[:, pl.ds(pl.multiple_of(step * tile, tile), tile)]
        pltpu.make_async_copy(held.at[step], target, sems.at[step]).start()
        return
    listed = blocks(step)
    for index, (row_at, column_at, x, core, z, y) in enumerate(listed):
        source = held.at[step, pl.ds(row_at, rows), pl.ds(column_at, cols)]
        sem = sems.at[step * len(listed) + index]
        far_x, far_y = x ^ spot_ref[0], y ^ spot_ref[3]
        first = far_x + core * (far_y - far_x)
        depth = z ^ spot_ref[2]
        slot = (depth & 1) + 2 * first + 4 * (far_x + far_y - first) + 8 * (depth >> 1)
        mine = (core ^ spot_ref[1]) == 0

        @pl.when(mine)
        def _():
            pltpu.make_async_copy(source, out_refs[0].at[slot, pl.ds(base, rows)], sem).start()

        @pl.when(jnp.logical_not(mine))
        def _():
            pltpu.make_async_copy(source, out_refs[1].at[slot, pl.ds(base, rows)], sem).start()


def emitted(plan, steps, held, out_refs, sems):
    tile, blocks, (rows, cols), _, base = plan
    if blocks is None:
        for step in range(steps):
            target = out_refs[0].at[:, pl.ds(step * tile, tile)]
            pltpu.make_async_copy(held.at[step], target, sems.at[step]).wait()
        return
    for index in range(32):
        source = held.at[0, pl.ds(0, rows), pl.ds(0, cols)]
        pltpu.make_async_copy(source, out_refs[0].at[0, pl.ds(base, rows)], sems.at[index]).wait()


def emit_shapes(plan, total, columns):
    _, blocks, (rows, cols), slot_rows, _ = plan
    if blocks is None:
        return (shape((total, columns), BF),)
    return (shape((16, slot_rows, cols), BF),) * 2


def clamped(width, last, tile=TILE):
    return pl.BlockSpec((tile, width), lambda i, s: (jnp.minimum(i, last), 0))


def project_out(spot, context, tokens, w_out, biases, gains):
    count, width = tokens.shape

    def body(spot_ref, c_ref, x_ref, bias_ref, gain_ref, w_ready, normal_ref, inverse_ref, low_ref):
        w_ref = w_ready()
        resid = x_ref[...].astype(F32) + (dot_nt(c_ref[...], w_ref[...]) + bias_ref[2:3])
        normal, inverse = layer_norm_parts(resid)
        normal_ref[...] = normal
        inverse_ref[...] = jnp.broadcast_to(inverse, inverse_ref.shape)
        low_ref[...] = (normal * gain_ref[0:1] + bias_ref[3:4]).astype(BF)

    return call(
        body, (count // TILE,), spot, (context, tokens, biases, gains),
        (row(width), row(width), fixed(*biases.shape), fixed(*gains.shape)), [w_out],
        (shape((count, width), F32), shape((count, 128), F32), shape((count, width), BF)),
        (row(width), row(128), row(width)),
        estimate=cost(2 * count * width * width, 10 * count * width),
    )


def ffn_in(spot, normed_low, w_in, in_bias):
    count, width = normed_low.shape
    wide = w_in[2][1]

    def body(spot_ref, x_ref, bias_ref, w_ready, hidden_ref, slope_ref):
        w_ref = w_ready()
        for start in range(0, wide, width):
            part = slice(start, start + width)
            pre = dot(x_ref[...], w_ref[:, part]) + bias_ref[:, part]
            cdf = 0.5 + 0.5 * lax.erf(pre * (1.0 / math.sqrt(2.0)))
            hidden_ref[:, part] = (pre * cdf).astype(BF)
            density = jnp.exp(pre * pre * -0.5) * (1.0 / math.sqrt(2.0 * math.pi))
            slope_ref[:, part] = (cdf + pre * density).astype(BF)

    return call(
        body, (count // TILE,), spot, (normed_low, in_bias), (row(width), fixed(1, wide)), [w_in],
        (shape((count, wide), BF),) * 2, (row(wide),) * 2,
        estimate=cost(2 * count * width * wide, 4 * count * wide, 2 * count * wide),
    )


def forward_rows(spot, hidden, normal_one, out_grad, w_back, biases, gains, plan):
    count, width = out_grad.shape
    wide = hidden.shape[1]
    steps = count // TILE
    tile = plan[0]
    columns = wide // tile
    shapes = emit_shapes(plan, width, wide)

    def body(spot_ref, h_ref, column_ref, n_ref, g_ref, bias_ref, gain_ref, wb_ready,
             out_ref, d_two_ref, d_low_ref, sums_ref, *refs):
        grads, (d_rows, turned, held, sems) = refs[: len(shapes)], refs[len(shapes) :]
        index = pl.program_id(0)
        zero_first(sums_ref)

        @pl.when(index < steps)
        def _():
            here = pl.ds(pl.multiple_of(index * TILE, TILE), TILE)
            resid = n_ref[...] * gain_ref[0:1] + bias_ref[3:4]
            w_ref = wb_ready()
            resid += dot_nt(h_ref[...], w_ref[...]) + bias_ref[4:5]
            normal, inverse = layer_norm_parts(resid)
            out_ref[...] = (normal * gain_ref[1:2] + bias_ref[5:6]).astype(BF)
            grad = g_ref[...].astype(F32)
            d_two = layer_norm_back(grad * gain_ref[1:2], normal, inverse)
            d_low = d_two.astype(BF)
            d_two_ref[...] = d_two
            d_low_ref[...] = d_low
            d_rows[here, :] = d_low
            add_rows(sums_ref.at[0:1], grad * normal)
            add_rows(sums_ref.at[1:2], grad)
            add_rows(sums_ref.at[2:3], d_low.astype(F32))

        @pl.when(index == steps)
        def _():
            turned[...] = d_rows[...].T

        @pl.when(index >= steps)
        def _():
            column = index - steps
            held[column] = dot(turned[...], column_ref[...]).astype(BF)
            emit(plan, column, held, spot_ref, grads, sems)

        @pl.when(index == steps + columns - 1)
        def _():
            emitted(plan, columns, held, grads, sems)

    last = steps - 1
    rows = lambda wide_: clamped(wide_, last)
    return call(
        body, (steps + columns,), spot, (hidden, hidden, normal_one, out_grad, biases, gains),
        (rows(wide), pl.BlockSpec((count, tile), lambda i, s: (0, jnp.maximum(i - steps, 0))),
         rows(width), rows(width), fixed(*biases.shape), fixed(*gains.shape)),
        [w_back],
        (shape((count, width), BF), shape((count, width), F32), shape((count, width), BF),
         shape((8, width), F32), *shapes),
        (rows(width), rows(width), rows(width), fixed(8, width), *[any_spec()] * len(shapes)),
        [pltpu.VMEM((count, width), BF),
         pltpu.VMEM((width, count), BF), pltpu.VMEM((columns, width, tile), BF),
         pltpu.SemaphoreType.DMA((32,))],
        cost(4 * count * width * wide, 14 * count * width + 4 * count * wide),
    )


def backward_rows(
    spot, d_low, slope, d_two, normal_one, inverse_one, normed_low, context, sums_two, w_back, w_in,
    w_out, gains, plan_in, plan_out,
):
    count, width = d_two.shape
    wide = slope.shape[1]
    steps = count // TILE
    tile_in, tile_out = plan_in[0], plan_out[0]
    columns_in, columns_out = wide // tile_in, width // tile_out
    shared = plan_in[1] is not None
    shapes = emit_shapes(plan_in, width, wide)
    if not shared:
        shapes += emit_shapes(plan_out, width, width)

    def body(spot_ref, dl_ref, s_ref, d2_ref, n_ref, i_ref, low_ref, c_ref, two_ref, gain_ref,
             wb_ready, wi_ready, wo_ready, d_one_ref, d_context_ref, sums_ref, *refs):
        grads = refs[: len(shapes)]
        d_pre, d_attn, turned, held_in, held_out, low_held, sems_in, sems_out, late = refs[
            len(shapes) :
        ]
        fetch_low = pltpu.make_async_copy(low_ref, low_held, late.at[0])
        grads_in, grads_out = (grads, grads) if shared else (grads[:1], grads[1:])
        index = pl.program_id(0)

        @pl.when(index == 0)
        def _():
            sums_ref[...] = jnp.zeros_like(sums_ref)
            sums_ref[0:8, :] = two_ref[...]
            fetch_low.start()

        @pl.when(index < steps)
        def _():
            here = pl.ds(pl.multiple_of(index * TILE, TILE), TILE)
            w_ref = wb_ready()
            pieces = []
            for start in range(0, wide, width):
                part = slice(start, start + width)
                d_hidden = dot(dl_ref[...], w_ref[:, part])
                piece = (d_hidden * s_ref[:, part].astype(F32)).astype(BF)
                d_pre[here, part] = piece
                pieces.append(piece)
                at = HIDDEN_SUM + start // width
                add_rows(sums_ref.at[at : at + 1], piece.astype(F32))
            w_ref = wi_ready()
            d_normed = d2_ref[...]
            for number, piece in enumerate(pieces):
                d_normed += dot_nt(piece, w_ref[:, number * width : (number + 1) * width])
            normal = n_ref[...]
            d_one = layer_norm_back(d_normed * gain_ref[0:1], normal, i_ref[:, 0:1])
            low = d_one.astype(BF)
            d_one_ref[...] = d_one
            d_attn[here, :] = low
            d_context_ref[...] = dot(low, wo_ready()[...]).astype(BF)
            add_rows(sums_ref.at[8:9], d_normed * normal)
            add_rows(sums_ref.at[9:10], d_normed)
            add_rows(sums_ref.at[10:11], low.astype(F32))

        @pl.when(index == steps)
        def _():
            fetch_low.wait()
            turned[...] = low_held[...].T

        @pl.when(jnp.logical_and(index >= steps, index < steps + columns_in))
        def _():
            column = index - steps
            at = pl.ds(pl.multiple_of(column * tile_in, tile_in), tile_in)
            held_in[column] = dot(turned[...], d_pre[:, at]).astype(BF)
            emit(plan_in, column, held_in, spot_ref, grads_in, sems_in)

        @pl.when(index == steps + columns_in)
        def _():
            turned[...] = d_attn[...].T

        @pl.when(index >= steps + columns_in)
        def _():
            column = index - steps - columns_in
            held_out[column] = dot(turned[...], c_ref[...]).astype(BF)
            emit(plan_out, column, held_out, spot_ref, grads_out, sems_out)

        @pl.when(index == steps + columns_in + columns_out - 1)
        def _():
            emitted(plan_in, columns_in, held_in, grads_in, sems_in)
            emitted(plan_out, columns_out, held_out, grads_out, sems_out)

    last, before = steps - 1, steps + columns_in
    rows = lambda wide_: clamped(wide_, last)
    return call(
        body, (steps + columns_in + columns_out,), spot,
        (d_low, slope, d_two, normal_one, inverse_one, normed_low, context, sums_two, gains),
        (rows(width), rows(wide), rows(width), rows(width), rows(128), any_spec(),
         pl.BlockSpec((count, tile_out), lambda i, s: (0, jnp.maximum(i - before, 0))),
         fixed(8, width), fixed(*gains.shape)),
        [w_back, w_in, w_out],
        (shape((count, width), F32), shape((count, width), BF), shape((24, width), F32), *shapes),
        (rows(width), rows(width), fixed(24, width), *[any_spec()] * len(shapes)),
        [pltpu.VMEM((count, wide), BF), pltpu.VMEM((count, width), BF),
         pltpu.VMEM((width, count), BF), pltpu.VMEM((columns_in, width, tile_in), BF),
         pltpu.VMEM((columns_out, width, tile_out), BF), pltpu.VMEM((count, width), BF),
         pltpu.SemaphoreType.DMA((32,)), pltpu.SemaphoreType.DMA((32,)),
         pltpu.SemaphoreType.DMA((1,))],
        cost(2 * count * width * (3 * wide + 2 * width), 18 * count * width + 2 * count * wide),
    )


def tokens_backward(spot, d_one, d_query, d_key, d_value, w_qkv):
    count, width = d_one.shape

    def body(spot_ref, d1_ref, q_ref, k_ref, v_ref, w_ready, out_ref):
        w_ref = w_ready()
        total = d1_ref[...] + dot(q_ref[...], w_ref[0:width, :])
        total += dot(k_ref[...], w_ref[width : 2 * width, :])
        total += dot(v_ref[...], w_ref[2 * width : 3 * width, :])
        out_ref[...] = total.astype(BF)

    return call(
        body, (count // TILE,), spot, (d_one, d_query, d_key, d_value), (row(width),) * 4, [w_qkv],
        shape((count, width), BF), row(width),
        estimate=cost(6 * count * width * width, 12 * count * width),
    )


def gradient(spot, lefts, right, plan):
    count, columns = right.shape
    width = lefts[0].shape[1]
    total = width * len(lefts)
    tile = plan[0]
    steps = columns // tile
    n_left = len(lefts)
    shapes = emit_shapes(plan, total, columns)

    def body(spot_ref, *refs):
        left_refs, right_ref = refs[:n_left], refs[n_left]
        grads = refs[n_left + 1 : n_left + 1 + len(shapes)]
        turned, held, sems = refs[-3:]
        step = pl.program_id(0)

        @pl.when(step == 0)
        def _():
            for index, ref in enumerate(left_refs):
                turned[index * width : (index + 1) * width, :] = ref[...].T

        for index in range(n_left):
            part = slice(index * width, (index + 1) * width)
            held[step, part, :] = dot(turned[part, :], right_ref[...]).astype(BF)
        emit(plan, step, held, spot_ref, grads, sems)

        @pl.when(step == steps - 1)
        def _():
            emitted(plan, steps, held, grads, sems)

    return call(
        body, (steps,), spot, (*lefts, right),
        (*[fixed(count, width)] * n_left, pl.BlockSpec((count, tile), lambda i, s: (0, i))), [],
        shapes, (any_spec(),) * len(shapes),
        [pltpu.VMEM((total, count), BF), pltpu.VMEM((steps, total, tile), BF),
         pltpu.SemaphoreType.DMA((32,))],
        cost(2 * count * total * columns, 2 * (count * (total + columns) + total * columns)),
    )


def widen(value):
    return value.astype(F32)


def exchange(value, stage):
    axes = ("x", "core", "z", "y")
    pairs = []
    for source in range(32):
        x, core, z, y = source >> 4, (source >> 3) & 1, (source >> 1) & 3, source & 1
        if stage in (Z1, Z2, Z3):
            z ^= {Z1: 1, Z2: 2, Z3: 3}[stage]
        elif stage == CORE:
            core ^= 1
        elif (stage == FIRST) == (core == 0):
            x ^= 1
        else:
            y ^= 1
        pairs.append((source, 16 * x + 8 * core + 2 * z + y))
    return lax.ppermute(value, axes, pairs)


class Parcel:
    def __init__(self, array, origins=((0, 0, 0, 0),)):
        self.array = array
        self.origins = tuple(origins)

    def moved(self, stage):
        def change(origin):
            core, second, first, depth = origin
            along_first = stage == (SECOND if core else FIRST)
            along_second = stage == (FIRST if core else SECOND)
            return (
                core ^ (stage == CORE),
                second ^ along_second,
                first ^ along_first,
                depth ^ {Z1: 1, Z2: 2}.get(stage, 0),
            )

        return Parcel(exchange(self.array, stage), [change(origin) for origin in self.origins])

    def __add__(self, other):
        return Parcel(jnp.concatenate([self.array, other.array]), self.origins + other.origins)


def sync(values, *parcels):
    values, arrays = lax.optimization_barrier((values, [parcel.array for parcel in parcels]))
    for parcel, array in zip(parcels, arrays):
        parcel.array = array
    return values


class Reduce:
    def __init__(self, near, far):
        self.near, self.far = near, Parcel(far)

    def send_core(self):
        self.core = Parcel(exchange(self.far.array, CORE))

    def sum(self, start, stop, *others):
        total = widen(self.near[start:stop]) + widen(self.core.array[start:stop])
        for parcel, at in others:
            total += widen(parcel.array[at : at + stop - start])
        return total

    def send(self, stage, start, stop, *others):
        return Parcel(exchange(self.sum(start, stop, *others).astype(BF), stage))

    def send_second_b(self):
        self.second_b = self.send(SECOND, 12, 16)

    def send_second_a(self):
        self.second_a = self.send(SECOND, 4, 8)

    def send_first_b(self):
        self.first_b = self.send(FIRST, 10, 12, (self.second_b, 2))

    def send_first_a(self):
        self.first_a = self.send(FIRST, 2, 4, (self.second_a, 2))

    def send_z2(self):
        self.z2 = self.send(Z2, 8, 10, (self.second_b, 0), (self.first_b, 0))

    def send_z1(self):
        self.z1 = self.send(Z1, 1, 2, (self.second_a, 1), (self.first_a, 1), (self.z2, 1))
        self.last = (self.z2, self.z1)

    def send_direct_b(self):
        self.z2 = self.send(Z2, 8, 9, (self.second_b, 0), (self.first_b, 0))
        self.z3 = self.send(Z3, 9, 10, (self.second_b, 1), (self.first_b, 1))

    def send_direct_a(self):
        self.z1 = self.send(Z1, 1, 2, (self.second_a, 1), (self.first_a, 1))
        self.last = (self.z1, self.z2, self.z3)

    def result(self):
        others = (self.second_a, self.first_a) + self.last
        return self.sum(0, 1, *[(parcel, 0) for parcel in others])[0]


def source_of(spot, origin):
    away, second, first, depth = origin
    core = spot[1] ^ away
    x = spot[0] ^ (first + core * (second - first))
    y = spot[3] ^ (second + core * (first - second))
    return core, x, 2 * (spot[2] ^ depth) + y


def weight_of(parcels, source_rows, place, dims):
    start, rows, cols = source_rows
    pieces, places = [], []
    for parcel in parcels:
        pieces.append(parcel.array)

        def at(spot_ref, ref, origins=parcel.origins):
            for index, origin in enumerate(origins):
                core, x, f = source_of(spot_ref, origin)
                row_at, column_at = place(x, core, f)
                yield (
                    ref.at[index, pl.ds(start, rows), :],
                    (
                        pl.ds(pl.multiple_of(row_at, 16), rows),
                        pl.ds(pl.multiple_of(column_at, 128), cols),
                    ),
                )

        places.append(at)
    return pieces, places, dims


def whole_weight(array):
    def at(spot_ref, ref):
        yield ref, (pl.ds(0, array.shape[0]), pl.ds(0, array.shape[1]))

    return [array], [at], array.shape


def device_slots(spot, origins):
    device = lax.broadcasted_iota(jnp.int32, (len(origins), len(origins)), 0)
    owners = []
    for origin in origins:
        core, x, f = source_of(spot, origin)
        owners.append(16 * x + 8 * core + f)
    return (device == jnp.stack(owners)[None, :]).astype(F32)


def small_vectors(every, shards):
    biases, in_bias, gains = shards
    devices = every.shape[0]
    first, second = biases.size, biases.size + in_bias.size
    third = second + gains.size
    return (
        every[:, :first].reshape(devices, 6, -1).transpose(1, 0, 2).reshape(6, -1),
        every[:, first:second].reshape(1, -1),
        every[:, second:third].reshape(devices, 2, -1).transpose(1, 0, 2).reshape(2, -1),
    )


def on_device(sizes, tokens, segment_ids, w_qkv, w_out, w_in, w_back, biases, in_bias, gains, out_grad):
    axes = ("x", "core", "z", "y")
    dp_axes, fsdp_axes = ("x", "core"), ("z", "y")
    devices = math.prod(sizes)
    by_permute = sizes == (2, 2, 4, 2)
    count, width = tokens.shape
    wide = w_back.shape[0] * sizes[0] * sizes[1]
    blocks = range(count // BLOCK)
    spot = jnp.stack([lax.axis_index(axis) for axis in axes]).astype(jnp.int32)
    core = spot[1]
    shards = (biases, in_bias, gains)
    segment_row = segment_ids.reshape(count // BLOCK, 1, BLOCK)

    qkv_cols, out_cols = w_qkv.shape[1], w_out.shape[1]
    pair_cols = 2 * w_qkv.shape[0]
    in_rows, in_cols = w_in.shape
    back_rows, back_cols = w_back.shape
    half_q, half_o = qkv_cols // 2, out_cols // 2

    if by_permute:

        def paired(turned):
            half = turned.shape[0] // 2
            first, second = turned[:half], turned[half:]
            mine = jnp.where(core == 0, first, second)
            other = exchange(jnp.where(core == 0, second, first), CORE)
            return jnp.where(
                core == 0,
                jnp.concatenate([mine, other], axis=1),
                jnp.concatenate([other, mine], axis=1),
            )

        to_qkv = Parcel(paired(w_qkv.T)[None])
        qkv_z1 = to_qkv.moved(Z1)
        own_vectors, w_in = sync(((biases, in_bias, gains), w_in), to_qkv)
        own_small = jnp.concatenate([part.reshape(-1) for part in own_vectors])
        to_small = Parcel(jnp.pad(own_small, (0, 1024 - own_small.size)).reshape(1, 8, 128))
        to_small += to_small.moved(CORE)
        w_in, w_out, w_back = sync((w_in, w_out, w_back), qkv_z1, to_small)
        qkv_near = to_qkv + qkv_z1
        qkv_z2 = qkv_near.moved(Z2)
        qkv_first_a = qkv_near.moved(FIRST)
        to_small += to_small.moved(FIRST)
        to_in = Parcel(jnp.concatenate([w_in, paired(w_out.T)], axis=0)[None])
        to_back = Parcel(w_back.T[None])
        sync((), qkv_first_a, to_small, to_in)
        qkv_a = qkv_near + qkv_first_a
        qkv_second_a = qkv_a.moved(SECOND)
        in_z1 = to_in.moved(Z1)
        to_small += to_small.moved(SECOND)
        sync((), qkv_z2)
        qkv_first_b = qkv_z2.moved(FIRST)
        sync((), qkv_z2, to_small)
        to_small += to_small.moved(Z1)
        sync((), qkv_first_b, to_small)
        qkv_b = qkv_z2 + qkv_first_b
        qkv_second_b = qkv_b.moved(SECOND)
        to_small += to_small.moved(Z2)
        sync((), qkv_first_b, qkv_second_a, to_small, in_z1)
        qkv_core_a = qkv_a.moved(CORE), qkv_second_a.moved(CORE)
        in_near = to_in + in_z1
        in_z2 = in_near.moved(Z2)
        sync((), qkv_second_b, in_near, to_back)
        qkv_core_b = qkv_b.moved(CORE), qkv_second_b.moved(CORE)
        in_first_a = in_near.moved(FIRST)
        back_z1 = to_back.moved(Z1)
        tokens = sync(tokens, *qkv_core_a, *qkv_core_b)
        qkv_parcels = (
            qkv_a, qkv_second_a, qkv_b, qkv_second_b, *qkv_core_a, *qkv_core_b
        )
        qkv_weight = weight_of(
            qkv_parcels, (0, half_q, pair_cols),
            lambda x, c, f: (f * qkv_cols + c * half_q, x * pair_cols), (3 * width, width),
        )
        slots = device_slots(spot, to_small.origins)
        arrived = widen(to_small.array).reshape(32, 1024)
        every = jnp.dot(slots, arrived, precision=lax.Precision.HIGHEST)

        def back_blocks(index):
            return [(f * back_cols, 0, index >> 1, index & 1, f >> 1, f & 1) for f in range(8)]

        def in_blocks(index):
            return [
                ((2 * x + c) * in_rows, y * in_cols, x, c, index, y)
                for x in range(2) for c in range(2) for y in range(2)
            ]

        def out_blocks(index):
            return [
                (f * out_cols + c * half_o, 0, index, c, f >> 1, f & 1)
                for f in range(8) for c in range(2)
            ]

        def qkv_blocks(index):
            return [
                (f * qkv_cols + c * half_q, 0, index, c, f >> 1, f & 1)
                for f in range(8) for c in range(2)
            ]

        plans = {
            "back": (back_rows, back_blocks, (back_cols, back_rows), back_cols, 0),
            "in": (2 * in_cols, in_blocks, (in_rows, in_cols), in_rows + half_o, 0),
            "out": (pair_cols, out_blocks, (half_o, pair_cols), in_rows + half_o, in_rows),
            "qkv": (pair_cols, qkv_blocks, (half_q, pair_cols), half_q, 0),
        }
    else:

        def full(shard):
            return lax.all_gather(
                lax.all_gather(shard, fsdp_axes, axis=1, tiled=True), dp_axes, axis=0, tiled=True
            )

        qkv_weight = whole_weight(full(w_qkv).T)
        out_weight = whole_weight(full(w_out).T)
        in_weight = whole_weight(full(w_in))
        back_weight = whole_weight(full(w_back).T)
        own_small = jnp.concatenate([biases.reshape(-1), in_bias, gains.reshape(-1)])
        every = widen(lax.all_gather(own_small, axes, axis=0, tiled=False))
        plans = {name: (width // 2, None, (0, 0), 0, 0) for name in ("back", "in", "out", "qkv")}

    bias_values, hidden_bias, gain_values = small_vectors(every, shards)
    qkv_bias = jnp.concatenate(
        [bias_values[0:1], jnp.zeros((1, width), F32), bias_values[1:2]], axis=1
    )

    bias_values, hidden_bias, gain_values, qkv_bias = sync(
        (bias_values, hidden_bias, gain_values, qkv_bias)
    )
    qkv = project_qkv(spot, tokens, qkv_weight, qkv_bias)
    if by_permute:
        qkv = sync(qkv, in_first_a, in_z2, back_z1)
        in_a = in_near + in_first_a
        in_second_a = in_a.moved(SECOND)
        in_first_b = in_z2.moved(FIRST)
        back_near = to_back + back_z1
        back_z2 = back_near.moved(Z2)
    attended = None
    for block in blocks:
        attended = attend_forward(block, qkv, segment_row, attended)
        if by_permute and block == 0:
            attended = sync(attended, in_second_a, in_first_b, back_z2)
            in_b = in_z2 + in_first_b
            in_second_b = in_b.moved(SECOND)
            in_core = in_a.moved(CORE), in_second_a.moved(CORE), in_b.moved(CORE)
            back_first_a = back_near.moved(FIRST)
    context, lse = attended
    if by_permute:
        context = sync(context, in_second_b, *in_core, back_first_a)
        in_cross = in_second_b.moved(CORE)
        back_a = back_near + back_first_a
        back_second_a = back_a.moved(SECOND)
        back_first_b = back_z2.moved(FIRST)
        context = sync(context, in_cross)
        in_parcels = (in_a, in_second_a, in_b, in_second_b, *in_core, in_cross)
        in_weight = weight_of(
            in_parcels, (0, in_rows, in_cols),
            lambda x, c, f: ((2 * x + c) * in_rows, f * in_cols), (width, wide),
        )
        out_weight = weight_of(
            in_parcels, (in_rows, half_o, pair_cols),
            lambda x, c, f: (f * out_cols + c * half_o, x * pair_cols), (width, width),
        )
    normal_one, inverse_one, normed_low = project_out(
        spot, context, tokens, out_weight, bias_values, gain_values
    )
    if by_permute:
        normed_low = sync(normed_low, back_second_a, back_first_b)
        back_b = back_z2 + back_first_b
        back_second_b = back_b.moved(SECOND)
        back_core = back_a.moved(CORE), back_second_a.moved(CORE), back_b.moved(CORE)
    hidden, slope = ffn_in(spot, normed_low, in_weight, hidden_bias)
    if by_permute:
        hidden = sync(hidden, back_second_b, *back_core)
        back_cross = back_second_b.moved(CORE)
        back_weight = weight_of(
            (back_a, back_second_a, back_b, back_second_b, *back_core, back_cross),
            (0, back_cols, back_rows),
            lambda x, c, f: (f * back_cols, (2 * x + c) * back_rows), (width, wide),
        )
    layer_out, d_two, d_low, sums_two, *grad_back = forward_rows(
        spot, hidden, normal_one, out_grad, back_weight, bias_values, gain_values, plans["back"]
    )
    if by_permute:
        from_back = Reduce(*grad_back)
        from_back.send_core()
        d_low = sync(d_low, from_back.core)
        from_back.send_second_b()
        from_back.send_second_a()
    d_one, d_context, small, *grads_in = backward_rows(
        spot, d_low, slope, d_two, normal_one, inverse_one, normed_low, context, sums_two,
        back_weight, in_weight, out_weight, gain_values, plans["in"], plans["out"],
    )
    if by_permute:
        from_in = Reduce(*grads_in)
        d_context = sync(d_context, from_back.second_a, from_back.second_b, from_in.far)
        from_in.send_core()
        from_back.send_first_b()
        from_back.send_first_a()
    else:
        grad_in, grad_out = grads_in
        grad_back, = grad_back
    attended = None
    for block in blocks:
        *attended, small = attend_backward(
            block, qkv, segment_row, lse, context, d_context, small, attended
        )
        if by_permute and block == 0:
            attended = sync(attended, from_back.first_a, from_back.first_b, from_in.core)
            from_in.send_second_b()
            from_back.send_z2()
        elif by_permute:
            attended, small = sync((attended, small), from_back.z2, from_in.second_b)
            from_in.send_second_a()
            from_in.send_first_b()
            from_back.send_z1()
            small_sent = Parcel(small).moved(CORE)
    grad_qkv = gradient(spot, attended, tokens, plans["qkv"])
    if by_permute:
        from_qkv = Reduce(*grad_qkv)
        small = sync(
            small, from_qkv.far, small_sent, from_in.second_a, from_in.first_b, from_back.z1
        )
        from_qkv.send_core()
        small = small + small_sent.array
        small_sent = Parcel(small).moved(Z1)
        from_in.send_z2()
        d_one = sync(d_one, from_qkv.core)
        from_qkv.send_second_b()
        from_qkv.send_second_a()
    else:
        grad_qkv, = grad_qkv
    tokens_grad = tokens_backward(spot, d_one, *attended, qkv_weight)

    if by_permute:

        def unpaired(sums):
            half = sums.shape[1] // 2
            left, right = sums[:, :half], sums[:, half:]
            mine = jnp.where(core == 0, left, right)
            other = widen(exchange(jnp.where(core == 0, right, left).astype(BF), CORE))
            return jnp.where(
                core == 0,
                jnp.concatenate([mine, other], axis=0),
                jnp.concatenate([other, mine], axis=0),
            )

        tokens_grad, small = sync(
            (tokens_grad, small), from_qkv.second_b, from_qkv.second_a, small_sent, from_in.second_a,
            from_in.z2,
        )
        from_qkv.send_first_b()
        from_qkv.send_first_a()
        small = small + small_sent.array
        small = sync(small, from_qkv.first_b, from_in.second_a)
        from_qkv.send_direct_b()
        from_in.send_first_a()
        small = sync(small, from_qkv.first_a)
        from_qkv.send_direct_a()
        small_sent = Parcel(small).moved(SECOND)
        small = sync(small, small_sent, from_in.first_a)
        from_in.send_z1()
        small = small + small_sent.array
        small_sent = Parcel(small).moved(FIRST)
        small = sync(small, small_sent)
        small = small + small_sent.array
        small_sent = Parcel(small).moved(Z2)
        small = sync(small, small_sent, from_in.z1)
        small = small + small_sent.array
        sums_in = from_in.result()
        own_back = from_back.result().T
        own_in = sums_in[:in_rows]
        own_out = unpaired(sums_in[in_rows:]).T
        own_qkv = unpaired(from_qkv.result()).T
    else:

        def scattered(total):
            part = lax.psum_scatter(total, dp_axes, scatter_dimension=0, tiled=True)
            part = lax.psum_scatter(part, fsdp_axes, scatter_dimension=1, tiled=True)
            return widen(part)

        own_back = scattered(grad_back.T)
        own_in = scattered(grad_in)
        own_out = scattered(grad_out.T)
        own_qkv = scattered(grad_qkv.T)
        small = lax.psum(small, axes)
    device = lax.axis_index(axes)
    queries = small[QUERY_SUM : QUERY_SUM + 2]
    bias_total = jnp.concatenate([queries, small[10:11], small[9:10], small[2:3], small[1:2]])
    gain_total = jnp.concatenate([small[8:9], small[0:1]])
    own_bias = lax.dynamic_slice_in_dim(bias_total, device * biases.shape[1], biases.shape[1], 1)
    own_gain = lax.dynamic_slice_in_dim(gain_total, device * gains.shape[1], gains.shape[1], 1)
    own_hidden = lax.dynamic_slice_in_dim(
        small[HIDDEN_SUM:QUERY_SUM].reshape(-1), device * in_bias.shape[0], in_bias.shape[0], 0
    )
    return (
        layer_out, tokens_grad, own_qkv, own_out, own_in, own_back, own_bias, own_hidden, own_gain,
    )


def solution(mesh):
    dp, fsdp = mesh.devices.shape
    sizes = (dp // 2, 2, fsdp // 2, 2)
    split = Mesh(mesh.devices.reshape(sizes), ("x", "core", "z", "y"))
    outer, inner = ("x", "core"), ("z", "y")
    every = outer + inner
    rows = P(every, None)
    weight = P(outer, inner)
    vectors = P(None, every)

    def placed(*arrays):
        return on_device(sizes, *arrays)

    return jax.shard_map(
        placed,
        mesh=split,
        in_specs=(rows, rows, weight, weight, weight, weight, vectors, P(every), vectors, rows),
        out_specs=(rows, rows, weight, weight, weight, weight, vectors, P(every), vectors),
        check_vma=False,
    )
```

```python
import math

import jax
import jax.numpy as jnp
from jax import lax
from jax.experimental import pallas as pl
from jax.experimental.pallas import tpu as pltpu
from jax.sharding import Mesh, PartitionSpec as P

HEADS = 12
HD = 64
DOCS = 8
BLOCK = 512
PAIR = 2 * HD
GROUP = 2
FORWARD_GROUP = 3
TILE = 256
WIDE_TILE = 512
VMEM = 58 * 1024 * 1024
BF = jnp.bfloat16
F32 = jnp.float32
Z1, Z2, FIRST, SECOND, CORE, Z3 = range(6)
HIDDEN_SUM, QUERY_SUM = 16, 20
NT = (((1,), (1,)), ((), ()))


def dot(a, b):
    return jnp.dot(a, b, preferred_element_type=F32)


def dot_nt(a, b):
    return lax.dot_general(a, b, NT, preferred_element_type=F32)


def any_spec():
    return pl.BlockSpec(memory_space=pl.ANY)


def params(*semantics):
    return pltpu.CompilerParams(
        dimension_semantics=semantics if semantics else None, vmem_limit_bytes=VMEM
    )


def cost(flops, nbytes, trans=0):
    return pl.CostEstimate(flops=flops, bytes_accessed=nbytes, transcendentals=trans)

def layer_norm_parts(rows):
    center = jnp.mean(rows, axis=-1, keepdims=True)
    centered = rows - center
    spread = jnp.mean(centered * centered, axis=-1, keepdims=True)
    inverse = lax.rsqrt(spread + 1e-05)
    return centered * inverse, inverse


def layer_norm_back(grad, normal, inverse):
    mean_grad = jnp.mean(grad, axis=-1, keepdims=True)
    mean_both = jnp.mean(grad * normal, axis=-1, keepdims=True)
    return (grad - mean_grad - normal * mean_both) * inverse


def add_rows(ref, values):
    ref[...] += jnp.sum(values, axis=0, keepdims=True)


def zero_first(*refs):
    @pl.when(pl.program_id(0) == 0)
    def _():
        for ref in refs:
            ref[...] = jnp.zeros_like(ref)


def call(
    body, grid, spot, arrays, specs, weights, outs, out_specs, scratch=(), estimate=None, aliases=()
):
    flat = [piece for pieces, _, _ in weights for piece in pieces]
    counts = [len(pieces) for pieces, _, _ in weights]
    n_arrays, n_flat, n_weights = len(arrays), len(flat), len(weights)
    n_outs = len(outs) if isinstance(outs, tuple) else 1

    def kernel(spot_ref, *refs):
        ins = refs[:n_arrays]
        piece_refs = refs[n_arrays : n_arrays + n_flat]
        out_refs = refs[n_arrays + n_flat : n_arrays + n_flat + n_outs]
        rest = refs[n_arrays + n_flat + n_outs :]
        held = rest[:n_weights]
        sems = rest[n_weights : 2 * n_weights]
        extra = rest[2 * n_weights :]
        first = pl.program_id(0) == 0

        def copies(number):
            start = sum(counts[:number])
            found = []
            for index in range(counts[number]):
                place = weights[number][1][index]
                for source, at in place(spot_ref, piece_refs[start + index]):
                    found.append(
                        pltpu.make_async_copy(
                            source, held[number].at[at], sems[number].at[len(found)]
                        )
                    )
            return found

        @pl.when(first)
        def _():
            for number in range(n_weights):
                for copy in copies(number):
                    copy.start()

        def ready(number):
            def wait():
                @pl.when(first)
                def _():
                    for copy in copies(number):
                        copy.wait()

                return held[number]

            return wait

        body(spot_ref, *ins, *[ready(number) for number in range(n_weights)], *out_refs, *extra)

    scratch_shapes = (
        [pltpu.VMEM(shape, BF) for _, _, shape in weights]
        + [pltpu.SemaphoreType.DMA((32,)) for _ in counts]
        + list(scratch)
    )
    return pl.pallas_call(
        kernel,
        out_shape=outs,
        grid_spec=pltpu.PrefetchScalarGridSpec(
            num_scalar_prefetch=1,
            grid=grid,
            in_specs=list(specs) + [any_spec()] * n_flat,
            out_specs=out_specs,
            scratch_shapes=scratch_shapes,
        ),
        compiler_params=params(*(["arbitrary"] * len(grid))),
        cost_estimate=estimate,
        input_output_aliases=dict(aliases),
    )(spot, *arrays, *flat)


def row(width, tile=TILE):
    return pl.BlockSpec((tile, width), lambda i, s: (i, 0))


def fixed(*shape):
    return pl.BlockSpec(shape, lambda *_: (0,) * len(shape))


def shape(dims, dtype):
    return jax.ShapeDtypeStruct(dims, dtype)


def project_qkv(spot, tokens, w_qkv, qkv_bias):
    count, width = tokens.shape
    wide = w_qkv[2][0]

    def body(spot_ref, x_ref, bias_ref, w_ready, out_ref):
        w_ref = w_ready()
        for start in range(0, wide, width):
            part = slice(start, start + width)
            out_ref[:, part] = (dot_nt(x_ref[...], w_ref[part, :]) + bias_ref[:, part]).astype(BF)

    return call(
        body, (count // TILE,), spot, (tokens, qkv_bias), (row(width), fixed(1, wide)), [w_qkv],
        shape((count, wide), BF), row(wide),
        estimate=cost(2 * count * width * wide, 2 * (count * width + wide * width + count * wide)),
    )


def lane_masks():
    lane = lax.broadcasted_iota(jnp.int32, (1, PAIR), 1)
    return [(lane // HD == head) for head in range(2)]


def same_segment(row_ref):
    numbers = row_ref[0].astype(F32)
    column = jnp.broadcast_to(numbers, (128, BLOCK)).T[:, 0:1]
    return column == numbers


def lanes():
    lane = lax.broadcasted_iota(jnp.int32, (1, PAIR), 1)
    return lane // HD, lane % HD


def segment_codes(row_ref, query_ref, key_ref):
    numbers = jnp.broadcast_to(row_ref[0].astype(F32), (PAIR, BLOCK)).T
    inner = lanes()[1].astype(F32)
    same = inner == numbers
    query_ref[...] = jnp.where(same, 1.0, 0.0).astype(BF)
    key_ref[...] = jnp.where(jnp.logical_or(same, inner >= DOCS), 0.0, -1e30).astype(BF)


def attend_forward(block, qkv, segment_row, into=None):
    count, wide = qkv.shape
    width = wide // 3
    pairs = width // PAIR
    steps = pairs // FORWARD_GROUP
    blocks = count // BLOCK

    def body(q_ref, k_ref, v_ref, row_ref, *refs):
        out_ref, lse_ref, query_code, key_code = refs[-4:]

        @pl.when(pl.program_id(0) == 0)
        def _():
            segment_codes(row_ref, query_code, key_code)

        ones = jnp.ones((16, BLOCK), BF)
        owner = lanes()[0]
        for pair in range(FORWARD_GROUP):
            at = slice(pair * PAIR, (pair + 1) * PAIR)
            query, key = q_ref[:, at] * BF(1.0 / math.sqrt(HD)), k_ref[:, at]
            value_turned = v_ref[:, at].T
            parts = []
            for head in range(2):
                scores = dot_nt(
                    jnp.where(owner == head, key, key_code[...]),
                    jnp.where(owner == head, query, query_code[...]),
                )
                highest = jnp.max(scores, axis=0, keepdims=True)
                exponent = jnp.exp(scores - highest).astype(BF)
                inside = slice(head * HD, (head + 1) * HD)
                part = dot(jnp.concatenate([value_turned[inside], ones], axis=0), exponent)
                total = part[HD : HD + 1]
                parts.append(part[:HD] / total)
                lse_ref[0, pair, head : head + 1, :] = highest + jnp.log(total)
            out_ref[:, at] = jnp.concatenate(parts, axis=0).T.astype(BF)

    flops = 4 * HEADS * BLOCK * BLOCK * HD
    given = () if into is None else into
    return pl.pallas_call(
        body,
        out_shape=(shape((count, width), BF), shape((blocks, pairs, 2, BLOCK), F32)),
        grid=(steps,),
        in_specs=[
            pl.BlockSpec((BLOCK, FORWARD_GROUP * PAIR), lambda p: (block, p)),
            pl.BlockSpec((BLOCK, FORWARD_GROUP * PAIR), lambda p: (block, steps + p)),
            pl.BlockSpec((BLOCK, FORWARD_GROUP * PAIR), lambda p: (block, 2 * steps + p)),
            pl.BlockSpec((1, 1, BLOCK), lambda p: (block, 0, 0)),
        ]
        + [any_spec()] * len(given),
        out_specs=(
            pl.BlockSpec((BLOCK, FORWARD_GROUP * PAIR), lambda p: (block, p)),
            pl.BlockSpec((1, FORWARD_GROUP, 2, BLOCK), lambda p: (block, p, 0, 0)),
        ),
        scratch_shapes=[pltpu.VMEM((BLOCK, PAIR), BF)] * 2,
        compiler_params=params("arbitrary"),
        cost_estimate=cost(4 * flops, 4 * count * width, HEADS * BLOCK * BLOCK),
        input_output_aliases={4 + index: index for index in range(len(given))},
    )(qkv, qkv, qkv, segment_row, *given)


def attend_backward(block, qkv, segment_row, lse, context, d_context, sums, into=None):
    count, wide = qkv.shape
    width = wide // 3
    pairs = width // PAIR
    steps = pairs // GROUP
    factor = 1.0 / math.sqrt(HD)

    def body(q_ref, k_ref, v_ref, o_ref, do_ref, row_ref, lse_ref, given_ref, *refs):
        dq_ref, dk_ref, dv_ref, sums_ref = refs[-4:]

        @pl.when(pl.program_id(0) == 0)
        def _():
            sums_ref[...] = given_ref[...]

        visible = same_segment(row_ref)
        masks = lane_masks()
        for pair in range(GROUP):
            at = slice(pair * PAIR, (pair + 1) * PAIR)
            query, key, value = q_ref[:, at] * BF(factor), k_ref[:, at], v_ref[:, at]
            d_out = do_ref[:, at]
            key_turned = key.T
            product = (d_out.astype(F32) * o_ref[:, at].astype(F32)).T
            d_query, d_key, d_value = [], [], []
            for head, chosen in enumerate(masks):
                inside = slice(head * HD, (head + 1) * HD)
                delta = jnp.sum(product[inside], axis=0, keepdims=True)
                scores = dot_nt(key, jnp.where(chosen, query, BF(0)))
                scores -= lse_ref[0, pair, head : head + 1, :]
                prob = jnp.exp(jnp.where(visible, scores, -1e30))
                d_prob = dot_nt(value, jnp.where(chosen, d_out, BF(0)))
                d_score = (prob * (d_prob - delta)).astype(BF)
                d_value.append(dot(prob.astype(BF), d_out))
                d_key.append(dot(d_score, query))
                d_query.append(dot(key_turned[inside], d_score) * factor)
            dq = jnp.concatenate(d_query, axis=0).T.astype(BF)
            dk = jnp.where(masks[0], d_key[0], d_key[1]).astype(BF)
            dv = jnp.where(masks[0], d_value[0], d_value[1]).astype(BF)
            dq_ref[:, at] = dq
            dk_ref[:, at] = dk
            dv_ref[:, at] = dv
            lane = (pl.program_id(0) * GROUP + pair) * PAIR
            here = pl.ds(pl.multiple_of(lane, PAIR), PAIR)
            add_rows(sums_ref.at[QUERY_SUM : QUERY_SUM + 1, here], dq.astype(F32))
            add_rows(sums_ref.at[QUERY_SUM + 1 : QUERY_SUM + 2, here], dv.astype(F32))

    tile = pl.BlockSpec((BLOCK, GROUP * PAIR), lambda p: (block, p))
    flops = 10 * HEADS * BLOCK * BLOCK * HD
    given = () if into is None else into
    return pl.pallas_call(
        body,
        out_shape=(shape((count, width), BF),) * 3 + (shape((24, width), F32),),
        grid=(steps,),
        in_specs=[
            tile,
            pl.BlockSpec((BLOCK, GROUP * PAIR), lambda p: (block, steps + p)),
            pl.BlockSpec((BLOCK, GROUP * PAIR), lambda p: (block, 2 * steps + p)),
            tile,
            tile,
            pl.BlockSpec((1, 1, BLOCK), lambda p: (block, 0, 0)),
            pl.BlockSpec((1, GROUP, 2, BLOCK), lambda p: (block, p, 0, 0)),
            fixed(24, width),
        ]
        + [any_spec()] * len(given),
        out_specs=(tile,) * 3 + (fixed(24, width),),
        compiler_params=params("arbitrary"),
        cost_estimate=cost(4 * flops, 8 * count * width, HEADS * BLOCK * BLOCK),
        input_output_aliases={8 + index: index for index in range(len(given))},
    )(qkv, qkv, qkv, context, d_context, segment_row, lse, sums, *given)


def emit(plan, step, held, spot_ref, out_refs, sems):
    tile, blocks, (rows, cols), _, base = plan
    if blocks is None:
        target = out_refs[0].at[:, pl.ds(pl.multiple_of(step * tile, tile), tile)]
        pltpu.make_async_copy(held.at[step], target, sems.at[step]).start()
        return
    listed = blocks(step)
    for index, (row_at, column_at, x, core, z, y) in enumerate(listed):
        source = held.at[step, pl.ds(row_at, rows), pl.ds(column_at, cols)]
        sem = sems.at[step * len(listed) + index]
        far_x, far_y = x ^ spot_ref[0], y ^ spot_ref[3]
        first = far_x + core * (far_y - far_x)
        depth = z ^ spot_ref[2]
        slot = (depth & 1) + 2 * first + 4 * (far_x + far_y - first) + 8 * (depth >> 1)
        mine = (core ^ spot_ref[1]) == 0

        @pl.when(mine)
        def _():
            pltpu.make_async_copy(source, out_refs[0].at[slot, pl.ds(base, rows)], sem).start()

        @pl.when(jnp.logical_not(mine))
        def _():
            pltpu.make_async_copy(source, out_refs[1].at[slot, pl.ds(base, rows)], sem).start()


def emitted(plan, steps, held, out_refs, sems):
    tile, blocks, (rows, cols), _, base = plan
    if blocks is None:
        for step in range(steps):
            target = out_refs[0].at[:, pl.ds(step * tile, tile)]
            pltpu.make_async_copy(held.at[step], target, sems.at[step]).wait()
        return
    for index in range(32):
        source = held.at[0, pl.ds(0, rows), pl.ds(0, cols)]
        pltpu.make_async_copy(source, out_refs[0].at[0, pl.ds(base, rows)], sems.at[index]).wait()


def emit_shapes(plan, total, columns):
    _, blocks, (rows, cols), slot_rows, _ = plan
    if blocks is None:
        return (shape((total, columns), BF),)
    return (shape((16, slot_rows, cols), BF),) * 2


def clamped(width, last, tile=TILE):
    return pl.BlockSpec((tile, width), lambda i, s: (jnp.minimum(i, last), 0))


def project_out(spot, context, tokens, w_out, biases, gains):
    count, width = tokens.shape

    def body(spot_ref, c_ref, x_ref, bias_ref, gain_ref, w_ready, normal_ref, inverse_ref, low_ref):
        w_ref = w_ready()
        resid = x_ref[...].astype(F32) + (dot_nt(c_ref[...], w_ref[...]) + bias_ref[2:3])
        normal, inverse = layer_norm_parts(resid)
        normal_ref[...] = normal
        inverse_ref[...] = jnp.broadcast_to(inverse, inverse_ref.shape)
        low_ref[...] = (normal * gain_ref[0:1] + bias_ref[3:4]).astype(BF)

    return call(
        body, (count // WIDE_TILE,), spot, (context, tokens, biases, gains),
        (row(width, WIDE_TILE), row(width, WIDE_TILE), fixed(*biases.shape), fixed(*gains.shape)), [w_out],
        (shape((count, width), F32), shape((count, 128), F32), shape((count, width), BF)),
        (row(width, WIDE_TILE), row(128, WIDE_TILE), row(width, WIDE_TILE)),
        estimate=cost(2 * count * width * width, 10 * count * width),
    )


def ffn_in(spot, normed_low, w_in, in_bias):
    count, width = normed_low.shape
    wide = w_in[2][1]

    def body(spot_ref, x_ref, bias_ref, w_ready, hidden_ref, slope_ref):
        w_ref = w_ready()
        for start in range(0, wide, width):
            part = slice(start, start + width)
            pre = dot(x_ref[...], w_ref[:, part]) + bias_ref[:, part]
            cdf = 0.5 + 0.5 * lax.erf(pre * (1.0 / math.sqrt(2.0)))
            hidden_ref[:, part] = (pre * cdf).astype(BF)
            density = jnp.exp(pre * pre * -0.5) * (1.0 / math.sqrt(2.0 * math.pi))
            slope_ref[:, part] = (cdf + pre * density).astype(BF)

    return call(
        body, (count // TILE,), spot, (normed_low, in_bias), (row(width), fixed(1, wide)), [w_in],
        (shape((count, wide), BF),) * 2, (row(wide),) * 2,
        estimate=cost(2 * count * width * wide, 4 * count * wide, 2 * count * wide),
    )


def forward_rows(spot, hidden, normal_one, out_grad, w_back, biases, gains, plan):
    count, width = out_grad.shape
    wide = hidden.shape[1]
    steps = count // TILE
    tile = plan[0]
    columns = wide // tile
    shapes = emit_shapes(plan, width, wide)

    def body(spot_ref, h_ref, column_ref, n_ref, g_ref, bias_ref, gain_ref, wb_ready,
             out_ref, d_two_ref, d_low_ref, sums_ref, *refs):
        grads, (d_rows, turned, held, sems) = refs[: len(shapes)], refs[len(shapes) :]
        index = pl.program_id(0)
        zero_first(sums_ref)

        @pl.when(index < steps)
        def _():
            here = pl.ds(pl.multiple_of(index * TILE, TILE), TILE)
            resid = n_ref[...] * gain_ref[0:1] + bias_ref[3:4]
            w_ref = wb_ready()
            resid += dot_nt(h_ref[...], w_ref[...]) + bias_ref[4:5]
            normal, inverse = layer_norm_parts(resid)
            out_ref[...] = (normal * gain_ref[1:2] + bias_ref[5:6]).astype(BF)
            grad = g_ref[...].astype(F32)
            d_two = layer_norm_back(grad * gain_ref[1:2], normal, inverse)
            d_low = d_two.astype(BF)
            d_two_ref[...] = d_two
            d_low_ref[...] = d_low
            d_rows[here, :] = d_low
            add_rows(sums_ref.at[0:1], grad * normal)
            add_rows(sums_ref.at[1:2], grad)
            add_rows(sums_ref.at[2:3], d_low.astype(F32))

        @pl.when(index == steps)
        def _():
            turned[...] = d_rows[...].T

        @pl.when(index >= steps)
        def _():
            column = index - steps
            held[column] = dot(turned[...], column_ref[...]).astype(BF)
            emit(plan, column, held, spot_ref, grads, sems)

        @pl.when(index == steps + columns - 1)
        def _():
            emitted(plan, columns, held, grads, sems)

    last = steps - 1
    rows = lambda wide_: clamped(wide_, last)
    return call(
        body, (steps + columns,), spot, (hidden, hidden, normal_one, out_grad, biases, gains),
        (rows(wide), pl.BlockSpec((count, tile), lambda i, s: (0, jnp.maximum(i - steps, 0))),
         rows(width), rows(width), fixed(*biases.shape), fixed(*gains.shape)),
        [w_back],
        (shape((count, width), BF), shape((count, width), F32), shape((count, width), BF),
         shape((8, width), F32), *shapes),
        (rows(width), rows(width), rows(width), fixed(8, width), *[any_spec()] * len(shapes)),
        [pltpu.VMEM((count, width), BF),
         pltpu.VMEM((width, count), BF), pltpu.VMEM((columns, width, tile), BF),
         pltpu.SemaphoreType.DMA((32,))],
        cost(4 * count * width * wide, 14 * count * width + 4 * count * wide),
    )


def backward_rows(
    spot, d_low, slope, d_two, normal_one, inverse_one, normed_low, context, sums_two, w_back, w_in,
    w_out, gains, plan_in, plan_out,
):
    count, width = d_two.shape
    wide = slope.shape[1]
    steps = count // TILE
    tile_in, tile_out = plan_in[0], plan_out[0]
    columns_in, columns_out = wide // tile_in, width // tile_out
    shared = plan_in[1] is not None
    shapes = emit_shapes(plan_in, width, wide)
    if not shared:
        shapes += emit_shapes(plan_out, width, width)

    def body(spot_ref, dl_ref, s_ref, d2_ref, n_ref, i_ref, low_ref, c_ref, two_ref, gain_ref,
             wb_ready, wi_ready, wo_ready, d_one_ref, d_context_ref, sums_ref, *refs):
        grads = refs[: len(shapes)]
        d_pre, d_attn, turned, held_in, held_out, low_held, sems_in, sems_out, late = refs[
            len(shapes) :
        ]
        fetch_low = pltpu.make_async_copy(low_ref, low_held, late.at[0])
        grads_in, grads_out = (grads, grads) if shared else (grads[:1], grads[1:])
        index = pl.program_id(0)

        @pl.when(index == 0)
        def _():
            sums_ref[...] = jnp.zeros_like(sums_ref)
            sums_ref[0:8, :] = two_ref[...]
            fetch_low.start()

        @pl.when(index < steps)
        def _():
            here = pl.ds(pl.multiple_of(index * TILE, TILE), TILE)
            w_ref = wb_ready()
            pieces = []
            for start in range(0, wide, width):
                part = slice(start, start + width)
                d_hidden = dot(dl_ref[...], w_ref[:, part])
                piece = (d_hidden * s_ref[:, part].astype(F32)).astype(BF)
                d_pre[here, part] = piece
                pieces.append(piece)
                at = HIDDEN_SUM + start // width
                add_rows(sums_ref.at[at : at + 1], piece.astype(F32))
            w_ref = wi_ready()
            d_normed = d2_ref[...]
            for number, piece in enumerate(pieces):
                d_normed += dot_nt(piece, w_ref[:, number * width : (number + 1) * width])
            normal = n_ref[...]
            d_one = layer_norm_back(d_normed * gain_ref[0:1], normal, i_ref[:, 0:1])
            low = d_one.astype(BF)
            d_one_ref[...] = d_one
            d_attn[here, :] = low
            d_context_ref[...] = dot(low, wo_ready()[...]).astype(BF)
            add_rows(sums_ref.at[8:9], d_normed * normal)
            add_rows(sums_ref.at[9:10], d_normed)
            add_rows(sums_ref.at[10:11], low.astype(F32))

        @pl.when(index == steps)
        def _():
            fetch_low.wait()
            turned[...] = low_held[...].T

        @pl.when(jnp.logical_and(index >= steps, index < steps + columns_in))
        def _():
            column = index - steps
            at = pl.ds(pl.multiple_of(column * tile_in, tile_in), tile_in)
            held_in[column] = dot(turned[...], d_pre[:, at]).astype(BF)
            emit(plan_in, column, held_in, spot_ref, grads_in, sems_in)

        @pl.when(index == steps + columns_in)
        def _():
            turned[...] = d_attn[...].T

        @pl.when(index >= steps + columns_in)
        def _():
            column = index - steps - columns_in
            held_out[column] = dot(turned[...], c_ref[...]).astype(BF)
            emit(plan_out, column, held_out, spot_ref, grads_out, sems_out)

        @pl.when(index == steps + columns_in + columns_out - 1)
        def _():
            emitted(plan_in, columns_in, held_in, grads_in, sems_in)
            emitted(plan_out, columns_out, held_out, grads_out, sems_out)

    last, before = steps - 1, steps + columns_in
    rows = lambda wide_: clamped(wide_, last)
    return call(
        body, (steps + columns_in + columns_out,), spot,
        (d_low, slope, d_two, normal_one, inverse_one, normed_low, context, sums_two, gains),
        (rows(width), rows(wide), rows(width), rows(width), rows(128), any_spec(),
         pl.BlockSpec((count, tile_out), lambda i, s: (0, jnp.maximum(i - before, 0))),
         fixed(8, width), fixed(*gains.shape)),
        [w_back, w_in, w_out],
        (shape((count, width), F32), shape((count, width), BF), shape((24, width), F32), *shapes),
        (rows(width), rows(width), fixed(24, width), *[any_spec()] * len(shapes)),
        [pltpu.VMEM((count, wide), BF), pltpu.VMEM((count, width), BF),
         pltpu.VMEM((width, count), BF), pltpu.VMEM((columns_in, width, tile_in), BF),
         pltpu.VMEM((columns_out, width, tile_out), BF), pltpu.VMEM((count, width), BF),
         pltpu.SemaphoreType.DMA((32,)), pltpu.SemaphoreType.DMA((32,)),
         pltpu.SemaphoreType.DMA((1,))],
        cost(2 * count * width * (3 * wide + 2 * width), 18 * count * width + 2 * count * wide),
    )


def tokens_backward(spot, d_one, d_query, d_key, d_value, w_qkv):
    count, width = d_one.shape

    def body(spot_ref, d1_ref, q_ref, k_ref, v_ref, w_ready, out_ref):
        w_ref = w_ready()
        total = d1_ref[...] + dot(q_ref[...], w_ref[0:width, :])
        total += dot(k_ref[...], w_ref[width : 2 * width, :])
        total += dot(v_ref[...], w_ref[2 * width : 3 * width, :])
        out_ref[...] = total.astype(BF)

    return call(
        body, (count // TILE,), spot, (d_one, d_query, d_key, d_value), (row(width),) * 4, [w_qkv],
        shape((count, width), BF), row(width),
        estimate=cost(6 * count * width * width, 12 * count * width),
    )


def gradient(spot, lefts, right, plan):
    count, columns = right.shape
    width = lefts[0].shape[1]
    total = width * len(lefts)
    tile = plan[0]
    steps = columns // tile
    n_left = len(lefts)
    shapes = emit_shapes(plan, total, columns)

    def body(spot_ref, *refs):
        left_refs, right_ref = refs[:n_left], refs[n_left]
        grads = refs[n_left + 1 : n_left + 1 + len(shapes)]
        turned, held, sems = refs[-3:]
        step = pl.program_id(0)

        @pl.when(step == 0)
        def _():
            for index, ref in enumerate(left_refs):
                turned[index * width : (index + 1) * width, :] = ref[...].T

        for index in range(n_left):
            part = slice(index * width, (index + 1) * width)
            held[step, part, :] = dot(turned[part, :], right_ref[...]).astype(BF)
        emit(plan, step, held, spot_ref, grads, sems)

        @pl.when(step == steps - 1)
        def _():
            emitted(plan, steps, held, grads, sems)

    return call(
        body, (steps,), spot, (*lefts, right),
        (*[fixed(count, width)] * n_left, pl.BlockSpec((count, tile), lambda i, s: (0, i))), [],
        shapes, (any_spec(),) * len(shapes),
        [pltpu.VMEM((total, count), BF), pltpu.VMEM((steps, total, tile), BF),
         pltpu.SemaphoreType.DMA((32,))],
        cost(2 * count * total * columns, 2 * (count * (total + columns) + total * columns)),
    )


def widen(value):
    return value.astype(F32)


def exchange(value, stage):
    axes = ("x", "core", "z", "y")
    pairs = []
    for source in range(32):
        x, core, z, y = source >> 4, (source >> 3) & 1, (source >> 1) & 3, source & 1
        if stage in (Z1, Z2, Z3):
            z ^= {Z1: 1, Z2: 2, Z3: 3}[stage]
        elif stage == CORE:
            core ^= 1
        elif (stage == FIRST) == (core == 0):
            x ^= 1
        else:
            y ^= 1
        pairs.append((source, 16 * x + 8 * core + 2 * z + y))
    return lax.ppermute(value, axes, pairs)


class Parcel:
    def __init__(self, array, origins=((0, 0, 0, 0),)):
        self.array = array
        self.origins = tuple(origins)

    def moved(self, stage):
        def change(origin):
            core, second, first, depth = origin
            along_first = stage == (SECOND if core else FIRST)
            along_second = stage == (FIRST if core else SECOND)
            return (
                core ^ (stage == CORE),
                second ^ along_second,
                first ^ along_first,
                depth ^ {Z1: 1, Z2: 2}.get(stage, 0),
            )

        return Parcel(exchange(self.array, stage), [change(origin) for origin in self.origins])

    def __add__(self, other):
        return Parcel(jnp.concatenate([self.array, other.array]), self.origins + other.origins)


def sync(values, *parcels):
    values, arrays = lax.optimization_barrier((values, [parcel.array for parcel in parcels]))
    for parcel, array in zip(parcels, arrays):
        parcel.array = array
    return values


class Reduce:
    def __init__(self, near, far):
        self.near, self.far = near, Parcel(far)

    def send_core(self):
        self.core = Parcel(exchange(self.far.array, CORE))

    def sum(self, start, stop, *others):
        total = widen(self.near[start:stop]) + widen(self.core.array[start:stop])
        for parcel, at in others:
            total += widen(parcel.array[at : at + stop - start])
        return total

    def send(self, stage, start, stop, *others):
        return Parcel(exchange(self.sum(start, stop, *others).astype(BF), stage))

    def send_second_b(self):
        self.second_b = self.send(SECOND, 12, 16)

    def send_second_a(self):
        self.second_a = self.send(SECOND, 4, 8)

    def send_first_b(self):
        self.first_b = self.send(FIRST, 10, 12, (self.second_b, 2))

    def send_first_a(self):
        self.first_a = self.send(FIRST, 2, 4, (self.second_a, 2))

    def send_z2(self):
        self.z2 = self.send(Z2, 8, 10, (self.second_b, 0), (self.first_b, 0))

    def send_z1(self):
        self.z1 = self.send(Z1, 1, 2, (self.second_a, 1), (self.first_a, 1), (self.z2, 1))
        self.last = (self.z2, self.z1)

    def send_direct_b(self):
        self.z2 = self.send(Z2, 8, 9, (self.second_b, 0), (self.first_b, 0))
        self.z3 = self.send(Z3, 9, 10, (self.second_b, 1), (self.first_b, 1))

    def send_direct_a(self):
        self.z1 = self.send(Z1, 1, 2, (self.second_a, 1), (self.first_a, 1))
        self.last = (self.z1, self.z2, self.z3)

    def result(self):
        others = (self.second_a, self.first_a) + self.last
        return self.sum(0, 1, *[(parcel, 0) for parcel in others])[0]


def source_of(spot, origin):
    away, second, first, depth = origin
    core = spot[1] ^ away
    x = spot[0] ^ (first + core * (second - first))
    y = spot[3] ^ (second + core * (first - second))
    return core, x, 2 * (spot[2] ^ depth) + y


def weight_of(parcels, source_rows, place, dims):
    start, rows, cols = source_rows
    pieces, places = [], []
    for parcel in parcels:
        pieces.append(parcel.array)

        def at(spot_ref, ref, origins=parcel.origins):
            for index, origin in enumerate(origins):
                core, x, f = source_of(spot_ref, origin)
                row_at, column_at = place(x, core, f)
                yield (
                    ref.at[index, pl.ds(start, rows), :],
                    (
                        pl.ds(pl.multiple_of(row_at, 16), rows),
                        pl.ds(pl.multiple_of(column_at, 128), cols),
                    ),
                )

        places.append(at)
    return pieces, places, dims


def whole_weight(array):
    def at(spot_ref, ref):
        yield ref, (pl.ds(0, array.shape[0]), pl.ds(0, array.shape[1]))

    return [array], [at], array.shape


def device_slots(spot, origins):
    device = lax.broadcasted_iota(jnp.int32, (len(origins), len(origins)), 0)
    owners = []
    for origin in origins:
        core, x, f = source_of(spot, origin)
        owners.append(16 * x + 8 * core + f)
    return (device == jnp.stack(owners)[None, :]).astype(F32)


def small_vectors(every, shards):
    biases, in_bias, gains = shards
    devices = every.shape[0]
    first, second = biases.size, biases.size + in_bias.size
    third = second + gains.size
    return (
        every[:, :first].reshape(devices, 6, -1).transpose(1, 0, 2).reshape(6, -1),
        every[:, first:second].reshape(1, -1),
        every[:, second:third].reshape(devices, 2, -1).transpose(1, 0, 2).reshape(2, -1),
    )


def on_device(sizes, tokens, segment_ids, w_qkv, w_out, w_in, w_back, biases, in_bias, gains, out_grad):
    axes = ("x", "core", "z", "y")
    dp_axes, fsdp_axes = ("x", "core"), ("z", "y")
    devices = math.prod(sizes)
    by_permute = sizes == (2, 2, 4, 2)
    count, width = tokens.shape
    wide = w_back.shape[0] * sizes[0] * sizes[1]
    blocks = range(count // BLOCK)
    spot = jnp.stack([lax.axis_index(axis) for axis in axes]).astype(jnp.int32)
    core = spot[1]
    shards = (biases, in_bias, gains)
    segment_row = segment_ids.reshape(count // BLOCK, 1, BLOCK)

    qkv_cols, out_cols = w_qkv.shape[1], w_out.shape[1]
    pair_cols = 2 * w_qkv.shape[0]
    in_rows, in_cols = w_in.shape
    back_rows, back_cols = w_back.shape
    half_q, half_o = qkv_cols // 2, out_cols // 2

    if by_permute:

        def paired(turned):
            half = turned.shape[0] // 2
            first, second = turned[:half], turned[half:]
            mine = jnp.where(core == 0, first, second)
            other = exchange(jnp.where(core == 0, second, first), CORE)
            return jnp.where(
                core == 0,
                jnp.concatenate([mine, other], axis=1),
                jnp.concatenate([other, mine], axis=1),
            )

        to_qkv = Parcel(paired(w_qkv.T)[None])
        qkv_z1 = to_qkv.moved(Z1)
        own_vectors, w_in = sync(((biases, in_bias, gains), w_in), to_qkv)
        own_small = jnp.concatenate([part.reshape(-1) for part in own_vectors])
        to_small = Parcel(jnp.pad(own_small, (0, 1024 - own_small.size)).reshape(1, 8, 128))
        to_small += to_small.moved(CORE)
        w_in, w_out, w_back = sync((w_in, w_out, w_back), qkv_z1, to_small)
        qkv_near = to_qkv + qkv_z1
        qkv_z2 = qkv_near.moved(Z2)
        qkv_first_a = qkv_near.moved(FIRST)
        to_small += to_small.moved(FIRST)
        to_in = Parcel(jnp.concatenate([w_in, paired(w_out.T)], axis=0)[None])
        to_back = Parcel(w_back.T[None])
        sync((), qkv_first_a, to_small, to_in)
        qkv_a = qkv_near + qkv_first_a
        qkv_second_a = qkv_a.moved(SECOND)
        in_z1 = to_in.moved(Z1)
        to_small += to_small.moved(SECOND)
        sync((), qkv_z2)
        qkv_first_b = qkv_z2.moved(FIRST)
        sync((), qkv_z2, to_small)
        to_small += to_small.moved(Z1)
        sync((), qkv_first_b, to_small)
        qkv_b = qkv_z2 + qkv_first_b
        qkv_second_b = qkv_b.moved(SECOND)
        to_small += to_small.moved(Z2)
        sync((), qkv_first_b, qkv_second_a, to_small, in_z1)
        qkv_core_a = qkv_a.moved(CORE), qkv_second_a.moved(CORE)
        in_near = to_in + in_z1
        in_z2 = in_near.moved(Z2)
        sync((), qkv_second_b, in_near, to_back)
        qkv_core_b = qkv_b.moved(CORE), qkv_second_b.moved(CORE)
        in_first_a = in_near.moved(FIRST)
        back_z1 = to_back.moved(Z1)
        tokens = sync(tokens, *qkv_core_a, *qkv_core_b)
        qkv_parcels = (
            qkv_a, qkv_second_a, qkv_b, qkv_second_b, *qkv_core_a, *qkv_core_b
        )
        qkv_weight = weight_of(
            qkv_parcels, (0, half_q, pair_cols),
            lambda x, c, f: (f * qkv_cols + c * half_q, x * pair_cols), (3 * width, width),
        )
        slots = device_slots(spot, to_small.origins)
        arrived = widen(to_small.array).reshape(32, 1024)
        every = jnp.dot(slots, arrived, precision=lax.Precision.HIGHEST)

        def back_blocks(index):
            return [(f * back_cols, 0, index >> 1, index & 1, f >> 1, f & 1) for f in range(8)]

        def in_blocks(index):
            return [
                ((2 * x + c) * in_rows, y * in_cols, x, c, index, y)
                for x in range(2) for c in range(2) for y in range(2)
            ]

        def out_blocks(index):
            return [
                (f * out_cols + c * half_o, 0, index, c, f >> 1, f & 1)
                for f in range(8) for c in range(2)
            ]

        def qkv_blocks(index):
            return [
                (f * qkv_cols + c * half_q, 0, index, c, f >> 1, f & 1)
                for f in range(8) for c in range(2)
            ]

        plans = {
            "back": (back_rows, back_blocks, (back_cols, back_rows), back_cols, 0),
            "in": (2 * in_cols, in_blocks, (in_rows, in_cols), in_rows + half_o, 0),
            "out": (pair_cols, out_blocks, (half_o, pair_cols), in_rows + half_o, in_rows),
            "qkv": (pair_cols, qkv_blocks, (half_q, pair_cols), half_q, 0),
        }
    else:

        def full(shard):
            return lax.all_gather(
                lax.all_gather(shard, fsdp_axes, axis=1, tiled=True), dp_axes, axis=0, tiled=True
            )

        qkv_weight = whole_weight(full(w_qkv).T)
        out_weight = whole_weight(full(w_out).T)
        in_weight = whole_weight(full(w_in))
        back_weight = whole_weight(full(w_back).T)
        own_small = jnp.concatenate([biases.reshape(-1), in_bias, gains.reshape(-1)])
        every = widen(lax.all_gather(own_small, axes, axis=0, tiled=False))
        plans = {name: (width // 2, None, (0, 0), 0, 0) for name in ("back", "in", "out", "qkv")}

    bias_values, hidden_bias, gain_values = small_vectors(every, shards)
    qkv_bias = jnp.concatenate(
        [bias_values[0:1], jnp.zeros((1, width), F32), bias_values[1:2]], axis=1
    )

    qkv = project_qkv(spot, tokens, qkv_weight, qkv_bias)
    if by_permute:
        qkv = sync(qkv, in_first_a, in_z2, back_z1)
        in_a = in_near + in_first_a
        in_second_a = in_a.moved(SECOND)
        in_first_b = in_z2.moved(FIRST)
        back_near = to_back + back_z1
        back_z2 = back_near.moved(Z2)
    attended = None
    for block in blocks:
        attended = attend_forward(block, qkv, segment_row, attended)
        if by_permute and block == 0:
            attended = sync(attended, in_second_a, in_first_b, back_z2)
            in_b = in_z2 + in_first_b
            in_second_b = in_b.moved(SECOND)
            in_core = in_a.moved(CORE), in_second_a.moved(CORE), in_b.moved(CORE)
            back_first_a = back_near.moved(FIRST)
    context, lse = attended
    if by_permute:
        context = sync(context, in_second_b, *in_core, back_first_a)
        in_cross = in_second_b.moved(CORE)
        back_a = back_near + back_first_a
        back_second_a = back_a.moved(SECOND)
        back_first_b = back_z2.moved(FIRST)
        context = sync(context, in_cross)
        in_parcels = (in_a, in_second_a, in_b, in_second_b, *in_core, in_cross)
        in_weight = weight_of(
            in_parcels, (0, in_rows, in_cols),
            lambda x, c, f: ((2 * x + c) * in_rows, f * in_cols), (width, wide),
        )
        out_weight = weight_of(
            in_parcels, (in_rows, half_o, pair_cols),
            lambda x, c, f: (f * out_cols + c * half_o, x * pair_cols), (width, width),
        )
    normal_one, inverse_one, normed_low = project_out(
        spot, context, tokens, out_weight, bias_values, gain_values
    )
    if by_permute:
        normed_low = sync(normed_low, back_second_a, back_first_b)
        back_b = back_z2 + back_first_b
        back_second_b = back_b.moved(SECOND)
        back_core = back_a.moved(CORE), back_second_a.moved(CORE), back_b.moved(CORE)
    hidden, slope = ffn_in(spot, normed_low, in_weight, hidden_bias)
    if by_permute:
        hidden = sync(hidden, back_second_b, *back_core)
        back_cross = back_second_b.moved(CORE)
        back_weight = weight_of(
            (back_a, back_second_a, back_b, back_second_b, *back_core, back_cross),
            (0, back_cols, back_rows),
            lambda x, c, f: (f * back_cols, (2 * x + c) * back_rows), (width, wide),
        )
    layer_out, d_two, d_low, sums_two, *grad_back = forward_rows(
        spot, hidden, normal_one, out_grad, back_weight, bias_values, gain_values, plans["back"]
    )
    if by_permute:
        from_back = Reduce(*grad_back)
        d_low = sync(d_low, from_back.far)
        from_back.send_core()
    d_one, d_context, small, *grads_in = backward_rows(
        spot, d_low, slope, d_two, normal_one, inverse_one, normed_low, context, sums_two,
        back_weight, in_weight, out_weight, gain_values, plans["in"], plans["out"],
    )
    if by_permute:
        from_in = Reduce(*grads_in)
        d_context = sync(d_context, from_back.core, from_in.far)
        from_back.send_second_b()
        from_back.send_second_a()
        from_in.send_core()
    else:
        grad_in, grad_out = grads_in
        grad_back, = grad_back
    attended = None
    for block in blocks:
        *attended, small = attend_backward(
            block, qkv, segment_row, lse, context, d_context, small, attended
        )
        if by_permute and block == 0:
            attended = sync(attended, from_back.second_a, from_back.second_b, from_in.core)
            from_back.send_first_b()
            from_back.send_first_a()
            from_in.send_second_b()
        elif by_permute:
            attended, small = sync(
                (attended, small), from_back.first_a, from_back.first_b, from_in.second_b
            )
            from_in.send_second_a()
            from_in.send_first_b()
            from_back.send_z2()
            small_sent = Parcel(small).moved(CORE)
    grad_qkv = gradient(spot, attended, tokens, plans["qkv"])
    if by_permute:
        from_qkv = Reduce(*grad_qkv)
        small = sync(small, from_qkv.far, small_sent, from_in.second_a, from_in.first_b)
        from_qkv.send_core()
        small = small + small_sent.array
        small_sent = Parcel(small).moved(Z1)
        from_in.send_z2()
        d_one = sync(d_one, from_qkv.core)
        from_qkv.send_second_b()
        from_qkv.send_second_a()
    else:
        grad_qkv, = grad_qkv
    tokens_grad = tokens_backward(spot, d_one, *attended, qkv_weight)

    if by_permute:

        def unpaired(sums):
            half = sums.shape[1] // 2
            left, right = sums[:, :half], sums[:, half:]
            mine = jnp.where(core == 0, left, right)
            other = widen(exchange(jnp.where(core == 0, right, left).astype(BF), CORE))
            return jnp.where(
                core == 0,
                jnp.concatenate([mine, other], axis=0),
                jnp.concatenate([other, mine], axis=0),
            )

        tokens_grad, small = sync(
            (tokens_grad, small), from_qkv.second_b, from_qkv.second_a, small_sent, from_back.z2
        )
        from_qkv.send_first_b()
        from_qkv.send_first_a()
        from_in.send_first_a()
        from_back.send_z1()
        small = small + small_sent.array
        small_sent = Parcel(small).moved(SECOND)
        sync((), from_qkv.first_b)
        from_qkv.send_direct_b()
        small = sync(small, from_qkv.first_a)
        from_qkv.send_direct_a()
        small = sync(small, small_sent, from_in.first_a, from_in.z2)
        from_in.send_z1()
        small = small + small_sent.array
        small_sent = Parcel(small).moved(FIRST)
        small = sync(small, small_sent, from_back.z1)
        small = small + small_sent.array
        small_sent = Parcel(small).moved(Z2)
        small = sync(small, small_sent, from_in.z1)
        small = small + small_sent.array
        sums_in = from_in.result()
        own_back = from_back.result().T
        own_in = sums_in[:in_rows]
        own_out = unpaired(sums_in[in_rows:]).T
        own_qkv = unpaired(from_qkv.result()).T
    else:

        def scattered(total):
            part = lax.psum_scatter(total, dp_axes, scatter_dimension=0, tiled=True)
            part = lax.psum_scatter(part, fsdp_axes, scatter_dimension=1, tiled=True)
            return widen(part)

        own_back = scattered(grad_back.T)
        own_in = scattered(grad_in)
        own_out = scattered(grad_out.T)
        own_qkv = scattered(grad_qkv.T)
        small = lax.psum(small, axes)
    device = lax.axis_index(axes)
    queries = small[QUERY_SUM : QUERY_SUM + 2]
    bias_total = jnp.concatenate([queries, small[10:11], small[9:10], small[2:3], small[1:2]])
    gain_total = jnp.concatenate([small[8:9], small[0:1]])
    own_bias = lax.dynamic_slice_in_dim(bias_total, device * biases.shape[1], biases.shape[1], 1)
    own_gain = lax.dynamic_slice_in_dim(gain_total, device * gains.shape[1], gains.shape[1], 1)
    own_hidden = lax.dynamic_slice_in_dim(
        small[HIDDEN_SUM:QUERY_SUM].reshape(-1), device * in_bias.shape[0], in_bias.shape[0], 0
    )
    return (
        layer_out, tokens_grad, own_qkv, own_out, own_in, own_back, own_bias, own_hidden, own_gain,
    )


def solution(mesh):
    dp, fsdp = mesh.devices.shape
    sizes = (dp // 2, 2, fsdp // 2, 2)
    split = Mesh(mesh.devices.reshape(sizes), ("x", "core", "z", "y"))
    outer, inner = ("x", "core"), ("z", "y")
    every = outer + inner
    rows = P(every, None)
    weight = P(outer, inner)
    vectors = P(None, every)

    def placed(*arrays):
        return on_device(sizes, *arrays)

    return jax.shard_map(
        placed,
        mesh=split,
        in_specs=(rows, rows, weight, weight, weight, weight, vectors, P(every), vectors, rows),
        out_specs=(rows, rows, weight, weight, weight, weight, vectors, P(every), vectors),
        check_vma=False,
    )
```

```python
import math

import jax
import jax.numpy as jnp
from jax import lax
from jax.experimental import pallas as pl
from jax.experimental.pallas import tpu as pltpu
from jax.sharding import Mesh, PartitionSpec as P

HEADS = 12
HD = 64
DOCS = 8
BLOCK = 512
PAIR = 2 * HD
GROUP = 2
FORWARD_GROUP = 3
TILE = 256
WIDE_TILE = 512
VMEM = 58 * 1024 * 1024
BF = jnp.bfloat16
F32 = jnp.float32
Z1, Z2, FIRST, SECOND, CORE, Z3 = range(6)
HIDDEN_SUM, QUERY_SUM = 16, 20
NT = (((1,), (1,)), ((), ()))


def dot(a, b):
    return jnp.dot(a, b, preferred_element_type=F32)


def dot_nt(a, b):
    return lax.dot_general(a, b, NT, preferred_element_type=F32)


def any_spec():
    return pl.BlockSpec(memory_space=pl.ANY)


def params(*semantics):
    return pltpu.CompilerParams(
        dimension_semantics=semantics if semantics else None, vmem_limit_bytes=VMEM
    )


def cost(flops, nbytes, trans=0):
    return pl.CostEstimate(flops=flops, bytes_accessed=nbytes, transcendentals=trans)

def layer_norm_parts(rows):
    center = jnp.mean(rows, axis=-1, keepdims=True)
    centered = rows - center
    spread = jnp.mean(centered * centered, axis=-1, keepdims=True)
    inverse = lax.rsqrt(spread + 1e-05)
    return centered * inverse, inverse


def layer_norm_back(grad, normal, inverse):
    mean_grad = jnp.mean(grad, axis=-1, keepdims=True)
    mean_both = jnp.mean(grad * normal, axis=-1, keepdims=True)
    return (grad - mean_grad - normal * mean_both) * inverse


def add_rows(ref, values):
    ref[...] += jnp.sum(values, axis=0, keepdims=True)


def zero_first(*refs):
    @pl.when(pl.program_id(0) == 0)
    def _():
        for ref in refs:
            ref[...] = jnp.zeros_like(ref)


def call(
    body, grid, spot, arrays, specs, weights, outs, out_specs, scratch=(), estimate=None, aliases=()
):
    flat = [piece for pieces, _, _ in weights for piece in pieces]
    counts = [len(pieces) for pieces, _, _ in weights]
    n_arrays, n_flat, n_weights = len(arrays), len(flat), len(weights)
    n_outs = len(outs) if isinstance(outs, tuple) else 1

    def kernel(spot_ref, *refs):
        ins = refs[:n_arrays]
        piece_refs = refs[n_arrays : n_arrays + n_flat]
        out_refs = refs[n_arrays + n_flat : n_arrays + n_flat + n_outs]
        rest = refs[n_arrays + n_flat + n_outs :]
        held = rest[:n_weights]
        sems = rest[n_weights : 2 * n_weights]
        extra = rest[2 * n_weights :]
        first = pl.program_id(0) == 0

        def copies(number):
            start = sum(counts[:number])
            found = []
            for index in range(counts[number]):
                place = weights[number][1][index]
                for source, at in place(spot_ref, piece_refs[start + index]):
                    found.append(
                        pltpu.make_async_copy(
                            source, held[number].at[at], sems[number].at[len(found)]
                        )
                    )
            return found

        @pl.when(first)
        def _():
            for number in range(n_weights):
                for copy in copies(number):
                    copy.start()

        def ready(number):
            def wait():
                @pl.when(first)
                def _():
                    for copy in copies(number):
                        copy.wait()

                return held[number]

            return wait

        body(spot_ref, *ins, *[ready(number) for number in range(n_weights)], *out_refs, *extra)

    scratch_shapes = (
        [pltpu.VMEM(shape, BF) for _, _, shape in weights]
        + [pltpu.SemaphoreType.DMA((32,)) for _ in counts]
        + list(scratch)
    )
    return pl.pallas_call(
        kernel,
        out_shape=outs,
        grid_spec=pltpu.PrefetchScalarGridSpec(
            num_scalar_prefetch=1,
            grid=grid,
            in_specs=list(specs) + [any_spec()] * n_flat,
            out_specs=out_specs,
            scratch_shapes=scratch_shapes,
        ),
        compiler_params=params(*(["arbitrary"] * len(grid))),
        cost_estimate=estimate,
        input_output_aliases=dict(aliases),
    )(spot, *arrays, *flat)


def row(width, tile=TILE):
    return pl.BlockSpec((tile, width), lambda i, s: (i, 0))


def fixed(*shape):
    return pl.BlockSpec(shape, lambda *_: (0,) * len(shape))


def shape(dims, dtype):
    return jax.ShapeDtypeStruct(dims, dtype)


def project_qkv(spot, tokens, w_qkv, qkv_bias):
    count, width = tokens.shape
    wide = w_qkv[2][0]

    def body(spot_ref, x_ref, bias_ref, w_ready, out_ref):
        w_ref = w_ready()
        for start in range(0, wide, width):
            part = slice(start, start + width)
            out_ref[:, part] = (dot_nt(x_ref[...], w_ref[part, :]) + bias_ref[:, part]).astype(BF)

    return call(
        body, (count // TILE,), spot, (tokens, qkv_bias), (row(width), fixed(1, wide)), [w_qkv],
        shape((count, wide), BF), row(wide),
        estimate=cost(2 * count * width * wide, 2 * (count * width + wide * width + count * wide)),
    )


def lane_masks():
    lane = lax.broadcasted_iota(jnp.int32, (1, PAIR), 1)
    return [(lane // HD == head) for head in range(2)]


def same_segment(row_ref):
    numbers = row_ref[0].astype(F32)
    column = jnp.broadcast_to(numbers, (128, BLOCK)).T[:, 0:1]
    return column == numbers


def lanes():
    lane = lax.broadcasted_iota(jnp.int32, (1, PAIR), 1)
    return lane // HD, lane % HD


def segment_codes(row_ref, query_ref, key_ref):
    numbers = jnp.broadcast_to(row_ref[0].astype(F32), (PAIR, BLOCK)).T
    inner = lanes()[1].astype(F32)
    same = inner == numbers
    query_ref[...] = jnp.where(same, 1.0, 0.0).astype(BF)
    key_ref[...] = jnp.where(jnp.logical_or(same, inner >= DOCS), 0.0, -1e30).astype(BF)


def attend_forward(block, qkv, segment_row, into=None):
    count, wide = qkv.shape
    width = wide // 3
    pairs = width // PAIR
    steps = pairs // FORWARD_GROUP
    blocks = count // BLOCK

    def body(q_ref, k_ref, v_ref, row_ref, *refs):
        out_ref, lse_ref, query_code, key_code = refs[-4:]

        @pl.when(pl.program_id(0) == 0)
        def _():
            segment_codes(row_ref, query_code, key_code)

        ones = jnp.ones((16, BLOCK), BF)
        owner = lanes()[0]
        for pair in range(FORWARD_GROUP):
            at = slice(pair * PAIR, (pair + 1) * PAIR)
            query, key = q_ref[:, at] * BF(1.0 / math.sqrt(HD)), k_ref[:, at]
            value_turned = v_ref[:, at].T
            parts = []
            for head in range(2):
                scores = dot_nt(
                    jnp.where(owner == head, key, key_code[...]),
                    jnp.where(owner == head, query, query_code[...]),
                )
                highest = jnp.max(scores, axis=0, keepdims=True)
                exponent = jnp.exp(scores - highest).astype(BF)
                inside = slice(head * HD, (head + 1) * HD)
                part = dot(jnp.concatenate([value_turned[inside], ones], axis=0), exponent)
                total = part[HD : HD + 1]
                parts.append(part[:HD] / total)
                lse_ref[0, pair, head : head + 1, :] = highest + jnp.log(total)
            out_ref[:, at] = jnp.concatenate(parts, axis=0).T.astype(BF)

    flops = 4 * HEADS * BLOCK * BLOCK * HD
    given = () if into is None else into
    return pl.pallas_call(
        body,
        out_shape=(shape((count, width), BF), shape((blocks, pairs, 2, BLOCK), F32)),
        grid=(steps,),
        in_specs=[
            pl.BlockSpec((BLOCK, FORWARD_GROUP * PAIR), lambda p: (block, p)),
            pl.BlockSpec((BLOCK, FORWARD_GROUP * PAIR), lambda p: (block, steps + p)),
            pl.BlockSpec((BLOCK, FORWARD_GROUP * PAIR), lambda p: (block, 2 * steps + p)),
            pl.BlockSpec((1, 1, BLOCK), lambda p: (block, 0, 0)),
        ]
        + [any_spec()] * len(given),
        out_specs=(
            pl.BlockSpec((BLOCK, FORWARD_GROUP * PAIR), lambda p: (block, p)),
            pl.BlockSpec((1, FORWARD_GROUP, 2, BLOCK), lambda p: (block, p, 0, 0)),
        ),
        scratch_shapes=[pltpu.VMEM((BLOCK, PAIR), BF)] * 2,
        compiler_params=params("arbitrary"),
        cost_estimate=cost(4 * flops, 4 * count * width, HEADS * BLOCK * BLOCK),
        input_output_aliases={4 + index: index for index in range(len(given))},
    )(qkv, qkv, qkv, segment_row, *given)


def attend_backward(block, qkv, segment_row, lse, context, d_context, sums, into=None):
    count, wide = qkv.shape
    width = wide // 3
    pairs = width // PAIR
    steps = pairs // GROUP
    factor = 1.0 / math.sqrt(HD)

    def body(q_ref, k_ref, v_ref, o_ref, do_ref, row_ref, lse_ref, given_ref, *refs):
        dq_ref, dk_ref, dv_ref, sums_ref = refs[-4:]

        @pl.when(pl.program_id(0) == 0)
        def _():
            sums_ref[...] = given_ref[...]

        visible = same_segment(row_ref)
        masks = lane_masks()
        for pair in range(GROUP):
            at = slice(pair * PAIR, (pair + 1) * PAIR)
            query, key, value = q_ref[:, at] * BF(factor), k_ref[:, at], v_ref[:, at]
            d_out = do_ref[:, at]
            key_turned = key.T
            product = (d_out.astype(F32) * o_ref[:, at].astype(F32)).T
            d_query, d_key, d_value = [], [], []
            for head, chosen in enumerate(masks):
                inside = slice(head * HD, (head + 1) * HD)
                delta = jnp.sum(product[inside], axis=0, keepdims=True)
                scores = dot_nt(key, jnp.where(chosen, query, BF(0)))
                scores -= lse_ref[0, pair, head : head + 1, :]
                prob = jnp.exp(jnp.where(visible, scores, -1e30))
                d_prob = dot_nt(value, jnp.where(chosen, d_out, BF(0)))
                d_score = (prob * (d_prob - delta)).astype(BF)
                d_value.append(dot(prob.astype(BF), d_out))
                d_key.append(dot(d_score, query))
                d_query.append(dot(key_turned[inside], d_score) * factor)
            dq = jnp.concatenate(d_query, axis=0).T.astype(BF)
            dk = jnp.where(masks[0], d_key[0], d_key[1]).astype(BF)
            dv = jnp.where(masks[0], d_value[0], d_value[1]).astype(BF)
            dq_ref[:, at] = dq
            dk_ref[:, at] = dk
            dv_ref[:, at] = dv
            lane = (pl.program_id(0) * GROUP + pair) * PAIR
            here = pl.ds(pl.multiple_of(lane, PAIR), PAIR)
            add_rows(sums_ref.at[QUERY_SUM : QUERY_SUM + 1, here], dq.astype(F32))
            add_rows(sums_ref.at[QUERY_SUM + 1 : QUERY_SUM + 2, here], dv.astype(F32))

    tile = pl.BlockSpec((BLOCK, GROUP * PAIR), lambda p: (block, p))
    flops = 10 * HEADS * BLOCK * BLOCK * HD
    given = () if into is None else into
    return pl.pallas_call(
        body,
        out_shape=(shape((count, width), BF),) * 3 + (shape((24, width), F32),),
        grid=(steps,),
        in_specs=[
            tile,
            pl.BlockSpec((BLOCK, GROUP * PAIR), lambda p: (block, steps + p)),
            pl.BlockSpec((BLOCK, GROUP * PAIR), lambda p: (block, 2 * steps + p)),
            tile,
            tile,
            pl.BlockSpec((1, 1, BLOCK), lambda p: (block, 0, 0)),
            pl.BlockSpec((1, GROUP, 2, BLOCK), lambda p: (block, p, 0, 0)),
            fixed(24, width),
        ]
        + [any_spec()] * len(given),
        out_specs=(tile,) * 3 + (fixed(24, width),),
        compiler_params=params("arbitrary"),
        cost_estimate=cost(4 * flops, 8 * count * width, HEADS * BLOCK * BLOCK),
        input_output_aliases={8 + index: index for index in range(len(given))},
    )(qkv, qkv, qkv, context, d_context, segment_row, lse, sums, *given)


def emit(plan, step, held, spot_ref, out_refs, sems):
    tile, blocks, (rows, cols), _, base = plan
    if blocks is None:
        target = out_refs[0].at[:, pl.ds(pl.multiple_of(step * tile, tile), tile)]
        pltpu.make_async_copy(held.at[step], target, sems.at[step]).start()
        return
    listed = blocks(step)
    for index, (row_at, column_at, x, core, z, y) in enumerate(listed):
        source = held.at[step, pl.ds(row_at, rows), pl.ds(column_at, cols)]
        sem = sems.at[step * len(listed) + index]
        far_x, far_y = x ^ spot_ref[0], y ^ spot_ref[3]
        first = far_x + core * (far_y - far_x)
        depth = z ^ spot_ref[2]
        slot = (depth & 1) + 2 * first + 4 * (far_x + far_y - first) + 8 * (depth >> 1)
        mine = (core ^ spot_ref[1]) == 0

        @pl.when(mine)
        def _():
            pltpu.make_async_copy(source, out_refs[0].at[slot, pl.ds(base, rows)], sem).start()

        @pl.when(jnp.logical_not(mine))
        def _():
            pltpu.make_async_copy(source, out_refs[1].at[slot, pl.ds(base, rows)], sem).start()


def emitted(plan, steps, held, out_refs, sems):
    tile, blocks, (rows, cols), _, base = plan
    if blocks is None:
        for step in range(steps):
            target = out_refs[0].at[:, pl.ds(step * tile, tile)]
            pltpu.make_async_copy(held.at[step], target, sems.at[step]).wait()
        return
    for index in range(32):
        source = held.at[0, pl.ds(0, rows), pl.ds(0, cols)]
        pltpu.make_async_copy(source, out_refs[0].at[0, pl.ds(base, rows)], sems.at[index]).wait()


def emit_shapes(plan, total, columns):
    _, blocks, (rows, cols), slot_rows, _ = plan
    if blocks is None:
        return (shape((total, columns), BF),)
    return (shape((16, slot_rows, cols), BF),) * 2


def clamped(width, last, tile=TILE):
    return pl.BlockSpec((tile, width), lambda i, s: (jnp.minimum(i, last), 0))


def project_out(spot, context, tokens, w_out, biases, gains):
    count, width = tokens.shape

    def body(spot_ref, c_ref, x_ref, bias_ref, gain_ref, w_ready, normal_ref, inverse_ref, low_ref):
        w_ref = w_ready()
        resid = x_ref[...].astype(F32) + (dot_nt(c_ref[...], w_ref[...]) + bias_ref[2:3])
        normal, inverse = layer_norm_parts(resid)
        normal_ref[...] = normal
        inverse_ref[...] = jnp.broadcast_to(inverse, inverse_ref.shape)
        low_ref[...] = (normal * gain_ref[0:1] + bias_ref[3:4]).astype(BF)

    return call(
        body, (count // WIDE_TILE,), spot, (context, tokens, biases, gains),
        (row(width, WIDE_TILE), row(width, WIDE_TILE), fixed(*biases.shape), fixed(*gains.shape)), [w_out],
        (shape((count, width), F32), shape((count, 128), F32), shape((count, width), BF)),
        (row(width, WIDE_TILE), row(128, WIDE_TILE), row(width, WIDE_TILE)),
        estimate=cost(2 * count * width * width, 10 * count * width),
    )


def ffn_in(spot, normed_low, w_in, in_bias):
    count, width = normed_low.shape
    wide = w_in[2][1]

    def body(spot_ref, x_ref, bias_ref, w_ready, hidden_ref, slope_ref):
        w_ref = w_ready()
        for start in range(0, wide, width):
            part = slice(start, start + width)
            pre = dot(x_ref[...], w_ref[:, part]) + bias_ref[:, part]
            cdf = 0.5 + 0.5 * lax.erf(pre * (1.0 / math.sqrt(2.0)))
            hidden_ref[:, part] = (pre * cdf).astype(BF)
            density = jnp.exp(pre * pre * -0.5) * (1.0 / math.sqrt(2.0 * math.pi))
            slope_ref[:, part] = (cdf + pre * density).astype(BF)

    return call(
        body, (count // TILE,), spot, (normed_low, in_bias), (row(width), fixed(1, wide)), [w_in],
        (shape((count, wide), BF),) * 2, (row(wide),) * 2,
        estimate=cost(2 * count * width * wide, 4 * count * wide, 2 * count * wide),
    )


def forward_rows(spot, hidden, normal_one, out_grad, w_back, biases, gains, plan):
    count, width = out_grad.shape
    wide = hidden.shape[1]
    steps = count // TILE
    tile = plan[0]
    columns = wide // tile
    shapes = emit_shapes(plan, width, wide)

    def body(spot_ref, h_ref, column_ref, n_ref, g_ref, bias_ref, gain_ref, wb_ready,
             out_ref, d_two_ref, d_low_ref, sums_ref, *refs):
        grads, (d_rows, turned, held, sems) = refs[: len(shapes)], refs[len(shapes) :]
        index = pl.program_id(0)
        zero_first(sums_ref)

        @pl.when(index < steps)
        def _():
            here = pl.ds(pl.multiple_of(index * TILE, TILE), TILE)
            resid = n_ref[...] * gain_ref[0:1] + bias_ref[3:4]
            w_ref = wb_ready()
            resid += dot_nt(h_ref[...], w_ref[...]) + bias_ref[4:5]
            normal, inverse = layer_norm_parts(resid)
            out_ref[...] = (normal * gain_ref[1:2] + bias_ref[5:6]).astype(BF)
            grad = g_ref[...].astype(F32)
            d_two = layer_norm_back(grad * gain_ref[1:2], normal, inverse)
            d_low = d_two.astype(BF)
            d_two_ref[...] = d_two
            d_low_ref[...] = d_low
            d_rows[here, :] = d_low
            add_rows(sums_ref.at[0:1], grad * normal)
            add_rows(sums_ref.at[1:2], grad)
            add_rows(sums_ref.at[2:3], d_low.astype(F32))

        @pl.when(index == steps)
        def _():
            turned[...] = d_rows[...].T

        @pl.when(index >= steps)
        def _():
            column = index - steps
            held[column] = dot(turned[...], column_ref[...]).astype(BF)
            emit(plan, column, held, spot_ref, grads, sems)

        @pl.when(index == steps + columns - 1)
        def _():
            emitted(plan, columns, held, grads, sems)

    last = steps - 1
    rows = lambda wide_: clamped(wide_, last)
    return call(
        body, (steps + columns,), spot, (hidden, hidden, normal_one, out_grad, biases, gains),
        (rows(wide), pl.BlockSpec((count, tile), lambda i, s: (0, jnp.maximum(i - steps, 0))),
         rows(width), rows(width), fixed(*biases.shape), fixed(*gains.shape)),
        [w_back],
        (shape((count, width), BF), shape((count, width), F32), shape((count, width), BF),
         shape((8, width), F32), *shapes),
        (rows(width), rows(width), rows(width), fixed(8, width), *[any_spec()] * len(shapes)),
        [pltpu.VMEM((count, width), BF),
         pltpu.VMEM((width, count), BF), pltpu.VMEM((columns, width, tile), BF),
         pltpu.SemaphoreType.DMA((32,))],
        cost(4 * count * width * wide, 14 * count * width + 4 * count * wide),
    )


def backward_rows(
    spot, d_low, slope, d_two, normal_one, inverse_one, normed_low, context, sums_two, w_back, w_in,
    w_out, gains, plan_in, plan_out,
):
    count, width = d_two.shape
    wide = slope.shape[1]
    steps = count // TILE
    tile_in, tile_out = plan_in[0], plan_out[0]
    columns_in, columns_out = wide // tile_in, width // tile_out
    shared = plan_in[1] is not None
    shapes = emit_shapes(plan_in, width, wide)
    if not shared:
        shapes += emit_shapes(plan_out, width, width)

    def body(spot_ref, dl_ref, s_ref, d2_ref, n_ref, i_ref, low_ref, c_ref, two_ref, gain_ref,
             wb_ready, wi_ready, wo_ready, d_one_ref, d_context_ref, sums_ref, *refs):
        grads = refs[: len(shapes)]
        d_pre, d_attn, turned, held_in, held_out, low_held, sems_in, sems_out, late = refs[
            len(shapes) :
        ]
        fetch_low = pltpu.make_async_copy(low_ref, low_held, late.at[0])
        grads_in, grads_out = (grads, grads) if shared else (grads[:1], grads[1:])
        index = pl.program_id(0)

        @pl.when(index == 0)
        def _():
            sums_ref[...] = jnp.zeros_like(sums_ref)
            sums_ref[0:8, :] = two_ref[...]
            fetch_low.start()

        @pl.when(index < steps)
        def _():
            here = pl.ds(pl.multiple_of(index * TILE, TILE), TILE)
            w_ref = wb_ready()
            pieces = []
            for start in range(0, wide, width):
                part = slice(start, start + width)
                d_hidden = dot(dl_ref[...], w_ref[:, part])
                piece = (d_hidden * s_ref[:, part].astype(F32)).astype(BF)
                d_pre[here, part] = piece
                pieces.append(piece)
                at = HIDDEN_SUM + start // width
                add_rows(sums_ref.at[at : at + 1], piece.astype(F32))
            w_ref = wi_ready()
            d_normed = d2_ref[...]
            for number, piece in enumerate(pieces):
                d_normed += dot_nt(piece, w_ref[:, number * width : (number + 1) * width])
            normal = n_ref[...]
            d_one = layer_norm_back(d_normed * gain_ref[0:1], normal, i_ref[:, 0:1])
            low = d_one.astype(BF)
            d_one_ref[...] = d_one
            d_attn[here, :] = low
            d_context_ref[...] = dot(low, wo_ready()[...]).astype(BF)
            add_rows(sums_ref.at[8:9], d_normed * normal)
            add_rows(sums_ref.at[9:10], d_normed)
            add_rows(sums_ref.at[10:11], low.astype(F32))

        @pl.when(index == steps)
        def _():
            fetch_low.wait()
            turned[...] = low_held[...].T

        @pl.when(jnp.logical_and(index >= steps, index < steps + columns_in))
        def _():
            column = index - steps
            at = pl.ds(pl.multiple_of(column * tile_in, tile_in), tile_in)
            held_in[column] = dot(turned[...], d_pre[:, at]).astype(BF)
            emit(plan_in, column, held_in, spot_ref, grads_in, sems_in)

        @pl.when(index == steps + columns_in)
        def _():
            turned[...] = d_attn[...].T

        @pl.when(index >= steps + columns_in)
        def _():
            column = index - steps - columns_in
            held_out[column] = dot(turned[...], c_ref[...]).astype(BF)
            emit(plan_out, column, held_out, spot_ref, grads_out, sems_out)

        @pl.when(index == steps + columns_in + columns_out - 1)
        def _():
            emitted(plan_in, columns_in, held_in, grads_in, sems_in)
            emitted(plan_out, columns_out, held_out, grads_out, sems_out)

    last, before = steps - 1, steps + columns_in
    rows = lambda wide_: clamped(wide_, last)
    return call(
        body, (steps + columns_in + columns_out,), spot,
        (d_low, slope, d_two, normal_one, inverse_one, normed_low, context, sums_two, gains),
        (rows(width), rows(wide), rows(width), rows(width), rows(128), any_spec(),
         pl.BlockSpec((count, tile_out), lambda i, s: (0, jnp.maximum(i - before, 0))),
         fixed(8, width), fixed(*gains.shape)),
        [w_back, w_in, w_out],
        (shape((count, width), F32), shape((count, width), BF), shape((24, width), F32), *shapes),
        (rows(width), rows(width), fixed(24, width), *[any_spec()] * len(shapes)),
        [pltpu.VMEM((count, wide), BF), pltpu.VMEM((count, width), BF),
         pltpu.VMEM((width, count), BF), pltpu.VMEM((columns_in, width, tile_in), BF),
         pltpu.VMEM((columns_out, width, tile_out), BF), pltpu.VMEM((count, width), BF),
         pltpu.SemaphoreType.DMA((32,)), pltpu.SemaphoreType.DMA((32,)),
         pltpu.SemaphoreType.DMA((1,))],
        cost(2 * count * width * (3 * wide + 2 * width), 18 * count * width + 2 * count * wide),
    )


def tokens_backward(spot, d_one, d_query, d_key, d_value, w_qkv):
    count, width = d_one.shape

    def body(spot_ref, d1_ref, q_ref, k_ref, v_ref, w_ready, out_ref):
        w_ref = w_ready()
        total = d1_ref[...] + dot(q_ref[...], w_ref[0:width, :])
        total += dot(k_ref[...], w_ref[width : 2 * width, :])
        total += dot(v_ref[...], w_ref[2 * width : 3 * width, :])
        out_ref[...] = total.astype(BF)

    return call(
        body, (count // TILE,), spot, (d_one, d_query, d_key, d_value), (row(width),) * 4, [w_qkv],
        shape((count, width), BF), row(width),
        estimate=cost(6 * count * width * width, 12 * count * width),
    )


def gradient(spot, lefts, right, plan):
    count, columns = right.shape
    width = lefts[0].shape[1]
    total = width * len(lefts)
    tile = plan[0]
    steps = columns // tile
    n_left = len(lefts)
    shapes = emit_shapes(plan, total, columns)

    def body(spot_ref, *refs):
        left_refs, right_ref = refs[:n_left], refs[n_left]
        grads = refs[n_left + 1 : n_left + 1 + len(shapes)]
        turned, held, sems = refs[-3:]
        step = pl.program_id(0)

        @pl.when(step == 0)
        def _():
            for index, ref in enumerate(left_refs):
                turned[index * width : (index + 1) * width, :] = ref[...].T

        for index in range(n_left):
            part = slice(index * width, (index + 1) * width)
            held[step, part, :] = dot(turned[part, :], right_ref[...]).astype(BF)
        emit(plan, step, held, spot_ref, grads, sems)

        @pl.when(step == steps - 1)
        def _():
            emitted(plan, steps, held, grads, sems)

    return call(
        body, (steps,), spot, (*lefts, right),
        (*[fixed(count, width)] * n_left, pl.BlockSpec((count, tile), lambda i, s: (0, i))), [],
        shapes, (any_spec(),) * len(shapes),
        [pltpu.VMEM((total, count), BF), pltpu.VMEM((steps, total, tile), BF),
         pltpu.SemaphoreType.DMA((32,))],
        cost(2 * count * total * columns, 2 * (count * (total + columns) + total * columns)),
    )


def widen(value):
    return value.astype(F32)


def exchange(value, stage):
    axes = ("x", "core", "z", "y")
    pairs = []
    for source in range(32):
        x, core, z, y = source >> 4, (source >> 3) & 1, (source >> 1) & 3, source & 1
        if stage in (Z1, Z2, Z3):
            z ^= {Z1: 1, Z2: 2, Z3: 3}[stage]
        elif stage == CORE:
            core ^= 1
        elif (stage == FIRST) == (core == 0):
            x ^= 1
        else:
            y ^= 1
        pairs.append((source, 16 * x + 8 * core + 2 * z + y))
    return lax.ppermute(value, axes, pairs)


class Parcel:
    def __init__(self, array, origins=((0, 0, 0, 0),)):
        self.array = array
        self.origins = tuple(origins)

    def moved(self, stage):
        def change(origin):
            core, second, first, depth = origin
            along_first = stage == (SECOND if core else FIRST)
            along_second = stage == (FIRST if core else SECOND)
            return (
                core ^ (stage == CORE),
                second ^ along_second,
                first ^ along_first,
                depth ^ {Z1: 1, Z2: 2}.get(stage, 0),
            )

        return Parcel(exchange(self.array, stage), [change(origin) for origin in self.origins])

    def __add__(self, other):
        return Parcel(jnp.concatenate([self.array, other.array]), self.origins + other.origins)


def sync(values, *parcels):
    values, arrays = lax.optimization_barrier((values, [parcel.array for parcel in parcels]))
    for parcel, array in zip(parcels, arrays):
        parcel.array = array
    return values


class Reduce:
    def __init__(self, near, far):
        self.near, self.far = near, Parcel(far)

    def send_core(self):
        self.core = Parcel(exchange(self.far.array, CORE))

    def sum(self, start, stop, *others):
        total = widen(self.near[start:stop]) + widen(self.core.array[start:stop])
        for parcel, at in others:
            total += widen(parcel.array[at : at + stop - start])
        return total

    def send(self, stage, start, stop, *others):
        return Parcel(exchange(self.sum(start, stop, *others).astype(BF), stage))

    def send_second_b(self):
        self.second_b = self.send(SECOND, 12, 16)

    def send_second_a(self):
        self.second_a = self.send(SECOND, 4, 8)

    def send_first_b(self):
        self.first_b = self.send(FIRST, 10, 12, (self.second_b, 2))

    def send_first_a(self):
        self.first_a = self.send(FIRST, 2, 4, (self.second_a, 2))

    def send_z2(self):
        self.z2 = self.send(Z2, 8, 10, (self.second_b, 0), (self.first_b, 0))

    def send_z1(self):
        self.z1 = self.send(Z1, 1, 2, (self.second_a, 1), (self.first_a, 1), (self.z2, 1))
        self.last = (self.z2, self.z1)

    def send_direct_b(self):
        self.z2 = self.send(Z2, 8, 9, (self.second_b, 0), (self.first_b, 0))
        self.z3 = self.send(Z3, 9, 10, (self.second_b, 1), (self.first_b, 1))

    def send_direct_a(self):
        self.z1 = self.send(Z1, 1, 2, (self.second_a, 1), (self.first_a, 1))
        self.last = (self.z1, self.z2, self.z3)

    def result(self):
        others = (self.second_a, self.first_a) + self.last
        return self.sum(0, 1, *[(parcel, 0) for parcel in others])[0]


def source_of(spot, origin):
    away, second, first, depth = origin
    core = spot[1] ^ away
    x = spot[0] ^ (first + core * (second - first))
    y = spot[3] ^ (second + core * (first - second))
    return core, x, 2 * (spot[2] ^ depth) + y


def weight_of(parcels, source_rows, place, dims):
    start, rows, cols = source_rows
    pieces, places = [], []
    for parcel in parcels:
        pieces.append(parcel.array)

        def at(spot_ref, ref, origins=parcel.origins):
            for index, origin in enumerate(origins):
                core, x, f = source_of(spot_ref, origin)
                row_at, column_at = place(x, core, f)
                yield (
                    ref.at[index, pl.ds(start, rows), :],
                    (
                        pl.ds(pl.multiple_of(row_at, 16), rows),
                        pl.ds(pl.multiple_of(column_at, 128), cols),
                    ),
                )

        places.append(at)
    return pieces, places, dims


def whole_weight(array):
    def at(spot_ref, ref):
        yield ref, (pl.ds(0, array.shape[0]), pl.ds(0, array.shape[1]))

    return [array], [at], array.shape


def device_slots(spot, origins):
    device = lax.broadcasted_iota(jnp.int32, (len(origins), len(origins)), 0)
    owners = []
    for origin in origins:
        core, x, f = source_of(spot, origin)
        owners.append(16 * x + 8 * core + f)
    return (device == jnp.stack(owners)[None, :]).astype(F32)


def small_vectors(every, shards):
    biases, in_bias, gains = shards
    devices = every.shape[0]
    first, second = biases.size, biases.size + in_bias.size
    third = second + gains.size
    return (
        every[:, :first].reshape(devices, 6, -1).transpose(1, 0, 2).reshape(6, -1),
        every[:, first:second].reshape(1, -1),
        every[:, second:third].reshape(devices, 2, -1).transpose(1, 0, 2).reshape(2, -1),
    )


def on_device(sizes, tokens, segment_ids, w_qkv, w_out, w_in, w_back, biases, in_bias, gains, out_grad):
    axes = ("x", "core", "z", "y")
    dp_axes, fsdp_axes = ("x", "core"), ("z", "y")
    devices = math.prod(sizes)
    by_permute = sizes == (2, 2, 4, 2)
    count, width = tokens.shape
    wide = w_back.shape[0] * sizes[0] * sizes[1]
    blocks = range(count // BLOCK)
    spot = jnp.stack([lax.axis_index(axis) for axis in axes]).astype(jnp.int32)
    core = spot[1]
    shards = (biases, in_bias, gains)
    segment_row = segment_ids.reshape(count // BLOCK, 1, BLOCK)

    qkv_cols, out_cols = w_qkv.shape[1], w_out.shape[1]
    pair_cols = 2 * w_qkv.shape[0]
    in_rows, in_cols = w_in.shape
    back_rows, back_cols = w_back.shape
    half_q, half_o = qkv_cols // 2, out_cols // 2

    if by_permute:

        def paired(turned):
            half = turned.shape[0] // 2
            first, second = turned[:half], turned[half:]
            mine = jnp.where(core == 0, first, second)
            other = exchange(jnp.where(core == 0, second, first), CORE)
            return jnp.where(
                core == 0,
                jnp.concatenate([mine, other], axis=1),
                jnp.concatenate([other, mine], axis=1),
            )

        to_qkv = Parcel(paired(w_qkv.T)[None])
        qkv_z1 = to_qkv.moved(Z1)
        own_vectors, w_in = sync(((biases, in_bias, gains), w_in), to_qkv)
        own_small = jnp.concatenate([part.reshape(-1) for part in own_vectors])
        to_small = Parcel(jnp.pad(own_small, (0, 1024 - own_small.size)).reshape(1, 8, 128))
        to_small += to_small.moved(CORE)
        w_in, w_out, w_back = sync((w_in, w_out, w_back), qkv_z1, to_small)
        qkv_near = to_qkv + qkv_z1
        qkv_z2 = qkv_near.moved(Z2)
        qkv_first_a = qkv_near.moved(FIRST)
        to_small += to_small.moved(FIRST)
        to_in = Parcel(jnp.concatenate([w_in, paired(w_out.T)], axis=0)[None])
        to_back = Parcel(w_back.T[None])
        sync((), qkv_first_a, to_small, to_in)
        qkv_a = qkv_near + qkv_first_a
        qkv_second_a = qkv_a.moved(SECOND)
        in_z1 = to_in.moved(Z1)
        to_small += to_small.moved(SECOND)
        sync((), qkv_z2)
        qkv_first_b = qkv_z2.moved(FIRST)
        sync((), qkv_z2, to_small)
        to_small += to_small.moved(Z1)
        sync((), qkv_first_b, to_small)
        qkv_b = qkv_z2 + qkv_first_b
        qkv_second_b = qkv_b.moved(SECOND)
        to_small += to_small.moved(Z2)
        sync((), qkv_first_b, qkv_second_a, to_small, in_z1)
        qkv_core_a = qkv_a.moved(CORE), qkv_second_a.moved(CORE)
        in_near = to_in + in_z1
        in_z2 = in_near.moved(Z2)
        sync((), qkv_second_b, in_near, to_back)
        qkv_core_b = qkv_b.moved(CORE), qkv_second_b.moved(CORE)
        in_first_a = in_near.moved(FIRST)
        back_z1 = to_back.moved(Z1)
        tokens = sync(tokens, *qkv_core_a, *qkv_core_b)
        qkv_parcels = (
            qkv_a, qkv_second_a, qkv_b, qkv_second_b, *qkv_core_a, *qkv_core_b
        )
        qkv_weight = weight_of(
            qkv_parcels, (0, half_q, pair_cols),
            lambda x, c, f: (f * qkv_cols + c * half_q, x * pair_cols), (3 * width, width),
        )
        slots = device_slots(spot, to_small.origins)
        arrived = widen(to_small.array).reshape(32, 1024)
        every = jnp.dot(slots, arrived, precision=lax.Precision.HIGHEST)

        def back_blocks(index):
            return [(f * back_cols, 0, index >> 1, index & 1, f >> 1, f & 1) for f in range(8)]

        def in_blocks(index):
            return [
                ((2 * x + c) * in_rows, y * in_cols, x, c, index, y)
                for x in range(2) for c in range(2) for y in range(2)
            ]

        def out_blocks(index):
            return [
                (f * out_cols + c * half_o, 0, index, c, f >> 1, f & 1)
                for f in range(8) for c in range(2)
            ]

        def qkv_blocks(index):
            return [
                (f * qkv_cols + c * half_q, 0, index, c, f >> 1, f & 1)
                for f in range(8) for c in range(2)
            ]

        plans = {
            "back": (back_rows, back_blocks, (back_cols, back_rows), back_cols, 0),
            "in": (2 * in_cols, in_blocks, (in_rows, in_cols), in_rows + half_o, 0),
            "out": (pair_cols, out_blocks, (half_o, pair_cols), in_rows + half_o, in_rows),
            "qkv": (pair_cols, qkv_blocks, (half_q, pair_cols), half_q, 0),
        }
    else:

        def full(shard):
            return lax.all_gather(
                lax.all_gather(shard, fsdp_axes, axis=1, tiled=True), dp_axes, axis=0, tiled=True
            )

        qkv_weight = whole_weight(full(w_qkv).T)
        out_weight = whole_weight(full(w_out).T)
        in_weight = whole_weight(full(w_in))
        back_weight = whole_weight(full(w_back).T)
        own_small = jnp.concatenate([biases.reshape(-1), in_bias, gains.reshape(-1)])
        every = widen(lax.all_gather(own_small, axes, axis=0, tiled=False))
        plans = {name: (width // 2, None, (0, 0), 0, 0) for name in ("back", "in", "out", "qkv")}

    bias_values, hidden_bias, gain_values = small_vectors(every, shards)
    qkv_bias = jnp.concatenate(
        [bias_values[0:1], jnp.zeros((1, width), F32), bias_values[1:2]], axis=1
    )

    qkv = project_qkv(spot, tokens, qkv_weight, qkv_bias)
    if by_permute:
        qkv = sync(qkv, in_first_a, in_z2, back_z1)
        in_a = in_near + in_first_a
        in_second_a = in_a.moved(SECOND)
        in_first_b = in_z2.moved(FIRST)
        back_near = to_back + back_z1
        back_z2 = back_near.moved(Z2)
    attended = None
    for block in blocks:
        attended = attend_forward(block, qkv, segment_row, attended)
        if by_permute and block == 0:
            attended = sync(attended, in_second_a, in_first_b, back_z2)
            in_b = in_z2 + in_first_b
            in_second_b = in_b.moved(SECOND)
            in_core = in_a.moved(CORE), in_second_a.moved(CORE), in_b.moved(CORE)
            back_first_a = back_near.moved(FIRST)
    context, lse = attended
    if by_permute:
        context = sync(context, in_second_b, *in_core, back_first_a)
        in_cross = in_second_b.moved(CORE)
        back_a = back_near + back_first_a
        back_second_a = back_a.moved(SECOND)
        back_first_b = back_z2.moved(FIRST)
        context = sync(context, in_cross)
        in_parcels = (in_a, in_second_a, in_b, in_second_b, *in_core, in_cross)
        in_weight = weight_of(
            in_parcels, (0, in_rows, in_cols),
            lambda x, c, f: ((2 * x + c) * in_rows, f * in_cols), (width, wide),
        )
        out_weight = weight_of(
            in_parcels, (in_rows, half_o, pair_cols),
            lambda x, c, f: (f * out_cols + c * half_o, x * pair_cols), (width, width),
        )
    normal_one, inverse_one, normed_low = project_out(
        spot, context, tokens, out_weight, bias_values, gain_values
    )
    if by_permute:
        normed_low = sync(normed_low, back_second_a, back_first_b)
        back_b = back_z2 + back_first_b
        back_second_b = back_b.moved(SECOND)
        back_core = back_a.moved(CORE), back_second_a.moved(CORE), back_b.moved(CORE)
    hidden, slope = ffn_in(spot, normed_low, in_weight, hidden_bias)
    if by_permute:
        hidden = sync(hidden, back_second_b, *back_core)
        back_cross = back_second_b.moved(CORE)
        back_weight = weight_of(
            (back_a, back_second_a, back_b, back_second_b, *back_core, back_cross),
            (0, back_cols, back_rows),
            lambda x, c, f: (f * back_cols, (2 * x + c) * back_rows), (width, wide),
        )
    layer_out, d_two, d_low, sums_two, *grad_back = forward_rows(
        spot, hidden, normal_one, out_grad, back_weight, bias_values, gain_values, plans["back"]
    )
    if by_permute:
        from_back = Reduce(*grad_back)
        d_low = sync(d_low, from_back.far)
        from_back.send_core()
    d_one, d_context, small, *grads_in = backward_rows(
        spot, d_low, slope, d_two, normal_one, inverse_one, normed_low, context, sums_two,
        back_weight, in_weight, out_weight, gain_values, plans["in"], plans["out"],
    )
    if by_permute:
        from_in = Reduce(*grads_in)
        d_context = sync(d_context, from_back.core, from_in.far)
        from_back.send_second_b()
        from_back.send_second_a()
        from_in.send_core()
    else:
        grad_in, grad_out = grads_in
        grad_back, = grad_back
    attended = None
    for block in blocks:
        *attended, small = attend_backward(
            block, qkv, segment_row, lse, context, d_context, small, attended
        )
        if by_permute and block == 0:
            attended = sync(attended, from_back.second_a, from_back.second_b, from_in.core)
            from_back.send_first_b()
            from_back.send_first_a()
            from_in.send_second_b()
        elif by_permute:
            attended, small = sync(
                (attended, small), from_back.first_a, from_back.first_b, from_in.second_b
            )
            from_in.send_second_a()
            from_in.send_first_b()
            from_back.send_z2()
            small_sent = Parcel(small).moved(CORE)
    grad_qkv = gradient(spot, attended, tokens, plans["qkv"])
    if by_permute:
        from_qkv = Reduce(*grad_qkv)
        small = sync(small, from_qkv.far, small_sent, from_in.second_a, from_in.first_b)
        from_qkv.send_core()
        small = small + small_sent.array
        small_sent = Parcel(small).moved(Z1)
        from_in.send_z2()
        from_in.send_first_a()
        d_one = sync(d_one, from_qkv.core)
        from_qkv.send_second_b()
        from_qkv.send_second_a()
    else:
        grad_qkv, = grad_qkv
    tokens_grad = tokens_backward(spot, d_one, *attended, qkv_weight)

    if by_permute:

        def unpaired(sums):
            half = sums.shape[1] // 2
            left, right = sums[:, :half], sums[:, half:]
            mine = jnp.where(core == 0, left, right)
            other = widen(exchange(jnp.where(core == 0, right, left).astype(BF), CORE))
            return jnp.where(
                core == 0,
                jnp.concatenate([mine, other], axis=0),
                jnp.concatenate([other, mine], axis=0),
            )

        tokens_grad = sync(
            tokens_grad, from_qkv.second_b, from_qkv.second_a, from_in.z2, from_in.first_a
        )
        from_qkv.send_first_b()
        from_qkv.send_first_a()
        small = small + small_sent.array
        small_sent = Parcel(small).moved(SECOND)
        small = sync(small, from_qkv.first_b, from_qkv.first_a)
        from_qkv.send_direct_b()
        from_qkv.send_direct_a()
        from_back.send_z1()
        from_in.send_z1()
        small = sync(small, small_sent)
        small = small + small_sent.array
        small_sent = Parcel(small).moved(FIRST)
        small = sync(small, small_sent, from_back.z1)
        small = small + small_sent.array
        small_sent = Parcel(small).moved(Z2)
        small = sync(small, small_sent, from_in.z1)
        small = small + small_sent.array
        sums_in = from_in.result()
        own_back = from_back.result().T
        own_in = sums_in[:in_rows]
        own_out = unpaired(sums_in[in_rows:]).T
        own_qkv = unpaired(from_qkv.result()).T
    else:

        def scattered(total):
            part = lax.psum_scatter(total, dp_axes, scatter_dimension=0, tiled=True)
            part = lax.psum_scatter(part, fsdp_axes, scatter_dimension=1, tiled=True)
            return widen(part)

        own_back = scattered(grad_back.T)
        own_in = scattered(grad_in)
        own_out = scattered(grad_out.T)
        own_qkv = scattered(grad_qkv.T)
        small = lax.psum(small, axes)
    device = lax.axis_index(axes)
    queries = small[QUERY_SUM : QUERY_SUM + 2]
    bias_total = jnp.concatenate([queries, small[10:11], small[9:10], small[2:3], small[1:2]])
    gain_total = jnp.concatenate([small[8:9], small[0:1]])
    own_bias = lax.dynamic_slice_in_dim(bias_total, device * biases.shape[1], biases.shape[1], 1)
    own_gain = lax.dynamic_slice_in_dim(gain_total, device * gains.shape[1], gains.shape[1], 1)
    own_hidden = lax.dynamic_slice_in_dim(
        small[HIDDEN_SUM:QUERY_SUM].reshape(-1), device * in_bias.shape[0], in_bias.shape[0], 0
    )
    return (
        layer_out, tokens_grad, own_qkv, own_out, own_in, own_back, own_bias, own_hidden, own_gain,
    )


def solution(mesh):
    dp, fsdp = mesh.devices.shape
    sizes = (dp // 2, 2, fsdp // 2, 2)
    split = Mesh(mesh.devices.reshape(sizes), ("x", "core", "z", "y"))
    outer, inner = ("x", "core"), ("z", "y")
    every = outer + inner
    rows = P(every, None)
    weight = P(outer, inner)
    vectors = P(None, every)

    def placed(*arrays):
        return on_device(sizes, *arrays)

    return jax.shard_map(
        placed,
        mesh=split,
        in_specs=(rows, rows, weight, weight, weight, weight, vectors, P(every), vectors, rows),
        out_specs=(rows, rows, weight, weight, weight, weight, vectors, P(every), vectors),
        check_vma=False,
    )
```
